32 devices in a mesh: rows: 8 (over z, x), seq: 4 (over y, core).
Axes of the slice: x: 2, y: 2, z: 4, core: 2. Of those that a mesh axis runs over, the one named last changes fastest.
Arguments:
- inputs: bfloat16 [8, 2048, 1024], P('rows', 'seq'), may hold values from -6 to 6
- skip_feats: bfloat16 [8, 2048, 1024], P('rows', 'seq'), may hold values from -6 to 6
- seg_ids: int32 [8, 2048], P('rows'), may hold values from 0 to 5, never falling along the last dimension, each value on 1 to 682 neighbouring positions
- frame_valid: int32 [8, 2048], P('rows'), may hold values 0 or 1
- w_skip: bfloat16 [2048, 1024], replicated, may hold values from -0.125 to 0.125
- gain_one: bfloat16 [1024], replicated, may hold values from 0.5 to 1.5
- w_qkv: bfloat16 [1024, 3072], replicated, may hold values from -0.1875 to 0.1875
- w_out: bfloat16 [1024, 1024], replicated, may hold values from -0.5 to 0.5
- gain_two: bfloat16 [1024], replicated, may hold values from 0.5 to 1.5
- w_up: bfloat16 [1024, 4096], replicated, may hold values from -0.1875 to 0.1875
- b_up: bfloat16 [4096], replicated, may hold values from -3 to 3
- w_down: bfloat16 [4096, 1024], replicated, may hold values from -0.09375 to 0.09375
- b_down: bfloat16 [1024], replicated, may hold values from -2 to 2
- cotangent: bfloat16 [8, 2048, 1024], P('rows', 'seq'), may hold values from -6 to 6
Outputs:
- output: bfloat16 [8, 2048, 1024], P('rows', 'seq')
- input_grad: bfloat16 [8, 2048, 1024], P('rows', 'seq')
- skip_grad: bfloat16 [8, 2048, 1024], P('rows', 'seq')
- w_skip_grad: float32 [2048, 1024], P(('rows', 'seq'))
- gain_one_grad: float32 [1024], P(('rows', 'seq'))
- w_qkv_grad: float32 [1024, 3072], P(('rows', 'seq'))
- w_out_grad: float32 [1024, 1024], P(('rows', 'seq'))
- gain_two_grad: float32 [1024], P(('rows', 'seq'))
- w_up_grad: float32 [1024, 4096], P(('rows', 'seq'))
- b_up_grad: float32 [4096], P(('rows', 'seq'))
- w_down_grad: float32 [4096, 1024], P(('rows', 'seq'))
- b_down_grad: float32 [1024], P(('rows', 'seq'))
The draws below stay inside these ranges and needn't reach their ends.
Inputs may be any that keep to these rules, and one draw needn't show every extreme that they name: `seg_ids`: in each row the segment numbers never fall along the frames; every segment has 1 to 682 frames and one has exactly 682.
All inputs are finite; a program needn't handle non-finite values. No bound on the sum of `frame_valid` on one device may be relied on, other than what follows from the above.
Results may differ from the reference program's by a relative error of at most 0.015.
Values may be sent and summed in bfloat16 or wider, within the bound.
A program may use at most 192 MiB of HBM per device.

```python
import math
import jax
import jax.numpy as jnp
import numpy as np
from jax import lax

D = 1024
H = 16
HD = 64
FF = 4096
U = 6
L = 2048
ROWS = 8
MOST = 682
QB = 512


def with_ends(drawn, own_key, low, top_value):
    longest = drawn.shape.index(max(drawn.shape))
    spots = []
    for shift in (0, 1):
        where = [jax.random.randint(jax.random.fold_in(own_key, axis), (), 0, length) for axis, length in enumerate(drawn.shape)]
        where[longest] = (where[longest] + shift) % drawn.shape[longest]
        spots.append(tuple(where))
    return drawn.at[spots[0]].set(low).at[spots[1]].set(top_value)


def block_levels(key, dims, cuts, smallest, largest):
    level = 1.0
    for axis_at, blocks in cuts:
        heights = jax.random.uniform(jax.random.fold_in(jax.random.fold_in(key, 6), axis_at), (blocks,), jnp.float32, smallest / len(cuts), largest / len(cuts))
        level = level * jnp.repeat(jnp.exp(heights), dims[axis_at] // blocks).reshape((-1,) + (1,) * (len(dims) - 1 - axis_at))
    return level


def profile(amount, total, bound, lean):
    portions = [(1 << 20) // math.isqrt(grade ** lean) + 1 for grade in range(2, amount + 1)]
    surplus, given = total - bound - (amount - 1), [1] * (amount - 1)
    while surplus > 0:
        free = [i for i in range(amount - 1) if given[i] < bound]
        whole, left = sum([portions[i] for i in free]), surplus
        for i in free:
            more = min(bound - given[i], max(1, left * portions[i] // whole), surplus)
            given[i] = given[i] + more
            surplus = surplus - more
    return np.array([bound] + given)


def uneven(key, amount, total, bound, slope):
    if amount == 2:
        one = jax.random.randint(key, (), max(1, total - bound), min(bound, total - 1) + 1)
        return jnp.stack([one, total - one])
    tallies = jnp.asarray(profile(amount, total, bound, slope), jnp.int32)
    couples = (amount - 1) // 2
    giver, sink = tallies[1:1 + 2 * couples:2], tallies[2:2 + 2 * couples:2]
    slack = jnp.minimum(giver - 1, bound - sink)
    passed = jax.random.randint(jax.random.fold_in(key, 1), (couples,), 0, 1 << 20) % (slack + 1)
    tallies = tallies.at[1:1 + 2 * couples:2].set(giver - passed).at[2:2 + 2 * couples:2].set(sink + passed)
    return tallies[jax.random.permutation(jax.random.fold_in(key, 2), amount)]


def bell_draw(key, shape, scale, most, pieces=(), dtype=jnp.bfloat16):
    entries = jax.random.normal(key, shape, jnp.float32) * scale
    if len(pieces) > 0:
        entries = block_levels(key, shape, pieces, -0.22, 0.18) * entries
    return jnp.clip(entries, min=-most, max=most).astype(dtype)


def setup_inputs(seed: int = 0) -> dict:
    keys = jax.random.split(jax.random.key(seed), 15)
    return {
        "inputs": bell_draw(keys[0], (ROWS, L, D), 1.0, 6.0, ((0, 8), (1, 4))),
        "skip_feats": bell_draw(keys[1], (ROWS, L, D), 1.0, 6.0, ((0, 8), (1, 4))),
        "seg_ids": jax.vmap(lambda own: jnp.searchsorted(jnp.cumsum(uneven(own, U, L, MOST, 2)), jnp.arange(L), side="right"))(jax.random.split(keys[2], ROWS)).reshape((ROWS, L)).astype(jnp.int32),
        "frame_valid": with_ends((jax.random.randint(keys[3], (ROWS, L), 0, 8) < 7).astype(jnp.int32), jax.random.fold_in(keys[3], 1), 0, 1),
        "w_skip": bell_draw(keys[4], (2 * D, D), (2 * D) ** -0.5, 0.125),
        "gain_one": jnp.clip(1.0 + 0.1 * jax.random.normal(keys[5], (D,), jnp.float32), 0.5, 1.5).astype(jnp.bfloat16),
        "w_qkv": bell_draw(keys[6], (D, 3 * D), D ** -0.5, 0.1875),
        "w_out": bell_draw(keys[7], (D, D), (D // 8) ** -0.5, 0.5),
        "gain_two": jnp.clip(1.0 + 0.1 * jax.random.normal(keys[8], (D,), jnp.float32), 0.5, 1.5).astype(jnp.bfloat16),
        "w_up": bell_draw(keys[9], (D, FF), D ** -0.5, 0.1875),
        "b_up": bell_draw(keys[10], (FF,), 0.5, 3.0),
        "w_down": bell_draw(keys[11], (FF, D), FF ** -0.5, 0.09375),
        "b_down": bell_draw(keys[12], (D,), 0.3, 2.0),
        "cotangent": bell_draw(keys[13], (ROWS, L, D), 1.0, 6.0, ((0, 8), (1, 4))),
    }


@jax.custom_vjp
def low(v):
    return lax.optimization_barrier(v.astype(jnp.bfloat16)).astype(jnp.float32)

@jax.custom_vjp
def low_back(v):
    return v

def low_keep(v):
    return (low(v), None)

def low_pass(kept, grad):
    return (grad,)

def back_keep(v):
    return (v, None)

def back_low(kept, grad):
    return (low(grad),)
low.defvjp(low_keep, low_pass)
low_back.defvjp(back_keep, back_low)
epsilon = 1e-05

def matmul(left, right):
    return jnp.dot(left, right, precision=lax.Precision.HIGHEST)

def normalize(value, gain_vec):
    center = value - lax.optimization_barrier(jnp.mean(value, axis=-1, keepdims=True))
    spread = lax.optimization_barrier(jnp.mean(center * center, axis=-1, keepdims=True))
    return center * lax.rsqrt(spread + epsilon) * gain_vec

def attend(queries, all_keys, all_values, seg_row, valid_row):
    slopes = jnp.exp2(-8.0 * (jnp.arange(H) + 1).astype(jnp.float32) / H)
    score_scale = 1.0 / math.sqrt(HD)
    key_pos = jnp.arange(L).astype(jnp.int32)
    blocks = L // QB
    q_blocks = queries.reshape(blocks, QB, H, HD)
    pos_blocks = key_pos.reshape(blocks, QB)
    seg_blocks = seg_row.reshape(blocks, QB)

    def one_block(block_in):
        q_blk, pos_blk, seg_blk = block_in
        scores = jnp.einsum('qhd,khd->hqk', q_blk, all_keys, precision=lax.Precision.HIGHEST) * score_scale
        distance = jnp.abs(pos_blk[:, None] - key_pos[None, :]).astype(jnp.float32)
        scores = low_back(scores - slopes[:, None, None] * distance[None])
        allowed = (seg_blk[:, None] == seg_row[None, :]) & ((valid_row[None, :] == 1) | (pos_blk[:, None] == key_pos[None, :]))
        scores = jnp.where(allowed[None], scores, -jnp.inf)
        peak = lax.optimization_barrier(jnp.max(scores, axis=-1, keepdims=True))
        log_total = peak + jnp.log(lax.optimization_barrier(jnp.sum(jnp.exp(scores - peak), axis=-1, keepdims=True)))
        attn_probs = low(jnp.exp(scores - log_total))
        return jnp.einsum('hqk,khd->qhd', attn_probs, all_values, precision=lax.Precision.HIGHEST)
    attended = lax.map(jax.checkpoint(one_block), (q_blocks, pos_blocks, seg_blocks))
    return attended.reshape(L, D)

def layer(params, row_inputs, row_skips, seg_row, valid_row):
    w_skip, gain_one, w_qkv, w_out, gain_two, w_up, b_up, w_down, b_down = params
    joined = jnp.concatenate([row_inputs, row_skips], axis=-1)
    stem_out = low_back(matmul(joined, w_skip))
    normed = low(normalize(stem_out, gain_one))
    packed = low_back(low(matmul(normed, w_qkv)))
    queries = packed[:, :D].reshape(L, H, HD)
    all_keys = packed[:, D:2 * D].reshape(L, H, HD)
    all_values = packed[:, 2 * D:].reshape(L, H, HD)
    mixed_out = low_back(low(attend(queries, all_keys, all_values, seg_row, valid_row)))
    middle = stem_out + low_back(matmul(mixed_out, w_out))
    second = low(normalize(middle, gain_two))
    hidden = low_back(matmul(second, w_up) + b_up)
    active = low(jax.nn.gelu(hidden, approximate=False))
    return middle + matmul(active, w_down) + b_down

def reference(inputs, skip_feats, seg_ids, frame_valid, w_skip, gain_one, w_qkv, w_out, gain_two, w_up, b_up, w_down, b_down, cotangent):
    params = (w_skip.astype(jnp.float32), gain_one.astype(jnp.float32), w_qkv.astype(jnp.float32), w_out.astype(jnp.float32), gain_two.astype(jnp.float32), w_up.astype(jnp.float32), b_up.astype(jnp.float32), w_down.astype(jnp.float32), b_down.astype(jnp.float32))

    def one_row(totals, row_data):
        row_inputs, row_skips, seg_row, valid_row, row_cot = row_data

        def row_layer(weights, first_in, second_in):
            return layer(weights, first_in, second_in, seg_row, valid_row)
        result, pullback = jax.vjp(row_layer, params, row_inputs.astype(jnp.float32), row_skips.astype(jnp.float32))
        grad_params, grad_inputs, grad_skips = pullback(row_cot.astype(jnp.float32))
        totals = jax.tree.map(jnp.add, totals, grad_params)
        return (totals, (result.astype(jnp.bfloat16), grad_inputs.astype(jnp.bfloat16), grad_skips.astype(jnp.bfloat16)))
    zero_grads = jax.tree.map(jnp.zeros_like, params)
    totals, outputs = lax.scan(one_row, zero_grads, (inputs, skip_feats, seg_ids, frame_valid, cotangent))
    return (outputs[0], outputs[1], outputs[2], totals[0], totals[1], totals[2], totals[3], totals[4], totals[5], totals[6], totals[7], totals[8])
```

```python
import functools
import math

import jax
import jax.numpy as jnp
from jax import lax
from jax.experimental import pallas as pl
from jax.experimental.pallas import tpu as pltpu
from jax.sharding import PartitionSpec as P

D = 1024
H = 16
HD = 64
MOST = 682

epsilon = 1e-05

F32 = jnp.float32
BF16 = jnp.bfloat16
LOG2E = 1.4426950408889634
FAR = 1e30
MESH = pl.DeviceIdType.MESH
VMEM = pltpu.MemorySpace.VMEM
SMEM = pltpu.MemorySpace.SMEM
HBM = pltpu.MemorySpace.HBM


def norm_forward(value, gain_vec):
    center = value - jnp.mean(value, axis=-1, keepdims=True)
    spread = jnp.mean(center * center, axis=-1, keepdims=True)
    inverse = lax.rsqrt(spread + epsilon)
    unit = center * inverse
    return (unit, inverse, unit * gain_vec)


def norm_backward(upstream, unit, inverse, gain_vec):
    scaled = upstream * gain_vec
    gain_grad = jnp.sum(upstream * unit, axis=tuple(range(upstream.ndim - 1)))
    inner = (
        scaled
        - jnp.mean(scaled, axis=-1, keepdims=True)
        - unit * jnp.mean(scaled * unit, axis=-1, keepdims=True)
    )
    return (inverse * inner, gain_grad)


def gelu_exact(value):
    return jax.nn.gelu(value, approximate=False)


def mm(equation, left, right):
    return jnp.einsum(equation, left, right, preferred_element_type=F32)


def dot(left, right):
    return jnp.dot(left, right, preferred_element_type=F32)


def set_distances(dist, key_at, query_at, key_code, query_seg):
    keys, queries = dist.shape
    rows = lax.broadcasted_iota(jnp.int32, (keys, queries), 0) + key_at
    cols = lax.broadcasted_iota(jnp.int32, (keys, queries), 1) + query_at
    apart = jnp.abs(rows - cols)
    allowed = (key_code == query_seg) | (apart == 0)
    dist[...] = jnp.where(allowed, apart.astype(F32), FAR)


def wide(code, queries):
    return jnp.concatenate([code] * (queries // 128), axis=1) if queries > 128 else code


def blocks_meet(kspan, qspan, j, i):
    return (kspan[0, j] <= qspan[1, i]) & (kspan[1, j] >= qspan[0, i])


def attend_kernel(
    bq, bk, heads, kspan, qspan, slopes, qt, kv, vt, kcode, qseg, out, lse, dist, acc, top, total
):
    width = heads * HD
    c1 = LOG2E / math.sqrt(HD)
    blank = jnp.zeros((HD, bq), BF16)

    def q_block(i, _):
        qs = pl.multiple_of(i * bq, bq)
        acc[...] = jnp.zeros_like(acc)
        total[...] = jnp.zeros_like(total)
        top[...] = jnp.full_like(top, -3e38)

        def k_block(j, _):
            @pl.when(blocks_meet(kspan, qspan, j, i))
            def _():
                ks = pl.multiple_of(j * bk, bk)
                set_distances(
                    dist,
                    kspan[2, j],
                    qspan[2, i],
                    wide(kcode[pl.ds(ks, bk), :], bq),
                    qseg[0:1, pl.ds(qs, bq)],
                )
                for h in range(heads):
                    mine = qt[pl.ds(HD * h, HD), pl.ds(qs, bq)]
                    pair = [mine, blank] if h % 2 == 0 else [blank, mine]
                    score = dot(
                        kv[pl.ds(ks, bk), pl.ds(128 * (h // 2), 128)],
                        jnp.concatenate(pair, axis=0),
                    )
                    score = score * c1 - dist[...] * slopes[h]
                    was = top[h : h + 1, :]
                    now = jnp.maximum(was, jnp.max(score, axis=0, keepdims=True))
                    prob = jnp.exp2(score - now)
                    fade = jnp.exp2(was - now)
                    total[h : h + 1, :] = total[h : h + 1, :] * fade + jnp.sum(
                        prob, axis=0, keepdims=True
                    )
                    top[h : h + 1, :] = now
                    acc[pl.ds(HD * h, HD), :] = acc[pl.ds(HD * h, HD), :] * fade + dot(
                        vt[pl.ds(HD * h, HD), pl.ds(ks, bk)], prob.astype(BF16)
                    )

            return 0

        lax.fori_loop(0, kv.shape[0] // bk, k_block, 0)
        for h in range(heads):
            acc[pl.ds(HD * h, HD), :] = acc[pl.ds(HD * h, HD), :] * (1.0 / total[h : h + 1, :])
        lse[:, pl.ds(qs, bq)] = top[...] + jnp.log2(total[...])
        out[pl.ds(qs, bq), :] = acc[...].T.astype(BF16)
        return 0

    lax.fori_loop(0, qt.shape[1] // bq, q_block, 0)


def attend(kspan, qspan, slopes, qt, kv, vt, kcode, qseg, bq, bk, heads):
    frames = qt.shape[1]
    vm, sm = pl.BlockSpec(memory_space=VMEM), pl.BlockSpec(memory_space=SMEM)
    return pl.pallas_call(
        functools.partial(attend_kernel, bq, bk, heads),
        out_shape=(
            jax.ShapeDtypeStruct((frames, heads * HD), BF16),
            jax.ShapeDtypeStruct((heads, frames), F32),
        ),
        in_specs=[sm] * 3 + [vm] * 5,
        out_specs=(vm, vm),
        scratch_shapes=[
            pltpu.VMEM((bk, bq), F32),
            pltpu.VMEM((heads * HD, bq), F32),
            pltpu.VMEM((heads, bq), F32),
            pltpu.VMEM((heads, bq), F32),
        ],
        name="attend",
        cost_estimate=pl.CostEstimate(
            flops=8_000_000_000, bytes_accessed=8_000_000, transcendentals=4_000_000
        ),
        compiler_params=pltpu.CompilerParams(vmem_limit_bytes=32 << 20),
    )(kspan, qspan, slopes, qt, kv, vt, kcode, qseg)


def attend_back_kernel(
    bq,
    bk,
    heads,
    kspan,
    qspan,
    slopes,
    q,
    qt,
    kv,
    kt,
    grad,
    gradt,
    lse,
    delta,
    kcode,
    qseg,
    dq,
    dkv,
    dist,
    dqt,
    sums,
):
    width = heads * HD
    c1 = LOG2E / math.sqrt(HD)
    scale = 1.0 / math.sqrt(HD)
    blank = jnp.zeros((HD, bq), BF16)
    lane = lax.broadcasted_iota(jnp.int32, (bq, 128), 1)
    sums[...] = jnp.zeros_like(sums)

    def q_block(i, _):
        qs = pl.multiple_of(i * bq, bq)
        dqt[...] = jnp.zeros_like(dqt)

        def k_block(j, _):
            @pl.when(blocks_meet(kspan, qspan, j, i))
            def _():
                ks = pl.multiple_of(j * bk, bk)
                set_distances(
                    dist,
                    kspan[2, j],
                    qspan[2, i],
                    wide(kcode[pl.ds(ks, bk), :], bq),
                    qseg[0:1, pl.ds(qs, bq)],
                )
                for pair in range(heads // 2):
                    at = pl.ds(128 * pair, 128)
                    keys = kv[pl.ds(ks, bk), at]
                    values = kv[pl.ds(ks, bk), pl.ds(width + 128 * pair, 128)]
                    grads = grad[pl.ds(qs, bq), at]
                    queries = q[pl.ds(qs, bq), at]
                    dk, dv = None, None
                    for e in range(2):
                        h = 2 * pair + e
                        keep = (lane < HD) if e == 0 else (lane >= HD)

                        def padded(ref):
                            mine = ref[pl.ds(HD * h, HD), pl.ds(qs, bq)]
                            return jnp.concatenate(
                                [mine, blank] if e == 0 else [blank, mine], axis=0
                            )

                        score = dot(keys, padded(qt))
                        prob = jnp.exp2(
                            score * c1
                            - dist[...] * slopes[h]
                            - lse[h : h + 1, pl.ds(qs, bq)]
                        )
                        prob_grad = dot(values, padded(gradt))
                        score_grad = (
                            prob * (prob_grad - delta[h : h + 1, pl.ds(qs, bq)])
                        ).astype(BF16)
                        dvh = dot(prob.astype(BF16), jnp.where(keep, grads, jnp.zeros_like(grads)))
                        dkh = dot(score_grad, jnp.where(keep, queries, jnp.zeros_like(queries)))
                        dv = dvh if dv is None else dv + dvh
                        dk = dkh if dk is None else dk + dkh
                        dqt[pl.ds(HD * h, HD), :] += dot(
                            kt[pl.ds(HD * h, HD), pl.ds(ks, bk)], score_grad
                        )
                    sums[pl.ds(ks, bk), at] += dk
                    sums[pl.ds(ks, bk), pl.ds(width + 128 * pair, 128)] += dv

            return 0

        lax.fori_loop(0, kv.shape[0] // bk, k_block, 0)
        dq[pl.ds(qs, bq), :] = (dqt[...] * scale).T.astype(BF16)
        return 0

    lax.fori_loop(0, q.shape[0] // bq, q_block, 0)
    dkv[:, :width] = (sums[:, :width] * scale).astype(BF16)
    dkv[:, width:] = sums[:, width:].astype(BF16)


def attend_back(
    kspan, qspan, slopes, q, qt, kv, kt, grad, gradt, lse, delta, kcode, qseg, bq, bk, heads
):
    vm, sm = pl.BlockSpec(memory_space=VMEM), pl.BlockSpec(memory_space=SMEM)
    return pl.pallas_call(
        functools.partial(attend_back_kernel, bq, bk, heads),
        out_shape=(
            jax.ShapeDtypeStruct(q.shape, BF16),
            jax.ShapeDtypeStruct(kv.shape, BF16),
        ),
        in_specs=[sm] * 3 + [vm] * 10,
        out_specs=(vm, vm),
        scratch_shapes=[
            pltpu.VMEM((bk, bq), F32),
            pltpu.VMEM((heads * HD, bq), F32),
            pltpu.VMEM(kv.shape, F32),
        ],
        name="attend_back",
        cost_estimate=pl.CostEstimate(
            flops=20_000_000_000, bytes_accessed=16_000_000, transcendentals=4_000_000
        ),
        compiler_params=pltpu.CompilerParams(vmem_limit_bytes=48 << 20),
    )(kspan, qspan, slopes, q, qt, kv, kt, grad, gradt, lse, delta, kcode, qseg)


ROWS, COLS = 32, 1024


def share_kernel(
    plan, down, up, gq, gkv, wo, skip, vec, *refs
):
    n_units, n_sums = len(plan), sum(u["core"] == "sum" for u in plan)
    o_down, o_up, o_qkv, o_wo, o_skip, o_vec = refs[:6]
    own, r0, r1, r2, r3, ownv, r0v, r1v, r2v, r3v, loads, sends, recvs = refs[6:]
    sources = {"down": down, "up": up, "gq": gq, "gkv": gkv, "wo": wo, "skip": skip}
    results = {"down": o_down, "up": o_up, "qkv": o_qkv, "wo": o_wo, "skip": o_skip}
    row, col = lax.axis_index("rows"), lax.axis_index("seq")
    z, x, y, c = row // 2, row % 2, col // 2, col % 2

    def device(pz, px, py, pc):
        return (pz * 2 + px, py * 2 + pc)

    over_core = device(z, x, y, 1 - c)
    over_y = device(z, x, 1 - y, c)
    over_x = device(z, 1 - x, y, c)
    z_at = [(z + d) % 4 for d in range(4)]
    over_z = [device(p, x, y, c) for p in z_at]
    barrier = pltpu.get_barrier_semaphore()
    peers = [over_core, over_y, over_x, over_z[1], over_z[2], over_z[3]]
    for peer in peers:
        pl.semaphore_signal(barrier, inc=1, device_id=peer, device_id_type=MESH)
    pl.semaphore_wait(barrier, len(peers))

    def remote(src, dst, sem, peer):
        copy = pltpu.make_async_remote_copy(
            src, dst, sends.at[sem], recvs.at[sem], device_id=peer, device_id_type=MESH
        )
        copy.start()
        return copy

    started = []
    core_in, local_in = {}, {}
    for k, unit in enumerate(plan):
        src = sources[unit["src"]]
        r, q = pl.ds(unit["row"], ROWS), pl.ds(unit["col"], unit["width"])
        if unit["core"] == "sum":
            dst = own.at[k]
            there = r0.at[unit["slot"]]
        else:
            part = pl.ds(pl.multiple_of(c * unit["width"], unit["width"]), unit["width"])
            dst = own.at[k, :, :, :, :, part]
            there = dst
        core_in[k] = remote(src.at[:, :, :, 1 - c, r, q], there, 6 * k, over_core)
        copy = pltpu.make_async_copy(src.at[:, :, :, c, r, q], dst, loads.at[k])
        copy.start()
        local_in[k] = copy
    k = n_units
    core_in[k] = remote(vec.at[:, :, :, 1 - c], r0v, 6 * k, over_core)
    local_in[k] = pltpu.make_async_copy(vec.at[:, :, :, c], ownv, loads.at[k])
    local_in[k].start()

    first_in, second_in, third_in = {}, {}, {}

    def mine(k):
        return ownv if k == n_units else own.at[k]

    def buffers(k):
        if k == n_units:
            return r1v, r2v, r3v
        return r1.at[k], r2.at[k], r3.at[k]

    def add_core(k):
        local_in[k].wait()
        core_in[k].wait_recv()
        a = mine(k)
        if k < n_units and plan[k]["core"] != "sum":
            return
        b = r0v if k == n_units else r0.at[plan[k]["slot"]]

        def step(i, _):
            for j in range(2):
                for m in range(2):
                    a[i, j, m] = a[i, j, m] + b[i, j, m]
            return 0

        lax.fori_loop(0, 4, step, 0)

    def send_first(k):
        a, to = mine(k), buffers(k)[0]
        if k % 2 == 0:
            first_in[k] = remote(a.at[:, :, 1 - y], to, 6 * k + 1, over_y)
        else:
            first_in[k] = remote(a.at[:, 1 - x], to, 6 * k + 1, over_x)

    def add_first(k):
        first_in[k].wait_recv()
        a, b = mine(k), buffers(k)[0]

        def step(i, _):
            for j in range(2):
                if k % 2 == 0:
                    a[i, j, y] = a[i, j, y] + b[i, j]
                else:
                    a[i, x, j] = a[i, x, j] + b[i, j]
            return 0

        lax.fori_loop(0, 4, step, 0)

    def send_second(k):
        a, to = mine(k), buffers(k)[1]
        if k % 2 == 0:
            second_in[k] = remote(a.at[:, 1 - x, y], to, 6 * k + 2, over_x)
        else:
            second_in[k] = remote(a.at[:, x, 1 - y], to, 6 * k + 2, over_y)

    def add_second(k):
        second_in[k].wait_recv()
        a, b = mine(k), buffers(k)[1]

        def step(i, _):
            a[i, x, y] = a[i, x, y] + b[i]
            return 0

        lax.fori_loop(0, 4, step, 0)

    def send_third(k):
        a, to = mine(k), buffers(k)[2]
        third_in[k] = [
            remote(a.at[z_at[d], x, y], to.at[d - 1], 6 * k + 2 + d, over_z[d])
            for d in (1, 2, 3)
        ]

    def finish(k):
        for copy in third_in[k]:
            copy.wait_recv()
        a, b = mine(k), buffers(k)[2]
        value = a[z, x, y].astype(F32)
        for d in range(3):
            value = value + b[d].astype(F32)
        if k == n_units:
            o_vec[...] = value
        else:
            unit = plan[k]
            results[unit["out"]][pl.ds(unit["row"], ROWS), pl.ds(unit["out_col"], COLS)] = value

    groups = [[k for k in (p, p + 1) if k < n_units] for p in range(0, n_units, 2)]
    groups[0] = groups[0] + [n_units]
    n = len(groups)
    for t in range(n + 3):
        if t < n:
            for k in groups[t]:
                add_core(k)
                send_first(k)
        if 0 <= t - 1 < n:
            for k in groups[t - 1]:
                add_first(k)
                send_second(k)
        if 0 <= t - 2 < n:
            for k in groups[t - 2]:
                add_second(k)
                send_third(k)
        if 0 <= t - 3 < n:
            for k in groups[t - 3]:
                finish(k)
    for k in range(n_units + 1):
        for copy in [core_in[k], first_in[k], second_in[k], *third_in[k]]:
            copy.wait_send()


def share_plan():
    def one(src, out, row, col, out_col, width=COLS, core="sum"):
        return dict(src=src, out=out, row=row, col=col, out_col=out_col, width=width, core=core)

    down = [one("down", "down", ROWS * i, 0, 0) for i in range(4)]
    up = [one("up", "up", 0, COLS * i, COLS * i) for i in range(4)]
    qkv = [
        one("gq", "qkv", 0, 0, 0, COLS // 2, "join"),
        one("gkv", "qkv", 0, 0, COLS, COLS // 2, "join"),
        one("gkv", "qkv", 0, COLS // 2, 2 * COLS, COLS // 2, "join"),
    ]
    skip = [one("skip", "skip", ROWS * i, 0, 0) for i in range(2)]
    wo = [one("wo", "wo", 0, 0, 0)]
    plan = [u for pair in zip(down, up) for u in pair]
    plan += [qkv[0], skip[0], qkv[1], skip[1], qkv[2], wo[0]]
    slot = 0
    for unit in plan:
        if unit["core"] == "sum":
            unit["slot"] = slot
            slot += 1
    return plan, slot


def share(down, up, gq, gkv, wo, skip, vec):
    plan, slots = share_plan()
    n = len(plan)

    def cut(value):
        return value.reshape(4, 2, 2, 2, value.shape[0] // 32, value.shape[1])

    hbm, vm = pl.BlockSpec(memory_space=HBM), pl.BlockSpec(memory_space=VMEM)
    unit = (ROWS, COLS)
    small = (8, 128)
    args = [cut(v) for v in (down, up, gq, gkv, wo, skip)] + [vec.reshape(4, 2, 2, 2, *small)]
    outs = [(128, 1024), (32, 4096), (32, 3072), (32, 1024), (64, 1024), small]
    return pl.pallas_call(
        functools.partial(share_kernel, plan),
        out_shape=[jax.ShapeDtypeStruct(s, F32) for s in outs],
        in_specs=[hbm] * 7,
        out_specs=[vm] * 6,
        scratch_shapes=[
            pltpu.VMEM((n, 4, 2, 2, *unit), BF16),
            pltpu.VMEM((slots, 4, 2, 2, *unit), BF16),
            pltpu.VMEM((n, 4, 2, *unit), BF16),
            pltpu.VMEM((n, 4, *unit), BF16),
            pltpu.VMEM((n, 3, *unit), BF16),
            pltpu.VMEM((4, 2, 2, *small), F32),
            pltpu.VMEM((4, 2, 2, *small), F32),
            pltpu.VMEM((4, 2, *small), F32),
            pltpu.VMEM((4, *small), F32),
            pltpu.VMEM((3, *small), F32),
            pltpu.SemaphoreType.DMA((n + 1,)),
            pltpu.SemaphoreType.DMA((6 * (n + 1),)),
            pltpu.SemaphoreType.DMA((6 * (n + 1),)),
        ],
        name="share",
        cost_estimate=pl.CostEstimate(flops=30_000_000, bytes_accessed=60_000_000, transcendentals=0),
        compiler_params=pltpu.CompilerParams(
            collective_id=0, has_side_effects=True, vmem_limit_bytes=52 << 20
        ),
    )(*args)


CHIP = 1024
HALO = 768


def swap_core(value):
    return lax.ppermute(value, "seq", [(i, i ^ 1) for i in range(4)])


def swap_chip(value):
    return lax.ppermute(value, "seq", [(i, i ^ 2) for i in range(4)])


def body_chips(
    inputs,
    skip_feats,
    seg_ids,
    frame_valid,
    w_skip,
    gain_one,
    w_qkv,
    w_out,
    gain_two,
    w_up,
    b_up,
    w_down,
    b_down,
    cotangent,
):
    here = lax.axis_index("seq")
    y, c = here // 2, here % 2
    frames = inputs.shape[1]
    heads = H // 2
    width = heads * HD
    first, second_in, cot = inputs[0], skip_feats[0], cotangent[0]
    gain_first = gain_one.astype(F32)
    gain_second = gain_two.astype(F32)

    halo_at = jnp.where(y == 0, CHIP, CHIP - HALO)
    own_at, other_at = here * frames, (here ^ 1) * frames
    seg_row = seg_ids[0]
    code_row = jnp.where(frame_valid[0] == 1, seg_row, -1)

    def seen(row):
        return jnp.concatenate(
            [
                lax.dynamic_slice(row, (own_at,), (frames,)),
                lax.dynamic_slice(row, (other_at,), (frames,)),
                lax.dynamic_slice(row, (halo_at,), (HALO,)),
            ]
        )

    seg_seen = seen(seg_row)
    kcode = jnp.broadcast_to(seen(code_row)[:, None], (CHIP + HALO, 128))
    qseg = jnp.broadcast_to(seg_seen[None, :CHIP], (8, CHIP))

    def spans(count, block):
        at = jnp.arange(0, count, block)
        base = jnp.where(at < frames, own_at, jnp.where(at < CHIP, other_at - frames, halo_at - CHIP))
        seg = seg_seen[:count].reshape(-1, block)
        return jnp.stack([seg[:, 0], seg[:, -1], base + at]).astype(jnp.int32)

    slopes = LOG2E * jnp.exp2(-8.0 * (c * heads + jnp.arange(heads) + 1).astype(F32) / H)

    w_heads = lax.dynamic_index_in_dim(w_qkv.reshape(D, 3, 2, width), c, 2, keepdims=False)
    w_q, w_kv = w_heads[:, 0], w_heads[:, 1:].reshape(D, 2 * width)

    joined = jnp.concatenate([first, second_in], axis=-1)
    stem_out = mm("fc,cd->fd", joined, w_skip)
    unit_one, inverse_one, normed = norm_forward(stem_out, gain_first)
    normed = normed.astype(BF16)
    normed_other = swap_core(normed)
    around = jnp.concatenate([normed, normed_other, normed], axis=0)
    half = HALO // 2
    part_at = c * frames + jnp.where(y == 0, CHIP - HALO, 0) + half * c
    halo_part = swap_chip(lax.dynamic_slice(around, (part_at, 0), (half, D)))
    halo_rest = swap_core(halo_part)
    halo_parts = jnp.concatenate([halo_part, halo_rest, halo_part], axis=0)
    halo = lax.dynamic_slice(halo_parts, (c * half, 0), (HALO, D))
    normed_seen = jnp.concatenate([normed, normed_other, halo], axis=0)
    q = mm("fd,de->fe", normed_seen[:CHIP], w_q).astype(BF16)
    kv = mm("fd,de->fe", normed_seen, w_kv).astype(BF16)

    attended, lse = attend(
        spans(CHIP + HALO, 128),
        spans(CHIP, 128),
        slopes,
        q.T,
        kv,
        kv[:, width:].T,
        kcode,
        qseg,
        128,
        128,
        heads,
    )
    attended_other = swap_core(attended[frames:])
    pair = jnp.concatenate([attended[:frames], attended_other, attended[:frames]], axis=1)
    mixed_out = lax.dynamic_slice(pair, (0, c * width), (frames, D))
    middle = stem_out + mm("fd,de->fe", mixed_out, w_out)
    unit_two, inverse_two, second = norm_forward(middle, gain_second)
    second = second.astype(BF16)
    hidden = mm("fd,dk->fk", second, w_up) + b_up.astype(F32)
    active_full, gelu_back = jax.vjp(gelu_exact, hidden)
    active = active_full.astype(BF16)
    result = middle + mm("fk,kd->fd", active, w_down) + b_down.astype(F32)
    output = result.astype(BF16)
    cot_full = cot.astype(F32)
    down_grad = mm("fk,fd->kd", active, cot).astype(BF16)
    bias_down_grad = jnp.sum(cot_full, axis=0)
    active_grad = mm("fd,kd->fk", cot, w_down)
    hidden_grad = gelu_back(active_grad)[0].astype(BF16)
    up_grad = mm("fd,fk->dk", second, hidden_grad).astype(BF16)
    bias_up_grad = jnp.sum(hidden_grad.astype(F32), axis=0)
    second_grad = mm("fk,dk->fd", hidden_grad, w_up)
    middle_part, gain_two_grad = norm_backward(second_grad, unit_two, inverse_two, gain_second)
    middle_grad = cot_full + middle_part
    middle_low = middle_grad.astype(BF16)
    out_grad = mm("fd,fe->de", mixed_out, middle_low).astype(BF16)
    mixed_grad = mm("fe,de->fd", middle_low, w_out).astype(BF16)
    mixed_halves = mixed_grad.reshape(frames, 2, width)
    grad_own = lax.dynamic_index_in_dim(mixed_halves, c, 1, keepdims=False)
    grad_other = swap_core(lax.dynamic_index_in_dim(mixed_halves, 1 - c, 1, keepdims=False))
    grad_heads = jnp.concatenate([grad_own, grad_other], axis=0)
    delta = jnp.sum(
        (attended.astype(F32) * grad_heads.astype(F32)).reshape(CHIP, heads, HD), axis=-1
    ).T
    dq, dkv = attend_back(
        spans(CHIP + HALO, 256),
        spans(CHIP, 512),
        slopes,
        q,
        q.T,
        kv,
        kv[:, :width].T,
        grad_heads,
        grad_heads.T,
        lse,
        delta,
        kcode,
        qseg,
        512,
        256,
        heads,
    )
    halo_grad = mm("fe,de->fd", dkv[CHIP:], w_kv).astype(BF16)
    halo_mine = lax.dynamic_slice(halo_grad, (c * half, 0), (half, D))
    halo_theirs = lax.dynamic_slice(halo_grad, ((1 - c) * half, 0), (half, D))
    halo_sum = (halo_mine.astype(F32) + swap_core(halo_theirs).astype(F32)).astype(BF16)
    back_part = swap_chip(halo_sum)
    back_rest = swap_core(back_part)
    back = lax.dynamic_slice(
        jnp.concatenate([back_part, back_rest, back_part], axis=0), (c * half, 0), (HALO, D)
    )
    edge = CHIP - HALO
    back = lax.dynamic_slice(
        jnp.pad(back, ((edge, edge), (0, 0))), (c * frames + y * edge, 0), (frames, D)
    )
    qkv_grad_q = mm("fd,fe->de", normed_seen[:CHIP], dq).astype(BF16)
    qkv_grad_kv = mm("fd,fe->de", normed_seen, dkv).astype(BF16)
    chip_grad = mm("fe,de->fd", dq, w_q) + mm("fe,de->fd", dkv[:CHIP], w_kv)
    from_core = swap_core(chip_grad[frames:].astype(BF16))
    normed_grad = chip_grad[:frames] + from_core.astype(F32) + back.astype(F32)
    stem_part, gain_one_grad = norm_backward(normed_grad, unit_one, inverse_one, gain_first)
    stem_low = (middle_grad + stem_part).astype(BF16)
    skip_w_grad = mm("fc,fd->cd", joined, stem_low).astype(BF16)
    joined_grad = mm("fd,cd->fc", stem_low, w_skip)
    input_grad = joined_grad[:, :D].astype(BF16)
    skip_grad = joined_grad[:, D:].astype(BF16)

    vec = jnp.concatenate(
        [
            bias_up_grad.reshape(32, 128),
            gain_one_grad.reshape(32, 32),
            gain_two_grad.reshape(32, 32),
            bias_down_grad.reshape(32, 32),
            jnp.zeros((32, 1024 - 224), F32),
        ],
        axis=1,
    )
    down_share, up_share, qkv_share, out_share, skip_share, vec_share = share(
        down_grad, up_grad, qkv_grad_q, qkv_grad_kv, out_grad, skip_w_grad, vec
    )
    small = vec_share[1]
    return (
        output[None],
        input_grad[None],
        skip_grad[None],
        skip_share,
        small[0:32],
        qkv_share,
        out_share,
        small[32:64],
        up_share,
        vec_share[0],
        down_share,
        small[64:96],
    )


def block_scores(q_blk, pos_blk, seg_blk, all_keys, seg_row, valid_row, slopes, score_scale):
    key_pos = jnp.arange(all_keys.shape[0])
    scores = (
        jnp.einsum("qhd,khd->hqk", q_blk, all_keys, preferred_element_type=jnp.float32)
        * score_scale
    )
    distance = jnp.abs(pos_blk[:, None] - key_pos[None, :]).astype(jnp.float32)
    scores = scores - slopes[:, None, None] * distance[None]
    allowed = (seg_blk[:, None] == seg_row[None, :]) & (
        (valid_row[None, :] == 1) | (pos_blk[:, None] == key_pos[None, :])
    )
    return jnp.where(allowed[None], scores, -jnp.inf)


def split_row(packed_row, heads_local):
    length = packed_row.shape[0]
    qkv_rows = packed_row.reshape(length, 3, heads_local, HD)
    return (qkv_rows[:, 0], qkv_rows[:, 1], qkv_rows[:, 2])


def attend_row(packed_row, seg_row, valid_row, slopes, heads_local, block_rows, score_scale):
    length = packed_row.shape[0]
    queries, all_keys, all_values = split_row(packed_row, heads_local)
    count = length // block_rows
    positions = jnp.arange(length)

    def one_block(block_in):
        q_blk, pos_blk, seg_blk = block_in
        scores = block_scores(
            q_blk, pos_blk, seg_blk, all_keys, seg_row, valid_row, slopes, score_scale
        )
        peak = jnp.max(scores, axis=-1, keepdims=True)
        log_total = peak + jnp.log(jnp.sum(jnp.exp(scores - peak), axis=-1, keepdims=True))
        attn_probs = jnp.exp(scores - log_total).astype(jnp.bfloat16)
        attended = jnp.einsum(
            "hqk,khd->qhd", attn_probs, all_values, preferred_element_type=jnp.float32
        )
        return (attended.astype(jnp.bfloat16), log_total[..., 0])

    attended, log_total = lax.map(
        one_block,
        (
            queries.reshape(count, block_rows, heads_local, HD),
            positions.reshape(count, block_rows),
            seg_row.reshape(count, block_rows),
        ),
    )
    return (attended.reshape(length, 1, heads_local * HD), log_total)


def attend_row_back(
    packed_row,
    log_total,
    grad_row,
    seg_row,
    valid_row,
    slopes,
    heads_local,
    block_rows,
    score_scale,
):
    length = packed_row.shape[0]
    queries, all_keys, all_values = split_row(packed_row, heads_local)
    count = length // block_rows
    positions = jnp.arange(length)
    grad_out = grad_row.reshape(count, block_rows, heads_local, HD)

    def one_block(carry, block_in):
        key_grad, value_grad = carry
        q_blk, pos_blk, seg_blk, total_blk, grad_blk = block_in
        scores = block_scores(
            q_blk, pos_blk, seg_blk, all_keys, seg_row, valid_row, slopes, score_scale
        )
        soft = jnp.exp(scores - total_blk[..., None])
        value_grad = value_grad + jnp.einsum(
            "hqk,qhd->khd", soft.astype(jnp.bfloat16), grad_blk, preferred_element_type=jnp.float32
        )
        prob_grad = jnp.einsum(
            "qhd,khd->hqk", grad_blk, all_values, preferred_element_type=jnp.float32
        )
        score_grad = (
            soft * (prob_grad - jnp.sum(soft * prob_grad, axis=-1, keepdims=True))
        ).astype(jnp.bfloat16)
        query_grad = (
            jnp.einsum("hqk,khd->qhd", score_grad, all_keys, preferred_element_type=jnp.float32)
            * score_scale
        )
        key_grad = (
            key_grad
            + jnp.einsum("hqk,qhd->khd", score_grad, q_blk, preferred_element_type=jnp.float32)
            * score_scale
        )
        return ((key_grad, value_grad), query_grad)

    zero_rows = jnp.zeros((length, heads_local, HD), jnp.float32)
    (key_grad, value_grad), query_grad = lax.scan(
        one_block,
        (zero_rows, zero_rows),
        (
            queries.reshape(count, block_rows, heads_local, HD),
            positions.reshape(count, block_rows),
            seg_row.reshape(count, block_rows),
            log_total,
            grad_out,
        ),
    )
    stacked = jnp.stack([query_grad.reshape(length, heads_local, HD), key_grad, value_grad], axis=1)
    return stacked.astype(jnp.bfloat16).reshape(length, 3, 1, heads_local * HD)


def body(
    inputs,
    skip_feats,
    seg_ids,
    frame_valid,
    w_skip,
    gain_one,
    w_qkv,
    w_out,
    gain_two,
    w_up,
    b_up,
    w_down,
    b_down,
    cotangent,
):
    parts = lax.axis_size("seq")
    heads_local = H // parts
    width_local = heads_local * HD
    rows_here = inputs.shape[0]
    frames = inputs.shape[1]
    length = frames * parts
    block_rows = min(512, length)
    score_scale = 1.0 / math.sqrt(HD)
    first_head = lax.axis_index("seq") * heads_local
    slopes = jnp.exp2(-8.0 * (first_head + jnp.arange(heads_local) + 1).astype(jnp.float32) / H)
    gain_first = gain_one.astype(jnp.float32)
    gain_second = gain_two.astype(jnp.float32)
    bias_up = b_up.astype(jnp.float32)
    joined = jnp.concatenate([inputs, skip_feats], axis=-1)
    stem_out = jnp.einsum("rfc,cd->rfd", joined, w_skip, preferred_element_type=jnp.float32)
    unit_one, inverse_one, normed = norm_forward(stem_out, gain_first)
    normed = normed.astype(jnp.bfloat16)
    packed = jnp.einsum("rfd,de->rfe", normed, w_qkv, preferred_element_type=jnp.float32).astype(
        jnp.bfloat16
    )
    packed = packed.reshape(rows_here, frames, 3, parts, width_local)
    by_heads = lax.all_to_all(packed, "seq", split_axis=3, concat_axis=1, tiled=True)

    def forward_row(row_data):
        return attend_row(
            row_data[0], row_data[1], row_data[2], slopes, heads_local, block_rows, score_scale
        )

    attended, log_total = lax.map(forward_row, (by_heads, seg_ids, frame_valid))
    by_frames = lax.all_to_all(attended, "seq", split_axis=1, concat_axis=2, tiled=True)
    mixed_out = by_frames.reshape(rows_here, frames, D)
    middle = stem_out + jnp.einsum(
        "rfd,de->rfe", mixed_out, w_out, preferred_element_type=jnp.float32
    )
    unit_two, inverse_two, second = norm_forward(middle, gain_second)
    second = second.astype(jnp.bfloat16)
    hidden = jnp.einsum("rfd,dk->rfk", second, w_up, preferred_element_type=jnp.float32) + bias_up
    active_full, gelu_back = jax.vjp(gelu_exact, hidden)
    active = active_full.astype(jnp.bfloat16)
    result = (
        middle
        + jnp.einsum("rfk,kd->rfd", active, w_down, preferred_element_type=jnp.float32)
        + b_down.astype(jnp.float32)
    )
    output = result.astype(jnp.bfloat16)
    cot_full = cotangent.astype(jnp.float32)
    down_grad = jnp.einsum("rfk,rfd->kd", active, cotangent, preferred_element_type=jnp.float32)
    bias_down_grad = jnp.sum(cot_full, axis=(0, 1))
    active_grad = jnp.einsum("rfd,kd->rfk", cotangent, w_down, preferred_element_type=jnp.float32)
    hidden_grad = gelu_back(active_grad)[0].astype(jnp.bfloat16)
    up_grad = jnp.einsum("rfd,rfk->dk", second, hidden_grad, preferred_element_type=jnp.float32)
    bias_up_grad = jnp.sum(hidden_grad.astype(jnp.float32), axis=(0, 1))
    second_grad = jnp.einsum("rfk,dk->rfd", hidden_grad, w_up, preferred_element_type=jnp.float32)
    middle_part, gain_two_grad = norm_backward(second_grad, unit_two, inverse_two, gain_second)
    middle_grad = cot_full + middle_part
    middle_low = middle_grad.astype(jnp.bfloat16)
    out_grad = jnp.einsum("rfd,rfe->de", mixed_out, middle_low, preferred_element_type=jnp.float32)
    mixed_grad = jnp.einsum(
        "rfe,de->rfd", middle_low, w_out, preferred_element_type=jnp.float32
    ).astype(jnp.bfloat16)
    grad_heads = lax.all_to_all(
        mixed_grad.reshape(rows_here, frames, parts, width_local),
        "seq",
        split_axis=2,
        concat_axis=1,
        tiled=True,
    )

    def backward_row(row_data):
        return attend_row_back(
            row_data[0],
            row_data[1],
            row_data[2],
            row_data[3],
            row_data[4],
            slopes,
            heads_local,
            block_rows,
            score_scale,
        )

    packed_grad = lax.map(backward_row, (by_heads, log_total, grad_heads, seg_ids, frame_valid))
    packed_back = lax.all_to_all(packed_grad, "seq", split_axis=1, concat_axis=3, tiled=True)
    packed_back = packed_back.reshape(rows_here, frames, 3 * D)
    qkv_grad = jnp.einsum("rfd,rfe->de", normed, packed_back, preferred_element_type=jnp.float32)
    normed_grad = jnp.einsum("rfe,de->rfd", packed_back, w_qkv, preferred_element_type=jnp.float32)
    stem_part, gain_one_grad = norm_backward(normed_grad, unit_one, inverse_one, gain_first)
    stem_low = (middle_grad + stem_part).astype(jnp.bfloat16)
    skip_w_grad = jnp.einsum("rfc,rfd->cd", joined, stem_low, preferred_element_type=jnp.float32)
    joined_grad = jnp.einsum("rfd,cd->rfc", stem_low, w_skip, preferred_element_type=jnp.float32)
    input_grad = joined_grad[..., :D].astype(jnp.bfloat16)
    skip_grad = joined_grad[..., D:].astype(jnp.bfloat16)
    (
        skip_share,
        gain_one_share,
        qkv_share,
        out_share,
        gain_two_share,
        up_share,
        bias_up_share,
        down_share,
        bias_down_share,
    ) = (
        lax.psum_scatter(skip_w_grad, ("rows", "seq"), scatter_dimension=0, tiled=True),
        lax.psum_scatter(gain_one_grad, ("rows", "seq"), scatter_dimension=0, tiled=True),
        lax.psum_scatter(qkv_grad, ("rows", "seq"), scatter_dimension=0, tiled=True),
        lax.psum_scatter(out_grad, ("rows", "seq"), scatter_dimension=0, tiled=True),
        lax.psum_scatter(gain_two_grad, ("rows", "seq"), scatter_dimension=0, tiled=True),
        lax.psum_scatter(up_grad, ("rows", "seq"), scatter_dimension=0, tiled=True),
        lax.psum_scatter(bias_up_grad, ("rows", "seq"), scatter_dimension=0, tiled=True),
        lax.psum_scatter(down_grad, ("rows", "seq"), scatter_dimension=0, tiled=True),
        lax.psum_scatter(bias_down_grad, ("rows", "seq"), scatter_dimension=0, tiled=True),
    )
    return (
        output,
        input_grad,
        skip_grad,
        skip_share,
        gain_one_share,
        qkv_share,
        out_share,
        gain_two_share,
        up_share,
        bias_up_share,
        down_share,
        bias_down_share,
    )


def solution(mesh):
    fits = (mesh.shape["rows"], mesh.shape["seq"]) == (8, 4)
    return jax.shard_map(
        body_chips if fits else body,
        mesh=mesh,
        in_specs=(
            P("rows", "seq", None),
            P("rows", "seq", None),
            P("rows", None),
            P("rows", None),
            P(),
            P(),
            P(),
            P(),
            P(),
            P(),
            P(),
            P(),
            P(),
            P("rows", "seq", None),
        ),
        out_specs=(
            P("rows", "seq", None),
            P("rows", "seq", None),
            P("rows", "seq", None),
            P(("rows", "seq"), None),
            P(("rows", "seq")),
            P(("rows", "seq"), None),
            P(("rows", "seq"), None),
            P(("rows", "seq")),
            P(("rows", "seq"), None),
            P(("rows", "seq")),
            P(("rows", "seq"), None),
            P(("rows", "seq")),
        ),
        check_vma=False,
    )
```

```python
import functools
import math

import jax
import jax.numpy as jnp
from jax import lax
from jax.experimental import pallas as pl
from jax.experimental.pallas import tpu as pltpu
from jax.sharding import PartitionSpec as P

D = 1024
H = 16
HD = 64
MOST = 682

epsilon = 1e-05

F32 = jnp.float32
BF16 = jnp.bfloat16
LOG2E = 1.4426950408889634
FAR = 1e30
MESH = pl.DeviceIdType.MESH
VMEM = pltpu.MemorySpace.VMEM
SMEM = pltpu.MemorySpace.SMEM
HBM = pltpu.MemorySpace.HBM


def norm_forward(value, gain_vec):
    center = value - jnp.mean(value, axis=-1, keepdims=True)
    spread = jnp.mean(center * center, axis=-1, keepdims=True)
    inverse = lax.rsqrt(spread + epsilon)
    unit = center * inverse
    return (unit, inverse, unit * gain_vec)


def norm_backward(upstream, unit, inverse, gain_vec):
    scaled = upstream * gain_vec
    gain_grad = jnp.sum(upstream * unit, axis=tuple(range(upstream.ndim - 1)))
    inner = (
        scaled
        - jnp.mean(scaled, axis=-1, keepdims=True)
        - unit * jnp.mean(scaled * unit, axis=-1, keepdims=True)
    )
    return (inverse * inner, gain_grad)


def gelu_exact(value):
    return jax.nn.gelu(value, approximate=False)


def mm(equation, left, right):
    return jnp.einsum(equation, left, right, preferred_element_type=F32)


def dot(left, right):
    return jnp.dot(left, right, preferred_element_type=F32)


def set_distances(dist, key_at, query_at, key_code, query_seg):
    keys, queries = dist.shape
    rows = lax.broadcasted_iota(jnp.int32, (keys, queries), 0) + key_at
    cols = lax.broadcasted_iota(jnp.int32, (keys, queries), 1) + query_at
    apart = jnp.abs(rows - cols)
    allowed = (key_code == query_seg) | (apart == 0)
    dist[...] = jnp.where(allowed, apart.astype(F32), FAR)


def wide(code, queries):
    return jnp.concatenate([code] * (queries // 128), axis=1) if queries > 128 else code


def blocks_meet(kspan, qspan, j, i):
    return (kspan[0, j] <= qspan[1, i]) & (kspan[1, j] >= qspan[0, i])


def attend_kernel(
    bq,
    bk,
    heads,
    kspan,
    qspan,
    slopes,
    q,
    kv,
    kcode,
    qseg,
    out,
    outt,
    lse,
    qt,
    vt,
    dist,
    acc,
    top,
    total,
):
    width = heads * HD
    c1 = LOG2E / math.sqrt(HD)
    blank = jnp.zeros((HD, bq), BF16)
    qt[...] = q[...].T
    vt[...] = kv[:, width:].T

    def q_block(i, _):
        qs = pl.multiple_of(i * bq, bq)
        acc[...] = jnp.zeros_like(acc)
        total[...] = jnp.zeros_like(total)
        top[...] = jnp.full_like(top, -3e38)

        def k_block(j, _):
            @pl.when(blocks_meet(kspan, qspan, j, i))
            def _():
                ks = pl.multiple_of(j * bk, bk)
                set_distances(
                    dist,
                    kspan[2, j],
                    qspan[2, i],
                    wide(kcode[pl.ds(ks, bk), :], bq),
                    qseg[0:1, pl.ds(qs, bq)],
                )
                for h in range(heads):
                    mine = qt[pl.ds(HD * h, HD), pl.ds(qs, bq)]
                    pair = [mine, blank] if h % 2 == 0 else [blank, mine]
                    score = dot(
                        kv[pl.ds(ks, bk), pl.ds(128 * (h // 2), 128)],
                        jnp.concatenate(pair, axis=0),
                    )
                    score = score * c1 - dist[...] * slopes[h]
                    was = top[h : h + 1, :]
                    now = jnp.maximum(was, jnp.max(score, axis=0, keepdims=True))
                    prob = jnp.exp2(score - now)
                    fade = jnp.exp2(was - now)
                    total[h : h + 1, :] = total[h : h + 1, :] * fade + jnp.sum(
                        prob, axis=0, keepdims=True
                    )
                    top[h : h + 1, :] = now
                    acc[pl.ds(HD * h, HD), :] = acc[pl.ds(HD * h, HD), :] * fade + dot(
                        vt[pl.ds(HD * h, HD), pl.ds(ks, bk)], prob.astype(BF16)
                    )

            return 0

        lax.fori_loop(0, kv.shape[0] // bk, k_block, 0)
        for h in range(heads):
            acc[pl.ds(HD * h, HD), :] = acc[pl.ds(HD * h, HD), :] * (1.0 / total[h : h + 1, :])
        lse[:, pl.ds(qs, bq)] = top[...] + jnp.log2(total[...])
        out[pl.ds(qs, bq), :] = acc[...].T.astype(BF16)
        outt[:, pl.ds(qs, bq)] = acc[...].astype(BF16)
        return 0

    lax.fori_loop(0, q.shape[0] // bq, q_block, 0)


def attend(kspan, qspan, slopes, q, kv, kcode, qseg, bq, bk, heads):
    frames = q.shape[0]
    vm, sm = pl.BlockSpec(memory_space=VMEM), pl.BlockSpec(memory_space=SMEM)
    return pl.pallas_call(
        functools.partial(attend_kernel, bq, bk, heads),
        out_shape=(
            jax.ShapeDtypeStruct((frames, heads * HD), BF16),
            jax.ShapeDtypeStruct((heads * HD, frames), BF16),
            jax.ShapeDtypeStruct((heads, frames), F32),
        ),
        in_specs=[sm] * 3 + [vm] * 4,
        out_specs=(vm, vm, vm),
        scratch_shapes=[
            pltpu.VMEM((heads * HD, frames), BF16),
            pltpu.VMEM((heads * HD, kv.shape[0]), BF16),
            pltpu.VMEM((bk, bq), F32),
            pltpu.VMEM((heads * HD, bq), F32),
            pltpu.VMEM((heads, bq), F32),
            pltpu.VMEM((heads, bq), F32),
        ],
        name="attend",
        cost_estimate=pl.CostEstimate(
            flops=8_000_000_000, bytes_accessed=8_000_000, transcendentals=4_000_000
        ),
        compiler_params=pltpu.CompilerParams(vmem_limit_bytes=32 << 20),
    )(kspan, qspan, slopes, q, kv, kcode, qseg)


def attend_back_kernel(
    bq,
    bk,
    heads,
    kspan,
    qspan,
    slopes,
    q,
    kv,
    grad,
    outt,
    lse,
    kcode,
    qseg,
    dq,
    dkv,
    qt,
    kt,
    gradt,
    delta,
    dist,
    dqt,
    sums,
):
    width = heads * HD
    c1 = LOG2E / math.sqrt(HD)
    scale = 1.0 / math.sqrt(HD)
    blank = jnp.zeros((HD, bq), BF16)
    lane = lax.broadcasted_iota(jnp.int32, (bq, 128), 1)
    sums[...] = jnp.zeros_like(sums)
    qt[...] = q[...].T
    kt[...] = kv[:, :width].T
    gradt[...] = grad[...].T
    for h in range(heads):
        at = pl.ds(HD * h, HD)
        delta[h : h + 1, :] = jnp.sum(
            outt[at, :].astype(F32) * gradt[at, :].astype(F32), axis=0, keepdims=True
        )

    def q_block(i, _):
        qs = pl.multiple_of(i * bq, bq)
        dqt[...] = jnp.zeros_like(dqt)

        def k_block(j, _):
            @pl.when(blocks_meet(kspan, qspan, j, i))
            def _():
                ks = pl.multiple_of(j * bk, bk)
                set_distances(
                    dist,
                    kspan[2, j],
                    qspan[2, i],
                    wide(kcode[pl.ds(ks, bk), :], bq),
                    qseg[0:1, pl.ds(qs, bq)],
                )
                for pair in range(heads // 2):
                    at = pl.ds(128 * pair, 128)
                    keys = kv[pl.ds(ks, bk), at]
                    values = kv[pl.ds(ks, bk), pl.ds(width + 128 * pair, 128)]
                    grads = grad[pl.ds(qs, bq), at]
                    queries = q[pl.ds(qs, bq), at]
                    dk, dv = None, None
                    for e in range(2):
                        h = 2 * pair + e
                        keep = (lane < HD) if e == 0 else (lane >= HD)

                        def padded(ref):
                            mine = ref[pl.ds(HD * h, HD), pl.ds(qs, bq)]
                            return jnp.concatenate(
                                [mine, blank] if e == 0 else [blank, mine], axis=0
                            )

                        score = dot(keys, padded(qt))
                        prob = jnp.exp2(
                            score * c1
                            - dist[...] * slopes[h]
                            - lse[h : h + 1, pl.ds(qs, bq)]
                        )
                        prob_grad = dot(values, padded(gradt))
                        score_grad = (
                            prob * (prob_grad - delta[h : h + 1, pl.ds(qs, bq)])
                        ).astype(BF16)
                        dvh = dot(prob.astype(BF16), jnp.where(keep, grads, jnp.zeros_like(grads)))
                        dkh = dot(score_grad, jnp.where(keep, queries, jnp.zeros_like(queries)))
                        dv = dvh if dv is None else dv + dvh
                        dk = dkh if dk is None else dk + dkh
                        dqt[pl.ds(HD * h, HD), :] += dot(
                            kt[pl.ds(HD * h, HD), pl.ds(ks, bk)], score_grad
                        )
                    sums[pl.ds(ks, bk), at] += dk
                    sums[pl.ds(ks, bk), pl.ds(width + 128 * pair, 128)] += dv

            return 0

        lax.fori_loop(0, kv.shape[0] // bk, k_block, 0)
        dq[pl.ds(qs, bq), :] = (dqt[...] * scale).T.astype(BF16)
        return 0

    lax.fori_loop(0, q.shape[0] // bq, q_block, 0)
    dkv[:, :width] = (sums[:, :width] * scale).astype(BF16)
    dkv[:, width:] = sums[:, width:].astype(BF16)


def attend_back(kspan, qspan, slopes, q, kv, grad, outt, lse, kcode, qseg, bq, bk, heads):
    vm, sm = pl.BlockSpec(memory_space=VMEM), pl.BlockSpec(memory_space=SMEM)
    return pl.pallas_call(
        functools.partial(attend_back_kernel, bq, bk, heads),
        out_shape=(
            jax.ShapeDtypeStruct(q.shape, BF16),
            jax.ShapeDtypeStruct(kv.shape, BF16),
        ),
        in_specs=[sm] * 3 + [vm] * 7,
        out_specs=(vm, vm),
        scratch_shapes=[
            pltpu.VMEM((heads * HD, q.shape[0]), BF16),
            pltpu.VMEM((heads * HD, kv.shape[0]), BF16),
            pltpu.VMEM((heads * HD, q.shape[0]), BF16),
            pltpu.VMEM((heads, q.shape[0]), F32),
            pltpu.VMEM((bk, bq), F32),
            pltpu.VMEM((heads * HD, bq), F32),
            pltpu.VMEM(kv.shape, F32),
        ],
        name="attend_back",
        cost_estimate=pl.CostEstimate(
            flops=20_000_000_000, bytes_accessed=16_000_000, transcendentals=4_000_000
        ),
        compiler_params=pltpu.CompilerParams(vmem_limit_bytes=48 << 20),
    )(kspan, qspan, slopes, q, kv, grad, outt, lse, kcode, qseg)


def dot_nt(left, right):
    return lax.dot_general(left, right, (((1,), (1,)), ((), ())), preferred_element_type=F32)


def dot_tn(left, right):
    return lax.dot_general(left, right, (((0,), (0,)), ((), ())), preferred_element_type=F32)


ROWS = 32
CHIP = 1024
HALO = 768
FRAMES = 512
HALF = HALO // 2
EDGE = CHIP - HALO
WIDTH = D // 2
SKIPS = 4
SKIP_COLS = D // SKIPS


class Links:
    def __init__(self, sends, recvs):
        row, col = lax.axis_index("rows"), lax.axis_index("seq")
        self.z, self.x, self.y, self.c = row // 2, row % 2, col // 2, col % 2
        z, x, y, c = self.z, self.x, self.y, self.c
        self.z_at = [(z + d) % 4 for d in range(4)]
        self.core = (row, y * 2 + 1 - c)
        self.over_y = (row, (1 - y) * 2 + c)
        self.over_x = (z * 2 + 1 - x, col)
        self.over_z = [(p * 2 + x, col) for p in self.z_at]
        self.sends, self.recvs, self.count, self.started = sends, recvs, 0, []

    def greet(self):
        barrier = pltpu.get_barrier_semaphore()
        peers = [self.core, self.over_y, self.over_x, *self.over_z[1:]]
        for peer in peers:
            pl.semaphore_signal(barrier, inc=1, device_id=peer, device_id_type=MESH)
        pl.semaphore_wait(barrier, len(peers))

    def reserve(self, number):
        self.count += number
        return self.count - number

    def copy(self, src, dst, at, peer):
        return pltpu.make_async_remote_copy(
            src, dst, self.sends.at[at], self.recvs.at[at], device_id=peer, device_id_type=MESH
        )

    def send(self, src, dst, peer):
        copy = self.copy(src, dst, self.reserve(1), peer)
        copy.start()
        self.started.append(copy)
        return copy

    def drain(self):
        assert self.count <= self.sends.shape[0]
        for copy in self.started:
            copy.wait_send()


class Unit:
    def __init__(self, links, own, r1, r2, r3, y_first, done):
        self.links, self.own, self.r1, self.r2, self.r3 = links, own, r1, r2, r3
        self.y_first, self.done = y_first, done

    def add_core(self, r0):
        a = self.own

        def step(i, _):
            for j in range(2):
                for m in range(2):
                    a[i, j, m] = a[i, j, m] + r0[i, j, m]
            return 0

        lax.fori_loop(0, 4, step, 0)

    def send_first(self):
        n, a = self.links, self.own
        if self.y_first:
            self.first = n.send(a.at[:, :, 1 - n.y], self.r1, n.over_y)
        else:
            self.first = n.send(a.at[:, 1 - n.x], self.r1, n.over_x)

    def add_first(self):
        self.first.wait_recv()
        n, a, b = self.links, self.own, self.r1

        def step(i, _):
            for j in range(2):
                if self.y_first:
                    a[i, j, n.y] = a[i, j, n.y] + b[i, j]
                else:
                    a[i, n.x, j] = a[i, n.x, j] + b[i, j]
            return 0

        lax.fori_loop(0, 4, step, 0)

    def send_second(self):
        n, a = self.links, self.own
        if self.y_first:
            self.second = n.send(a.at[:, 1 - n.x, n.y], self.r2, n.over_x)
        else:
            self.second = n.send(a.at[:, n.x, 1 - n.y], self.r2, n.over_y)

    def last(self, i):
        return self.own.at[i, self.links.x, self.links.y]

    def add_second(self):
        self.second.wait_recv()
        b = self.r2

        def step(i, _):
            a = self.last(i)
            a[...] = a[...] + b[i]
            return 0

        lax.fori_loop(0, 4, step, 0)

    def send_third(self):
        n = self.links
        self.third = [n.send(self.last(n.z_at[d]), self.r3.at[d - 1], n.over_z[d]) for d in (1, 2, 3)]

    def finish(self):
        for copy in self.third:
            copy.wait_recv()
        value = self.last(self.links.z)[...].astype(F32)
        for d in range(3):
            value = value + self.r3[d].astype(F32)
        self.done(value)

    def turn_first(self):
        self.add_first()
        self.send_second()

    def turn_second(self):
        self.add_second()
        self.send_third()


class LateUnit(Unit):
    def last(self, i):
        return self.own.at[i]

    def turn_second(self, *loads):
        for copy in loads:
            copy.wait()
        b = self.r2

        def step(i, _):
            a = self.last(i)
            a[...] = a[...] + b[i]
            return 0

        lax.fori_loop(0, 4, step, 0)
        self.send_third()


class Small:
    def __init__(self, links, steps, into, done):
        self.links, self.steps, self.into, self.done, self.at = links, steps, into, done, 0
        self.stages = [[links.core], [links.over_y], [links.over_x], links.over_z[1:]]

    def send(self):
        self.flying = [
            self.links.send(self.steps.at[self.at], self.into.at[self.at + i], peer)
            for i, peer in enumerate(self.stages[self.at])
        ]

    def turn(self):
        for copy in self.flying:
            copy.wait_recv()
        value = self.steps[self.at]
        for i in range(len(self.flying)):
            value = value + self.into[self.at + i]
        self.at += 1
        if self.at == len(self.stages):
            self.done(value)
        else:
            self.steps[self.at] = value
            self.send()


STEPS = 8
STEP = 256


def middle_kernel(*refs):
    (
        att_in_hbm,
        stem_in,
        wout_in,
        gain,
        up_hbm,
        down_hbm,
        bias_up,
        bias_down,
        cot_in,
    ) = refs[:9]
    o_out, o_grad, o_heads, o_wo, o_down, o_up, o_small = refs[9:16]
    (
        att,
        att_came,
        stem,
        wout,
        ups,
        downs,
        cot,
        second,
        second_t,
        unit,
        inverse,
        active,
        hidden_grad,
        out_sum,
        grad_sum,
        low,
        swap_out,
        swap_in,
        down_send,
        down_keep,
        down_came,
        up_send,
        up_keep,
        up_came,
        loads,
        sends,
        recvs,
    ) = refs[16:]
    links = Links(sends, recvs)
    x, y, c = links.x, links.y, links.c
    loading = []

    def load(src, dst):
        copy = pltpu.make_async_copy(src, dst, loads.at[len(loading)])
        copy.start()
        loading.append(copy)
        return copy

    own, other = pl.ds(0, FRAMES), pl.ds(FRAMES, FRAMES)
    got_att = load(att_in_hbm.at[own], att)
    got_wout = load(wout_in, wout)
    got_stem = load(stem_in, stem)
    got_cot = load(cot_in, cot.at[own])
    got_ups, got_downs = [], []
    for i in range(STEPS):
        for j in range(2):
            at = pl.multiple_of(128 * (4 * i + 2 * j + c), 128)
            part = pl.ds(128 * j, 128)
            got_ups.append(load(up_hbm.at[:, pl.ds(at, 128)], ups.at[i, :, part]))
            got_downs.append(load(down_hbm.at[pl.ds(at, 128), :], downs.at[i, part, :]))
    links.greet()
    att_core = links.send(att_in_hbm.at[other], att_came, links.core)
    cot_core = links.send(cot_in, cot.at[other], links.core)
    mine = pl.ds(pl.multiple_of(WIDTH * c, WIDTH), WIDTH)
    theirs = pl.ds(pl.multiple_of(WIDTH * (1 - c), WIDTH), WIDTH)

    got_att.wait()
    got_wout.wait()
    got_stem.wait()
    att_core.wait_recv()
    gains = gain[0:1, :]
    second_core = []
    for part in range(2):
        rows = pl.ds(256 * part, 256)
        value = stem[rows, :] + dot(att[rows, :], wout[mine, :]) + dot(att_came[rows, :], wout[theirs, :])
        stem[rows, :] = value
        center = value - jnp.mean(value, axis=-1, keepdims=True)
        rate = lax.rsqrt(jnp.mean(center * center, axis=-1, keepdims=True) + epsilon)
        normal = center * rate
        unit[rows, :] = normal
        inverse[rows, :] = jnp.broadcast_to(rate, (256, 128))
        second[rows, :] = (normal * gains).astype(BF16)
        second_core.append(
            links.send(second.at[rows], second.at[pl.ds(FRAMES + 256 * part, 256)], links.core)
        )
    second_t[:, :FRAMES] = second[own, :].T
    out_sum[...] = jnp.zeros_like(out_sum)
    grad_sum[...] = jnp.zeros_like(grad_sum)
    o_small[...] = jnp.zeros_like(o_small)
    for copy in [got_cot, *got_ups, *got_downs]:
        copy.wait()
    cot_core.wait_recv()
    for copy in second_core:
        copy.wait_recv()
    second_t[:, FRAMES:] = second[other, :].T

    down_at, up_at = links.reserve(STEPS), links.reserve(STEPS)

    def down_copy(i):
        return links.copy(down_send.at[i], down_came.at[i], down_at + i, links.over_y)

    def up_copy(i):
        return links.copy(up_send.at[i], up_came.at[i], up_at + i, links.over_x)

    def feed_step(i, _):
        up, down = ups[i], downs[i]
        bias = bias_up[0:1, pl.ds(pl.multiple_of(STEP * i, STEP), STEP)]
        total = jnp.zeros((1, STEP), F32)
        for half in (own, other):
            hidden = dot(second[half, :], up) + bias
            active_grad = dot_nt(cot[half, :], down)
            share = 0.5 + 0.5 * lax.erf(hidden * math.sqrt(0.5))
            slope = share + hidden * (
                jnp.exp(-0.5 * hidden * hidden) * (1.0 / math.sqrt(2.0 * math.pi))
            )
            a = (hidden * share).astype(BF16)
            g = (active_grad * slope).astype(BF16)
            active[half, :] = a
            hidden_grad[half, :] = g
            total = total + jnp.sum(g.astype(F32), axis=0, keepdims=True)
            out_sum[half, :] += dot(a, down)
            grad_sum[half, :] += dot_nt(g, up)
        for j in range(2):
            o_small[pl.ds(4 * i + 2 * j + c, 1), :] = total[:, 128 * j : 128 * (j + 1)]
        value = dot_tn(active[...], cot[...]).astype(BF16)
        down_send[i] = jnp.where(y == 0, value[128:], value[:128])
        down_keep[i] = jnp.where(y == 0, value[:128], value[128:])
        down_copy(i).start()
        value = dot(second_t[...], hidden_grad[...]).astype(BF16)
        for k in range(4):
            first, last = value[256 * k : 256 * k + 128], value[256 * k + 128 : 256 * (k + 1)]
            up_send[i, k] = jnp.where(x == 0, last, first)
            up_keep[i, k] = jnp.where(x == 0, first, last)
        up_copy(i).start()
        return 0

    lax.fori_loop(0, STEPS, feed_step, 0)

    swap_out[0] = grad_sum[other, :].astype(BF16)
    grad_core = links.send(swap_out.at[0], swap_in.at[0], links.core)
    swap_out[1] = out_sum[other, :].astype(BF16)
    out_core = links.send(swap_out.at[1], swap_in.at[1], links.core)
    grad_core.wait_recv()

    def norm_rows(i, totals):
        rows = pl.ds(pl.multiple_of(128 * i, 128), 128)
        upstream = grad_sum[rows, :] + swap_in[0, rows, :].astype(F32)
        normal = unit[rows, :]
        scaled = upstream * gains
        inner = (
            scaled
            - jnp.mean(scaled, axis=-1, keepdims=True)
            - normal * jnp.mean(scaled * normal, axis=-1, keepdims=True)
        )
        value = cot[rows, :].astype(F32)
        grad = value + inverse[rows, 0:1] * inner
        o_grad[rows, :] = grad
        low[rows, :] = grad.astype(BF16)
        return (
            totals[0] + jnp.sum(upstream * normal, axis=0, keepdims=True),
            totals[1] + jnp.sum(value, axis=0, keepdims=True),
        )

    zero = jnp.zeros((1, D), F32)
    totals = lax.fori_loop(0, 4, norm_rows, (zero, zero))
    for k, value in enumerate(totals):
        for j in range(8):
            o_small[pl.ds(32 + 8 * k + j, 1), :] = value[:, 128 * j : 128 * (j + 1)]
    swap_out[2, :, :WIDTH] = dot_nt(low[...], wout[theirs, :]).astype(BF16)
    heads_core = links.send(
        swap_out.at[2, :, pl.ds(0, WIDTH)], swap_in.at[2, :, pl.ds(0, WIDTH)], links.core
    )
    o_heads[own, :] = dot_nt(low[...], wout[mine, :]).astype(BF16)
    o_wo[mine, :] = dot_tn(att[...], low[...]).astype(BF16)
    o_wo[theirs, :] = dot_tn(att_came[...], low[...]).astype(BF16)
    out_core.wait_recv()

    def out_rows(i, _):
        rows = pl.ds(pl.multiple_of(128 * i, 128), 128)
        o_out[rows, :] = (
            stem[rows, :]
            + (out_sum[rows, :] + swap_in[1, rows, :].astype(F32))
            + bias_down[0:1, :]
        ).astype(BF16)
        return 0

    lax.fori_loop(0, 4, out_rows, 0)
    heads_core.wait_recv()
    o_heads[other, :] = swap_in[2, :, :WIDTH]

    def add_step(i, _):
        down_copy(i).wait()
        o_down[lax.rem(i + x, 2), i // 2] = down_keep[i] + down_came[i]
        up_copy(i).wait()
        columns = pl.ds(pl.multiple_of(STEP * i, STEP), STEP)
        for k in range(4):
            value = up_keep[i, k] + up_came[i, k]
            for j in range(2):
                o_up[lax.rem(j + y, 2), k, :, columns] = value[64 * j : 64 * (j + 1)]
        return 0

    lax.fori_loop(0, STEPS, add_step, 0)
    links.drain()


def middle(att, stem, wout, gain, w_up, w_down, bias_up, bias_down, cot):
    hbm, vm = pl.BlockSpec(memory_space=HBM), pl.BlockSpec(memory_space=VMEM)
    low = lambda *shape: pltpu.VMEM(shape, BF16)
    full = lambda *shape: pltpu.VMEM(shape, F32)
    copies = 24
    return pl.pallas_call(
        middle_kernel,
        out_shape=[
            jax.ShapeDtypeStruct((FRAMES, D), BF16),
            jax.ShapeDtypeStruct((FRAMES, D), F32),
            jax.ShapeDtypeStruct((CHIP, WIDTH), BF16),
            jax.ShapeDtypeStruct((D, D), BF16),
            jax.ShapeDtypeStruct((2, 4, 128, D), BF16),
            jax.ShapeDtypeStruct((2, 4, 64, 2 * D), BF16),
            jax.ShapeDtypeStruct((48, 128), F32),
        ],
        in_specs=[hbm] * 3 + [vm] + [hbm] * 2 + [vm] * 2 + [hbm],
        out_specs=[vm] * 7,
        scratch_shapes=[
            low(FRAMES, WIDTH),
            low(FRAMES, WIDTH),
            full(FRAMES, D),
            low(D, D),
            low(STEPS, D, STEP),
            low(STEPS, STEP, D),
            low(CHIP, D),
            low(CHIP, D),
            low(D, CHIP),
            full(FRAMES, D),
            full(FRAMES, 128),
            low(CHIP, STEP),
            low(CHIP, STEP),
            full(CHIP, D),
            full(CHIP, D),
            low(FRAMES, D),
            low(3, FRAMES, D),
            low(3, FRAMES, D),
            low(STEPS, 128, D),
            low(STEPS, 128, D),
            low(STEPS, 128, D),
            low(STEPS, 4, 128, STEP),
            low(STEPS, 4, 128, STEP),
            low(STEPS, 4, 128, STEP),
            pltpu.SemaphoreType.DMA((4 + 4 * STEPS,)),
            pltpu.SemaphoreType.DMA((copies,)),
            pltpu.SemaphoreType.DMA((copies,)),
        ],
        name="middle",
        cost_estimate=pl.CostEstimate(
            flops=28_000_000_000, bytes_accessed=40_000_000, transcendentals=4_000_000
        ),
        compiler_params=pltpu.CompilerParams(
            collective_id=1, has_side_effects=True, vmem_limit_bytes=63 << 20
        ),
    )(att, stem, wout, gain, w_up, w_down, bias_up, bias_down, cot)


def tail_kernel(*refs):
    (
        down_in,
        down_came,
        up_in,
        up_came,
        wo_in,
        small_in,
        dq_in,
        dkv_in,
        seen_in,
        wq_in,
        wkv_in,
        joint_in,
        stem_in,
        grad_in,
        gain,
        wskip_in,
    ) = refs[:16]
    o_in, o_skip, o_down, o_up, o_qkv, o_wo, o_wskip, o_small, o_gain = refs[16:25]
    (
        dq,
        dkv,
        wide_buf,
        wq,
        wkv,
        joint,
        stem,
        grad,
        chip_out,
        chip_in,
        chip_own,
        halo_out,
        halo_in,
        halo_sum,
        halo,
        low,
        down_own,
        down_r2,
        down_r3,
        up_own,
        up_r2,
        up_r3,
        up_out,
        up_in_last,
        unit_own,
        unit_r1,
        unit_r2,
        unit_r3,
        wo_r0,
        join_out,
        skip_own,
        skip_out,
        skip_r0,
        skip_r1,
        skip_r2,
        skip_r3,
        small_steps,
        small_into,
        gain_steps,
        gain_into,
        loads,
        sends,
        recvs,
    ) = refs[25:]
    links = Links(sends, recvs)
    z, x, y, c = links.z, links.x, links.y, links.c
    loading = []

    def load(src, dst):
        copy = pltpu.make_async_copy(src, dst, loads.at[len(loading)])
        copy.start()
        loading.append(copy)
        return copy

    seen = wide_buf.at[pl.ds(0, CHIP + HALO)]
    got_dkv = load(dkv_in, dkv)
    got_wkv = load(wkv_in, wkv)
    got_dq = load(dq_in, dq)
    got_wq = load(wq_in, wq)
    got_seen = load(seen_in, seen)
    got_wo = load(wo_in.at[:, :, :, c], unit_own.at[0])
    got_small = load(small_in, small_steps.at[0])
    got_down = [
        [
            load(down_in.at[0, :, pl.ds(64 * i, 64)], down_own.at[i]),
            load(down_came.at[:, pl.ds(64 * i, 64)], down_r2.at[i]),
        ]
        for i in range(2)
    ]
    got_up = []
    for i, core in enumerate((1 - c, c)):
        rows = pl.ds(pl.multiple_of(32 * core, 32), 32)
        got_up.append(
            [load(up_in.at[0, :, rows], up_own.at[i]), load(up_came.at[:, rows], up_r2.at[i])]
        )
    got_stem = load(stem_in, stem)
    got_grad = load(grad_in, grad)
    got_joint = load(joint_in, joint)
    halo[pl.ds(0, EDGE), :] = jnp.zeros((EDGE, D), BF16)
    halo[pl.ds(EDGE + HALO, EDGE), :] = jnp.zeros((EDGE, D), BF16)
    links.greet()

    def to_down(i):
        def done(value):
            o_down[pl.ds(64 * i, 64), :] = value

        return done

    def to_up_other(value):
        up_out[...] = value
        up_last.append(links.send(up_out, up_in_last, links.core))

    def to_up_mine(value):
        for b in range(16):
            at = pl.multiple_of(256 * b + 128 * c, 128)
            o_up[:, pl.ds(at, 128)] = value[:, 128 * b : 128 * (b + 1)]

    up_last = []
    downs = [
        LateUnit(links, down_own.at[i], None, down_r2.at[i], down_r3.at[i], True, to_down(i))
        for i in range(2)
    ]
    ups = [
        LateUnit(links, up_own.at[i], None, up_r2.at[i], up_r3.at[i], False, done)
        for i, done in enumerate((to_up_other, to_up_mine))
    ]

    def to_wo(value):
        o_wo[...] = value

    def to_qkv(i):
        def done(value):
            o_qkv[:, pl.ds(D * i, D)] = value

        return done

    def to_wskip(q, half):
        def done(value):
            o_wskip[pl.ds(ROWS * half, ROWS), pl.ds(SKIP_COLS * q, SKIP_COLS)] = value

        return done

    def unit(k, y_first, done):
        return Unit(
            links, unit_own.at[k], unit_r1.at[k], unit_r2.at[k], unit_r3.at[k], y_first, done
        )

    wo = unit(0, False, to_wo)
    unit_q, unit_k, unit_v = [
        unit(1 + i, first, to_qkv(i)) for i, first in enumerate((False, True, False))
    ]
    skips = [
        [
            Unit(
                links,
                skip_own.at[2 * q + half],
                skip_r1.at[2 * q + half],
                skip_r2.at[2 * q + half],
                skip_r3.at[2 * q + half],
                half == 0,
                to_wskip(q, half),
            )
            for half in range(2)
        ]
        for q in range(SKIPS)
    ]

    def to_small(value):
        o_small[...] = value

    def to_gain(value):
        o_gain[...] = value

    small = Small(links, small_steps, small_into, to_small)
    gain_sum = Small(links, gain_steps, gain_into, to_gain)

    wo_core = links.send(wo_in.at[:, :, :, 1 - c], wo_r0, links.core)

    got_dkv.wait()
    got_wkv.wait()

    def halo_part(core):
        at = pl.multiple_of(CHIP + HALF * core, 128)
        return dot_nt(dkv[pl.ds(at, HALF), :], wkv[...])

    halo_out[...] = halo_part(1 - c).astype(BF16)
    halo_core = links.send(halo_out, halo_in, links.core)
    mine = halo_part(c)
    halo_core.wait_recv()
    halo_sum[...] = (mine + halo_in[...].astype(F32)).astype(BF16)
    part_at = pl.ds(pl.multiple_of(EDGE + HALF * c, 128), HALF)
    part = halo.at[part_at]
    halo_y = links.send(halo_sum, part, links.over_y)
    for one, got in zip(downs + ups, got_down + got_up):
        one.turn_second(*got)

    got_dq.wait()
    got_wq.wait()

    def chip_part(at):
        rows = pl.ds(at, 256)
        return dot_nt(dq[rows, :], wq[...]) + dot_nt(dkv[rows, :], wkv[...])

    def other_frames(i, _):
        at = pl.multiple_of(256 * i, 256)
        chip_out[pl.ds(at, 256), :] = chip_part(FRAMES + at).astype(BF16)
        return 0

    lax.fori_loop(0, 2, other_frames, 0)
    chip_core = links.send(chip_out, chip_in, links.core)
    got_wo.wait()
    wo_core.wait_recv()
    wo.add_core(wo_r0)
    wo.send_first()
    got_small.wait()
    small.send()

    got_seen.wait()

    def qkv_rows(i, _):
        rows = seen[:, pl.ds(pl.multiple_of(256 * i, 256), 256)].T
        values = [
            dot(rows[:, :CHIP], dq[...]),
            dot(rows, dkv[:, :WIDTH]),
            dot(rows, dkv[:, WIDTH:]),
        ]
        columns = pl.ds(pl.multiple_of(WIDTH * c, WIDTH), WIDTH)
        for k, value in enumerate(values):
            value = value.astype(BF16)
            for j in range(2):
                for m in range(2):
                    at = 128 * j + 64 * m
                    first, second = value[at : at + 32], value[at + 32 : at + 64]
                    unit_own[1 + k, i, j, m, :, columns] = jnp.where(c == 0, first, second)
                    join_out[k, i, j, m] = jnp.where(c == 0, second, first)
        return 0

    lax.fori_loop(0, 4, qkv_rows, 0)
    columns = pl.ds(pl.multiple_of(WIDTH * c, WIDTH), WIDTH)
    joins = [
        links.send(join_out.at[k], unit_own.at[1 + k, :, :, :, :, columns], links.core)
        for k in range(3)
    ]
    got_wskip = load(wskip_in, wide_buf)
    small.turn()

    def own_frames(i, _):
        at = pl.multiple_of(256 * i, 256)
        chip_own[pl.ds(at, 256), :] = chip_part(at)
        return 0

    lax.fori_loop(0, 2, own_frames, 0)
    for k, one in ((2, unit_v), (1, unit_k), (0, unit_q)):
        joins[k].wait_recv()
        one.send_first()
    small.turn()

    halo_y.wait_recv()
    halo_rest = links.send(part, part, links.core)
    chip_core.wait_recv()
    got_stem.wait()
    got_grad.wait()
    halo_rest.wait_recv()
    gains = gain[0:1, :]

    def norm_rows(i, total):
        at = pl.multiple_of(128 * i, 128)
        rows = pl.ds(at, 128)
        upstream = (
            chip_own[rows, :]
            + chip_in[rows, :].astype(F32)
            + halo[pl.ds(pl.multiple_of(at + 256 * (2 * c + y), 128), 128), :].astype(F32)
        )
        value = stem[rows, :]
        center = value - jnp.mean(value, axis=-1, keepdims=True)
        inverse = lax.rsqrt(jnp.mean(center * center, axis=-1, keepdims=True) + epsilon)
        unit_value = center * inverse
        scaled = upstream * gains
        inner = (
            scaled
            - jnp.mean(scaled, axis=-1, keepdims=True)
            - unit_value * jnp.mean(scaled * unit_value, axis=-1, keepdims=True)
        )
        low[rows, :] = (grad[rows, :] + inverse * inner).astype(BF16)
        return total + jnp.sum(upstream * unit_value, axis=0, keepdims=True)

    total = lax.fori_loop(0, 4, norm_rows, jnp.zeros((1, D), F32))
    gain_steps[0] = jnp.concatenate([total[:, 128 * i : 128 * (i + 1)] for i in range(8)], axis=0)
    gain_sum.send()
    got_joint.wait()

    skip_core = []
    for q in range(SKIPS):

        def skip_rows(i, _, q=q):
            value = dot(
                joint[pl.ds(pl.multiple_of(512 * i, 512), 512), :],
                low[:, SKIP_COLS * q : SKIP_COLS * (q + 1)],
            ).astype(BF16)
            for j in range(2):
                for m in range(2):
                    for half in range(2):
                        at = 256 * j + 128 * m + 32 * half
                        first, second = value[at : at + 32], value[at + 64 : at + 96]
                        skip_own[2 * q + half, i, j, m] = jnp.where(c == 0, first, second)
                        skip_out[2 * q + half, i, j, m] = jnp.where(c == 0, second, first)
            return 0

        lax.fori_loop(0, 4, skip_rows, 0)
        both = pl.ds(2 * q, 2)
        skip_core.append(links.send(skip_out.at[both], skip_r0.at[both], links.core))
        if q > 0:
            skip_core[q - 1].wait_recv()
            for half in range(2):
                skips[q - 1][half].add_core(skip_r0.at[2 * (q - 1) + half])
                skips[q - 1][half].send_first()
    q = SKIPS - 1
    skip_core[q].wait_recv()
    for half in range(2):
        skips[q][half].add_core(skip_r0.at[2 * q + half])
        skips[q][half].send_first()

    got_wskip.wait()

    def joined_part(i):
        value = dot_nt(low[...], wide_buf[pl.ds(256 * i, 256), :]).astype(BF16)
        out = o_in if i < 4 else o_skip
        out[:, pl.ds(256 * (i % 4), 256)] = value

    joined_part(0)
    joined_part(1)
    wo.turn_first()
    joined_part(2)
    joined_part(3)
    small.turn()
    gain_sum.turn()
    joined_part(4)
    joined_part(5)
    unit_v.turn_first()
    joined_part(6)
    joined_part(7)
    downs[0].finish()
    small.turn()
    gain_sum.turn()
    downs[1].finish()
    unit_q.turn_first()
    unit_k.turn_first()
    gain_sum.turn()
    ups[0].finish()
    for q in range(SKIPS):
        for half in (1, 0):
            skips[q][half].turn_first()
    gain_sum.turn()
    wo.turn_second()
    ups[1].finish()
    unit_v.turn_second()
    unit_k.turn_second()
    unit_q.turn_second()
    up_last[0].wait_recv()
    for b in range(16):
        at = pl.multiple_of(256 * b + 128 * (1 - c), 128)
        o_up[:, pl.ds(at, 128)] = up_in_last[:, 128 * b : 128 * (b + 1)]
    wo.finish()
    for q in range(SKIPS):
        for half in (1, 0):
            skips[q][half].turn_second()
    unit_v.finish()
    unit_k.finish()
    unit_q.finish()
    for q in range(SKIPS):
        for half in (1, 0):
            skips[q][half].finish()
    links.drain()


def tail(down, down_came, up, up_came, wo, small, dq, dkv, seen, wq, wkv, joint, stem, grad, gain, wskip):
    hbm, vm = pl.BlockSpec(memory_space=HBM), pl.BlockSpec(memory_space=VMEM)
    n_small = small.shape[0]
    out_shape = [
        jax.ShapeDtypeStruct((FRAMES, D), BF16),
        jax.ShapeDtypeStruct((FRAMES, D), BF16),
        jax.ShapeDtypeStruct((128, D), F32),
        jax.ShapeDtypeStruct((32, 4096), F32),
        jax.ShapeDtypeStruct((32, 3 * D), F32),
        jax.ShapeDtypeStruct((32, D), F32),
        jax.ShapeDtypeStruct((64, D), F32),
        jax.ShapeDtypeStruct((n_small, 128), F32),
        jax.ShapeDtypeStruct((8, 128), F32),
    ]
    low = lambda *shape: pltpu.VMEM(shape, BF16)
    full = lambda *shape: pltpu.VMEM(shape, F32)
    skip = (ROWS, SKIP_COLS)
    copies = 104
    scratch = [
        low(CHIP, WIDTH),
        low(CHIP + HALO, D),
        low(2 * D, D),
        low(D, WIDTH),
        low(D, D),
        low(2 * D, FRAMES),
        full(FRAMES, D),
        full(FRAMES, D),
        low(FRAMES, D),
        low(FRAMES, D),
        full(FRAMES, D),
        low(HALF, D),
        low(HALF, D),
        low(HALF, D),
        low(HALO + 2 * EDGE, D),
        low(FRAMES, D),
        low(2, 4, 64, D),
        low(2, 4, 64, D),
        low(2, 3, 64, D),
        low(2, 4, 32, 2 * D),
        low(2, 4, 32, 2 * D),
        low(2, 3, 32, 2 * D),
        full(32, 2 * D),
        full(32, 2 * D),
        low(4, 4, 2, 2, ROWS, D),
        low(4, 4, 2, ROWS, D),
        low(4, 4, ROWS, D),
        low(4, 3, ROWS, D),
        low(4, 2, 2, ROWS, D),
        low(3, 4, 2, 2, ROWS, WIDTH),
        low(2 * SKIPS, 4, 2, 2, *skip),
        low(2 * SKIPS, 4, 2, 2, *skip),
        low(2 * SKIPS, 4, 2, 2, *skip),
        low(2 * SKIPS, 4, 2, *skip),
        low(2 * SKIPS, 4, *skip),
        low(2 * SKIPS, 3, *skip),
        full(4, n_small, 128),
        full(6, n_small, 128),
        full(4, 8, 128),
        full(6, 8, 128),
        pltpu.SemaphoreType.DMA((20,)),
        pltpu.SemaphoreType.DMA((copies,)),
        pltpu.SemaphoreType.DMA((copies,)),
    ]
    return pl.pallas_call(
        tail_kernel,
        out_shape=out_shape,
        in_specs=[hbm] * 14 + [vm, hbm],
        out_specs=[vm] * 9,
        scratch_shapes=scratch,
        name="tail",
        cost_estimate=pl.CostEstimate(
            flops=17_000_000_000, bytes_accessed=60_000_000, transcendentals=0
        ),
        compiler_params=pltpu.CompilerParams(
            collective_id=0, has_side_effects=True, vmem_limit_bytes=63 << 20
        ),
    )(
        down,
        down_came,
        up,
        up_came,
        wo.reshape(4, 2, 2, 2, 32, D),
        small,
        dq,
        dkv,
        seen,
        wq,
        wkv,
        joint,
        stem,
        grad,
        gain,
        wskip,
    )


def swap_x(value):
    return lax.ppermute(value, "rows", [(r, r ^ 1) for r in range(8)])


def swap_core(value):
    return lax.ppermute(value, "seq", [(i, i ^ 1) for i in range(4)])


def swap_chip(value):
    return lax.ppermute(value, "seq", [(i, i ^ 2) for i in range(4)])


def body_chips(
    inputs,
    skip_feats,
    seg_ids,
    frame_valid,
    w_skip,
    gain_one,
    w_qkv,
    w_out,
    gain_two,
    w_up,
    b_up,
    w_down,
    b_down,
    cotangent,
):
    here = lax.axis_index("seq")
    y, c = here // 2, here % 2
    frames = inputs.shape[1]
    heads = H // 2
    width = heads * HD
    first, second_in, cot = inputs[0], skip_feats[0], cotangent[0]
    gain_first = gain_one.astype(F32)
    gain_second = gain_two.astype(F32)

    halo_at = jnp.where(y == 0, CHIP, CHIP - HALO)
    own_at, other_at = here * frames, (here ^ 1) * frames
    seg_row = seg_ids[0]
    code_row = jnp.where(frame_valid[0] == 1, seg_row, -1)

    def seen(row):
        return jnp.concatenate(
            [
                lax.dynamic_slice(row, (own_at,), (frames,)),
                lax.dynamic_slice(row, (other_at,), (frames,)),
                lax.dynamic_slice(row, (halo_at,), (HALO,)),
            ]
        )

    seg_seen = seen(seg_row)
    kcode = jnp.broadcast_to(seen(code_row)[:, None], (CHIP + HALO, 128))
    qseg = jnp.broadcast_to(seg_seen[None, :CHIP], (8, CHIP))

    def spans(count, block):
        at = jnp.arange(0, count, block)
        base = jnp.where(at < frames, own_at, jnp.where(at < CHIP, other_at - frames, halo_at - CHIP))
        seg = seg_seen[:count].reshape(-1, block)
        return jnp.stack([seg[:, 0], seg[:, -1], base + at]).astype(jnp.int32)

    slopes = LOG2E * jnp.exp2(-8.0 * (c * heads + jnp.arange(heads) + 1).astype(F32) / H)

    w_q, w_k, w_v = [
        lax.dynamic_slice(w_qkv, (0, i * D + c * width), (D, width)) for i in range(3)
    ]
    w_kv = jnp.concatenate([w_k, w_v], axis=1)

    joined = jnp.concatenate([first, second_in], axis=-1)
    stem_out = mm("fc,cd->fd", joined, w_skip)
    unit_one, inverse_one, normed = norm_forward(stem_out, gain_first)
    normed = normed.astype(BF16)
    normed_other = swap_core(normed)
    around = jnp.concatenate([normed, normed_other, normed], axis=0)
    half = HALF
    part_at = c * frames + jnp.where(y == 0, CHIP - HALO, 0) + half * c
    halo_part = swap_chip(lax.dynamic_slice(around, (part_at, 0), (half, D)))
    halo_rest = swap_core(halo_part)
    halo_parts = jnp.concatenate([halo_part, halo_rest, halo_part], axis=0)
    halo = lax.dynamic_slice(halo_parts, (c * half, 0), (HALO, D))
    normed_seen = jnp.concatenate([normed, normed_other, halo], axis=0)
    q = mm("fd,de->fe", normed_seen[:CHIP], w_q).astype(BF16)
    kv = mm("fd,de->fe", normed_seen, w_kv).astype(BF16)

    attended, attended_t, lse = attend(
        spans(CHIP + HALO, 128), spans(CHIP, 128), slopes, q, kv, kcode, qseg, 128, 128, heads
    )
    bias = lax.dynamic_index_in_dim(b_up.astype(F32).reshape(16, 2, 128), c, 1, keepdims=False)
    output, middle_grad, grad_heads, out_grad, down_sum, up_sum, small = middle(
        attended,
        stem_out,
        w_out,
        jnp.broadcast_to(gain_second, (8, D)),
        w_up,
        w_down,
        jnp.broadcast_to(bias.reshape(1, -1), (8, 2 * D)),
        jnp.broadcast_to(b_down.astype(F32), (8, D)),
        cot,
    )
    down_came, up_came = swap_x(down_sum[1]), swap_chip(up_sum[1])
    dq, dkv = attend_back(
        spans(CHIP + HALO, 256),
        spans(CHIP, 512),
        slopes,
        q,
        kv,
        grad_heads,
        attended_t,
        lse,
        kcode,
        qseg,
        512,
        256,
        heads,
    )
    (
        input_grad,
        skip_grad,
        down_share,
        up_share,
        qkv_share,
        out_share,
        skip_share,
        small_sum,
        gain_sum,
    ) = tail(
        down_sum,
        down_came,
        up_sum,
        up_came,
        out_grad,
        small,
        dq,
        dkv,
        normed_seen,
        w_q,
        w_kv,
        joined.T,
        stem_out,
        middle_grad,
        jnp.broadcast_to(gain_first, (8, D)),
        w_skip,
    )
    device = lax.axis_index("rows") * 4 + here

    def mine(rows):
        size = rows.size // 32
        return lax.dynamic_slice(rows.reshape(-1), (device * size,), (size,))

    return (
        output[None],
        input_grad[None],
        skip_grad[None],
        skip_share,
        mine(gain_sum),
        qkv_share,
        out_share,
        mine(small_sum[32:40]),
        up_share,
        mine(small_sum[:32]),
        down_share,
        mine(small_sum[40:]),
    )


def block_scores(q_blk, pos_blk, seg_blk, all_keys, seg_row, valid_row, slopes, score_scale):
    key_pos = jnp.arange(all_keys.shape[0])
    scores = (
        jnp.einsum("qhd,khd->hqk", q_blk, all_keys, preferred_element_type=jnp.float32)
        * score_scale
    )
    distance = jnp.abs(pos_blk[:, None] - key_pos[None, :]).astype(jnp.float32)
    scores = scores - slopes[:, None, None] * distance[None]
    allowed = (seg_blk[:, None] == seg_row[None, :]) & (
        (valid_row[None, :] == 1) | (pos_blk[:, None] == key_pos[None, :])
    )
    return jnp.where(allowed[None], scores, -jnp.inf)


def split_row(packed_row, heads_local):
    length = packed_row.shape[0]
    qkv_rows = packed_row.reshape(length, 3, heads_local, HD)
    return (qkv_rows[:, 0], qkv_rows[:, 1], qkv_rows[:, 2])


def attend_row(packed_row, seg_row, valid_row, slopes, heads_local, block_rows, score_scale):
    length = packed_row.shape[0]
    queries, all_keys, all_values = split_row(packed_row, heads_local)
    count = length // block_rows
    positions = jnp.arange(length)

    def one_block(block_in):
        q_blk, pos_blk, seg_blk = block_in
        scores = block_scores(
            q_blk, pos_blk, seg_blk, all_keys, seg_row, valid_row, slopes, score_scale
        )
        peak = jnp.max(scores, axis=-1, keepdims=True)
        log_total = peak + jnp.log(jnp.sum(jnp.exp(scores - peak), axis=-1, keepdims=True))
        attn_probs = jnp.exp(scores - log_total).astype(jnp.bfloat16)
        attended = jnp.einsum(
            "hqk,khd->qhd", attn_probs, all_values, preferred_element_type=jnp.float32
        )
        return (attended.astype(jnp.bfloat16), log_total[..., 0])

    attended, log_total = lax.map(
        one_block,
        (
            queries.reshape(count, block_rows, heads_local, HD),
            positions.reshape(count, block_rows),
            seg_row.reshape(count, block_rows),
        ),
    )
    return (attended.reshape(length, 1, heads_local * HD), log_total)


def attend_row_back(
    packed_row,
    log_total,
    grad_row,
    seg_row,
    valid_row,
    slopes,
    heads_local,
    block_rows,
    score_scale,
):
    length = packed_row.shape[0]
    queries, all_keys, all_values = split_row(packed_row, heads_local)
    count = length // block_rows
    positions = jnp.arange(length)
    grad_out = grad_row.reshape(count, block_rows, heads_local, HD)

    def one_block(carry, block_in):
        key_grad, value_grad = carry
        q_blk, pos_blk, seg_blk, total_blk, grad_blk = block_in
        scores = block_scores(
            q_blk, pos_blk, seg_blk, all_keys, seg_row, valid_row, slopes, score_scale
        )
        soft = jnp.exp(scores - total_blk[..., None])
        value_grad = value_grad + jnp.einsum(
            "hqk,qhd->khd", soft.astype(jnp.bfloat16), grad_blk, preferred_element_type=jnp.float32
        )
        prob_grad = jnp.einsum(
            "qhd,khd->hqk", grad_blk, all_values, preferred_element_type=jnp.float32
        )
        score_grad = (
            soft * (prob_grad - jnp.sum(soft * prob_grad, axis=-1, keepdims=True))
        ).astype(jnp.bfloat16)
        query_grad = (
            jnp.einsum("hqk,khd->qhd", score_grad, all_keys, preferred_element_type=jnp.float32)
            * score_scale
        )
        key_grad = (
            key_grad
            + jnp.einsum("hqk,qhd->khd", score_grad, q_blk, preferred_element_type=jnp.float32)
            * score_scale
        )
        return ((key_grad, value_grad), query_grad)

    zero_rows = jnp.zeros((length, heads_local, HD), jnp.float32)
    (key_grad, value_grad), query_grad = lax.scan(
        one_block,
        (zero_rows, zero_rows),
        (
            queries.reshape(count, block_rows, heads_local, HD),
            positions.reshape(count, block_rows),
            seg_row.reshape(count, block_rows),
            log_total,
            grad_out,
        ),
    )
    stacked = jnp.stack([query_grad.reshape(length, heads_local, HD), key_grad, value_grad], axis=1)
    return stacked.astype(jnp.bfloat16).reshape(length, 3, 1, heads_local * HD)


def body(
    inputs,
    skip_feats,
    seg_ids,
    frame_valid,
    w_skip,
    gain_one,
    w_qkv,
    w_out,
    gain_two,
    w_up,
    b_up,
    w_down,
    b_down,
    cotangent,
):
    parts = lax.axis_size("seq")
    heads_local = H // parts
    width_local = heads_local * HD
    rows_here = inputs.shape[0]
    frames = inputs.shape[1]
    length = frames * parts
    block_rows = min(512, length)
    score_scale = 1.0 / math.sqrt(HD)
    first_head = lax.axis_index("seq") * heads_local
    slopes = jnp.exp2(-8.0 * (first_head + jnp.arange(heads_local) + 1).astype(jnp.float32) / H)
    gain_first = gain_one.astype(jnp.float32)
    gain_second = gain_two.astype(jnp.float32)
    bias_up = b_up.astype(jnp.float32)
    joined = jnp.concatenate([inputs, skip_feats], axis=-1)
    stem_out = jnp.einsum("rfc,cd->rfd", joined, w_skip, preferred_element_type=jnp.float32)
    unit_one, inverse_one, normed = norm_forward(stem_out, gain_first)
    normed = normed.astype(jnp.bfloat16)
    packed = jnp.einsum("rfd,de->rfe", normed, w_qkv, preferred_element_type=jnp.float32).astype(
        jnp.bfloat16
    )
    packed = packed.reshape(rows_here, frames, 3, parts, width_local)
    by_heads = lax.all_to_all(packed, "seq", split_axis=3, concat_axis=1, tiled=True)

    def forward_row(row_data):
        return attend_row(
            row_data[0], row_data[1], row_data[2], slopes, heads_local, block_rows, score_scale
        )

    attended, log_total = lax.map(forward_row, (by_heads, seg_ids, frame_valid))
    by_frames = lax.all_to_all(attended, "seq", split_axis=1, concat_axis=2, tiled=True)
    mixed_out = by_frames.reshape(rows_here, frames, D)
    middle = stem_out + jnp.einsum(
        "rfd,de->rfe", mixed_out, w_out, preferred_element_type=jnp.float32
    )
    unit_two, inverse_two, second = norm_forward(middle, gain_second)
    second = second.astype(jnp.bfloat16)
    hidden = jnp.einsum("rfd,dk->rfk", second, w_up, preferred_element_type=jnp.float32) + bias_up
    active_full, gelu_back = jax.vjp(gelu_exact, hidden)
    active = active_full.astype(jnp.bfloat16)
    result = (
        middle
        + jnp.einsum("rfk,kd->rfd", active, w_down, preferred_element_type=jnp.float32)
        + b_down.astype(jnp.float32)
    )
    output = result.astype(jnp.bfloat16)
    cot_full = cotangent.astype(jnp.float32)
    down_grad = jnp.einsum("rfk,rfd->kd", active, cotangent, preferred_element_type=jnp.float32)
    bias_down_grad = jnp.sum(cot_full, axis=(0, 1))
    active_grad = jnp.einsum("rfd,kd->rfk", cotangent, w_down, preferred_element_type=jnp.float32)
    hidden_grad = gelu_back(active_grad)[0].astype(jnp.bfloat16)
    up_grad = jnp.einsum("rfd,rfk->dk", second, hidden_grad, preferred_element_type=jnp.float32)
    bias_up_grad = jnp.sum(hidden_grad.astype(jnp.float32), axis=(0, 1))
    second_grad = jnp.einsum("rfk,dk->rfd", hidden_grad, w_up, preferred_element_type=jnp.float32)
    middle_part, gain_two_grad = norm_backward(second_grad, unit_two, inverse_two, gain_second)
    middle_grad = cot_full + middle_part
    middle_low = middle_grad.astype(jnp.bfloat16)
    out_grad = jnp.einsum("rfd,rfe->de", mixed_out, middle_low, preferred_element_type=jnp.float32)
    mixed_grad = jnp.einsum(
        "rfe,de->rfd", middle_low, w_out, preferred_element_type=jnp.float32
    ).astype(jnp.bfloat16)
    grad_heads = lax.all_to_all(
        mixed_grad.reshape(rows_here, frames, parts, width_local),
        "seq",
        split_axis=2,
        concat_axis=1,
        tiled=True,
    )

    def backward_row(row_data):
        return attend_row_back(
            row_data[0],
            row_data[1],
            row_data[2],
            row_data[3],
            row_data[4],
            slopes,
            heads_local,
            block_rows,
            score_scale,
        )

    packed_grad = lax.map(backward_row, (by_heads, log_total, grad_heads, seg_ids, frame_valid))
    packed_back = lax.all_to_all(packed_grad, "seq", split_axis=1, concat_axis=3, tiled=True)
    packed_back = packed_back.reshape(rows_here, frames, 3 * D)
    qkv_grad = jnp.einsum("rfd,rfe->de", normed, packed_back, preferred_element_type=jnp.float32)
    normed_grad = jnp.einsum("rfe,de->rfd", packed_back, w_qkv, preferred_element_type=jnp.float32)
    stem_part, gain_one_grad = norm_backward(normed_grad, unit_one, inverse_one, gain_first)
    stem_low = (middle_grad + stem_part).astype(jnp.bfloat16)
    skip_w_grad = jnp.einsum("rfc,rfd->cd", joined, stem_low, preferred_element_type=jnp.float32)
    joined_grad = jnp.einsum("rfd,cd->rfc", stem_low, w_skip, preferred_element_type=jnp.float32)
    input_grad = joined_grad[..., :D].astype(jnp.bfloat16)
    skip_grad = joined_grad[..., D:].astype(jnp.bfloat16)
    (
        skip_share,
        gain_one_share,
        qkv_share,
        out_share,
        gain_two_share,
        up_share,
        bias_up_share,
        down_share,
        bias_down_share,
    ) = (
        lax.psum_scatter(skip_w_grad, ("rows", "seq"), scatter_dimension=0, tiled=True),
        lax.psum_scatter(gain_one_grad, ("rows", "seq"), scatter_dimension=0, tiled=True),
        lax.psum_scatter(qkv_grad, ("rows", "seq"), scatter_dimension=0, tiled=True),
        lax.psum_scatter(out_grad, ("rows", "seq"), scatter_dimension=0, tiled=True),
        lax.psum_scatter(gain_two_grad, ("rows", "seq"), scatter_dimension=0, tiled=True),
        lax.psum_scatter(up_grad, ("rows", "seq"), scatter_dimension=0, tiled=True),
        lax.psum_scatter(bias_up_grad, ("rows", "seq"), scatter_dimension=0, tiled=True),
        lax.psum_scatter(down_grad, ("rows", "seq"), scatter_dimension=0, tiled=True),
        lax.psum_scatter(bias_down_grad, ("rows", "seq"), scatter_dimension=0, tiled=True),
    )
    return (
        output,
        input_grad,
        skip_grad,
        skip_share,
        gain_one_share,
        qkv_share,
        out_share,
        gain_two_share,
        up_share,
        bias_up_share,
        down_share,
        bias_down_share,
    )


def solution(mesh):
    fits = (mesh.shape["rows"], mesh.shape["seq"]) == (8, 4)
    return jax.shard_map(
        body_chips if fits else body,
        mesh=mesh,
        in_specs=(
            P("rows", "seq", None),
            P("rows", "seq", None),
            P("rows", None),
            P("rows", None),
            P(),
            P(),
            P(),
            P(),
            P(),
            P(),
            P(),
            P(),
            P(),
            P("rows", "seq", None),
        ),
        out_specs=(
            P("rows", "seq", None),
            P("rows", "seq", None),
            P("rows", "seq", None),
            P(("rows", "seq"), None),
            P(("rows", "seq")),
            P(("rows", "seq"), None),
            P(("rows", "seq"), None),
            P(("rows", "seq")),
            P(("rows", "seq"), None),
            P(("rows", "seq")),
            P(("rows", "seq"), None),
            P(("rows", "seq")),
        ),
        check_vma=False,
    )
```

```python
import functools
import math

import jax
import jax.numpy as jnp
from jax import lax
from jax.experimental import pallas as pl
from jax.experimental.pallas import tpu as pltpu
from jax.sharding import PartitionSpec as P

D = 1024
H = 16
HD = 64
MOST = 682

epsilon = 1e-05

F32 = jnp.float32
BF16 = jnp.bfloat16
LOG2E = 1.4426950408889634
ROWS = 32
CHIP = 1024
HALO = 768
FRAMES = 512
HALF = HALO // 2
EDGE = CHIP - HALO
WIDTH = D // 2
SKIPS = 4
SKIP_COLS = D // SKIPS
FAR = 1e30
MESH = pl.DeviceIdType.MESH
VMEM = pltpu.MemorySpace.VMEM
SMEM = pltpu.MemorySpace.SMEM
HBM = pltpu.MemorySpace.HBM


def norm_forward(value, gain_vec):
    center = value - jnp.mean(value, axis=-1, keepdims=True)
    spread = jnp.mean(center * center, axis=-1, keepdims=True)
    inverse = lax.rsqrt(spread + epsilon)
    unit = center * inverse
    return (unit, inverse, unit * gain_vec)


def norm_backward(upstream, unit, inverse, gain_vec):
    scaled = upstream * gain_vec
    gain_grad = jnp.sum(upstream * unit, axis=tuple(range(upstream.ndim - 1)))
    inner = (
        scaled
        - jnp.mean(scaled, axis=-1, keepdims=True)
        - unit * jnp.mean(scaled * unit, axis=-1, keepdims=True)
    )
    return (inverse * inner, gain_grad)


def gelu_exact(value):
    return jax.nn.gelu(value, approximate=False)


def mm(equation, left, right):
    return jnp.einsum(equation, left, right, preferred_element_type=F32)


def dot(left, right):
    return jnp.dot(left, right, preferred_element_type=F32)


def dot_nt(left, right):
    return lax.dot_general(left, right, (((1,), (1,)), ((), ())), preferred_element_type=F32)


def dot_tn(left, right):
    return lax.dot_general(left, right, (((0,), (0,)), ((), ())), preferred_element_type=F32)


class Links:
    def __init__(self, sends, recvs):
        row, col = lax.axis_index("rows"), lax.axis_index("seq")
        self.z, self.x, self.y, self.c = row // 2, row % 2, col // 2, col % 2
        z, x, y, c = self.z, self.x, self.y, self.c
        self.high, self.low = z // 2, z % 2
        self.core = (row, y * 2 + 1 - c)
        self.over_y = (row, (1 - y) * 2 + c)
        self.over_x = (z * 2 + 1 - x, col)
        self.over_low = ((self.high * 2 + 1 - self.low) * 2 + x, col)
        self.over_high = (((1 - self.high) * 2 + self.low) * 2 + x, col)
        self.sends, self.recvs, self.count, self.started = sends, recvs, 0, []

    def greet(self, near=False):
        barrier = pltpu.get_barrier_semaphore()
        peers = [self.core, self.over_y] if near else [self.core, self.over_y, self.over_x, self.over_low, self.over_high]
        for peer in peers:
            pl.semaphore_signal(barrier, inc=1, device_id=peer, device_id_type=MESH)
        pl.semaphore_wait(barrier, len(peers))

    def reserve(self, number):
        self.count += number
        return self.count - number

    def copy(self, src, dst, at, peer):
        return pltpu.make_async_remote_copy(
            src, dst, self.sends.at[at], self.recvs.at[at], device_id=peer, device_id_type=MESH
        )

    def send(self, src, dst, peer):
        copy = self.copy(src, dst, self.reserve(1), peer)
        copy.start()
        self.started.append(copy)
        return copy

    def drain(self):
        assert self.count <= self.sends.shape[0]
        for copy in self.started:
            copy.wait_send()


def head_columns(wqkv, part, core):
    return wqkv.at[:, pl.ds(pl.multiple_of(D * part + WIDTH * core, WIDTH), WIDTH)]


def front_kernel(*refs):
    first_in, second_in, wskip_in, gain, wqkv_in = refs[:5]
    outs = refs[5:10]
    first, second, wskip, wq, wkv, o_stem, o_seen, o_q, o_kv, o_joint, loads, stores, sends, recvs = refs[10:]
    storing = []

    def store(k, *at):
        src, dst = (o_stem, o_seen, o_q, o_kv, o_joint)[k].at[*at], outs[k].at[*at]
        copy = pltpu.make_async_copy(src, dst, stores.at[len(storing)])
        copy.start()
        storing.append(copy)

    links = Links(sends, recvs)
    y, c = links.y, links.c
    loading = []

    def load(src, dst):
        copy = pltpu.make_async_copy(src, dst, loads.at[len(loading)])
        copy.start()
        loading.append(copy)
        return copy

    got = [load(first_in, first), load(second_in, second), load(wskip_in, wskip)]
    got_wkv = [
        load(head_columns(wqkv_in, 1 + i, c), wkv.at[:, pl.ds(WIDTH * i, WIDTH)]) for i in (0, 1)
    ]
    got_wq = load(head_columns(wqkv_in, 0, c), wq)
    links.greet(near=True)
    for copy in got:
        copy.wait()
    gains = gain[0:1, :]
    base = jnp.where(y == 0, EDGE, 0) + HALF * c

    def piece(i, chip):
        return 128 * jnp.where(chip == 0, i, 2 - i)

    def send_piece(i):
        at = lax.rem(base + piece(i, y) + FRAMES * c, CHIP)
        there = CHIP + HALF * c + piece(i, y)
        src = o_seen.at[pl.ds(pl.multiple_of(at, 128), 128)]
        dst = o_seen.at[pl.ds(pl.multiple_of(there, 128), 128)]
        return links.send(src, dst, links.over_y)

    pieces, across = [], []
    for turn in range(2):
        at = pl.multiple_of(256 * (1 - c if turn == 0 else c), 256)
        rows = pl.ds(at, 256)
        value = dot(first[rows, :], wskip[:D, :]) + dot(second[rows, :], wskip[D:, :])
        o_stem[rows, :] = value
        center = value - jnp.mean(value, axis=-1, keepdims=True)
        rate = lax.rsqrt(jnp.mean(center * center, axis=-1, keepdims=True) + epsilon)
        o_seen[rows, :] = (center * rate * gains).astype(BF16)
        pieces.append(send_piece(turn))
        there = o_seen.at[pl.ds(pl.multiple_of(FRAMES + at, 256), 256)]
        across.append(links.send(o_seen.at[rows], there, links.core))
    store(0, pl.ds(0, FRAMES))
    for copy in across:
        copy.wait_recv()
    pieces.append(send_piece(2))
    store(1, pl.ds(0, CHIP))
    for copy in (*got_wkv, got_wq):
        copy.wait()

    def own_part(i, _):
        rows = pl.ds(pl.multiple_of(256 * i, 256), 256)
        o_q[rows, :] = dot(o_seen[rows, :], wq[...]).astype(BF16)
        o_kv[rows, :] = dot(o_seen[rows, :], wkv[...]).astype(BF16)
        return 0

    lax.fori_loop(0, 4, own_part, 0)
    store(2, pl.ds(0, CHIP))
    store(3, pl.ds(0, CHIP))
    o_joint[:D, :] = first[...].T
    forward = []

    def far_part(i, core):
        at = pl.multiple_of(CHIP + HALF * core + piece(i, 1 - y), 128)
        rows = pl.ds(at, 128)
        o_kv[rows, :] = dot(o_seen[rows, :], wkv[...]).astype(BF16)

    for i in range(3):
        pieces[i].wait_recv()
        at = pl.multiple_of(CHIP + HALF * c + piece(i, 1 - y), 128)
        rows = o_seen.at[pl.ds(at, 128)]
        forward.append(links.send(rows, rows, links.core))
        if i == 0:
            o_joint[D:, :] = second[...].T
            store(4, pl.ds(0, 2 * D))
        far_part(i, c)
        if i > 0:
            forward[i - 1].wait_recv()
            far_part(i - 1, 1 - c)
    forward[2].wait_recv()
    store(1, pl.ds(CHIP, HALO))
    far_part(2, 1 - c)
    store(3, pl.ds(CHIP, HALO))
    links.drain()
    for copy in storing:
        copy.wait()


def front(first, second, wskip, gain, wqkv):
    hbm, vm = pl.BlockSpec(memory_space=HBM), pl.BlockSpec(memory_space=VMEM)
    low = lambda *shape: pltpu.VMEM(shape, BF16)
    return pl.pallas_call(
        front_kernel,
        out_shape=[
            jax.ShapeDtypeStruct((FRAMES, D), F32),
            jax.ShapeDtypeStruct((CHIP + HALO, D), BF16),
            jax.ShapeDtypeStruct((CHIP, WIDTH), BF16),
            jax.ShapeDtypeStruct((CHIP + HALO, 2 * WIDTH), BF16),
            jax.ShapeDtypeStruct((2 * D, FRAMES), BF16),
        ],
        in_specs=[hbm] * 3 + [vm, hbm],
        out_specs=[hbm] * 5,
        scratch_shapes=[
            low(FRAMES, D),
            low(FRAMES, D),
            low(2 * D, D),
            low(D, WIDTH),
            low(D, 2 * WIDTH),
            pltpu.VMEM((FRAMES, D), F32),
            low(CHIP + HALO, D),
            low(CHIP, WIDTH),
            low(CHIP + HALO, 2 * WIDTH),
            low(2 * D, FRAMES),
            pltpu.SemaphoreType.DMA((6,)),
            pltpu.SemaphoreType.DMA((7,)),
            pltpu.SemaphoreType.DMA((8,)),
            pltpu.SemaphoreType.DMA((8,)),
        ],
        name="front",
        cost_estimate=pl.CostEstimate(
            flops=8_000_000_000, bytes_accessed=24_000_000, transcendentals=0
        ),
        compiler_params=pltpu.CompilerParams(
            collective_id=2, has_side_effects=True, vmem_limit_bytes=63 << 20
        ),
    )(first, second, wskip, gain, wqkv)


class Frames:
    def __init__(self, seg_at, seg, valid, key_code, query_seg):
        here = lax.axis_index("seq")
        self.seg_at = seg_at
        self.own, self.other = FRAMES * here, FRAMES * (here + 1 - 2 * (here % 2))
        self.halo = jnp.where(here // 2 == 0, CHIP, CHIP - HALO)
        self.core = here % 2
        places = [(0, FRAMES, self.own), (FRAMES, FRAMES, self.other), (CHIP, HALO, self.halo)]
        for at, count, frame in places:
            span = pl.ds(pl.multiple_of(frame, 256), count)
            code = jnp.where(valid[0:1, span] == 1, seg[0:1, span], -1).astype(F32)
            key_code[pl.ds(at, count), :] = jnp.broadcast_to(code, (128, count)).T
            if at < CHIP:
                query_seg[:, pl.ds(at, count)] = jnp.broadcast_to(
                    seg[0:1, span].astype(F32), (8, count)
                )

    def frame(self, at):
        late = jnp.where(at < CHIP, self.other - FRAMES, self.halo - CHIP)
        return at + jnp.where(at < FRAMES, self.own, late)

    def meet(self, keys_at, keys, queries_at, queries):
        k, q = self.frame(keys_at), self.frame(queries_at)
        return (self.seg_at[0, k] <= self.seg_at[0, q + queries - 1]) & (
            self.seg_at[0, k + keys - 1] >= self.seg_at[0, q]
        )

    def slope(self, h):
        values = [LOG2E * 2.0 ** (-8.0 * (core * H // 2 + h + 1) / H) for core in (0, 1)]
        return jnp.where(self.core == 0, values[0], values[1])


def set_distances(dist, key_at, query_at, key_code, query_seg):
    keys, queries = dist.shape
    rows = lax.broadcasted_iota(jnp.int32, (keys, queries), 0) + key_at
    cols = lax.broadcasted_iota(jnp.int32, (keys, queries), 1) + query_at
    apart = jnp.abs(rows - cols)
    allowed = (key_code == query_seg) | (apart == 0)
    dist[...] = jnp.where(allowed, apart.astype(F32), FAR)


def wide(code, queries):
    return jnp.concatenate([code] * (queries // 128), axis=1) if queries > 128 else code


def both_heads(ref, pair, queries):
    first = ref[pl.ds(128 * pair, HD), queries]
    second = ref[pl.ds(128 * pair + HD, HD), queries]
    blank = jnp.zeros_like(first)
    return jnp.concatenate(
        [
            jnp.concatenate([first, blank], axis=0),
            jnp.concatenate([blank, second], axis=0),
        ],
        axis=1,
    )


def both_slopes(dist, frames, pair):
    value = dist[...]
    return jnp.concatenate(
        [value * frames.slope(2 * pair), value * frames.slope(2 * pair + 1)], axis=1
    )


def attend_kernel(
    bq,
    bk,
    heads,
    seg_at,
    q_in,
    kv_in,
    seg,
    valid,
    o_out,
    o_outt,
    lse,
    q,
    kv,
    out,
    outt,
    loads,
    stores,
    kcode,
    qseg,
    qt,
    vt,
    dist,
    acc,
    top,
    total,
    heads_q,
    scores,
    probs,
):
    width = heads * HD
    pairs = range(heads // 2)
    c1 = LOG2E / math.sqrt(HD)
    keys, values = pl.ds(0, width), pl.ds(width, width)
    got = [
        pltpu.make_async_copy(q_in, q, loads.at[0]),
        pltpu.make_async_copy(kv_in.at[:, values], kv.at[:, values], loads.at[1]),
        pltpu.make_async_copy(kv_in.at[:, keys], kv.at[:, keys], loads.at[2]),
    ]
    for copy in got:
        copy.start()
    frames = Frames(seg_at, seg, valid, kcode, qseg)
    got[0].wait()
    qt[...] = q[...].T
    got[1].wait()
    vt[...] = kv[:, width:].T
    got[2].wait()

    def results(i):
        rows = pl.ds(pl.multiple_of(i * bq, bq), bq)
        return [
            pltpu.make_async_copy(out.at[rows], o_out.at[rows], stores.at[0, i]),
            pltpu.make_async_copy(outt.at[:, rows], o_outt.at[:, rows], stores.at[1, i]),
        ]

    def q_block(i, _):
        queries = pl.ds(pl.multiple_of(i * bq, bq), bq)
        acc[...] = jnp.zeros_like(acc)
        total[...] = jnp.zeros_like(total)
        top[...] = jnp.full_like(top, -3e38)
        for pair in pairs:
            heads_q[pair] = both_heads(qt, pair, queries)

        def k_block(j, _):
            @pl.when(frames.meet(j * bk, bk, i * bq, bq))
            def _():
                ks = pl.ds(pl.multiple_of(j * bk, bk), bk)
                set_distances(
                    dist,
                    frames.frame(j * bk),
                    frames.frame(i * bq),
                    wide(kcode[ks, :], bq),
                    qseg[0:1, queries],
                )
                for pair in pairs:
                    scores[pair] = dot(kv[ks, pl.ds(128 * pair, 128)], heads_q[pair])
                fades = []
                for pair in pairs:
                    line = pl.ds(pair, 1)
                    score = scores[pair] * c1 - both_slopes(dist, frames, pair)
                    was = top[line, :]
                    now = jnp.maximum(was, jnp.max(score, axis=0, keepdims=True))
                    prob = jnp.exp2(score - now)
                    fade = jnp.exp2(was - now)
                    total[line, :] = total[line, :] * fade + jnp.sum(prob, axis=0, keepdims=True)
                    top[line, :] = now
                    probs[pair] = prob.astype(BF16)
                    fades.append(fade)
                for pair in pairs:
                    value = dot(vt[pl.ds(128 * pair, 128), ks], probs[pair])
                    for e in range(2):
                        at, lanes = pl.ds(128 * pair + HD * e, HD), slice(bq * e, bq * (e + 1))
                        acc[at, :] = (
                            acc[at, :] * fades[pair][:, lanes]
                            + value[HD * e : HD * (e + 1), lanes]
                        )

            return 0

        lax.fori_loop(0, kv.shape[0] // bk, k_block, 0)
        for pair in pairs:
            rate = 1.0 / total[pl.ds(pair, 1), :]
            for e in range(2):
                at = pl.ds(128 * pair + HD * e, HD)
                acc[at, :] = acc[at, :] * rate[:, bq * e : bq * (e + 1)]
        lse[:, pl.ds(pl.multiple_of(2 * i * bq, 2 * bq), 2 * bq)] = top[...] + jnp.log2(total[...])
        out[queries, :] = acc[...].T.astype(BF16)
        outt[:, queries] = acc[...].astype(BF16)
        for copy in results(i):
            copy.start()
        return 0

    count = q.shape[0] // bq
    lax.fori_loop(0, count, q_block, 0)

    def settle(i, _):
        for copy in results(i):
            copy.wait()
        return 0

    lax.fori_loop(0, count, settle, 0)


def attend(q, kv, seg, valid, bq, bk, heads):
    frames = q.shape[0]
    vm, sm, hbm = [pl.BlockSpec(memory_space=m) for m in (VMEM, SMEM, HBM)]
    return pl.pallas_call(
        functools.partial(attend_kernel, bq, bk, heads),
        out_shape=(
            jax.ShapeDtypeStruct((frames, heads * HD), BF16),
            jax.ShapeDtypeStruct((heads * HD, frames), BF16),
            jax.ShapeDtypeStruct((heads // 2, 2 * frames), F32),
        ),
        in_specs=[sm, hbm, hbm, vm, vm],
        out_specs=(hbm, hbm, vm),
        scratch_shapes=[
            pltpu.VMEM(q.shape, BF16),
            pltpu.VMEM(kv.shape, BF16),
            pltpu.VMEM((frames, heads * HD), BF16),
            pltpu.VMEM((heads * HD, frames), BF16),
            pltpu.SemaphoreType.DMA((3,)),
            pltpu.SemaphoreType.DMA((2, frames // bq)),
            pltpu.VMEM((kv.shape[0], 128), F32),
            pltpu.VMEM((8, frames), F32),
            pltpu.VMEM((heads * HD, frames), BF16),
            pltpu.VMEM((heads * HD, kv.shape[0]), BF16),
            pltpu.VMEM((bk, bq), F32),
            pltpu.VMEM((heads * HD, bq), F32),
            pltpu.VMEM((heads // 2, 2 * bq), F32),
            pltpu.VMEM((heads // 2, 2 * bq), F32),
            pltpu.VMEM((heads // 2, 2 * HD, 2 * bq), BF16),
            pltpu.VMEM((heads // 2, bk, 2 * bq), F32),
            pltpu.VMEM((heads // 2, bk, 2 * bq), BF16),
        ],
        name="attend",
        cost_estimate=pl.CostEstimate(
            flops=8_000_000_000, bytes_accessed=8_000_000, transcendentals=4_000_000
        ),
        compiler_params=pltpu.CompilerParams(vmem_limit_bytes=63 << 20),
    )(seg, q, kv, seg, valid)


def attend_back_kernel(
    bq,
    bk,
    heads,
    seg_at,
    q_in,
    kv_in,
    grad_in,
    outt_in,
    lse,
    seg,
    valid,
    passed_in,
    o_dq,
    o_dkv,
    o_passed,
    q,
    kv,
    grad,
    outt,
    passed,
    dq,
    dkv,
    loads,
    stores,
    kcode,
    qseg,
    qt,
    kt,
    gradt,
    delta,
    dist,
    dqt,
    sums,
    heads_q,
    heads_g,
    rows_q,
    rows_g,
    scores,
    prob_grads,
    probs,
    score_grads,
):
    width = heads * HD
    pairs = range(heads // 2)
    c1 = LOG2E / math.sqrt(HD)
    scale = 1.0 / math.sqrt(HD)
    lane = lax.broadcasted_iota(jnp.int32, (bq, 128), 1)
    places = [(q_in, q), (grad_in, grad), (outt_in, outt), (kv_in, kv), (passed_in, passed)]
    got = [pltpu.make_async_copy(a, b, loads.at[i]) for i, (a, b) in enumerate(places)]
    for copy in got:
        copy.start()
    sums[...] = jnp.zeros_like(sums)
    frames = Frames(seg_at, seg, valid, kcode, qseg)
    got[0].wait()
    qt[...] = q[...].T
    got[1].wait()
    gradt[...] = grad[...].T
    got[2].wait()
    got[3].wait()
    kt[...] = kv[:, :width].T
    got[4].wait()
    stored = [pltpu.make_async_copy(passed, o_passed, stores.at[0])]
    stored[0].start()

    def dq_copy(i):
        rows = pl.ds(pl.multiple_of(i * bq, bq), bq)
        return pltpu.make_async_copy(dq.at[rows], o_dq.at[rows], stores.at[1 + i])

    def q_block(i, _):
        qs = pl.multiple_of(i * bq, bq)
        queries = pl.ds(qs, bq)
        dqt[...] = jnp.zeros_like(dqt)
        for pair in pairs:
            at = pl.ds(128 * pair, 128)
            heads_q[pair] = both_heads(qt, pair, queries)
            heads_g[pair] = both_heads(gradt, pair, queries)
            product = outt[at, queries].astype(F32) * gradt[at, queries].astype(F32)
            for e in range(2):
                rows = pl.ds(bq * e, bq)
                keep = (lane < HD) if e == 0 else (lane >= HD)
                for to, ref in ((rows_q, q), (rows_g, grad)):
                    value = ref[queries, at]
                    to[pair, rows, :] = jnp.where(keep, value, jnp.zeros_like(value))
                delta[pl.ds(pair, 1), rows] = jnp.sum(
                    product[HD * e : HD * (e + 1)], axis=0, keepdims=True
                )

        def k_block(j, _):
            @pl.when(frames.meet(j * bk, bk, i * bq, bq))
            def _():
                ks = pl.ds(pl.multiple_of(j * bk, bk), bk)
                set_distances(
                    dist,
                    frames.frame(j * bk),
                    frames.frame(i * bq),
                    wide(kcode[ks, :], bq),
                    qseg[0:1, queries],
                )
                for pair in pairs:
                    scores[pair] = dot(kv[ks, pl.ds(128 * pair, 128)], heads_q[pair])
                    prob_grads[pair] = dot(
                        kv[ks, pl.ds(width + 128 * pair, 128)], heads_g[pair]
                    )
                lines = pl.ds(pl.multiple_of(2 * qs, 2 * bq), 2 * bq)
                for pair in pairs:
                    line = pl.ds(pair, 1)
                    prob = jnp.exp2(
                        scores[pair] * c1 - both_slopes(dist, frames, pair) - lse[line, lines]
                    )
                    probs[pair] = prob.astype(BF16)
                    score_grads[pair] = (prob * (prob_grads[pair] - delta[line, :])).astype(BF16)
                for pair in pairs:
                    at = pl.ds(128 * pair, 128)
                    sums[ks, pl.ds(width + 128 * pair, 128)] += dot(probs[pair], rows_g[pair])
                    sums[ks, at] += dot(score_grads[pair], rows_q[pair])
                    value = dot(kt[at, ks], score_grads[pair])
                    for e in range(2):
                        dqt[pl.ds(128 * pair + HD * e, HD), :] += value[
                            HD * e : HD * (e + 1), bq * e : bq * (e + 1)
                        ]

            return 0

        lax.fori_loop(0, kv.shape[0] // bk, k_block, 0)
        dq[pl.ds(qs, bq), :] = (dqt[...] * scale).T.astype(BF16)
        dq_copy(i).start()
        return 0

    count = q.shape[0] // bq
    lax.fori_loop(0, count, q_block, 0)
    parts = [(CHIP, HALO), (0, FRAMES), (FRAMES, FRAMES)]
    for i, (at, rows) in enumerate(parts):
        part = pl.ds(at, rows)
        dkv[part, :width] = (sums[part, :width] * scale).astype(BF16)
        dkv[part, width:] = sums[part, width:].astype(BF16)
        copy = pltpu.make_async_copy(dkv.at[part], o_dkv.at[part], stores.at[1 + count + i])
        copy.start()
        stored.append(copy)
    for copy in [*stored, *[dq_copy(i) for i in range(count)]]:
        copy.wait()


def attend_back(q, kv, grad, outt, lse, seg, valid, passed, bq, bk, heads):
    vm, sm, hbm = [pl.BlockSpec(memory_space=m) for m in (VMEM, SMEM, HBM)]
    return pl.pallas_call(
        functools.partial(attend_back_kernel, bq, bk, heads),
        out_shape=(
            jax.ShapeDtypeStruct(q.shape, BF16),
            jax.ShapeDtypeStruct(kv.shape, BF16),
            jax.ShapeDtypeStruct(passed.shape, passed.dtype),
        ),
        in_specs=[sm] + [hbm] * 4 + [vm] * 3 + [hbm],
        out_specs=(hbm, hbm, hbm),
        scratch_shapes=[
            pltpu.VMEM(q.shape, BF16),
            pltpu.VMEM(kv.shape, BF16),
            pltpu.VMEM(grad.shape, BF16),
            pltpu.VMEM(outt.shape, BF16),
            pltpu.VMEM(passed.shape, passed.dtype),
            pltpu.VMEM(q.shape, BF16),
            pltpu.VMEM(kv.shape, BF16),
            pltpu.SemaphoreType.DMA((5,)),
            pltpu.SemaphoreType.DMA((4 + q.shape[0] // bq,)),
            pltpu.VMEM((kv.shape[0], 128), F32),
            pltpu.VMEM((8, q.shape[0]), F32),
            pltpu.VMEM((heads * HD, q.shape[0]), BF16),
            pltpu.VMEM((heads * HD, kv.shape[0]), BF16),
            pltpu.VMEM((heads * HD, q.shape[0]), BF16),
            pltpu.VMEM((heads // 2, 2 * bq), F32),
            pltpu.VMEM((bk, bq), F32),
            pltpu.VMEM((heads * HD, bq), F32),
            pltpu.VMEM(kv.shape, F32),
            *[pltpu.VMEM((heads // 2, 2 * HD, 2 * bq), BF16)] * 2,
            *[pltpu.VMEM((heads // 2, 2 * bq, 2 * HD), BF16)] * 2,
            *[pltpu.VMEM((heads // 2, bk, 2 * bq), F32)] * 2,
            *[pltpu.VMEM((heads // 2, bk, 2 * bq), BF16)] * 2,
        ],
        name="attend_back",
        cost_estimate=pl.CostEstimate(
            flops=20_000_000_000, bytes_accessed=16_000_000, transcendentals=4_000_000
        ),
        compiler_params=pltpu.CompilerParams(vmem_limit_bytes=63 << 20),
    )(seg, q, kv, grad, outt, lse, seg, valid, passed)


def add_into(value, other):
    def step(i, _):
        value[i] = value[i] + other[i]
        return 0

    lax.fori_loop(0, value.shape[0], step, 0)


class Unit:
    def __init__(self, links, own, came, y_first, done):
        self.links, self.own, self.came, self.y_first, self.done = links, own, came, y_first, done

    def add_core(self, r0):
        for k in range(2):
            for i in range(2):
                for j in range(2):
                    add_into(self.own.at[k, i, j], r0.at[k, i, j])

    def send_first(self):
        n, a = self.links, self.own
        if self.y_first:
            self.first = n.send(a.at[:, :, :, 1 - n.y], self.came[0], n.over_y)
        else:
            self.first = n.send(a.at[:, :, 1 - n.x], self.came[0], n.over_x)

    def turn_first(self):
        self.first.wait_recv()
        n, a, b = self.links, self.own, self.came[0]
        for k in range(2):
            for i in range(2):
                part = a.at[k, i, :, n.y] if self.y_first else a.at[k, i, n.x]
                add_into(part, b.at[k, i])
        if self.y_first:
            self.second = n.send(a.at[:, :, 1 - n.x, n.y], self.came[1], n.over_x)
        else:
            self.second = n.send(a.at[:, :, n.x, 1 - n.y], self.came[1], n.over_y)

    def chip(self, *at):
        return self.own.at[*at, self.links.x, self.links.y]

    def turn_second(self):
        self.second.wait_recv()
        self.after_second()

    def after_second(self):
        n = self.links
        for k in range(2):
            add_into(self.chip(k, slice(None)), self.came[1].at[k])
        self.third = n.send(self.chip(slice(None), 1 - n.low), self.came[2], n.over_low)

    def turn_third(self):
        n = self.links
        self.third.wait_recv()
        add_into(self.chip(slice(None), n.low), self.came[2])
        self.fourth = n.send(self.chip(1 - n.high, n.low), self.came[3], n.over_high)

    def finish(self):
        n = self.links
        self.fourth.wait_recv()
        self.done(self.chip(n.high, n.low)[...].astype(F32) + self.came[3][...].astype(F32))


class LateUnit(Unit):
    def chip(self, *at):
        return self.own.at[*at]

    def turn_second(self, *loads):
        for copy in loads:
            copy.wait()
        self.after_second()


class Small:
    def __init__(self, links, steps, into, done):
        self.links, self.steps, self.into, self.done, self.at = links, steps, into, done, 0
        self.stages = [links.core, links.over_y, links.over_x, links.over_low, links.over_high]

    def send(self):
        self.flying = self.links.send(
            self.steps.at[self.at], self.into.at[self.at], self.stages[self.at]
        )

    def turn(self):
        self.flying.wait_recv()
        value = self.steps[self.at] + self.into[self.at]
        self.at += 1
        if self.at == len(self.stages):
            self.done(value)
        else:
            self.steps[self.at] = value
            self.send()


STEPS = 8
STEP = 256


def middle_kernel(*refs):
    (
        att_in_hbm,
        stem_in,
        wout_in,
        gain,
        up_hbm,
        down_hbm,
        bias_up,
        bias_down,
        cot_in,
    ) = refs[:9]
    o_out, o_grad, o_heads, o_wo, o_down, o_down_away, o_up, o_up_away, o_small = refs[9:18]
    (
        att,
        att_came,
        stem,
        wout,
        ups,
        downs,
        cot,
        second,
        second_t,
        unit,
        inverse,
        active,
        hidden_grad,
        out_sum,
        grad_sum,
        low,
        swap_out,
        swap_in,
        down_send,
        down_keep,
        down_came,
        up_send,
        up_keep,
        up_came,
        loads,
        sends,
        recvs,
    ) = refs[18:]
    links = Links(sends, recvs)
    x, y, c = links.x, links.y, links.c
    loading = []

    def load(src, dst):
        copy = pltpu.make_async_copy(src, dst, loads.at[len(loading)])
        copy.start()
        loading.append(copy)
        return copy

    own, other = pl.ds(0, FRAMES), pl.ds(FRAMES, FRAMES)
    got_att = load(att_in_hbm.at[own], att)
    got_wout = load(wout_in, wout)
    got_stem = load(stem_in, stem)
    got_cot = load(cot_in, cot.at[own])
    got_ups, got_downs = [], []
    for i in range(STEPS):
        for j in range(2):
            at = pl.multiple_of(128 * (4 * i + 2 * j + c), 128)
            part = pl.ds(128 * j, 128)
            got_ups.append(load(up_hbm.at[:, pl.ds(at, 128)], ups.at[i, :, part]))
            got_downs.append(load(down_hbm.at[pl.ds(at, 128), :], downs.at[i, part, :]))
    links.greet()
    att_core = links.send(att_in_hbm.at[other], att_came, links.core)
    cot_core = links.send(cot_in, cot.at[other], links.core)
    mine = pl.ds(pl.multiple_of(WIDTH * c, WIDTH), WIDTH)
    theirs = pl.ds(pl.multiple_of(WIDTH * (1 - c), WIDTH), WIDTH)

    got_att.wait()
    got_wout.wait()
    got_stem.wait()
    att_core.wait_recv()
    gains = gain[0:1, :]
    second_core = []
    for part in range(2):
        rows = pl.ds(256 * part, 256)
        value = stem[rows, :] + dot(att[rows, :], wout[mine, :]) + dot(att_came[rows, :], wout[theirs, :])
        stem[rows, :] = value
        center = value - jnp.mean(value, axis=-1, keepdims=True)
        rate = lax.rsqrt(jnp.mean(center * center, axis=-1, keepdims=True) + epsilon)
        normal = center * rate
        unit[rows, :] = normal
        inverse[rows, :] = jnp.broadcast_to(rate, (256, 128))
        second[rows, :] = (normal * gains).astype(BF16)
        second_core.append(
            links.send(second.at[rows], second.at[pl.ds(FRAMES + 256 * part, 256)], links.core)
        )
    second_t[:, :FRAMES] = second[own, :].T
    out_sum[...] = jnp.zeros_like(out_sum)
    grad_sum[...] = jnp.zeros_like(grad_sum)
    o_small[...] = jnp.zeros_like(o_small)
    for copy in [got_cot, *got_ups, *got_downs]:
        copy.wait()
    cot_core.wait_recv()
    for copy in second_core:
        copy.wait_recv()
    second_t[:, FRAMES:] = second[other, :].T

    down_at, up_at = links.reserve(STEPS), links.reserve(STEPS)

    def down_copy(i):
        return links.copy(down_send.at[i], down_came.at[i], down_at + i, links.over_y)

    def up_copy(i):
        return links.copy(up_send.at[i], up_came.at[i], up_at + i, links.over_x)

    def feed_step(i, _):
        up, down = ups[i], downs[i]
        bias = bias_up[0:1, pl.ds(pl.multiple_of(STEP * i, STEP), STEP)]
        total = jnp.zeros((1, STEP), F32)
        for half in (own, other):
            hidden = dot(second[half, :], up) + bias
            active_grad = dot_nt(cot[half, :], down)
            share = 0.5 + 0.5 * lax.erf(hidden * math.sqrt(0.5))
            slope = share + hidden * (
                jnp.exp(-0.5 * hidden * hidden) * (1.0 / math.sqrt(2.0 * math.pi))
            )
            a = (hidden * share).astype(BF16)
            g = (active_grad * slope).astype(BF16)
            active[half, :] = a
            hidden_grad[half, :] = g
            total = total + jnp.sum(g.astype(F32), axis=0, keepdims=True)
            out_sum[half, :] += dot(a, down)
            grad_sum[half, :] += dot_nt(g, up)
        for j in range(2):
            o_small[pl.ds(4 * i + 2 * j + c, 1), :] = total[:, 128 * j : 128 * (j + 1)]
        value = dot_tn(active[...], cot[...]).astype(BF16)
        down_send[i] = jnp.where(y == 0, value[128:], value[:128])
        down_keep[i] = jnp.where(y == 0, value[:128], value[128:])
        down_copy(i).start()
        value = dot(second_t[...], hidden_grad[...]).astype(BF16)
        for k in range(4):
            first, last = value[256 * k : 256 * k + 128], value[256 * k + 128 : 256 * (k + 1)]
            up_send[i, k] = jnp.where(x == 0, last, first)
            up_keep[i, k] = jnp.where(x == 0, first, last)
        up_copy(i).start()
        return 0

    lax.fori_loop(0, STEPS, feed_step, 0)

    swap_out[0] = grad_sum[other, :].astype(BF16)
    grad_core = links.send(swap_out.at[0], swap_in.at[0], links.core)
    swap_out[1] = out_sum[other, :].astype(BF16)
    out_core = links.send(swap_out.at[1], swap_in.at[1], links.core)
    grad_core.wait_recv()

    def norm_rows(i, totals):
        rows = pl.ds(pl.multiple_of(128 * i, 128), 128)
        upstream = grad_sum[rows, :] + swap_in[0, rows, :].astype(F32)
        normal = unit[rows, :]
        scaled = upstream * gains
        inner = (
            scaled
            - jnp.mean(scaled, axis=-1, keepdims=True)
            - normal * jnp.mean(scaled * normal, axis=-1, keepdims=True)
        )
        value = cot[rows, :].astype(F32)
        grad = value + inverse[rows, 0:1] * inner
        o_grad[rows, :] = grad
        low[rows, :] = grad.astype(BF16)
        return (
            totals[0] + jnp.sum(upstream * normal, axis=0, keepdims=True),
            totals[1] + jnp.sum(value, axis=0, keepdims=True),
        )

    zero = jnp.zeros((1, D), F32)
    totals = lax.fori_loop(0, 4, norm_rows, (zero, zero))
    for k, value in enumerate(totals):
        for j in range(8):
            o_small[pl.ds(32 + 8 * k + j, 1), :] = value[:, 128 * j : 128 * (j + 1)]
    swap_out[2, :, :WIDTH] = dot_nt(low[...], wout[theirs, :]).astype(BF16)
    heads_core = links.send(
        swap_out.at[2, :, pl.ds(0, WIDTH)], swap_in.at[2, :, pl.ds(0, WIDTH)], links.core
    )
    o_heads[own, :] = dot_nt(low[...], wout[mine, :]).astype(BF16)
    o_wo[mine, :] = dot_tn(att[...], low[...]).astype(BF16)
    o_wo[theirs, :] = dot_tn(att_came[...], low[...]).astype(BF16)
    out_core.wait_recv()

    def out_rows(i, _):
        rows = pl.ds(pl.multiple_of(128 * i, 128), 128)
        o_out[rows, :] = (
            stem[rows, :]
            + (out_sum[rows, :] + swap_in[1, rows, :].astype(F32))
            + bias_down[0:1, :]
        ).astype(BF16)
        return 0

    lax.fori_loop(0, 4, out_rows, 0)
    heads_core.wait_recv()
    o_heads[other, :] = swap_in[2, :, :WIDTH]

    def add_step(i, _):
        down_copy(i).wait()
        value = down_keep[i] + down_came[i]
        stays = lax.rem(i + x, 2) == 0

        @pl.when(stays)
        def _():
            o_down[i // 2] = value

        @pl.when(jnp.logical_not(stays))
        def _():
            o_down_away[i // 2] = value

        up_copy(i).wait()
        columns = pl.ds(pl.multiple_of(STEP * i, STEP), STEP)
        for k in range(4):
            value = up_keep[i, k] + up_came[i, k]
            o_up[k, :, columns] = jnp.where(y == 0, value[:64], value[64:])
            o_up_away[k, :, columns] = jnp.where(y == 0, value[64:], value[:64])
        return 0

    lax.fori_loop(0, STEPS, add_step, 0)
    links.drain()


def middle(att, stem, wout, gain, w_up, w_down, bias_up, bias_down, cot):
    hbm, vm = pl.BlockSpec(memory_space=HBM), pl.BlockSpec(memory_space=VMEM)
    low = lambda *shape: pltpu.VMEM(shape, BF16)
    full = lambda *shape: pltpu.VMEM(shape, F32)
    copies = 24
    return pl.pallas_call(
        middle_kernel,
        out_shape=[
            jax.ShapeDtypeStruct((FRAMES, D), BF16),
            jax.ShapeDtypeStruct((FRAMES, D), F32),
            jax.ShapeDtypeStruct((CHIP, WIDTH), BF16),
            jax.ShapeDtypeStruct((D, D), BF16),
            *[jax.ShapeDtypeStruct((4, 128, D), BF16)] * 2,
            *[jax.ShapeDtypeStruct((4, 64, 2 * D), BF16)] * 2,
            jax.ShapeDtypeStruct((48, 128), F32),
        ],
        in_specs=[hbm] * 3 + [vm] + [hbm] * 2 + [vm] * 2 + [hbm],
        out_specs=[vm] * 9,
        scratch_shapes=[
            low(FRAMES, WIDTH),
            low(FRAMES, WIDTH),
            full(FRAMES, D),
            low(D, D),
            low(STEPS, D, STEP),
            low(STEPS, STEP, D),
            low(CHIP, D),
            low(CHIP, D),
            low(D, CHIP),
            full(FRAMES, D),
            full(FRAMES, 128),
            low(CHIP, STEP),
            low(CHIP, STEP),
            full(CHIP, D),
            full(CHIP, D),
            low(FRAMES, D),
            low(3, FRAMES, D),
            low(3, FRAMES, D),
            low(STEPS, 128, D),
            low(STEPS, 128, D),
            low(STEPS, 128, D),
            low(STEPS, 4, 128, STEP),
            low(STEPS, 4, 128, STEP),
            low(STEPS, 4, 128, STEP),
            pltpu.SemaphoreType.DMA((4 + 4 * STEPS,)),
            pltpu.SemaphoreType.DMA((copies,)),
            pltpu.SemaphoreType.DMA((copies,)),
        ],
        name="middle",
        cost_estimate=pl.CostEstimate(
            flops=28_000_000_000, bytes_accessed=40_000_000, transcendentals=4_000_000
        ),
        compiler_params=pltpu.CompilerParams(
            collective_id=1, has_side_effects=True, vmem_limit_bytes=63 << 20
        ),
    )(att, stem, wout, gain, w_up, w_down, bias_up, bias_down, cot)


def tail_kernel(*refs):
    (
        down_in,
        down_came,
        up_in,
        up_came,
        wo_in,
        small_in,
        dq_in,
        dkv_in,
        seen_in,
        wqkv_in,
        joint_in,
        stem_in,
        grad_in,
        gain,
        wskip_in,
    ) = refs[:15]
    o_in, o_skip, o_down, o_up, o_qkv, o_wo, o_wskip, o_small, o_gain = refs[15:24]
    (
        dq,
        dkv,
        wide_buf,
        wq,
        wkv,
        joint,
        stem,
        grad,
        chip_out,
        chip_in,
        chip_own,
        halo_out,
        halo_in,
        halo_sum,
        halo,
        low,
        down_own,
        down_r2,
        down_r3,
        down_r4,
        up_own,
        up_r2,
        up_r3,
        up_r4,
        up_out,
        up_in_last,
        unit_own,
        unit_r1,
        unit_r2,
        unit_r3,
        unit_r4,
        wo_r0,
        join_out,
        skip_own,
        skip_out,
        skip_r0,
        skip_r1,
        skip_r2,
        skip_r3,
        skip_r4,
        small_steps,
        small_into,
        gain_steps,
        gain_into,
        loads,
        sends,
        recvs,
    ) = refs[24:]
    links = Links(sends, recvs)
    y, c = links.y, links.c
    loading = []

    def load(src, dst):
        copy = pltpu.make_async_copy(src, dst, loads.at[len(loading)])
        copy.start()
        loading.append(copy)
        return copy

    seen = wide_buf.at[pl.ds(0, CHIP + HALO)]
    far, near = pl.ds(CHIP, HALO), pl.ds(0, CHIP)
    got_wkv = [load(head_columns(wqkv_in, 1 + i, c), wkv.at[:, pl.ds(WIDTH * i, WIDTH)]) for i in (0, 1)]
    got_far = load(dkv_in.at[far], dkv.at[far])
    links.greet()
    wo_core = links.send(wo_in.at[:, :, :, :, 1 - c], wo_r0, links.core)
    got_dq = load(dq_in, dq)
    got_near = load(dkv_in.at[near], dkv.at[near])
    got_seen = load(seen_in, seen)
    got_wo = load(wo_in.at[:, :, :, :, c], unit_own.at[0])
    got_small = load(small_in, small_steps.at[0])
    got_down = [
        [
            load(down_in.at[:, :, pl.ds(64 * i, 64)], down_own.at[i]),
            load(down_came.at[:, :, pl.ds(64 * i, 64)], down_r2.at[i]),
        ]
        for i in range(2)
    ]
    got_up = []
    for i, core in enumerate((1 - c, c)):
        rows = pl.ds(pl.multiple_of(32 * core, 32), 32)
        got_up.append(
            [
                load(up_in.at[:, :, rows], up_own.at[i]),
                load(up_came.at[:, :, rows], up_r2.at[i]),
            ]
        )
    got_wq = load(head_columns(wqkv_in, 0, c), wq)
    got_stem = load(stem_in, stem)
    got_grad = load(grad_in, grad)
    got_joint = load(joint_in, joint)
    halo[pl.ds(0, EDGE), :] = jnp.zeros((EDGE, D), BF16)
    halo[pl.ds(EDGE + HALO, EDGE), :] = jnp.zeros((EDGE, D), BF16)

    def to_down(i):
        def done(value):
            o_down[pl.ds(64 * i, 64), :] = value

        return done

    def to_up_other(value):
        up_out[...] = value
        up_last.append(links.send(up_out, up_in_last, links.core))

    def to_up_mine(value):
        for b in range(16):
            at = pl.multiple_of(256 * b + 128 * c, 128)
            o_up[:, pl.ds(at, 128)] = value[:, 128 * b : 128 * (b + 1)]

    up_last = []
    downs = [
        LateUnit(
            links,
            down_own.at[i],
            (None, down_r2.at[i], down_r3.at[i], down_r4.at[i]),
            True,
            to_down(i),
        )
        for i in range(2)
    ]
    ups = [
        LateUnit(
            links, up_own.at[i], (None, up_r2.at[i], up_r3.at[i], up_r4.at[i]), False, done
        )
        for i, done in enumerate((to_up_other, to_up_mine))
    ]

    def to_wo(value):
        o_wo[...] = value

    def to_qkv(i):
        def done(value):
            o_qkv[:, pl.ds(D * i, D)] = value

        return done

    def to_wskip(q, half):
        def done(value):
            o_wskip[pl.ds(ROWS * half, ROWS), pl.ds(SKIP_COLS * q, SKIP_COLS)] = value

        return done

    def unit(k, y_first, done):
        came = (unit_r1.at[k], unit_r2.at[k], unit_r3.at[k], unit_r4.at[k])
        return Unit(links, unit_own.at[k], came, y_first, done)

    wo = unit(0, False, to_wo)
    unit_q, unit_k, unit_v = [unit(1 + i, i == 1, to_qkv(i)) for i in range(3)]

    def skip_unit(k, y_first, done):
        came = (skip_r1.at[k], skip_r2.at[k], skip_r3.at[k], skip_r4.at[k])
        return Unit(links, skip_own.at[k], came, y_first, done)

    skips = [
        [skip_unit(2 * q + half, half == 0, to_wskip(q, half)) for half in range(2)]
        for q in range(SKIPS)
    ]

    def to_small(value):
        o_small[...] = value

    def to_gain(value):
        o_gain[...] = value

    small = Small(links, small_steps, small_into, to_small)
    gain_sum = Small(links, gain_steps, gain_into, to_gain)

    for copy in (*got_wkv, got_far):
        copy.wait()

    def halo_part(core):
        at = pl.multiple_of(CHIP + HALF * core, 128)
        return dot_nt(dkv[pl.ds(at, HALF), :], wkv[...])

    halo_out[...] = halo_part(1 - c).astype(BF16)
    halo_core = links.send(halo_out, halo_in, links.core)
    mine = halo_part(c)
    halo_core.wait_recv()
    halo_sum[...] = (mine + halo_in[...].astype(F32)).astype(BF16)
    part_at = pl.ds(pl.multiple_of(EDGE + HALF * c, 128), HALF)
    part = halo.at[part_at]
    halo_y = links.send(halo_sum, part, links.over_y)
    got_near.wait()
    got_seen.wait()
    columns = pl.ds(pl.multiple_of(WIDTH * c, WIDTH), WIDTH)

    def place(k, i, value):
        value = value.astype(BF16)
        for j in range(2):
            for m in range(2):
                at = 128 * j + 64 * m
                first, second = value[at : at + 32], value[at + 32 : at + 64]
                mine, theirs = jnp.where(c == 0, first, second), jnp.where(c == 0, second, first)
                unit_own[1 + k, i // 2, i % 2, j, m, :, columns] = mine
                join_out[k, i // 2, i % 2, j, m] = theirs

    def join(k):
        there = unit_own.at[1 + k, :, :, :, :, :, columns]
        return links.send(join_out.at[k], there, links.core)

    def kv_rows(i, _):
        value = dot(seen[:, pl.ds(pl.multiple_of(256 * i, 256), 256)].T, dkv[...])
        place(1, i, value[:, :WIDTH])
        place(2, i, value[:, WIDTH:])
        return 0

    def q_rows(i, _):
        place(0, i, dot(seen[near, pl.ds(pl.multiple_of(256 * i, 256), 256)].T, dq[...]))
        return 0

    got_wo.wait()
    wo_core.wait_recv()
    wo.add_core(wo_r0)
    wo.send_first()
    lax.fori_loop(0, 4, kv_rows, 0)
    join_v, join_k = join(2), join(1)
    for one, got in zip(downs + ups, got_down + got_up):
        one.turn_second(*got)
    got_small.wait()
    small.send()
    join_v.wait_recv()
    unit_v.send_first()
    join_k.wait_recv()
    unit_k.send_first()
    got_dq.wait()
    lax.fori_loop(0, 4, q_rows, 0)
    join_q = join(0)
    got_wskip = load(wskip_in, wide_buf)
    wo.turn_first()
    join_q.wait_recv()
    unit_q.send_first()

    got_wq.wait()

    def chip_part(at):
        rows = pl.ds(at, 256)
        return dot_nt(dq[rows, :], wq[...]) + dot_nt(dkv[rows, :], wkv[...])

    def other_frames(i, _):
        at = pl.multiple_of(256 * i, 256)
        chip_out[pl.ds(at, 256), :] = chip_part(FRAMES + at).astype(BF16)
        return 0

    lax.fori_loop(0, 2, other_frames, 0)
    chip_core = links.send(chip_out, chip_in, links.core)
    small.turn()

    def own_frames(i, _):
        at = pl.multiple_of(256 * i, 256)
        chip_own[pl.ds(at, 256), :] = chip_part(at)
        return 0

    lax.fori_loop(0, 2, own_frames, 0)
    for one in downs:
        one.turn_third()

    halo_y.wait_recv()
    halo_rest = links.send(part, part, links.core)
    chip_core.wait_recv()
    got_stem.wait()
    got_grad.wait()
    halo_rest.wait_recv()
    gains = gain[0:1, :]

    def norm_rows(i, total):
        at = pl.multiple_of(128 * i, 128)
        rows = pl.ds(at, 128)
        upstream = (
            chip_own[rows, :]
            + chip_in[rows, :].astype(F32)
            + halo[pl.ds(pl.multiple_of(at + 256 * (2 * c + y), 128), 128), :].astype(F32)
        )
        value = stem[rows, :]
        center = value - jnp.mean(value, axis=-1, keepdims=True)
        inverse = lax.rsqrt(jnp.mean(center * center, axis=-1, keepdims=True) + epsilon)
        unit_value = center * inverse
        scaled = upstream * gains
        inner = (
            scaled
            - jnp.mean(scaled, axis=-1, keepdims=True)
            - unit_value * jnp.mean(scaled * unit_value, axis=-1, keepdims=True)
        )
        low[rows, :] = (grad[rows, :] + inverse * inner).astype(BF16)
        return total + jnp.sum(upstream * unit_value, axis=0, keepdims=True)

    total = lax.fori_loop(0, 4, norm_rows, jnp.zeros((1, D), F32))
    gain_steps[0] = jnp.concatenate([total[:, 128 * i : 128 * (i + 1)] for i in range(8)], axis=0)
    gain_sum.send()
    got_joint.wait()

    skip_core = []
    for q in range(SKIPS):

        def skip_rows(i, _, q=q):
            value = dot(
                joint[pl.ds(pl.multiple_of(512 * i, 512), 512), :],
                low[:, SKIP_COLS * q : SKIP_COLS * (q + 1)],
            ).astype(BF16)
            for j in range(2):
                for m in range(2):
                    for half in range(2):
                        at = 256 * j + 128 * m + 32 * half
                        first, second = value[at : at + 32], value[at + 64 : at + 96]
                        skip_own[2 * q + half, i // 2, i % 2, j, m] = jnp.where(c == 0, first, second)
                        skip_out[2 * q + half, i // 2, i % 2, j, m] = jnp.where(c == 0, second, first)
            return 0

        lax.fori_loop(0, 4, skip_rows, 0)
        both = pl.ds(2 * q, 2)
        skip_core.append(links.send(skip_out.at[both], skip_r0.at[both], links.core))
        if q > 0:
            skip_core[q - 1].wait_recv()
            for half in range(2):
                skips[q - 1][half].add_core(skip_r0.at[2 * (q - 1) + half])
                skips[q - 1][half].send_first()
    q = SKIPS - 1
    skip_core[q].wait_recv()
    for half in range(2):
        skips[q][half].add_core(skip_r0.at[2 * q + half])
        skips[q][half].send_first()

    got_wskip.wait()

    def joined_part(i):
        value = dot_nt(low[...], wide_buf[pl.ds(256 * i, 256), :]).astype(BF16)
        out = o_in if i < 4 else o_skip
        out[:, pl.ds(256 * (i % 4), 256)] = value

    unit_v.turn_first()
    joined_part(0)
    for one in ups:
        one.turn_third()
    joined_part(1)
    joined_part(2)
    gain_sum.turn()
    small.turn()
    joined_part(3)
    unit_q.turn_first()
    unit_k.turn_first()
    joined_part(4)
    gain_sum.turn()
    small.turn()
    wo.turn_second()
    joined_part(5)
    joined_part(6)
    for one in downs:
        one.finish()
    joined_part(7)
    gain_sum.turn()
    small.turn()
    for one in ups:
        one.finish()
    for q in range(SKIPS):
        skips[q][1].turn_first()
    unit_v.turn_second()
    gain_sum.turn()
    small.turn()
    wo.turn_third()
    unit_q.turn_second()
    for q in range(SKIPS):
        skips[q][0].turn_first()
    unit_k.turn_second()
    unit_v.turn_third()
    up_last[0].wait_recv()
    for b in range(16):
        at = pl.multiple_of(256 * b + 128 * (1 - c), 128)
        o_up[:, pl.ds(at, 128)] = up_in_last[:, 128 * b : 128 * (b + 1)]
    gain_sum.turn()
    wo.finish()
    unit_q.turn_third()
    for q in range(SKIPS):
        skips[q][1].turn_second()
    unit_v.finish()
    unit_k.turn_third()
    for q in range(SKIPS):
        skips[q][0].turn_second()
    unit_q.finish()
    for q in range(SKIPS):
        skips[q][1].turn_third()
    unit_k.finish()
    for q in range(SKIPS):
        skips[q][0].turn_third()
    for q in range(SKIPS):
        skips[q][1].finish()
    for q in range(SKIPS):
        skips[q][0].finish()
    links.drain()


def tail(down, down_came, up, up_came, wo, small, dq, dkv, seen, wqkv, joint, stem, grad, gain, wskip):
    hbm, vm = pl.BlockSpec(memory_space=HBM), pl.BlockSpec(memory_space=VMEM)
    n_small = small.shape[0]
    out_shape = [
        jax.ShapeDtypeStruct((FRAMES, D), BF16),
        jax.ShapeDtypeStruct((FRAMES, D), BF16),
        jax.ShapeDtypeStruct((128, D), F32),
        jax.ShapeDtypeStruct((32, 4096), F32),
        jax.ShapeDtypeStruct((32, 3 * D), F32),
        jax.ShapeDtypeStruct((32, D), F32),
        jax.ShapeDtypeStruct((64, D), F32),
        jax.ShapeDtypeStruct((n_small, 128), F32),
        jax.ShapeDtypeStruct((8, 128), F32),
    ]
    low = lambda *shape: pltpu.VMEM(shape, BF16)
    full = lambda *shape: pltpu.VMEM(shape, F32)
    skip = (ROWS, SKIP_COLS)
    copies = 104
    scratch = [
        low(CHIP, WIDTH),
        low(CHIP + HALO, D),
        low(2 * D, D),
        low(D, WIDTH),
        low(D, D),
        low(2 * D, FRAMES),
        full(FRAMES, D),
        full(FRAMES, D),
        low(FRAMES, D),
        low(FRAMES, D),
        full(FRAMES, D),
        low(HALF, D),
        low(HALF, D),
        low(HALF, D),
        low(HALO + 2 * EDGE, D),
        low(FRAMES, D),
        low(2, 2, 2, 64, D),
        low(2, 2, 2, 64, D),
        low(2, 2, 64, D),
        low(2, 64, D),
        low(2, 2, 2, 32, 2 * D),
        low(2, 2, 2, 32, 2 * D),
        low(2, 2, 32, 2 * D),
        low(2, 32, 2 * D),
        full(32, 2 * D),
        full(32, 2 * D),
        low(4, 2, 2, 2, 2, ROWS, D),
        low(4, 2, 2, 2, ROWS, D),
        low(4, 2, 2, ROWS, D),
        low(4, 2, ROWS, D),
        low(4, ROWS, D),
        low(2, 2, 2, 2, ROWS, D),
        low(3, 2, 2, 2, 2, ROWS, WIDTH),
        low(2 * SKIPS, 2, 2, 2, 2, *skip),
        low(2 * SKIPS, 2, 2, 2, 2, *skip),
        low(2 * SKIPS, 2, 2, 2, 2, *skip),
        low(2 * SKIPS, 2, 2, 2, *skip),
        low(2 * SKIPS, 2, 2, *skip),
        low(2 * SKIPS, 2, *skip),
        low(2 * SKIPS, *skip),
        full(5, n_small, 128),
        full(5, n_small, 128),
        full(5, 8, 128),
        full(5, 8, 128),
        pltpu.SemaphoreType.DMA((24,)),
        pltpu.SemaphoreType.DMA((copies,)),
        pltpu.SemaphoreType.DMA((copies,)),
    ]
    return pl.pallas_call(
        tail_kernel,
        out_shape=out_shape,
        in_specs=[hbm] * 13 + [vm, hbm],
        out_specs=[vm] * 9,
        scratch_shapes=scratch,
        name="tail",
        cost_estimate=pl.CostEstimate(
            flops=17_000_000_000, bytes_accessed=60_000_000, transcendentals=0
        ),
        compiler_params=pltpu.CompilerParams(
            collective_id=0, has_side_effects=True, vmem_limit_bytes=63 << 20
        ),
    )(
        down.reshape(2, 2, 128, D),
        down_came.reshape(2, 2, 128, D),
        up.reshape(2, 2, 64, 2 * D),
        up_came.reshape(2, 2, 64, 2 * D),
        wo.reshape(2, 2, 2, 2, 2, 32, D),
        small,
        dq,
        dkv,
        seen,
        wqkv,
        joint,
        stem,
        grad,
        gain,
        wskip,
    )


def finish_kernel(count, *refs):
    ins, small, gain = refs[:count], refs[count], refs[count + 1]
    outs, o_small = refs[count + 2 : 2 * count + 2], refs[2 * count + 2]
    held, loads, stores = refs[2 * count + 3 : 3 * count + 3], refs[-2], refs[-1]
    got = [pltpu.make_async_copy(a, b, loads.at[i]) for i, (a, b) in enumerate(zip(ins, held))]
    for copy in got:
        copy.start()
    device = lax.axis_index("rows") * 4 + lax.axis_index("seq")
    o_small[0:1, :] = small[pl.ds(device, 1), :]
    row, lane = device // 4, lax.rem(device, 4) * 32
    values = [gain[pl.ds(row, 1), :], small[pl.ds(32 + row, 1), :], small[pl.ds(40 + row, 1), :]]
    for i, value in enumerate(values):
        o_small[1 + i : 2 + i, :] = pltpu.roll(value, lax.rem(128 - lane, 128), 1)
    put = [pltpu.make_async_copy(a, b, stores.at[i]) for i, (a, b) in enumerate(zip(held, outs))]
    for copy, after in zip(got, put):
        copy.wait()
        after.start()
    for copy in put:
        copy.wait()


def finish(results, small, gain):
    hbm, vm = pl.BlockSpec(memory_space=HBM), pl.BlockSpec(memory_space=VMEM)
    count = len(results)
    return pl.pallas_call(
        functools.partial(finish_kernel, count),
        out_shape=[
            *[jax.ShapeDtypeStruct(a.shape, a.dtype) for a in results],
            jax.ShapeDtypeStruct((8, 128), F32),
        ],
        in_specs=[hbm] * count + [vm] * 2,
        out_specs=[hbm] * count + [vm],
        scratch_shapes=[
            *[pltpu.VMEM(a.shape, a.dtype) for a in results],
            pltpu.SemaphoreType.DMA((count,)),
            pltpu.SemaphoreType.DMA((count,)),
        ],
        name="finish",
        compiler_params=pltpu.CompilerParams(vmem_limit_bytes=63 << 20),
    )(*results, small, gain)


def swap_x(value):
    return lax.ppermute(value, "rows", [(r, r ^ 1) for r in range(8)])


def swap_chip(value):
    return lax.ppermute(value, "seq", [(i, i ^ 2) for i in range(4)])


def body_chips(
    inputs,
    skip_feats,
    seg_ids,
    frame_valid,
    w_skip,
    gain_one,
    w_qkv,
    w_out,
    gain_two,
    w_up,
    b_up,
    w_down,
    b_down,
    cotangent,
):
    here = lax.axis_index("seq")
    c = here % 2
    heads = H // 2
    first, second_in, cot = inputs[0], skip_feats[0], cotangent[0]
    gain_first = jnp.broadcast_to(gain_one.astype(F32), (8, D))
    gain_second = jnp.broadcast_to(gain_two.astype(F32), (8, D))
    stem_out, normed_seen, q, kv, joint = front(first, second_in, w_skip, gain_first, w_qkv)
    attended, attended_t, lse = attend(q, kv, seg_ids, frame_valid, 128, 256, heads)
    bias = lax.dynamic_index_in_dim(b_up.astype(F32).reshape(16, 2, 128), c, 1, keepdims=False)
    output, middle_grad, grad_heads, out_grad, down_sum, down_away, up_sum, up_away, small = middle(
        attended,
        stem_out,
        w_out,
        gain_second,
        w_up,
        w_down,
        jnp.broadcast_to(bias.reshape(1, -1), (8, 2 * D)),
        jnp.broadcast_to(b_down.astype(F32), (8, D)),
        cot,
    )
    down_came, up_came = swap_x(down_away), swap_chip(up_away)
    dq, dkv, output = attend_back(
        q, kv, grad_heads, attended_t, lse, seg_ids, frame_valid, output, 128, 256, heads
    )
    *results, small_sum, gain_sum = tail(
        down_sum,
        down_came,
        up_sum,
        up_came,
        out_grad,
        small,
        dq,
        dkv,
        normed_seen,
        w_qkv,
        joint,
        stem_out,
        middle_grad,
        gain_first,
        w_skip,
    )
    results = finish(results, small_sum, gain_sum)
    input_grad, skip_grad, down_share, up_share, qkv_share, out_share, skip_share, mine = results
    return (
        output[None],
        input_grad[None],
        skip_grad[None],
        skip_share,
        mine[1, :32],
        qkv_share,
        out_share,
        mine[2, :32],
        up_share,
        mine[0],
        down_share,
        mine[3, :32],
    )


def block_scores(q_blk, pos_blk, seg_blk, all_keys, seg_row, valid_row, slopes, score_scale):
    key_pos = jnp.arange(all_keys.shape[0])
    scores = (
        jnp.einsum("qhd,khd->hqk", q_blk, all_keys, preferred_element_type=jnp.float32)
        * score_scale
    )
    distance = jnp.abs(pos_blk[:, None] - key_pos[None, :]).astype(jnp.float32)
    scores = scores - slopes[:, None, None] * distance[None]
    allowed = (seg_blk[:, None] == seg_row[None, :]) & (
        (valid_row[None, :] == 1) | (pos_blk[:, None] == key_pos[None, :])
    )
    return jnp.where(allowed[None], scores, -jnp.inf)


def split_row(packed_row, heads_local):
    length = packed_row.shape[0]
    qkv_rows = packed_row.reshape(length, 3, heads_local, HD)
    return (qkv_rows[:, 0], qkv_rows[:, 1], qkv_rows[:, 2])


def attend_row(packed_row, seg_row, valid_row, slopes, heads_local, block_rows, score_scale):
    length = packed_row.shape[0]
    queries, all_keys, all_values = split_row(packed_row, heads_local)
    count = length // block_rows
    positions = jnp.arange(length)

    def one_block(block_in):
        q_blk, pos_blk, seg_blk = block_in
        scores = block_scores(
            q_blk, pos_blk, seg_blk, all_keys, seg_row, valid_row, slopes, score_scale
        )
        peak = jnp.max(scores, axis=-1, keepdims=True)
        log_total = peak + jnp.log(jnp.sum(jnp.exp(scores - peak), axis=-1, keepdims=True))
        attn_probs = jnp.exp(scores - log_total).astype(jnp.bfloat16)
        attended = jnp.einsum(
            "hqk,khd->qhd", attn_probs, all_values, preferred_element_type=jnp.float32
        )
        return (attended.astype(jnp.bfloat16), log_total[..., 0])

    attended, log_total = lax.map(
        one_block,
        (
            queries.reshape(count, block_rows, heads_local, HD),
            positions.reshape(count, block_rows),
            seg_row.reshape(count, block_rows),
        ),
    )
    return (attended.reshape(length, 1, heads_local * HD), log_total)


def attend_row_back(
    packed_row,
    log_total,
    grad_row,
    seg_row,
    valid_row,
    slopes,
    heads_local,
    block_rows,
    score_scale,
):
    length = packed_row.shape[0]
    queries, all_keys, all_values = split_row(packed_row, heads_local)
    count = length // block_rows
    positions = jnp.arange(length)
    grad_out = grad_row.reshape(count, block_rows, heads_local, HD)

    def one_block(carry, block_in):
        key_grad, value_grad = carry
        q_blk, pos_blk, seg_blk, total_blk, grad_blk = block_in
        scores = block_scores(
            q_blk, pos_blk, seg_blk, all_keys, seg_row, valid_row, slopes, score_scale
        )
        soft = jnp.exp(scores - total_blk[..., None])
        value_grad = value_grad + jnp.einsum(
            "hqk,qhd->khd", soft.astype(jnp.bfloat16), grad_blk, preferred_element_type=jnp.float32
        )
        prob_grad = jnp.einsum(
            "qhd,khd->hqk", grad_blk, all_values, preferred_element_type=jnp.float32
        )
        score_grad = (
            soft * (prob_grad - jnp.sum(soft * prob_grad, axis=-1, keepdims=True))
        ).astype(jnp.bfloat16)
        query_grad = (
            jnp.einsum("hqk,khd->qhd", score_grad, all_keys, preferred_element_type=jnp.float32)
            * score_scale
        )
        key_grad = (
            key_grad
            + jnp.einsum("hqk,qhd->khd", score_grad, q_blk, preferred_element_type=jnp.float32)
            * score_scale
        )
        return ((key_grad, value_grad), query_grad)

    zero_rows = jnp.zeros((length, heads_local, HD), jnp.float32)
    (key_grad, value_grad), query_grad = lax.scan(
        one_block,
        (zero_rows, zero_rows),
        (
            queries.reshape(count, block_rows, heads_local, HD),
            positions.reshape(count, block_rows),
            seg_row.reshape(count, block_rows),
            log_total,
            grad_out,
        ),
    )
    stacked = jnp.stack([query_grad.reshape(length, heads_local, HD), key_grad, value_grad], axis=1)
    return stacked.astype(jnp.bfloat16).reshape(length, 3, 1, heads_local * HD)


def body(
    inputs,
    skip_feats,
    seg_ids,
    frame_valid,
    w_skip,
    gain_one,
    w_qkv,
    w_out,
    gain_two,
    w_up,
    b_up,
    w_down,
    b_down,
    cotangent,
):
    parts = lax.axis_size("seq")
    heads_local = H // parts
    width_local = heads_local * HD
    rows_here = inputs.shape[0]
    frames = inputs.shape[1]
    length = frames * parts
    block_rows = min(512, length)
    score_scale = 1.0 / math.sqrt(HD)
    first_head = lax.axis_index("seq") * heads_local
    slopes = jnp.exp2(-8.0 * (first_head + jnp.arange(heads_local) + 1).astype(jnp.float32) / H)
    gain_first = gain_one.astype(jnp.float32)
    gain_second = gain_two.astype(jnp.float32)
    bias_up = b_up.astype(jnp.float32)
    joined = jnp.concatenate([inputs, skip_feats], axis=-1)
    stem_out = jnp.einsum("rfc,cd->rfd", joined, w_skip, preferred_element_type=jnp.float32)
    unit_one, inverse_one, normed = norm_forward(stem_out, gain_first)
    normed = normed.astype(jnp.bfloat16)
    packed = jnp.einsum("rfd,de->rfe", normed, w_qkv, preferred_element_type=jnp.float32).astype(
        jnp.bfloat16
    )
    packed = packed.reshape(rows_here, frames, 3, parts, width_local)
    by_heads = lax.all_to_all(packed, "seq", split_axis=3, concat_axis=1, tiled=True)

    def forward_row(row_data):
        return attend_row(
            row_data[0], row_data[1], row_data[2], slopes, heads_local, block_rows, score_scale
        )

    attended, log_total = lax.map(forward_row, (by_heads, seg_ids, frame_valid))
    by_frames = lax.all_to_all(attended, "seq", split_axis=1, concat_axis=2, tiled=True)
    mixed_out = by_frames.reshape(rows_here, frames, D)
    middle = stem_out + jnp.einsum(
        "rfd,de->rfe", mixed_out, w_out, preferred_element_type=jnp.float32
    )
    unit_two, inverse_two, second = norm_forward(middle, gain_second)
    second = second.astype(jnp.bfloat16)
    hidden = jnp.einsum("rfd,dk->rfk", second, w_up, preferred_element_type=jnp.float32) + bias_up
    active_full, gelu_back = jax.vjp(gelu_exact, hidden)
    active = active_full.astype(jnp.bfloat16)
    result = (
        middle
        + jnp.einsum("rfk,kd->rfd", active, w_down, preferred_element_type=jnp.float32)
        + b_down.astype(jnp.float32)
    )
    output = result.astype(jnp.bfloat16)
    cot_full = cotangent.astype(jnp.float32)
    down_grad = jnp.einsum("rfk,rfd->kd", active, cotangent, preferred_element_type=jnp.float32)
    bias_down_grad = jnp.sum(cot_full, axis=(0, 1))
    active_grad = jnp.einsum("rfd,kd->rfk", cotangent, w_down, preferred_element_type=jnp.float32)
    hidden_grad = gelu_back(active_grad)[0].astype(jnp.bfloat16)
    up_grad = jnp.einsum("rfd,rfk->dk", second, hidden_grad, preferred_element_type=jnp.float32)
    bias_up_grad = jnp.sum(hidden_grad.astype(jnp.float32), axis=(0, 1))
    second_grad = jnp.einsum("rfk,dk->rfd", hidden_grad, w_up, preferred_element_type=jnp.float32)
    middle_part, gain_two_grad = norm_backward(second_grad, unit_two, inverse_two, gain_second)
    middle_grad = cot_full + middle_part
    middle_low = middle_grad.astype(jnp.bfloat16)
    out_grad = jnp.einsum("rfd,rfe->de", mixed_out, middle_low, preferred_element_type=jnp.float32)
    mixed_grad = jnp.einsum(
        "rfe,de->rfd", middle_low, w_out, preferred_element_type=jnp.float32
    ).astype(jnp.bfloat16)
    grad_heads = lax.all_to_all(
        mixed_grad.reshape(rows_here, frames, parts, width_local),
        "seq",
        split_axis=2,
        concat_axis=1,
        tiled=True,
    )

    def backward_row(row_data):
        return attend_row_back(
            row_data[0],
            row_data[1],
            row_data[2],
            row_data[3],
            row_data[4],
            slopes,
            heads_local,
            block_rows,
            score_scale,
        )

    packed_grad = lax.map(backward_row, (by_heads, log_total, grad_heads, seg_ids, frame_valid))
    packed_back = lax.all_to_all(packed_grad, "seq", split_axis=1, concat_axis=3, tiled=True)
    packed_back = packed_back.reshape(rows_here, frames, 3 * D)
    qkv_grad = jnp.einsum("rfd,rfe->de", normed, packed_back, preferred_element_type=jnp.float32)
    normed_grad = jnp.einsum("rfe,de->rfd", packed_back, w_qkv, preferred_element_type=jnp.float32)
    stem_part, gain_one_grad = norm_backward(normed_grad, unit_one, inverse_one, gain_first)
    stem_low = (middle_grad + stem_part).astype(jnp.bfloat16)
    skip_w_grad = jnp.einsum("rfc,rfd->cd", joined, stem_low, preferred_element_type=jnp.float32)
    joined_grad = jnp.einsum("rfd,cd->rfc", stem_low, w_skip, preferred_element_type=jnp.float32)
    input_grad = joined_grad[..., :D].astype(jnp.bfloat16)
    skip_grad = joined_grad[..., D:].astype(jnp.bfloat16)
    (
        skip_share,
        gain_one_share,
        qkv_share,
        out_share,
        gain_two_share,
        up_share,
        bias_up_share,
        down_share,
        bias_down_share,
    ) = (
        lax.psum_scatter(skip_w_grad, ("rows", "seq"), scatter_dimension=0, tiled=True),
        lax.psum_scatter(gain_one_grad, ("rows", "seq"), scatter_dimension=0, tiled=True),
        lax.psum_scatter(qkv_grad, ("rows", "seq"), scatter_dimension=0, tiled=True),
        lax.psum_scatter(out_grad, ("rows", "seq"), scatter_dimension=0, tiled=True),
        lax.psum_scatter(gain_two_grad, ("rows", "seq"), scatter_dimension=0, tiled=True),
        lax.psum_scatter(up_grad, ("rows", "seq"), scatter_dimension=0, tiled=True),
        lax.psum_scatter(bias_up_grad, ("rows", "seq"), scatter_dimension=0, tiled=True),
        lax.psum_scatter(down_grad, ("rows", "seq"), scatter_dimension=0, tiled=True),
        lax.psum_scatter(bias_down_grad, ("rows", "seq"), scatter_dimension=0, tiled=True),
    )
    return (
        output,
        input_grad,
        skip_grad,
        skip_share,
        gain_one_share,
        qkv_share,
        out_share,
        gain_two_share,
        up_share,
        bias_up_share,
        down_share,
        bias_down_share,
    )


def solution(mesh):
    fits = (mesh.shape["rows"], mesh.shape["seq"]) == (8, 4)
    return jax.shard_map(
        body_chips if fits else body,
        mesh=mesh,
        in_specs=(
            P("rows", "seq", None),
            P("rows", "seq", None),
            P("rows", None),
            P("rows", None),
            P(),
            P(),
            P(),
            P(),
            P(),
            P(),
            P(),
            P(),
            P(),
            P("rows", "seq", None),
        ),
        out_specs=(
            P("rows", "seq", None),
            P("rows", "seq", None),
            P("rows", "seq", None),
            P(("rows", "seq"), None),
            P(("rows", "seq")),
            P(("rows", "seq"), None),
            P(("rows", "seq"), None),
            P(("rows", "seq")),
            P(("rows", "seq"), None),
            P(("rows", "seq")),
            P(("rows", "seq"), None),
            P(("rows", "seq")),
        ),
        check_vma=False,
    )
```

```python
import functools
import math

import jax
import jax.numpy as jnp
from jax import lax
from jax.experimental import pallas as pl
from jax.experimental.pallas import tpu as pltpu
from jax.sharding import PartitionSpec as P

D = 1024
H = 16
HD = 64
MOST = 682

epsilon = 1e-05

F32 = jnp.float32
BF16 = jnp.bfloat16
LOG2E = 1.4426950408889634
ROWS = 32
CHIP = 1024
HALO = 768
FRAMES = 512
HALF = HALO // 2
EDGE = CHIP - HALO
WIDTH = D // 2
SKIPS = 4
SKIP_COLS = D // SKIPS
FAR = 1e30
MESH = pl.DeviceIdType.MESH
VMEM = pltpu.MemorySpace.VMEM
SMEM = pltpu.MemorySpace.SMEM
HBM = pltpu.MemorySpace.HBM


def norm_forward(value, gain_vec):
    center = value - jnp.mean(value, axis=-1, keepdims=True)
    spread = jnp.mean(center * center, axis=-1, keepdims=True)
    inverse = lax.rsqrt(spread + epsilon)
    unit = center * inverse
    return (unit, inverse, unit * gain_vec)


def norm_backward(upstream, unit, inverse, gain_vec):
    scaled = upstream * gain_vec
    gain_grad = jnp.sum(upstream * unit, axis=tuple(range(upstream.ndim - 1)))
    inner = (
        scaled
        - jnp.mean(scaled, axis=-1, keepdims=True)
        - unit * jnp.mean(scaled * unit, axis=-1, keepdims=True)
    )
    return (inverse * inner, gain_grad)


def gelu_exact(value):
    return jax.nn.gelu(value, approximate=False)


def mm(equation, left, right):
    return jnp.einsum(equation, left, right, preferred_element_type=F32)


def dot(left, right):
    return jnp.dot(left, right, preferred_element_type=F32)


def dot_nt(left, right):
    return lax.dot_general(left, right, (((1,), (1,)), ((), ())), preferred_element_type=F32)


def dot_tn(left, right):
    return lax.dot_general(left, right, (((0,), (0,)), ((), ())), preferred_element_type=F32)


class Links:
    def __init__(self, sends, recvs):
        row, col = lax.axis_index("rows"), lax.axis_index("seq")
        self.z, self.x, self.y, self.c = row // 2, row % 2, col // 2, col % 2
        z, x, y, c = self.z, self.x, self.y, self.c
        self.high, self.low = z // 2, z % 2
        self.is_end = z == 3 * self.high
        self.is_inner = z == 1 + self.high
        self.core = (row, y * 2 + 1 - c)
        self.over_y = (row, (1 - y) * 2 + c)
        self.over_x = (z * 2 + 1 - x, col)
        self.over_low = ((self.high * 2 + 1 - self.low) * 2 + x, col)
        self.over_high = (((1 - self.high) * 2 + self.low) * 2 + x, col)
        self.over_mirror = ((3 - z) * 2 + x, col)
        self.sends, self.recvs, self.count, self.started = sends, recvs, 0, []

    def greet(self, near=False):
        barrier = pltpu.get_barrier_semaphore()
        peers = [self.core, self.over_y]
        if not near:
            peers += [self.over_x, self.over_low, self.over_high, self.over_mirror]
        for peer in peers:
            pl.semaphore_signal(barrier, inc=1, device_id=peer, device_id_type=MESH)
        pl.semaphore_wait(barrier, len(peers))

    def reserve(self, number):
        self.count += number
        return self.count - number

    def copy(self, src, dst, at, peer):
        return pltpu.make_async_remote_copy(
            src, dst, self.sends.at[at], self.recvs.at[at], device_id=peer, device_id_type=MESH
        )

    def send(self, src, dst, peer, here=None):
        copy = self.copy(src, dst, self.reserve(1), peer)
        if here is None:
            copy.start()
        else:
            pl.when(here)(copy.start)
        self.started.append((copy, here))
        return copy

    def drain(self):
        assert self.count <= self.sends.shape[0]
        for copy, here in self.started:
            if here is None:
                copy.wait_send()
            else:
                pl.when(here)(copy.wait_send)


def head_columns(wqkv, part, core):
    return wqkv.at[:, pl.ds(pl.multiple_of(D * part + WIDTH * core, WIDTH), WIDTH)]


def front_kernel(*refs):
    first_in, second_in, wskip_in, gain, wqkv_in = refs[:5]
    outs = refs[5:10]
    first, second, wskip, wq, wkv, o_stem, o_seen, o_q, o_kv, o_joint, loads, stores, sends, recvs = refs[10:]
    storing = []

    def store(k, *at):
        src, dst = (o_stem, o_seen, o_q, o_kv, o_joint)[k].at[*at], outs[k].at[*at]
        copy = pltpu.make_async_copy(src, dst, stores.at[len(storing)])
        copy.start()
        storing.append(copy)

    links = Links(sends, recvs)
    y, c = links.y, links.c
    loading = []

    def load(src, dst):
        copy = pltpu.make_async_copy(src, dst, loads.at[len(loading)])
        copy.start()
        loading.append(copy)
        return copy

    got = [load(first_in, first), load(second_in, second), load(wskip_in, wskip)]
    got_wkv = [
        load(head_columns(wqkv_in, 1 + i, c), wkv.at[:, pl.ds(WIDTH * i, WIDTH)]) for i in (0, 1)
    ]
    got_wq = load(head_columns(wqkv_in, 0, c), wq)
    links.greet(near=True)
    for copy in got:
        copy.wait()
    gains = gain[0:1, :]
    base = jnp.where(y == 0, EDGE, 0) + HALF * c

    def piece(i, chip):
        return 128 * jnp.where(chip == 0, i, 2 - i)

    def send_piece(i):
        at = lax.rem(base + piece(i, y) + FRAMES * c, CHIP)
        there = CHIP + HALF * c + piece(i, y)
        src = o_seen.at[pl.ds(pl.multiple_of(at, 128), 128)]
        dst = o_seen.at[pl.ds(pl.multiple_of(there, 128), 128)]
        return links.send(src, dst, links.over_y)

    pieces, across = [], []
    for turn in range(2):
        at = pl.multiple_of(256 * (1 - c if turn == 0 else c), 256)
        rows = pl.ds(at, 256)
        value = dot(first[rows, :], wskip[:D, :]) + dot(second[rows, :], wskip[D:, :])
        o_stem[rows, :] = value
        center = value - jnp.mean(value, axis=-1, keepdims=True)
        rate = lax.rsqrt(jnp.mean(center * center, axis=-1, keepdims=True) + epsilon)
        o_seen[rows, :] = (center * rate * gains).astype(BF16)
        pieces.append(send_piece(turn))
        there = o_seen.at[pl.ds(pl.multiple_of(FRAMES + at, 256), 256)]
        across.append(links.send(o_seen.at[rows], there, links.core))
    store(0, pl.ds(0, FRAMES))
    for copy in across:
        copy.wait_recv()
    pieces.append(send_piece(2))
    store(1, pl.ds(0, CHIP))
    for copy in (*got_wkv, got_wq):
        copy.wait()

    def own_part(i, _):
        rows = pl.ds(pl.multiple_of(256 * i, 256), 256)
        o_q[rows, :] = dot(o_seen[rows, :], wq[...]).astype(BF16)
        o_kv[rows, :] = dot(o_seen[rows, :], wkv[...]).astype(BF16)
        return 0

    lax.fori_loop(0, 4, own_part, 0)
    store(2, pl.ds(0, CHIP))
    store(3, pl.ds(0, CHIP))
    o_joint[:D, :] = first[...].T
    forward = []

    def far_part(i, core):
        at = pl.multiple_of(CHIP + HALF * core + piece(i, 1 - y), 128)
        rows = pl.ds(at, 128)
        o_kv[rows, :] = dot(o_seen[rows, :], wkv[...]).astype(BF16)

    for i in range(3):
        pieces[i].wait_recv()
        at = pl.multiple_of(CHIP + HALF * c + piece(i, 1 - y), 128)
        rows = o_seen.at[pl.ds(at, 128)]
        forward.append(links.send(rows, rows, links.core))
        if i == 0:
            o_joint[D:, :] = second[...].T
            store(4, pl.ds(0, 2 * D))
        far_part(i, c)
        if i > 0:
            forward[i - 1].wait_recv()
            far_part(i - 1, 1 - c)
    forward[2].wait_recv()
    store(1, pl.ds(CHIP, HALO))
    far_part(2, 1 - c)
    store(3, pl.ds(CHIP, HALO))
    links.drain()
    for copy in storing:
        copy.wait()


def front(first, second, wskip, gain, wqkv):
    hbm, vm = pl.BlockSpec(memory_space=HBM), pl.BlockSpec(memory_space=VMEM)
    low = lambda *shape: pltpu.VMEM(shape, BF16)
    return pl.pallas_call(
        front_kernel,
        out_shape=[
            jax.ShapeDtypeStruct((FRAMES, D), F32),
            jax.ShapeDtypeStruct((CHIP + HALO, D), BF16),
            jax.ShapeDtypeStruct((CHIP, WIDTH), BF16),
            jax.ShapeDtypeStruct((CHIP + HALO, 2 * WIDTH), BF16),
            jax.ShapeDtypeStruct((2 * D, FRAMES), BF16),
        ],
        in_specs=[hbm] * 3 + [vm, hbm],
        out_specs=[hbm] * 5,
        scratch_shapes=[
            low(FRAMES, D),
            low(FRAMES, D),
            low(2 * D, D),
            low(D, WIDTH),
            low(D, 2 * WIDTH),
            pltpu.VMEM((FRAMES, D), F32),
            low(CHIP + HALO, D),
            low(CHIP, WIDTH),
            low(CHIP + HALO, 2 * WIDTH),
            low(2 * D, FRAMES),
            pltpu.SemaphoreType.DMA((6,)),
            pltpu.SemaphoreType.DMA((7,)),
            pltpu.SemaphoreType.DMA((8,)),
            pltpu.SemaphoreType.DMA((8,)),
        ],
        name="front",
        cost_estimate=pl.CostEstimate(
            flops=8_000_000_000, bytes_accessed=24_000_000, transcendentals=0
        ),
        compiler_params=pltpu.CompilerParams(
            collective_id=2, has_side_effects=True, vmem_limit_bytes=63 << 20
        ),
    )(first, second, wskip, gain, wqkv)


class Frames:
    def __init__(self, seg_at, seg, valid, key_code, query_seg):
        here = lax.axis_index("seq")
        self.seg_at = seg_at
        self.own, self.other = FRAMES * here, FRAMES * (here + 1 - 2 * (here % 2))
        self.halo = jnp.where(here // 2 == 0, CHIP, CHIP - HALO)
        self.core = here % 2
        places = [(0, FRAMES, self.own), (FRAMES, FRAMES, self.other), (CHIP, HALO, self.halo)]
        for at, count, frame in places:
            span = pl.ds(pl.multiple_of(frame, 256), count)
            code = jnp.where(valid[0:1, span] == 1, seg[0:1, span], -1).astype(F32)
            key_code[pl.ds(at, count), :] = jnp.broadcast_to(code, (128, count)).T
            if at < CHIP:
                query_seg[:, pl.ds(at, count)] = jnp.broadcast_to(
                    seg[0:1, span].astype(F32), (8, count)
                )

    def frame(self, at):
        late = jnp.where(at < CHIP, self.other - FRAMES, self.halo - CHIP)
        return at + jnp.where(at < FRAMES, self.own, late)

    def meet(self, keys_at, keys, queries_at, queries):
        k, q = self.frame(keys_at), self.frame(queries_at)
        return (self.seg_at[0, k] <= self.seg_at[0, q + queries - 1]) & (
            self.seg_at[0, k + keys - 1] >= self.seg_at[0, q]
        )

    def slope(self, h):
        values = [LOG2E * 2.0 ** (-8.0 * (core * H // 2 + h + 1) / H) for core in (0, 1)]
        return jnp.where(self.core == 0, values[0], values[1])


def set_distances(dist, key_at, query_at, key_code, query_seg):
    keys, queries = dist.shape
    rows = lax.broadcasted_iota(jnp.int32, (keys, queries), 0) + key_at
    cols = lax.broadcasted_iota(jnp.int32, (keys, queries), 1) + query_at
    apart = jnp.abs(rows - cols)
    allowed = (key_code == query_seg) | (apart == 0)
    dist[...] = jnp.where(allowed, apart.astype(F32), FAR)


def wide(code, queries):
    return jnp.concatenate([code] * (queries // 128), axis=1) if queries > 128 else code


def both_heads(ref, pair, queries):
    first = ref[pl.ds(128 * pair, HD), queries]
    second = ref[pl.ds(128 * pair + HD, HD), queries]
    blank = jnp.zeros_like(first)
    return jnp.concatenate(
        [
            jnp.concatenate([first, blank], axis=0),
            jnp.concatenate([blank, second], axis=0),
        ],
        axis=1,
    )


def both_slopes(dist, frames, pair):
    value = dist[...]
    return jnp.concatenate(
        [value * frames.slope(2 * pair), value * frames.slope(2 * pair + 1)], axis=1
    )


def attend_kernel(
    bq,
    bk,
    heads,
    seg_at,
    q_in,
    kv_in,
    seg,
    valid,
    o_out,
    o_outt,
    lse,
    q,
    kv,
    out,
    outt,
    loads,
    stores,
    kcode,
    qseg,
    qt,
    vt,
    dist,
    acc,
    top,
    total,
    heads_q,
    scores,
    probs,
):
    width = heads * HD
    pairs = range(heads // 2)
    c1 = LOG2E / math.sqrt(HD)
    keys, values = pl.ds(0, width), pl.ds(width, width)
    got = [
        pltpu.make_async_copy(q_in, q, loads.at[0]),
        pltpu.make_async_copy(kv_in.at[:, values], kv.at[:, values], loads.at[1]),
        pltpu.make_async_copy(kv_in.at[:, keys], kv.at[:, keys], loads.at[2]),
    ]
    for copy in got:
        copy.start()
    frames = Frames(seg_at, seg, valid, kcode, qseg)
    got[0].wait()
    qt[...] = q[...].T
    got[1].wait()
    vt[...] = kv[:, width:].T
    got[2].wait()

    def results(i):
        rows = pl.ds(pl.multiple_of(i * bq, bq), bq)
        return [
            pltpu.make_async_copy(out.at[rows], o_out.at[rows], stores.at[0, i]),
            pltpu.make_async_copy(outt.at[:, rows], o_outt.at[:, rows], stores.at[1, i]),
        ]

    def q_block(i, _):
        queries = pl.ds(pl.multiple_of(i * bq, bq), bq)
        acc[...] = jnp.zeros_like(acc)
        total[...] = jnp.zeros_like(total)
        top[...] = jnp.full_like(top, -3e38)
        for pair in pairs:
            heads_q[pair] = both_heads(qt, pair, queries)

        def k_block(j, _):
            @pl.when(frames.meet(j * bk, bk, i * bq, bq))
            def _():
                ks = pl.ds(pl.multiple_of(j * bk, bk), bk)
                set_distances(
                    dist,
                    frames.frame(j * bk),
                    frames.frame(i * bq),
                    wide(kcode[ks, :], bq),
                    qseg[0:1, queries],
                )
                for pair in pairs:
                    scores[pair] = dot(kv[ks, pl.ds(128 * pair, 128)], heads_q[pair])
                fades = []
                for pair in pairs:
                    line = pl.ds(pair, 1)
                    score = scores[pair] * c1 - both_slopes(dist, frames, pair)
                    was = top[line, :]
                    now = jnp.maximum(was, jnp.max(score, axis=0, keepdims=True))
                    prob = jnp.exp2(score - now)
                    fade = jnp.exp2(was - now)
                    total[line, :] = total[line, :] * fade + jnp.sum(prob, axis=0, keepdims=True)
                    top[line, :] = now
                    probs[pair] = prob.astype(BF16)
                    fades.append(fade)
                for pair in pairs:
                    value = dot(vt[pl.ds(128 * pair, 128), ks], probs[pair])
                    for e in range(2):
                        at, lanes = pl.ds(128 * pair + HD * e, HD), slice(bq * e, bq * (e + 1))
                        acc[at, :] = (
                            acc[at, :] * fades[pair][:, lanes]
                            + value[HD * e : HD * (e + 1), lanes]
                        )

            return 0

        lax.fori_loop(0, kv.shape[0] // bk, k_block, 0)
        for pair in pairs:
            rate = 1.0 / total[pl.ds(pair, 1), :]
            for e in range(2):
                at = pl.ds(128 * pair + HD * e, HD)
                acc[at, :] = acc[at, :] * rate[:, bq * e : bq * (e + 1)]
        lse[:, pl.ds(pl.multiple_of(2 * i * bq, 2 * bq), 2 * bq)] = top[...] + jnp.log2(total[...])
        out[queries, :] = acc[...].T.astype(BF16)
        outt[:, queries] = acc[...].astype(BF16)
        for copy in results(i):
            copy.start()
        return 0

    count = q.shape[0] // bq
    lax.fori_loop(0, count, q_block, 0)

    def settle(i, _):
        for copy in results(i):
            copy.wait()
        return 0

    lax.fori_loop(0, count, settle, 0)


def attend(q, kv, seg, valid, bq, bk, heads):
    frames = q.shape[0]
    vm, sm, hbm = [pl.BlockSpec(memory_space=m) for m in (VMEM, SMEM, HBM)]
    return pl.pallas_call(
        functools.partial(attend_kernel, bq, bk, heads),
        out_shape=(
            jax.ShapeDtypeStruct((frames, heads * HD), BF16),
            jax.ShapeDtypeStruct((heads * HD, frames), BF16),
            jax.ShapeDtypeStruct((heads // 2, 2 * frames), F32),
        ),
        in_specs=[sm, hbm, hbm, vm, vm],
        out_specs=(hbm, hbm, vm),
        scratch_shapes=[
            pltpu.VMEM(q.shape, BF16),
            pltpu.VMEM(kv.shape, BF16),
            pltpu.VMEM((frames, heads * HD), BF16),
            pltpu.VMEM((heads * HD, frames), BF16),
            pltpu.SemaphoreType.DMA((3,)),
            pltpu.SemaphoreType.DMA((2, frames // bq)),
            pltpu.VMEM((kv.shape[0], 128), F32),
            pltpu.VMEM((8, frames), F32),
            pltpu.VMEM((heads * HD, frames), BF16),
            pltpu.VMEM((heads * HD, kv.shape[0]), BF16),
            pltpu.VMEM((bk, bq), F32),
            pltpu.VMEM((heads * HD, bq), F32),
            pltpu.VMEM((heads // 2, 2 * bq), F32),
            pltpu.VMEM((heads // 2, 2 * bq), F32),
            pltpu.VMEM((heads // 2, 2 * HD, 2 * bq), BF16),
            pltpu.VMEM((heads // 2, bk, 2 * bq), F32),
            pltpu.VMEM((heads // 2, bk, 2 * bq), BF16),
        ],
        name="attend",
        cost_estimate=pl.CostEstimate(
            flops=8_000_000_000, bytes_accessed=8_000_000, transcendentals=4_000_000
        ),
        compiler_params=pltpu.CompilerParams(vmem_limit_bytes=63 << 20),
    )(seg, q, kv, seg, valid)


def attend_back_kernel(
    bq,
    bk,
    heads,
    seg_at,
    q_in,
    kv_in,
    grad_in,
    outt_in,
    lse,
    seg,
    valid,
    passed_in,
    o_dq,
    o_dkv,
    o_passed,
    q,
    kv,
    grad,
    outt,
    passed,
    dq,
    dkv,
    loads,
    stores,
    kcode,
    qseg,
    qt,
    kt,
    gradt,
    delta,
    dist,
    dqt,
    sums,
    heads_q,
    heads_g,
    rows_q,
    rows_g,
    scores,
    prob_grads,
    probs,
    score_grads,
):
    width = heads * HD
    pairs = range(heads // 2)
    c1 = LOG2E / math.sqrt(HD)
    scale = 1.0 / math.sqrt(HD)
    lane = lax.broadcasted_iota(jnp.int32, (bq, 128), 1)
    places = [(q_in, q), (grad_in, grad), (outt_in, outt), (kv_in, kv), (passed_in, passed)]
    got = [pltpu.make_async_copy(a, b, loads.at[i]) for i, (a, b) in enumerate(places)]
    for copy in got:
        copy.start()
    sums[...] = jnp.zeros_like(sums)
    frames = Frames(seg_at, seg, valid, kcode, qseg)
    got[0].wait()
    qt[...] = q[...].T
    got[1].wait()
    gradt[...] = grad[...].T
    got[2].wait()
    got[3].wait()
    kt[...] = kv[:, :width].T
    got[4].wait()
    stored = [pltpu.make_async_copy(passed, o_passed, stores.at[0])]
    stored[0].start()

    def dq_copy(i):
        rows = pl.ds(pl.multiple_of(i * bq, bq), bq)
        return pltpu.make_async_copy(dq.at[rows], o_dq.at[rows], stores.at[1 + i])

    def q_block(i, _):
        qs = pl.multiple_of(i * bq, bq)
        queries = pl.ds(qs, bq)
        dqt[...] = jnp.zeros_like(dqt)
        for pair in pairs:
            at = pl.ds(128 * pair, 128)
            heads_q[pair] = both_heads(qt, pair, queries)
            heads_g[pair] = both_heads(gradt, pair, queries)
            product = outt[at, queries].astype(F32) * gradt[at, queries].astype(F32)
            for e in range(2):
                rows = pl.ds(bq * e, bq)
                keep = (lane < HD) if e == 0 else (lane >= HD)
                for to, ref in ((rows_q, q), (rows_g, grad)):
                    value = ref[queries, at]
                    to[pair, rows, :] = jnp.where(keep, value, jnp.zeros_like(value))
                delta[pl.ds(pair, 1), rows] = jnp.sum(
                    product[HD * e : HD * (e + 1)], axis=0, keepdims=True
                )

        def k_block(j, _):
            @pl.when(frames.meet(j * bk, bk, i * bq, bq))
            def _():
                ks = pl.ds(pl.multiple_of(j * bk, bk), bk)
                set_distances(
                    dist,
                    frames.frame(j * bk),
                    frames.frame(i * bq),
                    wide(kcode[ks, :], bq),
                    qseg[0:1, queries],
                )
                for pair in pairs:
                    scores[pair] = dot(kv[ks, pl.ds(128 * pair, 128)], heads_q[pair])
                    prob_grads[pair] = dot(
                        kv[ks, pl.ds(width + 128 * pair, 128)], heads_g[pair]
                    )
                lines = pl.ds(pl.multiple_of(2 * qs, 2 * bq), 2 * bq)
                for pair in pairs:
                    line = pl.ds(pair, 1)
                    prob = jnp.exp2(
                        scores[pair] * c1 - both_slopes(dist, frames, pair) - lse[line, lines]
                    )
                    probs[pair] = prob.astype(BF16)
                    score_grads[pair] = (prob * (prob_grads[pair] - delta[line, :])).astype(BF16)
                for pair in pairs:
                    at = pl.ds(128 * pair, 128)
                    sums[ks, pl.ds(width + 128 * pair, 128)] += dot(probs[pair], rows_g[pair])
                    sums[ks, at] += dot(score_grads[pair], rows_q[pair])
                    value = dot(kt[at, ks], score_grads[pair])
                    for e in range(2):
                        dqt[pl.ds(128 * pair + HD * e, HD), :] += value[
                            HD * e : HD * (e + 1), bq * e : bq * (e + 1)
                        ]

            return 0

        lax.fori_loop(0, kv.shape[0] // bk, k_block, 0)
        dq[pl.ds(qs, bq), :] = (dqt[...] * scale).T.astype(BF16)
        dq_copy(i).start()
        return 0

    count = q.shape[0] // bq
    lax.fori_loop(0, count, q_block, 0)
    parts = [(CHIP, HALO), (0, FRAMES), (FRAMES, FRAMES)]
    for i, (at, rows) in enumerate(parts):
        part = pl.ds(at, rows)
        dkv[part, :width] = (sums[part, :width] * scale).astype(BF16)
        dkv[part, width:] = sums[part, width:].astype(BF16)
        copy = pltpu.make_async_copy(dkv.at[part], o_dkv.at[part], stores.at[1 + count + i])
        copy.start()
        stored.append(copy)
    for copy in [*stored, *[dq_copy(i) for i in range(count)]]:
        copy.wait()


def attend_back(q, kv, grad, outt, lse, seg, valid, passed, bq, bk, heads):
    vm, sm, hbm = [pl.BlockSpec(memory_space=m) for m in (VMEM, SMEM, HBM)]
    return pl.pallas_call(
        functools.partial(attend_back_kernel, bq, bk, heads),
        out_shape=(
            jax.ShapeDtypeStruct(q.shape, BF16),
            jax.ShapeDtypeStruct(kv.shape, BF16),
            jax.ShapeDtypeStruct(passed.shape, passed.dtype),
        ),
        in_specs=[sm] + [hbm] * 4 + [vm] * 3 + [hbm],
        out_specs=(hbm, hbm, hbm),
        scratch_shapes=[
            pltpu.VMEM(q.shape, BF16),
            pltpu.VMEM(kv.shape, BF16),
            pltpu.VMEM(grad.shape, BF16),
            pltpu.VMEM(outt.shape, BF16),
            pltpu.VMEM(passed.shape, passed.dtype),
            pltpu.VMEM(q.shape, BF16),
            pltpu.VMEM(kv.shape, BF16),
            pltpu.SemaphoreType.DMA((5,)),
            pltpu.SemaphoreType.DMA((4 + q.shape[0] // bq,)),
            pltpu.VMEM((kv.shape[0], 128), F32),
            pltpu.VMEM((8, q.shape[0]), F32),
            pltpu.VMEM((heads * HD, q.shape[0]), BF16),
            pltpu.VMEM((heads * HD, kv.shape[0]), BF16),
            pltpu.VMEM((heads * HD, q.shape[0]), BF16),
            pltpu.VMEM((heads // 2, 2 * bq), F32),
            pltpu.VMEM((bk, bq), F32),
            pltpu.VMEM((heads * HD, bq), F32),
            pltpu.VMEM(kv.shape, F32),
            *[pltpu.VMEM((heads // 2, 2 * HD, 2 * bq), BF16)] * 2,
            *[pltpu.VMEM((heads // 2, 2 * bq, 2 * HD), BF16)] * 2,
            *[pltpu.VMEM((heads // 2, bk, 2 * bq), F32)] * 2,
            *[pltpu.VMEM((heads // 2, bk, 2 * bq), BF16)] * 2,
        ],
        name="attend_back",
        cost_estimate=pl.CostEstimate(
            flops=20_000_000_000, bytes_accessed=16_000_000, transcendentals=4_000_000
        ),
        compiler_params=pltpu.CompilerParams(vmem_limit_bytes=63 << 20),
    )(seg, q, kv, grad, outt, lse, seg, valid, passed)


def add_into(value, other):
    def step(i, _):
        value[i] = value[i] + other[i]
        return 0

    lax.fori_loop(0, value.shape[0], step, 0)


class Unit:
    def __init__(self, links, own, came, sums, y_first, done, straight=False):
        self.links, self.own, self.came, self.sums = links, own, came, sums
        self.y_first, self.done, self.straight = y_first, done, straight

    def add_core(self, r0):
        for k in range(4):
            for i in range(2):
                add_into(self.own.at[k, i], r0.at[k, i])

    def send_first(self):
        n, a = self.links, self.own
        if self.y_first:
            self.first = n.send(a.at[:, :, 1 - n.y], self.came[0], n.over_y)
        else:
            self.first = n.send(a.at[:, 1 - n.x], self.came[0], n.over_x)

    def turn_first(self):
        self.first.wait_recv()
        n, a, b = self.links, self.own, self.came[0]
        for k in range(4):
            add_into(a.at[k, :, n.y] if self.y_first else a.at[k, n.x], b.at[k])
        if self.y_first:
            self.second = n.send(a.at[:, 1 - n.x, n.y], self.came[1], n.over_x)
        else:
            self.second = n.send(a.at[:, n.x, 1 - n.y], self.came[1], n.over_y)

    def chip(self, at):
        return self.own.at[at, self.links.x, self.links.y]

    def turn_second(self):
        self.second.wait_recv()
        self.after_second()

    def after_second(self):
        n, to = self.links, self.came[2]
        add_into(self.chip(slice(None)), self.came[1])
        if self.straight:
            low, high = 1 - n.low, 1 - n.high
            places = [(2 * n.high + low, n.over_low), (2 * high + n.low, n.over_high), (3 - n.z, n.over_mirror)]
            self.third = [n.send(self.chip(p), to.at[j], peer) for j, (p, peer) in enumerate(places)]
        else:
            part = self.chip(pl.ds(1 - n.high, 3))
            self.third = n.send(part, to.at[pl.ds(0, 3)], n.over_low, n.is_end)

    def turn_third(self):
        n = self.links

        @pl.when(n.is_inner)
        def _():
            self.third.wait_recv()
            add_into(self.chip(pl.ds(1 - n.high, 3)), self.came[2].at[pl.ds(0, 3)])

        part = self.chip(pl.ds(2 - 2 * n.high, 2))
        self.fourth = n.send(part, self.came[2].at[pl.ds(3, 2)], n.over_mirror, n.is_inner)

    def turn_fourth(self):
        n = self.links

        @pl.when(n.is_inner)
        def _():
            self.fourth.wait_recv()
            add_into(self.chip(pl.ds(2 * n.high, 2)), self.came[2].at[pl.ds(3, 2)])

        self.fifth = n.send(self.chip(3 * n.high), self.came[2].at[5], n.over_low, n.is_inner)

    def finish(self):
        n = self.links
        if self.straight:
            for copy in self.third:
                copy.wait_recv()
            value = self.chip(n.z)[...].astype(F32)
            for j in range(3):
                value = value + self.came[2][j].astype(F32)
            self.done(value)
            return
        self.sums[...] = self.chip(n.z)[...].astype(F32)

        @pl.when(n.is_end)
        def _():
            self.fifth.wait_recv()
            self.sums[...] += self.came[2][5].astype(F32)

        self.done(self.sums[...])


class LowUnit(Unit):
    def send_first(self):
        n = self.links
        self.first = n.send(self.own.at[:, 1 - n.low], self.came[0], n.over_low)

    def turn_first(self):
        self.first.wait_recv()
        n = self.links
        for k in range(2):
            for i in range(2):
                add_into(self.own.at[k, n.low, i], self.came[0].at[k, i])
        self.second = n.send(self.own.at[:, n.low, 1 - n.x], self.came[1], n.over_x)

    def turn_second(self):
        self.second.wait_recv()
        n = self.links
        for k in range(2):
            add_into(self.own.at[k, n.low, n.x], self.came[1].at[k])
        self.third = n.send(self.own.at[:, n.low, n.x, 1 - n.y], self.came[2], n.over_y)

    def turn_third(self):
        self.third.wait_recv()
        n = self.links
        add_into(self.own.at[:, n.low, n.x, n.y], self.came[2])
        self.fourth = n.send(self.own.at[1 - n.high, n.low, n.x, n.y], self.came[3], n.over_high)

    def finish(self):
        self.fourth.wait_recv()
        n = self.links
        value = self.own[n.high, n.low, n.x, n.y].astype(F32)
        self.done(value + self.came[3][...].astype(F32))


class LateUnit(Unit):
    def chip(self, at):
        return self.own.at[at]

    def begin(self, *loads):
        for copy in loads:
            copy.wait()
        self.after_second()


class PairUnit:
    def __init__(self, links, own, came, over_x, done):
        self.links, self.own, self.came, self.done = links, own, came, done
        self.at, self.peer = (links.x, links.over_x) if over_x else (links.y, links.over_y)

    def begin(self, *loads):
        for copy in loads:
            copy.wait()
        for k in range(2):
            add_into(self.own.at[k], self.came[0].at[k])
        self.third = self.links.send(self.own.at[:, 1 - self.at], self.came[1], self.peer)

    def turn_third(self):
        n = self.links
        self.third.wait_recv()
        for k in range(2):
            value = self.own.at[k, self.at]
            value[...] = value[...] + self.came[1][k]
        self.fourth = n.send(self.own.at[1 - n.high, self.at], self.came[2], n.over_high)

    def finish(self):
        self.fourth.wait_recv()
        value = self.own[self.links.high, self.at].astype(F32)
        self.done(value + self.came[2][...].astype(F32))


class Small:
    def __init__(self, links, steps, into, done):
        self.links, self.steps, self.into, self.done, self.at = links, steps, into, done, 0
        self.stages = [links.core, links.over_y, links.over_x, links.over_low, links.over_high]

    def send(self):
        self.flying = self.links.send(
            self.steps.at[self.at], self.into.at[self.at], self.stages[self.at]
        )

    def turn(self):
        self.flying.wait_recv()
        value = self.steps[self.at] + self.into[self.at]
        self.at += 1
        if self.at == len(self.stages):
            self.done(value)
        else:
            self.steps[self.at] = value
            self.send()


STEPS = 8
STEP = 256
P_COLS = 640
X_STEPS = 6
X_COLS = STEP * X_STEPS


def middle_kernel(*refs):
    (
        att_in_hbm,
        stem_in,
        wout_in,
        gain,
        up_hbm,
        down_hbm,
        bias_up,
        bias_down,
        cot_in,
    ) = refs[:9]
    o_out, o_grad, o_heads, o_wo, o_small = refs[9:14]
    o_p, o_p_away, o_q, o_q_away, o_x, o_x_away, o_z, o_z_away = refs[14:22]
    (
        att,
        att_came,
        stem,
        wout,
        ups,
        downs,
        cot,
        second,
        second_t,
        unit,
        inverse,
        active,
        hidden_grad,
        out_sum,
        grad_sum,
        low,
        swap_out,
        swap_in,
        p_send,
        p_keep,
        p_came,
        q_send,
        q_keep,
        q_came,
        x_send,
        x_keep,
        x_came,
        z_send,
        z_keep,
        z_came,
        loads,
        sends,
        recvs,
    ) = refs[22:]
    links = Links(sends, recvs)
    x, y, c = links.x, links.y, links.c
    loading = []

    def load(src, dst):
        copy = pltpu.make_async_copy(src, dst, loads.at[len(loading)])
        copy.start()
        loading.append(copy)
        return copy

    own, other = pl.ds(0, FRAMES), pl.ds(FRAMES, FRAMES)
    got_att = load(att_in_hbm.at[own], att)
    got_wout = load(wout_in, wout)
    got_stem = load(stem_in, stem)
    got_cot = load(cot_in, cot.at[own])
    got_ups, got_downs = [], []
    for i in range(STEPS):
        for j in range(2):
            at = pl.multiple_of(128 * (4 * i + 2 * j + c), 128)
            part = pl.ds(128 * j, 128)
            got_ups.append(load(up_hbm.at[:, pl.ds(at, 128)], ups.at[i, :, part]))
            got_downs.append(load(down_hbm.at[pl.ds(at, 128), :], downs.at[i, part, :]))
    links.greet()
    att_core = links.send(att_in_hbm.at[other], att_came, links.core)
    cot_core = links.send(cot_in, cot.at[other], links.core)
    mine = pl.ds(pl.multiple_of(WIDTH * c, WIDTH), WIDTH)
    theirs = pl.ds(pl.multiple_of(WIDTH * (1 - c), WIDTH), WIDTH)

    got_att.wait()
    got_wout.wait()
    got_stem.wait()
    att_core.wait_recv()
    gains = gain[0:1, :]
    second_core = []
    for part in range(2):
        rows = pl.ds(256 * part, 256)
        value = stem[rows, :] + dot(att[rows, :], wout[mine, :]) + dot(att_came[rows, :], wout[theirs, :])
        stem[rows, :] = value
        center = value - jnp.mean(value, axis=-1, keepdims=True)
        rate = lax.rsqrt(jnp.mean(center * center, axis=-1, keepdims=True) + epsilon)
        normal = center * rate
        unit[rows, :] = normal
        inverse[rows, :] = jnp.broadcast_to(rate, (256, 128))
        second[rows, :] = (normal * gains).astype(BF16)
        second_core.append(
            links.send(second.at[rows], second.at[pl.ds(FRAMES + 256 * part, 256)], links.core)
        )
    second_t[:, :FRAMES] = second[own, :].T
    out_sum[...] = jnp.zeros_like(out_sum)
    grad_sum[...] = jnp.zeros_like(grad_sum)
    o_small[...] = jnp.zeros_like(o_small)
    for copy in [got_cot, *got_ups, *got_downs]:
        copy.wait()
    cot_core.wait_recv()
    for copy in second_core:
        copy.wait_recv()
    second_t[:, FRAMES:] = second[other, :].T

    p_at, q_at, x_at, z_at = [links.reserve(k) for k in (STEPS, 4, X_STEPS, STEPS - X_STEPS)]

    def p_copy(i):
        return links.copy(p_send.at[i], p_came.at[i], p_at + i, links.over_y)

    def q_copy(i):
        return links.copy(q_send.at[i], q_came.at[i], q_at + i, links.over_low)

    def x_copy(i):
        return links.copy(x_send.at[i], x_came.at[i], x_at + i, links.over_x)

    def z_copy(i):
        return links.copy(z_send.at[i], z_came.at[i], z_at + i, links.over_low)

    def feed_step(i, _):
        up, down = ups[i], downs[i]
        bias = bias_up[0:1, pl.ds(pl.multiple_of(STEP * i, STEP), STEP)]
        total = jnp.zeros((1, STEP), F32)
        for half in (own, other):
            hidden = dot(second[half, :], up) + bias
            active_grad = dot_nt(cot[half, :], down)
            share = 0.5 + 0.5 * lax.erf(hidden * math.sqrt(0.5))
            slope = share + hidden * (
                jnp.exp(-0.5 * hidden * hidden) * (1.0 / math.sqrt(2.0 * math.pi))
            )
            a = (hidden * share).astype(BF16)
            g = (active_grad * slope).astype(BF16)
            active[half, :] = a
            hidden_grad[half, :] = g
            total = total + jnp.sum(g.astype(F32), axis=0, keepdims=True)
            out_sum[half, :] += dot(a, down)
            grad_sum[half, :] += dot_nt(g, up)
        for j in range(2):
            o_small[pl.ds(4 * i + 2 * j + c, 1), :] = total[:, 128 * j : 128 * (j + 1)]
        value = dot_tn(active[...], cot[...]).astype(BF16)
        p_send[i] = jnp.where(y == 0, value[128:, :P_COLS], value[:128, :P_COLS])
        p_keep[i] = jnp.where(y == 0, value[:128, :P_COLS], value[128:, :P_COLS])
        p_copy(i).start()
        stays = lax.rem(i // 2, 2) == links.low
        slot = 2 * (i // 4) + lax.rem(i, 2)
        rest = value[:, P_COLS:].reshape(2, 128, D - P_COLS)

        @pl.when(stays)
        def _():
            q_keep[slot] = rest

        @pl.when(jnp.logical_not(stays))
        def _():
            q_send[slot] = rest
            q_copy(slot).start()

        value = dot(second_t[...], hidden_grad[...]).astype(BF16)

        @pl.when(i < X_STEPS)
        def _():
            for k in range(4):
                first, last = value[256 * k : 256 * k + 128], value[256 * k + 128 : 256 * (k + 1)]
                x_send[i, k] = jnp.where(x == 0, last, first)
                x_keep[i, k] = jnp.where(x == 0, first, last)
            x_copy(i).start()

        @pl.when(i >= X_STEPS)
        def _():
            j = i - X_STEPS
            for k in range(2):
                first, last = value[512 * k : 512 * k + 256], value[512 * k + 256 : 512 * (k + 1)]
                z_send[j, k] = jnp.where(links.low == 0, last, first)
                z_keep[j, k] = jnp.where(links.low == 0, first, last)
            z_copy(j).start()

        return 0

    lax.fori_loop(0, STEPS, feed_step, 0)

    swap_out[0] = grad_sum[other, :].astype(BF16)
    grad_core = links.send(swap_out.at[0], swap_in.at[0], links.core)
    swap_out[1] = out_sum[other, :].astype(BF16)
    out_core = links.send(swap_out.at[1], swap_in.at[1], links.core)
    grad_core.wait_recv()

    def norm_rows(i, totals):
        rows = pl.ds(pl.multiple_of(128 * i, 128), 128)
        upstream = grad_sum[rows, :] + swap_in[0, rows, :].astype(F32)
        normal = unit[rows, :]
        scaled = upstream * gains
        inner = (
            scaled
            - jnp.mean(scaled, axis=-1, keepdims=True)
            - normal * jnp.mean(scaled * normal, axis=-1, keepdims=True)
        )
        value = cot[rows, :].astype(F32)
        grad = value + inverse[rows, 0:1] * inner
        o_grad[rows, :] = grad
        low[rows, :] = grad.astype(BF16)
        return (
            totals[0] + jnp.sum(upstream * normal, axis=0, keepdims=True),
            totals[1] + jnp.sum(value, axis=0, keepdims=True),
        )

    zero = jnp.zeros((1, D), F32)
    totals = lax.fori_loop(0, 4, norm_rows, (zero, zero))
    for k, value in enumerate(totals):
        for j in range(8):
            o_small[pl.ds(32 + 8 * k + j, 1), :] = value[:, 128 * j : 128 * (j + 1)]
    swap_out[2, :, :WIDTH] = dot_nt(low[...], wout[theirs, :]).astype(BF16)
    heads_core = links.send(
        swap_out.at[2, :, pl.ds(0, WIDTH)], swap_in.at[2, :, pl.ds(0, WIDTH)], links.core
    )
    o_heads[own, :] = dot_nt(low[...], wout[mine, :]).astype(BF16)
    o_wo[mine, :] = dot_tn(att[...], low[...]).astype(BF16)
    o_wo[theirs, :] = dot_tn(att_came[...], low[...]).astype(BF16)
    out_core.wait_recv()

    def out_rows(i, _):
        rows = pl.ds(pl.multiple_of(128 * i, 128), 128)
        o_out[rows, :] = (
            stem[rows, :]
            + (out_sum[rows, :] + swap_in[1, rows, :].astype(F32))
            + bias_down[0:1, :]
        ).astype(BF16)
        return 0

    lax.fori_loop(0, 4, out_rows, 0)
    heads_core.wait_recv()
    o_heads[other, :] = swap_in[2, :, :WIDTH]

    def add_p(i, _):
        p_copy(i).wait()
        value = p_keep[i] + p_came[i]
        stays = lax.rem(i, 2) == x

        @pl.when(stays)
        def _():
            o_p[i // 2] = value

        @pl.when(jnp.logical_not(stays))
        def _():
            o_p_away[i // 2] = value

        return 0

    def add_q(i, _):
        q_copy(i).wait()
        o_q[i // 2, lax.rem(i, 2)] = q_keep[i, y] + q_came[i, y]
        o_q_away[i // 2, lax.rem(i, 2)] = q_keep[i, 1 - y] + q_came[i, 1 - y]
        return 0

    def columns(i):
        return pl.ds(pl.multiple_of(STEP * i, STEP), STEP)

    def add_x(i, _):
        x_copy(i).wait()
        for k in range(4):
            value = x_keep[i, k] + x_came[i, k]
            o_x[k, :, columns(i)] = jnp.where(y == 0, value[:64], value[64:])
            o_x_away[k, :, columns(i)] = jnp.where(y == 0, value[64:], value[:64])
        return 0

    def add_z(i, _):
        z_copy(i).wait()
        for k in range(2):
            value = z_keep[i, k] + z_came[i, k]
            o_z[k, :, columns(i)] = jnp.where(x == 0, value[:128], value[128:])
            o_z_away[k, :, columns(i)] = jnp.where(x == 0, value[128:], value[:128])
        return 0

    lax.fori_loop(0, STEPS, add_p, 0)
    lax.fori_loop(0, 4, add_q, 0)
    lax.fori_loop(0, X_STEPS, add_x, 0)
    lax.fori_loop(0, STEPS - X_STEPS, add_z, 0)
    links.drain()


def middle(att, stem, wout, gain, w_up, w_down, bias_up, bias_down, cot):
    hbm, vm = pl.BlockSpec(memory_space=HBM), pl.BlockSpec(memory_space=VMEM)
    low = lambda *shape: pltpu.VMEM(shape, BF16)
    full = lambda *shape: pltpu.VMEM(shape, F32)
    copies = 28
    return pl.pallas_call(
        middle_kernel,
        out_shape=[
            jax.ShapeDtypeStruct((FRAMES, D), BF16),
            jax.ShapeDtypeStruct((FRAMES, D), F32),
            jax.ShapeDtypeStruct((CHIP, WIDTH), BF16),
            jax.ShapeDtypeStruct((D, D), BF16),
            jax.ShapeDtypeStruct((48, 128), F32),
            *[jax.ShapeDtypeStruct((4, 128, P_COLS), BF16)] * 2,
            *[jax.ShapeDtypeStruct((2, 2, 128, D - P_COLS), BF16)] * 2,
            *[jax.ShapeDtypeStruct((4, 64, X_COLS), BF16)] * 2,
            *[jax.ShapeDtypeStruct((2, 128, 2 * D - X_COLS), BF16)] * 2,
        ],
        in_specs=[hbm] * 3 + [vm] + [hbm] * 2 + [vm] * 2 + [hbm],
        out_specs=[vm] * 13,
        scratch_shapes=[
            low(FRAMES, WIDTH),
            low(FRAMES, WIDTH),
            full(FRAMES, D),
            low(D, D),
            low(STEPS, D, STEP),
            low(STEPS, STEP, D),
            low(CHIP, D),
            low(CHIP, D),
            low(D, CHIP),
            full(FRAMES, D),
            full(FRAMES, 128),
            low(CHIP, STEP),
            low(CHIP, STEP),
            full(CHIP, D),
            full(CHIP, D),
            low(FRAMES, D),
            low(3, FRAMES, D),
            low(3, FRAMES, D),
            *[low(STEPS, 128, P_COLS)] * 3,
            *[low(4, 2, 128, D - P_COLS)] * 3,
            *[low(X_STEPS, 4, 128, STEP)] * 3,
            *[low(STEPS - X_STEPS, 2, 256, STEP)] * 3,
            pltpu.SemaphoreType.DMA((4 + 4 * STEPS,)),
            pltpu.SemaphoreType.DMA((copies,)),
            pltpu.SemaphoreType.DMA((copies,)),
        ],
        name="middle",
        cost_estimate=pl.CostEstimate(
            flops=28_000_000_000, bytes_accessed=40_000_000, transcendentals=4_000_000
        ),
        compiler_params=pltpu.CompilerParams(
            collective_id=1, has_side_effects=True, vmem_limit_bytes=63 << 20
        ),
    )(att, stem, wout, gain, w_up, w_down, bias_up, bias_down, cot)


def tail_kernel(*refs):
    (
        p_in,
        p_came,
        q_in,
        q_came,
        x_in,
        x_came,
        z_in,
        z_came,
        wo_in,
        small_in,
        dq_in,
        dkv_in,
        seen_in,
        wqkv_in,
        joint_in,
        stem_in,
        grad_in,
        gain,
        wskip_in,
    ) = refs[:19]
    o_in, o_skip, o_down, o_up, o_qkv, o_wo, o_wskip, o_small, o_gain = refs[19:28]
    (
        dq,
        dkv,
        wide_buf,
        wq,
        wkv,
        joint,
        stem,
        grad,
        chip_out,
        chip_in,
        chip_own,
        halo_out,
        halo_in,
        halo_sum,
        halo,
        low,
        low_own,
        low_r1,
        low_r2,
        low_r3,
        low_r4,
        join_low,
        p_own,
        p_r2,
        p_r3,
        q_own,
        q_r2,
        q_r3,
        q_r4,
        x_own,
        x_r2,
        x_r3,
        z_own,
        z_r2,
        z_r3,
        z_r4,
        up_out,
        up_in_last,
        unit_own,
        unit_r1,
        unit_r2,
        unit_r3,
        wo_r0,
        join_out,
        skip_own,
        skip_out,
        skip_r0,
        skip_r1,
        skip_r2,
        skip_r3,
        sums,
        small_steps,
        small_into,
        gain_steps,
        gain_into,
        loads,
        sends,
        recvs,
    ) = refs[28:]
    links = Links(sends, recvs)
    y, c = links.y, links.c
    loading = []

    def load(src, dst):
        copy = pltpu.make_async_copy(src, dst, loads.at[len(loading)])
        copy.start()
        loading.append(copy)
        return copy

    seen = wide_buf.at[pl.ds(0, CHIP + HALO)]
    far, near = pl.ds(CHIP, HALO), pl.ds(0, CHIP)
    got_wkv = [load(head_columns(wqkv_in, 1 + i, c), wkv.at[:, pl.ds(WIDTH * i, WIDTH)]) for i in (0, 1)]
    got_far = load(dkv_in.at[far], dkv.at[far])
    links.greet()
    wo_core = links.send(wo_in.at[:, :, :, 1 - c], wo_r0, links.core)
    got_dq = load(dq_in, dq)
    got_near = load(dkv_in.at[near], dkv.at[near])
    got_seen = load(seen_in, seen)
    got_wo = load(wo_in.at[:, :, :, c], unit_own.at[0])
    got_small = load(small_in, small_steps.at[0])
    got_p = [
        [
            load(p_in.at[:, pl.ds(64 * i, 64)], p_own.at[i]),
            load(p_came.at[:, pl.ds(64 * i, 64)], p_r2.at[i]),
        ]
        for i in range(2)
    ]
    got_x = []
    for i, core in enumerate((1 - c, c)):
        rows = pl.ds(pl.multiple_of(32 * core, 32), 32)
        got_x.append([load(x_in.at[:, rows], x_own.at[i]), load(x_came.at[:, rows], x_r2.at[i])])
    got_q = [load(q_in, q_own), load(q_came, q_r2)]
    got_z = [load(z_in, z_own), load(z_came, z_r2)]
    got_wq = load(head_columns(wqkv_in, 0, c), wq)
    got_stem = load(stem_in, stem)
    got_grad = load(grad_in, grad)
    got_joint = load(joint_in, joint)
    halo[pl.ds(0, EDGE), :] = jnp.zeros((EDGE, D), BF16)
    halo[pl.ds(EDGE + HALO, EDGE), :] = jnp.zeros((EDGE, D), BF16)

    def to_down(i):
        def done(value):
            o_down[pl.ds(64 * i, 64), pl.ds(0, P_COLS)] = value

        return done

    def to_down_rest(value):
        o_down[:, pl.ds(P_COLS, D - P_COLS)] = value

    def put_up(b, core, value):
        o_up[:, pl.ds(pl.multiple_of(256 * b + 128 * core, 128), 128)] = value

    def pass_up(at, value):
        part = pl.ds(at, value.shape[1])
        up_out[:, part] = value
        up_last.append(links.send(up_out.at[:, part], up_in_last.at[:, part], links.core))

    def to_up_other(value):
        pass_up(0, value)

    def to_up_mine(value):
        for b in range(X_COLS // 128):
            put_up(b, c, value[:, 128 * b : 128 * (b + 1)])

    def to_up_rest(value):
        pass_up(X_COLS, jnp.where(c == 0, value[32:], value[:32]))
        mine = jnp.where(c == 0, value[:32], value[32:])
        for b in range(X_COLS // 128, 16):
            at = 128 * b - X_COLS
            put_up(b, c, mine[:, at : at + 128])

    def take_up():
        for copy in up_last:
            copy.wait_recv()
        for b in range(16):
            put_up(b, 1 - c, up_in_last[:, 128 * b : 128 * (b + 1)])

    up_last = []

    def room(rows, cols):
        return sums.at[pl.ds(0, rows), pl.ds(0, cols)]

    p0, p1 = [
        LateUnit(
            links, p_own.at[i], (None, p_r2.at[i], p_r3.at[i]), room(64, P_COLS), True, to_down(i)
        )
        for i in range(2)
    ]
    x0, x1 = [
        LateUnit(
            links, x_own.at[i], (None, x_r2.at[i], x_r3.at[i]), room(32, X_COLS), False, done
        )
        for i, done in enumerate((to_up_other, to_up_mine))
    ]
    rest_q = PairUnit(links, q_own, (q_r2, q_r3, q_r4), True, to_down_rest)
    rest_z = PairUnit(links, z_own, (z_r2, z_r3, z_r4), False, to_up_rest)

    def to_wo(value):
        o_wo[...] = value

    def to_qkv(i):
        def done(value):
            o_qkv[:, pl.ds(D * i, D)] = value

        return done

    def to_wskip(q, half):
        def done(value):
            o_wskip[pl.ds(ROWS * half, ROWS), pl.ds(SKIP_COLS * q, SKIP_COLS)] = value

        return done

    def unit(k, y_first, done):
        came = (unit_r1.at[k], unit_r2.at[k], unit_r3.at[k])
        return Unit(links, unit_own.at[k], came, room(ROWS, D), y_first, done)

    wo = unit(0, False, to_wo)
    unit_q, unit_v = unit(1, False, to_qkv(0)), unit(2, True, to_qkv(2))
    unit_k = LowUnit(links, low_own, (low_r1, low_r2, low_r3, low_r4), None, False, to_qkv(1))

    def skip_unit(k, y_first, done):
        came = (skip_r1.at[k], skip_r2.at[k], skip_r3.at[k])
        return Unit(links, skip_own.at[k], came, None, y_first, done, straight=True)

    skips = [
        [skip_unit(2 * q + half, half == 0, to_wskip(q, half)) for half in range(2)]
        for q in range(SKIPS)
    ]

    def to_small(value):
        o_small[...] = value

    def to_gain(value):
        o_gain[...] = value

    small = Small(links, small_steps, small_into, to_small)
    gain_sum = Small(links, gain_steps, gain_into, to_gain)

    for copy in (*got_wkv, got_far):
        copy.wait()

    def halo_part(core):
        at = pl.multiple_of(CHIP + HALF * core, 128)
        return dot_nt(dkv[pl.ds(at, HALF), :], wkv[...])

    halo_out[...] = halo_part(1 - c).astype(BF16)
    halo_core = links.send(halo_out, halo_in, links.core)
    mine = halo_part(c)
    halo_core.wait_recv()
    halo_sum[...] = (mine + halo_in[...].astype(F32)).astype(BF16)
    part_at = pl.ds(pl.multiple_of(EDGE + HALF * c, 128), HALF)
    part = halo.at[part_at]
    halo_y = links.send(halo_sum, part, links.over_y)
    got_near.wait()
    got_seen.wait()
    columns = pl.ds(pl.multiple_of(WIDTH * c, WIDTH), WIDTH)

    def place(k, i, value):
        value = value.astype(BF16)
        for j in range(2):
            for m in range(2):
                at = 128 * j + 64 * m
                first, second = value[at : at + 32], value[at + 32 : at + 64]
                mine, theirs = jnp.where(c == 0, first, second), jnp.where(c == 0, second, first)
                if k == 1:
                    low_own[i // 2, i % 2, j, m, :, columns] = mine
                else:
                    unit_own[1 + k // 2, i, j, m, :, columns] = mine
                if k == 1:
                    join_low[i // 2, i % 2, j, m] = theirs
                else:
                    join_out[k // 2, i, j, m] = theirs

    def join(k):
        if k == 1:
            return links.send(join_low, low_own.at[:, :, :, :, :, columns], links.core)
        there = unit_own.at[1 + k // 2, :, :, :, :, columns]
        return links.send(join_out.at[k // 2], there, links.core)

    def kv_rows(i, _):
        value = dot(seen[:, pl.ds(pl.multiple_of(256 * i, 256), 256)].T, dkv[...])
        place(1, i, value[:, :WIDTH])
        place(2, i, value[:, WIDTH:])
        return 0

    def q_rows(i, _):
        place(0, i, dot(seen[near, pl.ds(pl.multiple_of(256 * i, 256), 256)].T, dq[...]))
        return 0

    def chip_part(at):
        rows = pl.ds(at, 256)
        return dot_nt(dq[rows, :], wq[...]) + dot_nt(dkv[rows, :], wkv[...])

    def other_frames(i, _):
        at = pl.multiple_of(256 * i, 256)
        chip_out[pl.ds(at, 256), :] = chip_part(FRAMES + at).astype(BF16)
        return 0

    def own_frames(i, _):
        at = pl.multiple_of(256 * i, 256)
        chip_own[pl.ds(at, 256), :] = chip_part(at)
        return 0

    gains = gain[0:1, :]

    def norm_rows(i, total):
        at = pl.multiple_of(128 * i, 128)
        rows = pl.ds(at, 128)
        upstream = (
            chip_own[rows, :]
            + chip_in[rows, :].astype(F32)
            + halo[pl.ds(pl.multiple_of(at + 256 * (2 * c + y), 128), 128), :].astype(F32)
        )
        value = stem[rows, :]
        center = value - jnp.mean(value, axis=-1, keepdims=True)
        inverse = lax.rsqrt(jnp.mean(center * center, axis=-1, keepdims=True) + epsilon)
        unit_value = center * inverse
        scaled = upstream * gains
        inner = (
            scaled
            - jnp.mean(scaled, axis=-1, keepdims=True)
            - unit_value * jnp.mean(scaled * unit_value, axis=-1, keepdims=True)
        )
        low[rows, :] = (grad[rows, :] + inverse * inner).astype(BF16)
        return total + jnp.sum(upstream * unit_value, axis=0, keepdims=True)

    def skip_part(q):
        def skip_rows(i, _):
            value = dot(
                joint[pl.ds(pl.multiple_of(512 * i, 512), 512), :],
                low[:, SKIP_COLS * q : SKIP_COLS * (q + 1)],
            ).astype(BF16)
            for j in range(2):
                for m in range(2):
                    for half in range(2):
                        at = 256 * j + 128 * m + 32 * half
                        first, second = value[at : at + 32], value[at + 64 : at + 96]
                        skip_own[2 * q + half, i, j, m] = jnp.where(c == 0, first, second)
                        skip_out[2 * q + half, i, j, m] = jnp.where(c == 0, second, first)
            return 0

        lax.fori_loop(0, 4, skip_rows, 0)
        both = pl.ds(2 * q, 2)
        return links.send(skip_out.at[both], skip_r0.at[both], links.core)

    def skip_begin(q, copy):
        copy.wait_recv()
        for half in range(2):
            skips[q][half].add_core(skip_r0.at[2 * q + half])
            skips[q][half].send_first()

    def joined_part(i):
        value = dot_nt(low[...], wide_buf[pl.ds(256 * i, 256), :]).astype(BF16)
        out = o_in if i < 4 else o_skip
        out[:, pl.ds(256 * (i % 4), 256)] = value

    got_wo.wait()
    wo_core.wait_recv()
    wo.add_core(wo_r0)
    wo.send_first()
    lax.fori_loop(0, 4, kv_rows, 0)
    join_v, join_k = join(2), join(1)
    for one, got in ((p0, got_p[0]), (p1, got_p[1]), (x0, got_x[0]), (x1, got_x[1])):
        one.begin(*got)
    rest_q.begin(*got_q)
    rest_z.begin(*got_z)
    got_small.wait()
    small.send()
    join_v.wait_recv()
    unit_v.send_first()
    join_k.wait_recv()
    unit_k.send_first()
    got_dq.wait()
    lax.fori_loop(0, 4, q_rows, 0)
    join_q = join(0)
    got_wskip = load(wskip_in, wide_buf)
    got_wq.wait()
    lax.fori_loop(0, 2, other_frames, 0)
    chip_core = links.send(chip_out, chip_in, links.core)
    join_q.wait_recv()
    unit_q.send_first()
    lax.fori_loop(0, 2, own_frames, 0)
    halo_y.wait_recv()
    halo_rest = links.send(part, part, links.core)
    small.turn()
    chip_core.wait_recv()
    got_stem.wait()
    got_grad.wait()
    halo_rest.wait_recv()
    total = lax.fori_loop(0, 4, norm_rows, jnp.zeros((1, D), F32))
    gain_steps[0] = jnp.concatenate(
        [total[:, 128 * i : 128 * (i + 1)] for i in range(8)], axis=0
    )
    gain_sum.send()
    got_joint.wait()
    wo.turn_first()
    p0.turn_third()
    skip_core0 = skip_part(0)
    skip_core1 = skip_part(1)
    rest_q.turn_third()
    skip_begin(0, skip_core0)
    skip_core2 = skip_part(2)
    p1.turn_third()
    skip_begin(1, skip_core1)
    skip_core3 = skip_part(3)
    rest_z.turn_third()
    skip_begin(2, skip_core2)
    skip_begin(3, skip_core3)
    got_wskip.wait()
    joined_part(0)
    joined_part(1)
    gain_sum.turn()
    joined_part(2)
    joined_part(3)
    x0.turn_third()
    joined_part(4)
    joined_part(5)
    joined_part(6)
    joined_part(7)
    unit_q.turn_first()
    p0.turn_fourth()
    skips[0][1].turn_first()
    unit_v.turn_first()
    x1.turn_third()
    small.turn()
    rest_q.finish()
    skips[1][1].turn_first()
    p1.turn_fourth()
    skips[2][1].turn_first()
    wo.turn_second()
    skips[3][1].turn_first()
    rest_z.finish()
    p0.finish()
    skips[0][0].turn_first()
    p1.finish()
    unit_k.turn_first()
    skips[1][0].turn_first()
    x0.turn_fourth()
    unit_v.turn_second()
    small.turn()
    skips[2][0].turn_first()
    wo.turn_third()
    skips[0][0].turn_second()
    x0.finish()
    x1.turn_fourth()
    take_up()
    skips[3][0].turn_first()
    gain_sum.turn()
    unit_v.turn_third()
    x1.finish()
    wo.turn_fourth()
    small.turn()
    unit_k.turn_second()
    skips[1][0].turn_second()
    unit_q.turn_second()
    skips[0][0].finish()
    wo.finish()
    skips[2][0].turn_second()
    skips[0][1].turn_second()
    unit_v.turn_fourth()
    skips[3][0].turn_second()
    gain_sum.turn()
    skips[1][1].turn_second()
    small.turn()
    skips[2][1].turn_second()
    skips[1][0].finish()
    unit_v.finish()
    skips[3][1].turn_second()
    unit_q.turn_third()
    unit_k.turn_third()
    skips[2][0].finish()
    gain_sum.turn()
    skips[0][1].finish()
    unit_q.turn_fourth()
    skips[3][0].finish()
    skips[1][1].finish()
    unit_q.finish()
    unit_k.finish()
    gain_sum.turn()
    skips[2][1].finish()
    skips[3][1].finish()
    links.drain()


def tail(late, wo, small, dq, dkv, seen, wqkv, joint, stem, grad, gain, wskip):
    hbm, vm = pl.BlockSpec(memory_space=HBM), pl.BlockSpec(memory_space=VMEM)
    n_small = small.shape[0]
    out_shape = [
        jax.ShapeDtypeStruct((FRAMES, D), BF16),
        jax.ShapeDtypeStruct((FRAMES, D), BF16),
        jax.ShapeDtypeStruct((128, D), F32),
        jax.ShapeDtypeStruct((32, 4096), F32),
        jax.ShapeDtypeStruct((32, 3 * D), F32),
        jax.ShapeDtypeStruct((32, D), F32),
        jax.ShapeDtypeStruct((64, D), F32),
        jax.ShapeDtypeStruct((n_small, 128), F32),
        jax.ShapeDtypeStruct((8, 128), F32),
    ]
    low = lambda *shape: pltpu.VMEM(shape, BF16)
    full = lambda *shape: pltpu.VMEM(shape, F32)
    skip = (ROWS, SKIP_COLS)
    copies = 116
    scratch = [
        low(CHIP, WIDTH),
        low(CHIP + HALO, D),
        low(2 * D, D),
        low(D, WIDTH),
        low(D, D),
        low(2 * D, FRAMES),
        full(FRAMES, D),
        full(FRAMES, D),
        low(FRAMES, D),
        low(FRAMES, D),
        full(FRAMES, D),
        low(HALF, D),
        low(HALF, D),
        low(HALF, D),
        low(HALO + 2 * EDGE, D),
        low(FRAMES, D),
        low(2, 2, 2, 2, ROWS, D),
        low(2, 2, 2, ROWS, D),
        low(2, 2, ROWS, D),
        low(2, ROWS, D),
        low(ROWS, D),
        low(2, 2, 2, 2, ROWS, WIDTH),
        low(2, 4, 64, P_COLS),
        low(2, 4, 64, P_COLS),
        low(2, 6, 64, P_COLS),
        low(2, 2, 128, D - P_COLS),
        low(2, 2, 128, D - P_COLS),
        low(2, 128, D - P_COLS),
        low(128, D - P_COLS),
        low(2, 4, 32, X_COLS),
        low(2, 4, 32, X_COLS),
        low(2, 6, 32, X_COLS),
        low(2, 2, 64, 2 * D - X_COLS),
        low(2, 2, 64, 2 * D - X_COLS),
        low(2, 64, 2 * D - X_COLS),
        low(64, 2 * D - X_COLS),
        full(32, 2 * D),
        full(32, 2 * D),
        low(3, 4, 2, 2, ROWS, D),
        low(3, 4, 2, ROWS, D),
        low(3, 4, ROWS, D),
        low(3, 6, ROWS, D),
        low(4, 2, 2, ROWS, D),
        low(2, 4, 2, 2, ROWS, WIDTH),
        low(2 * SKIPS, 4, 2, 2, *skip),
        low(2 * SKIPS, 4, 2, 2, *skip),
        low(2 * SKIPS, 4, 2, 2, *skip),
        low(2 * SKIPS, 4, 2, *skip),
        low(2 * SKIPS, 4, *skip),
        low(2 * SKIPS, 3, *skip),
        full(64, X_COLS),
        full(5, n_small, 128),
        full(5, n_small, 128),
        full(5, 8, 128),
        full(5, 8, 128),
        pltpu.SemaphoreType.DMA((28,)),
        pltpu.SemaphoreType.DMA((copies,)),
        pltpu.SemaphoreType.DMA((copies,)),
    ]
    return pl.pallas_call(
        tail_kernel,
        out_shape=out_shape,
        in_specs=[hbm] * 17 + [vm, hbm],
        out_specs=[vm] * 9,
        scratch_shapes=scratch,
        name="tail",
        cost_estimate=pl.CostEstimate(
            flops=17_000_000_000, bytes_accessed=60_000_000, transcendentals=0
        ),
        compiler_params=pltpu.CompilerParams(
            collective_id=0, has_side_effects=True, vmem_limit_bytes=63 << 20
        ),
    )(
        *late[:6],
        *[value.reshape(2, 2, 64, 2 * D - X_COLS) for value in late[6:]],
        wo.reshape(4, 2, 2, 2, 32, D),
        small,
        dq,
        dkv,
        seen,
        wqkv,
        joint,
        stem,
        grad,
        gain,
        wskip,
    )


def finish_kernel(count, *refs):
    ins, small, gain = refs[:count], refs[count], refs[count + 1]
    outs, o_small = refs[count + 2 : 2 * count + 2], refs[2 * count + 2]
    held, loads, stores = refs[2 * count + 3 : 3 * count + 3], refs[-2], refs[-1]
    got = [pltpu.make_async_copy(a, b, loads.at[i]) for i, (a, b) in enumerate(zip(ins, held))]
    for copy in got:
        copy.start()
    device = lax.axis_index("rows") * 4 + lax.axis_index("seq")
    o_small[0:1, :] = small[pl.ds(device, 1), :]
    row, lane = device // 4, lax.rem(device, 4) * 32
    values = [gain[pl.ds(row, 1), :], small[pl.ds(32 + row, 1), :], small[pl.ds(40 + row, 1), :]]
    for i, value in enumerate(values):
        o_small[1 + i : 2 + i, :] = pltpu.roll(value, lax.rem(128 - lane, 128), 1)
    put = [pltpu.make_async_copy(a, b, stores.at[i]) for i, (a, b) in enumerate(zip(held, outs))]
    for copy, after in zip(got, put):
        copy.wait()
        after.start()
    for copy in put:
        copy.wait()


def finish(results, small, gain):
    hbm, vm = pl.BlockSpec(memory_space=HBM), pl.BlockSpec(memory_space=VMEM)
    count = len(results)
    return pl.pallas_call(
        functools.partial(finish_kernel, count),
        out_shape=[
            *[jax.ShapeDtypeStruct(a.shape, a.dtype) for a in results],
            jax.ShapeDtypeStruct((8, 128), F32),
        ],
        in_specs=[hbm] * count + [vm] * 2,
        out_specs=[hbm] * count + [vm],
        scratch_shapes=[
            *[pltpu.VMEM(a.shape, a.dtype) for a in results],
            pltpu.SemaphoreType.DMA((count,)),
            pltpu.SemaphoreType.DMA((count,)),
        ],
        name="finish",
        compiler_params=pltpu.CompilerParams(vmem_limit_bytes=63 << 20),
    )(*results, small, gain)


def swap_x(value):
    return lax.ppermute(value, "rows", [(r, r ^ 1) for r in range(8)])


def swap_chip(value):
    return lax.ppermute(value, "seq", [(i, i ^ 2) for i in range(4)])


def body_chips(
    inputs,
    skip_feats,
    seg_ids,
    frame_valid,
    w_skip,
    gain_one,
    w_qkv,
    w_out,
    gain_two,
    w_up,
    b_up,
    w_down,
    b_down,
    cotangent,
):
    here = lax.axis_index("seq")
    c = here % 2
    heads = H // 2
    first, second_in, cot = inputs[0], skip_feats[0], cotangent[0]
    gain_first = jnp.broadcast_to(gain_one.astype(F32), (8, D))
    gain_second = jnp.broadcast_to(gain_two.astype(F32), (8, D))
    stem_out, normed_seen, q, kv, joint = front(first, second_in, w_skip, gain_first, w_qkv)
    attended, attended_t, lse = attend(q, kv, seg_ids, frame_valid, 128, 256, heads)
    bias = lax.dynamic_index_in_dim(b_up.astype(F32).reshape(16, 2, 128), c, 1, keepdims=False)
    output, middle_grad, grad_heads, out_grad, small, *sums = middle(
        attended,
        stem_out,
        w_out,
        gain_second,
        w_up,
        w_down,
        jnp.broadcast_to(bias.reshape(1, -1), (8, 2 * D)),
        jnp.broadcast_to(b_down.astype(F32), (8, D)),
        cot,
    )
    late = []
    for here, away, swap in zip(sums[::2], sums[1::2], (swap_x, swap_chip, swap_chip, swap_x)):
        late += [here, swap(away)]
    dq, dkv, output = attend_back(
        q, kv, grad_heads, attended_t, lse, seg_ids, frame_valid, output, 128, 256, heads
    )
    *results, small_sum, gain_sum = tail(
        late,
        out_grad,
        small,
        dq,
        dkv,
        normed_seen,
        w_qkv,
        joint,
        stem_out,
        middle_grad,
        gain_first,
        w_skip,
    )
    results = finish(results, small_sum, gain_sum)
    input_grad, skip_grad, down_share, up_share, qkv_share, out_share, skip_share, mine = results
    return (
        output[None],
        input_grad[None],
        skip_grad[None],
        skip_share,
        mine[1, :32],
        qkv_share,
        out_share,
        mine[2, :32],
        up_share,
        mine[0],
        down_share,
        mine[3, :32],
    )


def block_scores(q_blk, pos_blk, seg_blk, all_keys, seg_row, valid_row, slopes, score_scale):
    key_pos = jnp.arange(all_keys.shape[0])
    scores = (
        jnp.einsum("qhd,khd->hqk", q_blk, all_keys, preferred_element_type=jnp.float32)
        * score_scale
    )
    distance = jnp.abs(pos_blk[:, None] - key_pos[None, :]).astype(jnp.float32)
    scores = scores - slopes[:, None, None] * distance[None]
    allowed = (seg_blk[:, None] == seg_row[None, :]) & (
        (valid_row[None, :] == 1) | (pos_blk[:, None] == key_pos[None, :])
    )
    return jnp.where(allowed[None], scores, -jnp.inf)


def split_row(packed_row, heads_local):
    length = packed_row.shape[0]
    qkv_rows = packed_row.reshape(length, 3, heads_local, HD)
    return (qkv_rows[:, 0], qkv_rows[:, 1], qkv_rows[:, 2])


def attend_row(packed_row, seg_row, valid_row, slopes, heads_local, block_rows, score_scale):
    length = packed_row.shape[0]
    queries, all_keys, all_values = split_row(packed_row, heads_local)
    count = length // block_rows
    positions = jnp.arange(length)

    def one_block(block_in):
        q_blk, pos_blk, seg_blk = block_in
        scores = block_scores(
            q_blk, pos_blk, seg_blk, all_keys, seg_row, valid_row, slopes, score_scale
        )
        peak = jnp.max(scores, axis=-1, keepdims=True)
        log_total = peak + jnp.log(jnp.sum(jnp.exp(scores - peak), axis=-1, keepdims=True))
        attn_probs = jnp.exp(scores - log_total).astype(jnp.bfloat16)
        attended = jnp.einsum(
            "hqk,khd->qhd", attn_probs, all_values, preferred_element_type=jnp.float32
        )
        return (attended.astype(jnp.bfloat16), log_total[..., 0])

    attended, log_total = lax.map(
        one_block,
        (
            queries.reshape(count, block_rows, heads_local, HD),
            positions.reshape(count, block_rows),
            seg_row.reshape(count, block_rows),
        ),
    )
    return (attended.reshape(length, 1, heads_local * HD), log_total)


def attend_row_back(
    packed_row,
    log_total,
    grad_row,
    seg_row,
    valid_row,
    slopes,
    heads_local,
    block_rows,
    score_scale,
):
    length = packed_row.shape[0]
    queries, all_keys, all_values = split_row(packed_row, heads_local)
    count = length // block_rows
    positions = jnp.arange(length)
    grad_out = grad_row.reshape(count, block_rows, heads_local, HD)

    def one_block(carry, block_in):
        key_grad, value_grad = carry
        q_blk, pos_blk, seg_blk, total_blk, grad_blk = block_in
        scores = block_scores(
            q_blk, pos_blk, seg_blk, all_keys, seg_row, valid_row, slopes, score_scale
        )
        soft = jnp.exp(scores - total_blk[..., None])
        value_grad = value_grad + jnp.einsum(
            "hqk,qhd->khd", soft.astype(jnp.bfloat16), grad_blk, preferred_element_type=jnp.float32
        )
        prob_grad = jnp.einsum(
            "qhd,khd->hqk", grad_blk, all_values, preferred_element_type=jnp.float32
        )
        score_grad = (
            soft * (prob_grad - jnp.sum(soft * prob_grad, axis=-1, keepdims=True))
        ).astype(jnp.bfloat16)
        query_grad = (
            jnp.einsum("hqk,khd->qhd", score_grad, all_keys, preferred_element_type=jnp.float32)
            * score_scale
        )
        key_grad = (
            key_grad
            + jnp.einsum("hqk,qhd->khd", score_grad, q_blk, preferred_element_type=jnp.float32)
            * score_scale
        )
        return ((key_grad, value_grad), query_grad)

    zero_rows = jnp.zeros((length, heads_local, HD), jnp.float32)
    (key_grad, value_grad), query_grad = lax.scan(
        one_block,
        (zero_rows, zero_rows),
        (
            queries.reshape(count, block_rows, heads_local, HD),
            positions.reshape(count, block_rows),
            seg_row.reshape(count, block_rows),
            log_total,
            grad_out,
        ),
    )
    stacked = jnp.stack([query_grad.reshape(length, heads_local, HD), key_grad, value_grad], axis=1)
    return stacked.astype(jnp.bfloat16).reshape(length, 3, 1, heads_local * HD)


def body(
    inputs,
    skip_feats,
    seg_ids,
    frame_valid,
    w_skip,
    gain_one,
    w_qkv,
    w_out,
    gain_two,
    w_up,
    b_up,
    w_down,
    b_down,
    cotangent,
):
    parts = lax.axis_size("seq")
    heads_local = H // parts
    width_local = heads_local * HD
    rows_here = inputs.shape[0]
    frames = inputs.shape[1]
    length = frames * parts
    block_rows = min(512, length)
    score_scale = 1.0 / math.sqrt(HD)
    first_head = lax.axis_index("seq") * heads_local
    slopes = jnp.exp2(-8.0 * (first_head + jnp.arange(heads_local) + 1).astype(jnp.float32) / H)
    gain_first = gain_one.astype(jnp.float32)
    gain_second = gain_two.astype(jnp.float32)
    bias_up = b_up.astype(jnp.float32)
    joined = jnp.concatenate([inputs, skip_feats], axis=-1)
    stem_out = jnp.einsum("rfc,cd->rfd", joined, w_skip, preferred_element_type=jnp.float32)
    unit_one, inverse_one, normed = norm_forward(stem_out, gain_first)
    normed = normed.astype(jnp.bfloat16)
    packed = jnp.einsum("rfd,de->rfe", normed, w_qkv, preferred_element_type=jnp.float32).astype(
        jnp.bfloat16
    )
    packed = packed.reshape(rows_here, frames, 3, parts, width_local)
    by_heads = lax.all_to_all(packed, "seq", split_axis=3, concat_axis=1, tiled=True)

    def forward_row(row_data):
        return attend_row(
            row_data[0], row_data[1], row_data[2], slopes, heads_local, block_rows, score_scale
        )

    attended, log_total = lax.map(forward_row, (by_heads, seg_ids, frame_valid))
    by_frames = lax.all_to_all(attended, "seq", split_axis=1, concat_axis=2, tiled=True)
    mixed_out = by_frames.reshape(rows_here, frames, D)
    middle = stem_out + jnp.einsum(
        "rfd,de->rfe", mixed_out, w_out, preferred_element_type=jnp.float32
    )
    unit_two, inverse_two, second = norm_forward(middle, gain_second)
    second = second.astype(jnp.bfloat16)
    hidden = jnp.einsum("rfd,dk->rfk", second, w_up, preferred_element_type=jnp.float32) + bias_up
    active_full, gelu_back = jax.vjp(gelu_exact, hidden)
    active = active_full.astype(jnp.bfloat16)
    result = (
        middle
        + jnp.einsum("rfk,kd->rfd", active, w_down, preferred_element_type=jnp.float32)
        + b_down.astype(jnp.float32)
    )
    output = result.astype(jnp.bfloat16)
    cot_full = cotangent.astype(jnp.float32)
    down_grad = jnp.einsum("rfk,rfd->kd", active, cotangent, preferred_element_type=jnp.float32)
    bias_down_grad = jnp.sum(cot_full, axis=(0, 1))
    active_grad = jnp.einsum("rfd,kd->rfk", cotangent, w_down, preferred_element_type=jnp.float32)
    hidden_grad = gelu_back(active_grad)[0].astype(jnp.bfloat16)
    up_grad = jnp.einsum("rfd,rfk->dk", second, hidden_grad, preferred_element_type=jnp.float32)
    bias_up_grad = jnp.sum(hidden_grad.astype(jnp.float32), axis=(0, 1))
    second_grad = jnp.einsum("rfk,dk->rfd", hidden_grad, w_up, preferred_element_type=jnp.float32)
    middle_part, gain_two_grad = norm_backward(second_grad, unit_two, inverse_two, gain_second)
    middle_grad = cot_full + middle_part
    middle_low = middle_grad.astype(jnp.bfloat16)
    out_grad = jnp.einsum("rfd,rfe->de", mixed_out, middle_low, preferred_element_type=jnp.float32)
    mixed_grad = jnp.einsum(
        "rfe,de->rfd", middle_low, w_out, preferred_element_type=jnp.float32
    ).astype(jnp.bfloat16)
    grad_heads = lax.all_to_all(
        mixed_grad.reshape(rows_here, frames, parts, width_local),
        "seq",
        split_axis=2,
        concat_axis=1,
        tiled=True,
    )

    def backward_row(row_data):
        return attend_row_back(
            row_data[0],
            row_data[1],
            row_data[2],
            row_data[3],
            row_data[4],
            slopes,
            heads_local,
            block_rows,
            score_scale,
        )

    packed_grad = lax.map(backward_row, (by_heads, log_total, grad_heads, seg_ids, frame_valid))
    packed_back = lax.all_to_all(packed_grad, "seq", split_axis=1, concat_axis=3, tiled=True)
    packed_back = packed_back.reshape(rows_here, frames, 3 * D)
    qkv_grad = jnp.einsum("rfd,rfe->de", normed, packed_back, preferred_element_type=jnp.float32)
    normed_grad = jnp.einsum("rfe,de->rfd", packed_back, w_qkv, preferred_element_type=jnp.float32)
    stem_part, gain_one_grad = norm_backward(normed_grad, unit_one, inverse_one, gain_first)
    stem_low = (middle_grad + stem_part).astype(jnp.bfloat16)
    skip_w_grad = jnp.einsum("rfc,rfd->cd", joined, stem_low, preferred_element_type=jnp.float32)
    joined_grad = jnp.einsum("rfd,cd->rfc", stem_low, w_skip, preferred_element_type=jnp.float32)
    input_grad = joined_grad[..., :D].astype(jnp.bfloat16)
    skip_grad = joined_grad[..., D:].astype(jnp.bfloat16)
    (
        skip_share,
        gain_one_share,
        qkv_share,
        out_share,
        gain_two_share,
        up_share,
        bias_up_share,
        down_share,
        bias_down_share,
    ) = (
        lax.psum_scatter(skip_w_grad, ("rows", "seq"), scatter_dimension=0, tiled=True),
        lax.psum_scatter(gain_one_grad, ("rows", "seq"), scatter_dimension=0, tiled=True),
        lax.psum_scatter(qkv_grad, ("rows", "seq"), scatter_dimension=0, tiled=True),
        lax.psum_scatter(out_grad, ("rows", "seq"), scatter_dimension=0, tiled=True),
        lax.psum_scatter(gain_two_grad, ("rows", "seq"), scatter_dimension=0, tiled=True),
        lax.psum_scatter(up_grad, ("rows", "seq"), scatter_dimension=0, tiled=True),
        lax.psum_scatter(bias_up_grad, ("rows", "seq"), scatter_dimension=0, tiled=True),
        lax.psum_scatter(down_grad, ("rows", "seq"), scatter_dimension=0, tiled=True),
        lax.psum_scatter(bias_down_grad, ("rows", "seq"), scatter_dimension=0, tiled=True),
    )
    return (
        output,
        input_grad,
        skip_grad,
        skip_share,
        gain_one_share,
        qkv_share,
        out_share,
        gain_two_share,
        up_share,
        bias_up_share,
        down_share,
        bias_down_share,
    )


def solution(mesh):
    fits = (mesh.shape["rows"], mesh.shape["seq"]) == (8, 4)
    return jax.shard_map(
        body_chips if fits else body,
        mesh=mesh,
        in_specs=(
            P("rows", "seq", None),
            P("rows", "seq", None),
            P("rows", None),
            P("rows", None),
            P(),
            P(),
            P(),
            P(),
            P(),
            P(),
            P(),
            P(),
            P(),
            P("rows", "seq", None),
        ),
        out_specs=(
            P("rows", "seq", None),
            P("rows", "seq", None),
            P("rows", "seq", None),
            P(("rows", "seq"), None),
            P(("rows", "seq")),
            P(("rows", "seq"), None),
            P(("rows", "seq"), None),
            P(("rows", "seq")),
            P(("rows", "seq"), None),
            P(("rows", "seq")),
            P(("rows", "seq"), None),
            P(("rows", "seq")),
        ),
        check_vma=False,
    )
```

```python
import functools
import math

import jax
import jax.numpy as jnp
from jax import lax
from jax.experimental import pallas as pl
from jax.experimental.pallas import tpu as pltpu
from jax.sharding import PartitionSpec as P

D = 1024
H = 16
HD = 64
MOST = 682

epsilon = 1e-05

F32 = jnp.float32
BF16 = jnp.bfloat16
LOG2E = 1.4426950408889634
ROWS = 32
CHIP = 1024
HALO = 768
FRAMES = 512
HALF = HALO // 2
EDGE = CHIP - HALO
WIDTH = D // 2
SKIPS = 4
SKIP_COLS = D // SKIPS
FAR = 1e30
MESH = pl.DeviceIdType.MESH
VMEM = pltpu.MemorySpace.VMEM
SMEM = pltpu.MemorySpace.SMEM
HBM = pltpu.MemorySpace.HBM


def norm_forward(value, gain_vec):
    center = value - jnp.mean(value, axis=-1, keepdims=True)
    spread = jnp.mean(center * center, axis=-1, keepdims=True)
    inverse = lax.rsqrt(spread + epsilon)
    unit = center * inverse
    return (unit, inverse, unit * gain_vec)


def norm_backward(upstream, unit, inverse, gain_vec):
    scaled = upstream * gain_vec
    gain_grad = jnp.sum(upstream * unit, axis=tuple(range(upstream.ndim - 1)))
    inner = (
        scaled
        - jnp.mean(scaled, axis=-1, keepdims=True)
        - unit * jnp.mean(scaled * unit, axis=-1, keepdims=True)
    )
    return (inverse * inner, gain_grad)


def gelu_exact(value):
    return jax.nn.gelu(value, approximate=False)


def mm(equation, left, right):
    return jnp.einsum(equation, left, right, preferred_element_type=F32)


def dot(left, right):
    return jnp.dot(left, right, preferred_element_type=F32)


def dot_nt(left, right):
    return lax.dot_general(left, right, (((1,), (1,)), ((), ())), preferred_element_type=F32)


def dot_tn(left, right):
    return lax.dot_general(left, right, (((0,), (0,)), ((), ())), preferred_element_type=F32)


class Links:
    def __init__(self, sends, recvs):
        row, col = lax.axis_index("rows"), lax.axis_index("seq")
        self.z, self.x, self.y, self.c = row // 2, row % 2, col // 2, col % 2
        z, x, y, c = self.z, self.x, self.y, self.c
        self.high, self.low = z // 2, z % 2
        self.is_end = z == 3 * self.high
        self.is_inner = z == 1 + self.high
        self.core = (row, y * 2 + 1 - c)
        self.over_y = (row, (1 - y) * 2 + c)
        self.over_x = (z * 2 + 1 - x, col)
        self.over_low = ((self.high * 2 + 1 - self.low) * 2 + x, col)
        self.over_high = (((1 - self.high) * 2 + self.low) * 2 + x, col)
        self.over_mirror = ((3 - z) * 2 + x, col)
        self.sends, self.recvs, self.count, self.started = sends, recvs, 0, []

    def greet(self, near=False):
        barrier = pltpu.get_barrier_semaphore()
        peers = [self.core, self.over_y]
        if not near:
            peers += [self.over_x, self.over_low, self.over_high, self.over_mirror]
        for peer in peers:
            pl.semaphore_signal(barrier, inc=1, device_id=peer, device_id_type=MESH)
        pl.semaphore_wait(barrier, len(peers))

    def reserve(self, number):
        self.count += number
        return self.count - number

    def copy(self, src, dst, at, peer):
        return pltpu.make_async_remote_copy(
            src, dst, self.sends.at[at], self.recvs.at[at], device_id=peer, device_id_type=MESH
        )

    def send(self, src, dst, peer, here=None):
        copy = self.copy(src, dst, self.reserve(1), peer)
        if here is None:
            copy.start()
        else:
            pl.when(here)(copy.start)
        self.started.append((copy, here))
        return copy

    def drain(self):
        assert self.count <= self.sends.shape[0]
        for copy, here in self.started:
            if here is None:
                copy.wait_send()
            else:
                pl.when(here)(copy.wait_send)


def head_columns(wqkv, part, core):
    return wqkv.at[:, pl.ds(pl.multiple_of(D * part + WIDTH * core, WIDTH), WIDTH)]


def front_kernel(*refs):
    first_in, second_in, wskip_in, gain, wqkv_in = refs[:5]
    outs = refs[5:10]
    first, second, wskip, wq, wkv, o_stem, o_seen, o_q, o_kv, o_joint, loads, stores, sends, recvs = refs[10:]
    storing = []

    def store(k, *at):
        src, dst = (o_stem, o_seen, o_q, o_kv, o_joint)[k].at[*at], outs[k].at[*at]
        copy = pltpu.make_async_copy(src, dst, stores.at[len(storing)])
        copy.start()
        storing.append(copy)

    links = Links(sends, recvs)
    y, c = links.y, links.c
    loading = []

    def load(src, dst):
        copy = pltpu.make_async_copy(src, dst, loads.at[len(loading)])
        copy.start()
        loading.append(copy)
        return copy

    got = [load(first_in, first), load(second_in, second), load(wskip_in, wskip)]
    got_wkv = [
        load(head_columns(wqkv_in, 1 + i, c), wkv.at[:, pl.ds(WIDTH * i, WIDTH)]) for i in (0, 1)
    ]
    got_wq = load(head_columns(wqkv_in, 0, c), wq)
    links.greet(near=True)
    for copy in got:
        copy.wait()
    gains = gain[...].astype(F32).reshape(1, D)
    base = jnp.where(y == 0, EDGE, 0) + HALF * c

    def piece(i, chip):
        return 128 * jnp.where(chip == 0, i, 2 - i)

    def send_piece(i):
        at = lax.rem(base + piece(i, y) + FRAMES * c, CHIP)
        there = CHIP + HALF * c + piece(i, y)
        src = o_seen.at[pl.ds(pl.multiple_of(at, 128), 128)]
        dst = o_seen.at[pl.ds(pl.multiple_of(there, 128), 128)]
        return links.send(src, dst, links.over_y)

    pieces, across = [], []
    for turn in range(2):
        at = pl.multiple_of(256 * (1 - c if turn == 0 else c), 256)
        rows = pl.ds(at, 256)
        value = dot(first[rows, :], wskip[:D, :]) + dot(second[rows, :], wskip[D:, :])
        o_stem[rows, :] = value
        center = value - jnp.mean(value, axis=-1, keepdims=True)
        rate = lax.rsqrt(jnp.mean(center * center, axis=-1, keepdims=True) + epsilon)
        o_seen[rows, :] = (center * rate * gains).astype(BF16)
        pieces.append(send_piece(turn))
        there = o_seen.at[pl.ds(pl.multiple_of(FRAMES + at, 256), 256)]
        across.append(links.send(o_seen.at[rows], there, links.core))
    store(0, pl.ds(0, FRAMES))
    for copy in across:
        copy.wait_recv()
    pieces.append(send_piece(2))
    store(1, pl.ds(0, CHIP))
    for copy in (*got_wkv, got_wq):
        copy.wait()

    def own_part(i, _):
        rows = pl.ds(pl.multiple_of(256 * i, 256), 256)
        o_q[rows, :] = dot(o_seen[rows, :], wq[...]).astype(BF16)
        o_kv[rows, :] = dot(o_seen[rows, :], wkv[...]).astype(BF16)
        return 0

    lax.fori_loop(0, 4, own_part, 0)
    store(2, pl.ds(0, CHIP))
    store(3, pl.ds(0, CHIP))
    o_joint[:D, :] = first[...].T
    forward = []

    def far_part(i, core):
        at = pl.multiple_of(CHIP + HALF * core + piece(i, 1 - y), 128)
        rows = pl.ds(at, 128)
        o_kv[rows, :] = dot(o_seen[rows, :], wkv[...]).astype(BF16)

    for i in range(3):
        pieces[i].wait_recv()
        at = pl.multiple_of(CHIP + HALF * c + piece(i, 1 - y), 128)
        rows = o_seen.at[pl.ds(at, 128)]
        forward.append(links.send(rows, rows, links.core))
        if i == 0:
            o_joint[D:, :] = second[...].T
            store(4, pl.ds(0, 2 * D))
        far_part(i, c)
        if i > 0:
            forward[i - 1].wait_recv()
            far_part(i - 1, 1 - c)
    forward[2].wait_recv()
    store(1, pl.ds(CHIP, HALO))
    far_part(2, 1 - c)
    store(3, pl.ds(CHIP, HALO))
    links.drain()
    for copy in storing:
        copy.wait()


def front(first, second, wskip, gain, wqkv):
    hbm, vm = pl.BlockSpec(memory_space=HBM), pl.BlockSpec(memory_space=VMEM)
    low = lambda *shape: pltpu.VMEM(shape, BF16)
    return pl.pallas_call(
        front_kernel,
        out_shape=[
            jax.ShapeDtypeStruct((FRAMES, D), F32),
            jax.ShapeDtypeStruct((CHIP + HALO, D), BF16),
            jax.ShapeDtypeStruct((CHIP, WIDTH), BF16),
            jax.ShapeDtypeStruct((CHIP + HALO, 2 * WIDTH), BF16),
            jax.ShapeDtypeStruct((2 * D, FRAMES), BF16),
        ],
        in_specs=[hbm] * 3 + [vm, hbm],
        out_specs=[hbm] * 5,
        scratch_shapes=[
            low(FRAMES, D),
            low(FRAMES, D),
            low(2 * D, D),
            low(D, WIDTH),
            low(D, 2 * WIDTH),
            pltpu.VMEM((FRAMES, D), F32),
            low(CHIP + HALO, D),
            low(CHIP, WIDTH),
            low(CHIP + HALO, 2 * WIDTH),
            low(2 * D, FRAMES),
            pltpu.SemaphoreType.DMA((6,)),
            pltpu.SemaphoreType.DMA((7,)),
            pltpu.SemaphoreType.DMA((8,)),
            pltpu.SemaphoreType.DMA((8,)),
        ],
        name="front",
        cost_estimate=pl.CostEstimate(
            flops=8_000_000_000, bytes_accessed=24_000_000, transcendentals=0
        ),
        compiler_params=pltpu.CompilerParams(
            collective_id=2, has_side_effects=True, vmem_limit_bytes=63 << 20
        ),
    )(first, second, wskip, gain, wqkv)


class Frames:
    def __init__(self, seg_at, seg, valid, key_code, query_seg):
        here = lax.axis_index("seq")
        self.seg_at = seg_at
        self.own, self.other = FRAMES * here, FRAMES * (here + 1 - 2 * (here % 2))
        self.halo = jnp.where(here // 2 == 0, CHIP, CHIP - HALO)
        self.core = here % 2
        places = [(0, FRAMES, self.own), (FRAMES, FRAMES, self.other), (CHIP, HALO, self.halo)]
        for at, count, frame in places:
            span = pl.ds(pl.multiple_of(frame, 256), count)
            code = jnp.where(valid[0:1, span] == 1, seg[0:1, span], -1).astype(F32)
            key_code[pl.ds(at, count), :] = jnp.broadcast_to(code, (128, count)).T
            if at < CHIP:
                query_seg[:, pl.ds(at, count)] = jnp.broadcast_to(
                    seg[0:1, span].astype(F32), (8, count)
                )

    def frame(self, at):
        late = jnp.where(at < CHIP, self.other - FRAMES, self.halo - CHIP)
        return at + jnp.where(at < FRAMES, self.own, late)

    def meet(self, keys_at, keys, queries_at, queries):
        k, q = self.frame(keys_at), self.frame(queries_at)
        return (self.seg_at[0, k] <= self.seg_at[0, q + queries - 1]) & (
            self.seg_at[0, k + keys - 1] >= self.seg_at[0, q]
        )

    def slope(self, h):
        values = [LOG2E * 2.0 ** (-8.0 * (core * H // 2 + h + 1) / H) for core in (0, 1)]
        return jnp.where(self.core == 0, values[0], values[1])


def set_distances(dist, key_at, query_at, key_code, query_seg):
    keys, queries = dist.shape
    rows = lax.broadcasted_iota(jnp.int32, (keys, queries), 0) + key_at
    cols = lax.broadcasted_iota(jnp.int32, (keys, queries), 1) + query_at
    apart = jnp.abs(rows - cols)
    allowed = (key_code == query_seg) | (apart == 0)
    dist[...] = jnp.where(allowed, apart.astype(F32), FAR)


def wide(code, queries):
    return jnp.concatenate([code] * (queries // 128), axis=1) if queries > 128 else code


def both_heads(ref, pair, queries):
    first = ref[pl.ds(128 * pair, HD), queries]
    second = ref[pl.ds(128 * pair + HD, HD), queries]
    blank = jnp.zeros_like(first)
    return jnp.concatenate(
        [
            jnp.concatenate([first, blank], axis=0),
            jnp.concatenate([blank, second], axis=0),
        ],
        axis=1,
    )


def both_slopes(dist, frames, pair):
    value = dist[...]
    return jnp.concatenate(
        [value * frames.slope(2 * pair), value * frames.slope(2 * pair + 1)], axis=1
    )


def attend_kernel(
    bq,
    bk,
    heads,
    seg_at,
    q_in,
    kv_in,
    seg,
    valid,
    o_out,
    o_outt,
    lse,
    q,
    kv,
    out,
    outt,
    loads,
    stores,
    kcode,
    qseg,
    qt,
    vt,
    dist,
    acc,
    top,
    total,
    heads_q,
    scores,
    probs,
):
    width = heads * HD
    pairs = range(heads // 2)
    c1 = LOG2E / math.sqrt(HD)
    keys, values = pl.ds(0, width), pl.ds(width, width)
    got = [
        pltpu.make_async_copy(q_in, q, loads.at[0]),
        pltpu.make_async_copy(kv_in.at[:, values], kv.at[:, values], loads.at[1]),
        pltpu.make_async_copy(kv_in.at[:, keys], kv.at[:, keys], loads.at[2]),
    ]
    for copy in got:
        copy.start()
    frames = Frames(seg_at, seg, valid, kcode, qseg)
    got[0].wait()
    qt[...] = q[...].T
    got[1].wait()
    vt[...] = kv[:, width:].T
    got[2].wait()

    def results(i):
        rows = pl.ds(pl.multiple_of(i * bq, bq), bq)
        return [
            pltpu.make_async_copy(out.at[rows], o_out.at[rows], stores.at[0, i]),
            pltpu.make_async_copy(outt.at[:, rows], o_outt.at[:, rows], stores.at[1, i]),
        ]

    def q_block(i, _):
        queries = pl.ds(pl.multiple_of(i * bq, bq), bq)
        acc[...] = jnp.zeros_like(acc)
        total[...] = jnp.zeros_like(total)
        top[...] = jnp.full_like(top, -3e38)
        for pair in pairs:
            heads_q[pair] = both_heads(qt, pair, queries)

        def k_block(j, _):
            @pl.when(frames.meet(j * bk, bk, i * bq, bq))
            def _():
                ks = pl.ds(pl.multiple_of(j * bk, bk), bk)
                set_distances(
                    dist,
                    frames.frame(j * bk),
                    frames.frame(i * bq),
                    wide(kcode[ks, :], bq),
                    qseg[0:1, queries],
                )
                for pair in pairs:
                    scores[pair] = dot(kv[ks, pl.ds(128 * pair, 128)], heads_q[pair])
                fades = []
                for pair in pairs:
                    line = pl.ds(pair, 1)
                    score = scores[pair] * c1 - both_slopes(dist, frames, pair)
                    was = top[line, :]
                    now = jnp.maximum(was, jnp.max(score, axis=0, keepdims=True))
                    prob = jnp.exp2(score - now)
                    fade = jnp.exp2(was - now)
                    total[line, :] = total[line, :] * fade + jnp.sum(prob, axis=0, keepdims=True)
                    top[line, :] = now
                    probs[pair] = prob.astype(BF16)
                    fades.append(fade)
                for pair in pairs:
                    value = dot(vt[pl.ds(128 * pair, 128), ks], probs[pair])
                    for e in range(2):
                        at, lanes = pl.ds(128 * pair + HD * e, HD), slice(bq * e, bq * (e + 1))
                        acc[at, :] = (
                            acc[at, :] * fades[pair][:, lanes]
                            + value[HD * e : HD * (e + 1), lanes]
                        )

            return 0

        lax.fori_loop(0, kv.shape[0] // bk, k_block, 0)
        for pair in pairs:
            rate = 1.0 / total[pl.ds(pair, 1), :]
            for e in range(2):
                at = pl.ds(128 * pair + HD * e, HD)
                acc[at, :] = acc[at, :] * rate[:, bq * e : bq * (e + 1)]
        lse[:, pl.ds(pl.multiple_of(2 * i * bq, 2 * bq), 2 * bq)] = top[...] + jnp.log2(total[...])
        out[queries, :] = acc[...].T.astype(BF16)
        outt[:, queries] = acc[...].astype(BF16)
        for copy in results(i):
            copy.start()
        return 0

    count = q.shape[0] // bq
    lax.fori_loop(0, count, q_block, 0)

    def settle(i, _):
        for copy in results(i):
            copy.wait()
        return 0

    lax.fori_loop(0, count, settle, 0)


def attend(q, kv, seg, valid, bq, bk, heads):
    frames = q.shape[0]
    vm, sm, hbm = [pl.BlockSpec(memory_space=m) for m in (VMEM, SMEM, HBM)]
    return pl.pallas_call(
        functools.partial(attend_kernel, bq, bk, heads),
        out_shape=(
            jax.ShapeDtypeStruct((frames, heads * HD), BF16),
            jax.ShapeDtypeStruct((heads * HD, frames), BF16),
            jax.ShapeDtypeStruct((heads // 2, 2 * frames), F32),
        ),
        in_specs=[sm, hbm, hbm, vm, vm],
        out_specs=(hbm, hbm, vm),
        scratch_shapes=[
            pltpu.VMEM(q.shape, BF16),
            pltpu.VMEM(kv.shape, BF16),
            pltpu.VMEM((frames, heads * HD), BF16),
            pltpu.VMEM((heads * HD, frames), BF16),
            pltpu.SemaphoreType.DMA((3,)),
            pltpu.SemaphoreType.DMA((2, frames // bq)),
            pltpu.VMEM((kv.shape[0], 128), F32),
            pltpu.VMEM((8, frames), F32),
            pltpu.VMEM((heads * HD, frames), BF16),
            pltpu.VMEM((heads * HD, kv.shape[0]), BF16),
            pltpu.VMEM((bk, bq), F32),
            pltpu.VMEM((heads * HD, bq), F32),
            pltpu.VMEM((heads // 2, 2 * bq), F32),
            pltpu.VMEM((heads // 2, 2 * bq), F32),
            pltpu.VMEM((heads // 2, 2 * HD, 2 * bq), BF16),
            pltpu.VMEM((heads // 2, bk, 2 * bq), F32),
            pltpu.VMEM((heads // 2, bk, 2 * bq), BF16),
        ],
        name="attend",
        cost_estimate=pl.CostEstimate(
            flops=8_000_000_000, bytes_accessed=8_000_000, transcendentals=4_000_000
        ),
        compiler_params=pltpu.CompilerParams(vmem_limit_bytes=63 << 20),
    )(seg, q, kv, seg, valid)


def attend_back_kernel(
    bq,
    bk,
    heads,
    seg_at,
    q_in,
    kv_in,
    grad_in,
    outt_in,
    lse,
    seg,
    valid,
    passed_in,
    o_dq,
    o_dkv,
    o_passed,
    q,
    kv,
    grad,
    outt,
    passed,
    dq,
    dkv,
    loads,
    stores,
    kcode,
    qseg,
    qt,
    kt,
    gradt,
    delta,
    dist,
    dqt,
    sums,
    heads_q,
    heads_g,
    rows_q,
    rows_g,
    scores,
    prob_grads,
    probs,
    score_grads,
):
    width = heads * HD
    pairs = range(heads // 2)
    c1 = LOG2E / math.sqrt(HD)
    scale = 1.0 / math.sqrt(HD)
    lane = lax.broadcasted_iota(jnp.int32, (bq, 128), 1)
    places = [(q_in, q), (grad_in, grad), (outt_in, outt), (kv_in, kv), (passed_in, passed)]
    got = [pltpu.make_async_copy(a, b, loads.at[i]) for i, (a, b) in enumerate(places)]
    for copy in got:
        copy.start()
    sums[...] = jnp.zeros_like(sums)
    frames = Frames(seg_at, seg, valid, kcode, qseg)
    got[0].wait()
    qt[...] = q[...].T
    got[1].wait()
    gradt[...] = grad[...].T
    got[2].wait()
    got[3].wait()
    kt[...] = kv[:, :width].T
    got[4].wait()
    stored = [pltpu.make_async_copy(passed, o_passed, stores.at[0])]
    stored[0].start()

    def dq_copy(i):
        rows = pl.ds(pl.multiple_of(i * bq, bq), bq)
        return pltpu.make_async_copy(dq.at[rows], o_dq.at[rows], stores.at[1 + i])

    def q_block(i, _):
        qs = pl.multiple_of(i * bq, bq)
        queries = pl.ds(qs, bq)
        dqt[...] = jnp.zeros_like(dqt)
        for pair in pairs:
            at = pl.ds(128 * pair, 128)
            heads_q[pair] = both_heads(qt, pair, queries)
            heads_g[pair] = both_heads(gradt, pair, queries)
            product = outt[at, queries].astype(F32) * gradt[at, queries].astype(F32)
            for e in range(2):
                rows = pl.ds(bq * e, bq)
                keep = (lane < HD) if e == 0 else (lane >= HD)
                for to, ref in ((rows_q, q), (rows_g, grad)):
                    value = ref[queries, at]
                    to[pair, rows, :] = jnp.where(keep, value, jnp.zeros_like(value))
                delta[pl.ds(pair, 1), rows] = jnp.sum(
                    product[HD * e : HD * (e + 1)], axis=0, keepdims=True
                )

        def k_block(j, _):
            @pl.when(frames.meet(j * bk, bk, i * bq, bq))
            def _():
                ks = pl.ds(pl.multiple_of(j * bk, bk), bk)
                set_distances(
                    dist,
                    frames.frame(j * bk),
                    frames.frame(i * bq),
                    wide(kcode[ks, :], bq),
                    qseg[0:1, queries],
                )
                for pair in pairs:
                    scores[pair] = dot(kv[ks, pl.ds(128 * pair, 128)], heads_q[pair])
                    prob_grads[pair] = dot(
                        kv[ks, pl.ds(width + 128 * pair, 128)], heads_g[pair]
                    )
                lines = pl.ds(pl.multiple_of(2 * qs, 2 * bq), 2 * bq)
                for pair in pairs:
                    line = pl.ds(pair, 1)
                    prob = jnp.exp2(
                        scores[pair] * c1 - both_slopes(dist, frames, pair) - lse[line, lines]
                    )
                    probs[pair] = prob.astype(BF16)
                    score_grads[pair] = (prob * (prob_grads[pair] - delta[line, :])).astype(BF16)
                for pair in pairs:
                    at = pl.ds(128 * pair, 128)
                    sums[ks, pl.ds(width + 128 * pair, 128)] += dot(probs[pair], rows_g[pair])
                    sums[ks, at] += dot(score_grads[pair], rows_q[pair])
                    value = dot(kt[at, ks], score_grads[pair])
                    for e in range(2):
                        dqt[pl.ds(128 * pair + HD * e, HD), :] += value[
                            HD * e : HD * (e + 1), bq * e : bq * (e + 1)
                        ]

            return 0

        lax.fori_loop(0, kv.shape[0] // bk, k_block, 0)
        dq[pl.ds(qs, bq), :] = (dqt[...] * scale).T.astype(BF16)
        dq_copy(i).start()
        return 0

    count = q.shape[0] // bq
    lax.fori_loop(0, count, q_block, 0)
    parts = [(CHIP, HALO), (0, FRAMES), (FRAMES, FRAMES)]
    for i, (at, rows) in enumerate(parts):
        part = pl.ds(at, rows)
        dkv[part, :width] = (sums[part, :width] * scale).astype(BF16)
        dkv[part, width:] = sums[part, width:].astype(BF16)
        copy = pltpu.make_async_copy(dkv.at[part], o_dkv.at[part], stores.at[1 + count + i])
        copy.start()
        stored.append(copy)
    for copy in [*stored, *[dq_copy(i) for i in range(count)]]:
        copy.wait()


def attend_back(q, kv, grad, outt, lse, seg, valid, passed, bq, bk, heads):
    vm, sm, hbm = [pl.BlockSpec(memory_space=m) for m in (VMEM, SMEM, HBM)]
    return pl.pallas_call(
        functools.partial(attend_back_kernel, bq, bk, heads),
        out_shape=(
            jax.ShapeDtypeStruct(q.shape, BF16),
            jax.ShapeDtypeStruct(kv.shape, BF16),
            jax.ShapeDtypeStruct(passed.shape, passed.dtype),
        ),
        in_specs=[sm] + [hbm] * 4 + [vm] * 3 + [hbm],
        out_specs=(hbm, hbm, hbm),
        scratch_shapes=[
            pltpu.VMEM(q.shape, BF16),
            pltpu.VMEM(kv.shape, BF16),
            pltpu.VMEM(grad.shape, BF16),
            pltpu.VMEM(outt.shape, BF16),
            pltpu.VMEM(passed.shape, passed.dtype),
            pltpu.VMEM(q.shape, BF16),
            pltpu.VMEM(kv.shape, BF16),
            pltpu.SemaphoreType.DMA((5,)),
            pltpu.SemaphoreType.DMA((4 + q.shape[0] // bq,)),
            pltpu.VMEM((kv.shape[0], 128), F32),
            pltpu.VMEM((8, q.shape[0]), F32),
            pltpu.VMEM((heads * HD, q.shape[0]), BF16),
            pltpu.VMEM((heads * HD, kv.shape[0]), BF16),
            pltpu.VMEM((heads * HD, q.shape[0]), BF16),
            pltpu.VMEM((heads // 2, 2 * bq), F32),
            pltpu.VMEM((bk, bq), F32),
            pltpu.VMEM((heads * HD, bq), F32),
            pltpu.VMEM(kv.shape, F32),
            *[pltpu.VMEM((heads // 2, 2 * HD, 2 * bq), BF16)] * 2,
            *[pltpu.VMEM((heads // 2, 2 * bq, 2 * HD), BF16)] * 2,
            *[pltpu.VMEM((heads // 2, bk, 2 * bq), F32)] * 2,
            *[pltpu.VMEM((heads // 2, bk, 2 * bq), BF16)] * 2,
        ],
        name="attend_back",
        cost_estimate=pl.CostEstimate(
            flops=20_000_000_000, bytes_accessed=16_000_000, transcendentals=4_000_000
        ),
        compiler_params=pltpu.CompilerParams(vmem_limit_bytes=63 << 20),
    )(seg, q, kv, grad, outt, lse, seg, valid, passed)


def add_into(value, other):
    def step(i, _):
        value[i] = value[i] + other[i]
        return 0

    lax.fori_loop(0, value.shape[0], step, 0)


class Unit:
    def __init__(self, links, own, came, sums, y_first, done, straight=False):
        self.links, self.own, self.came, self.sums = links, own, came, sums
        self.y_first, self.done, self.straight = y_first, done, straight

    def add_core(self, r0):
        for k in range(4):
            for i in range(2):
                add_into(self.own.at[k, i], r0.at[k, i])

    def send_first(self):
        n, a = self.links, self.own
        if self.y_first:
            self.first = n.send(a.at[:, :, 1 - n.y], self.came[0], n.over_y)
        else:
            self.first = n.send(a.at[:, 1 - n.x], self.came[0], n.over_x)

    def turn_first(self):
        self.first.wait_recv()
        n, a, b = self.links, self.own, self.came[0]
        for k in range(4):
            add_into(a.at[k, :, n.y] if self.y_first else a.at[k, n.x], b.at[k])
        if self.y_first:
            self.second = n.send(a.at[:, 1 - n.x, n.y], self.came[1], n.over_x)
        else:
            self.second = n.send(a.at[:, n.x, 1 - n.y], self.came[1], n.over_y)

    def chip(self, at):
        return self.own.at[at, self.links.x, self.links.y]

    def turn_second(self):
        self.second.wait_recv()
        self.after_second()

    def after_second(self):
        n, to = self.links, self.came[2]
        add_into(self.chip(slice(None)), self.came[1])
        if self.straight:
            low, high = 1 - n.low, 1 - n.high
            places = [(2 * n.high + low, n.over_low), (2 * high + n.low, n.over_high), (3 - n.z, n.over_mirror)]
            self.third = [n.send(self.chip(p), to.at[j], peer) for j, (p, peer) in enumerate(places)]
        else:
            part = self.chip(pl.ds(1 - n.high, 3))
            self.third = n.send(part, to.at[pl.ds(0, 3)], n.over_low, n.is_end)

    def turn_third(self):
        n = self.links

        @pl.when(n.is_inner)
        def _():
            self.third.wait_recv()
            add_into(self.chip(pl.ds(1 - n.high, 3)), self.came[2].at[pl.ds(0, 3)])

        part = self.chip(pl.ds(2 - 2 * n.high, 2))
        self.fourth = n.send(part, self.came[2].at[pl.ds(3, 2)], n.over_mirror, n.is_inner)

    def turn_fourth(self):
        n = self.links

        @pl.when(n.is_inner)
        def _():
            self.fourth.wait_recv()
            add_into(self.chip(pl.ds(2 * n.high, 2)), self.came[2].at[pl.ds(3, 2)])

        self.fifth = n.send(self.chip(3 * n.high), self.came[2].at[5], n.over_low, n.is_inner)

    def finish(self):
        n = self.links
        if self.straight:
            for copy in self.third:
                copy.wait_recv()
            value = self.chip(n.z)[...].astype(F32)
            for j in range(3):
                value = value + self.came[2][j].astype(F32)
            self.done(value)
            return
        self.sums[...] = self.chip(n.z)[...].astype(F32)

        @pl.when(n.is_end)
        def _():
            self.fifth.wait_recv()
            self.sums[...] += self.came[2][5].astype(F32)

        self.done(self.sums[...])


class LowUnit(Unit):
    def send_first(self):
        n = self.links
        self.first = n.send(self.own.at[:, 1 - n.low], self.came[0], n.over_low)

    def turn_first(self):
        self.first.wait_recv()
        n = self.links
        for k in range(2):
            for i in range(2):
                add_into(self.own.at[k, n.low, i], self.came[0].at[k, i])
        self.second = n.send(self.own.at[:, n.low, 1 - n.x], self.came[1], n.over_x)

    def turn_second(self):
        self.second.wait_recv()
        n = self.links
        for k in range(2):
            add_into(self.own.at[k, n.low, n.x], self.came[1].at[k])
        self.third = n.send(self.own.at[:, n.low, n.x, 1 - n.y], self.came[2], n.over_y)

    def turn_third(self):
        self.third.wait_recv()
        n = self.links
        add_into(self.own.at[:, n.low, n.x, n.y], self.came[2])
        self.fourth = n.send(self.own.at[1 - n.high, n.low, n.x, n.y], self.came[3], n.over_high)

    def finish(self):
        self.fourth.wait_recv()
        n = self.links
        value = self.own[n.high, n.low, n.x, n.y].astype(F32)
        self.done(value + self.came[3][...].astype(F32))


class HighUnit:
    def __init__(self, links, own, came, done):
        self.links, self.own, self.came, self.done = links, own, came, done

    def begin(self, *loads):
        for copy in loads:
            copy.wait()
        n = self.links
        for k in range(2):
            for i in range(2):
                add_into(self.own.at[k, i], self.came[0].at[k, i])
        self.second = n.send(self.own.at[:, 1 - n.x], self.came[1], n.over_x)

    def turn_second(self):
        self.second.wait_recv()
        n = self.links
        for k in range(2):
            add_into(self.own.at[k, n.x], self.came[1].at[k])
        self.third = n.send(self.own.at[:, n.x, 1 - n.y], self.came[2], n.over_y)

    def turn_third(self):
        self.third.wait_recv()
        n = self.links
        add_into(self.own.at[:, n.x, n.y], self.came[2])
        self.fourth = n.send(self.own.at[1 - n.high, n.x, n.y], self.came[3], n.over_high)

    def finish(self):
        self.fourth.wait_recv()
        n = self.links
        self.done(self.own[n.high, n.x, n.y].astype(F32) + self.came[3][...].astype(F32))


class LateUnit(Unit):
    def chip(self, at):
        return self.own.at[at]

    def begin(self, *loads):
        for copy in loads:
            copy.wait()
        self.after_second()


class PairUnit:
    def __init__(self, links, own, came, over_x, done):
        self.links, self.own, self.came, self.done = links, own, came, done
        self.at, self.peer = (links.x, links.over_x) if over_x else (links.y, links.over_y)

    def begin(self, *loads):
        for copy in loads:
            copy.wait()
        for k in range(2):
            add_into(self.own.at[k], self.came[0].at[k])
        self.third = self.links.send(self.own.at[:, 1 - self.at], self.came[1], self.peer)

    def turn_third(self):
        n = self.links
        self.third.wait_recv()
        for k in range(2):
            value = self.own.at[k, self.at]
            value[...] = value[...] + self.came[1][k]
        self.fourth = n.send(self.own.at[1 - n.high, self.at], self.came[2], n.over_high)

    def finish(self):
        self.fourth.wait_recv()
        value = self.own[self.links.high, self.at].astype(F32)
        self.done(value + self.came[2][...].astype(F32))


class Small:
    def __init__(self, links, steps, into, done):
        self.links, self.steps, self.into, self.done, self.at = links, steps, into, done, 0
        self.stages = [links.core, links.over_y, links.over_x, links.over_low, links.over_high]

    def send(self):
        self.flying = self.links.send(
            self.steps.at[self.at], self.into.at[self.at], self.stages[self.at]
        )

    def turn(self):
        self.flying.wait_recv()
        value = self.steps[self.at] + self.into[self.at]
        self.at += 1
        if self.at == len(self.stages):
            self.done(value)
        else:
            self.steps[self.at] = value
            self.send()


STEPS = 8
STEP = 256
P_COLS = 640
X_STEPS = 6
X_COLS = STEP * X_STEPS
UP_BLOCKS = [2 * i + j for i in (0, 2, 3, 5, 6, 7, 1, 4) for j in (0, 1)]


def middle_kernel(*refs):
    (
        att_in_hbm,
        stem_in,
        wout_in,
        gain,
        up_hbm,
        down_hbm,
        bias_up,
        bias_down,
        cot_in,
    ) = refs[:9]
    o_out, o_grad, o_heads, o_small = refs[9:13]
    o_p, o_p_away, o_q, o_q_away, o_x, o_x_away, o_z, o_z_away, o_wo, o_wo_away = refs[13:23]
    (
        att,
        att_came,
        stem,
        wout,
        ups,
        downs,
        cot,
        second,
        second_t,
        unit,
        inverse,
        active,
        hidden_grad,
        out_sum,
        grad_sum,
        low,
        swap_out,
        swap_in,
        p_send,
        p_keep,
        p_came,
        q_send,
        q_keep,
        q_came,
        x_send,
        x_keep,
        x_came,
        z_send,
        z_keep,
        z_came,
        biases,
        loads,
        sends,
        recvs,
    ) = refs[23:]
    links = Links(sends, recvs)
    x, y, c = links.x, links.y, links.c
    loading = []

    def load(src, dst):
        copy = pltpu.make_async_copy(src, dst, loads.at[len(loading)])
        copy.start()
        loading.append(copy)
        return copy

    own, other = pl.ds(0, FRAMES), pl.ds(FRAMES, FRAMES)
    got_att = load(att_in_hbm.at[own], att)
    got_wout = load(wout_in, wout)
    got_stem = load(stem_in, stem)
    got_cot = load(cot_in, cot.at[own])
    got_ups, got_downs = [], []
    for i in range(STEPS):
        for j in range(2):
            at = pl.multiple_of(128 * (4 * i + 2 * j + c), 128)
            part = pl.ds(128 * j, 128)
            got_ups.append(load(up_hbm.at[:, pl.ds(at, 128)], ups.at[i, :, part]))
            got_downs.append(load(down_hbm.at[pl.ds(at, 128), :], downs.at[i, part, :]))
    links.greet()
    att_core = links.send(att_in_hbm.at[other], att_came, links.core)
    cot_core = links.send(cot_in, cot.at[other], links.core)
    mine = pl.ds(pl.multiple_of(WIDTH * c, WIDTH), WIDTH)
    theirs = pl.ds(pl.multiple_of(WIDTH * (1 - c), WIDTH), WIDTH)

    got_att.wait()
    got_wout.wait()
    got_stem.wait()
    att_core.wait_recv()
    gains = gain[...].astype(F32).reshape(1, D)
    second_core = []
    for part in range(2):
        rows = pl.ds(256 * part, 256)
        value = stem[rows, :] + dot(att[rows, :], wout[mine, :]) + dot(att_came[rows, :], wout[theirs, :])
        stem[rows, :] = value
        center = value - jnp.mean(value, axis=-1, keepdims=True)
        rate = lax.rsqrt(jnp.mean(center * center, axis=-1, keepdims=True) + epsilon)
        normal = center * rate
        unit[rows, :] = normal
        inverse[rows, :] = jnp.broadcast_to(rate, (256, 128))
        second[rows, :] = (normal * gains).astype(BF16)
        second_core.append(
            links.send(second.at[rows], second.at[pl.ds(FRAMES + 256 * part, 256)], links.core)
        )
    second_t[:, :FRAMES] = second[own, :].T
    biases[...] = bias_up[...].astype(F32)
    out_sum[...] = jnp.zeros_like(out_sum)
    grad_sum[...] = jnp.zeros_like(grad_sum)
    o_small[...] = jnp.zeros_like(o_small)
    for copy in [got_cot, *got_ups, *got_downs]:
        copy.wait()
    cot_core.wait_recv()
    for copy in second_core:
        copy.wait_recv()
    second_t[:, FRAMES:] = second[other, :].T

    p_at, q_at, x_at, z_at = [links.reserve(k) for k in (STEPS, 4, X_STEPS, STEPS - X_STEPS)]

    def p_copy(i):
        return links.copy(p_send.at[i], p_came.at[i], p_at + i, links.over_y)

    def q_copy(i):
        return links.copy(q_send.at[i], q_came.at[i], q_at + i, links.over_low)

    def x_copy(i):
        return links.copy(x_send.at[i], x_came.at[i], x_at + i, links.over_x)

    def z_copy(i):
        return links.copy(z_send.at[i], z_came.at[i], z_at + i, links.over_low)

    def feed_step(i, _):
        up, down = ups[i], downs[i]
        bias = jnp.concatenate([biases[pl.ds(4 * i + 2 * j + c, 1), :] for j in (0, 1)], axis=1)
        total = jnp.zeros((1, STEP), F32)
        for half in (own, other):
            hidden = dot(second[half, :], up) + bias
            active_grad = dot_nt(cot[half, :], down)
            share = 0.5 + 0.5 * lax.erf(hidden * math.sqrt(0.5))
            slope = share + hidden * (
                jnp.exp(-0.5 * hidden * hidden) * (1.0 / math.sqrt(2.0 * math.pi))
            )
            a = (hidden * share).astype(BF16)
            g = (active_grad * slope).astype(BF16)
            active[half, :] = a
            hidden_grad[half, :] = g
            total = total + jnp.sum(g.astype(F32), axis=0, keepdims=True)
            out_sum[half, :] += dot(a, down)
            grad_sum[half, :] += dot_nt(g, up)
        for j in range(2):
            o_small[pl.ds(4 * i + 2 * j + c, 1), :] = total[:, 128 * j : 128 * (j + 1)]
        value = dot_tn(active[...], cot[...]).astype(BF16)
        p_send[i] = jnp.where(y == 0, value[128:, :P_COLS], value[:128, :P_COLS])
        p_keep[i] = jnp.where(y == 0, value[:128, :P_COLS], value[128:, :P_COLS])
        p_copy(i).start()
        stays = lax.rem(i // 2, 2) == links.low
        slot = 2 * (i // 4) + lax.rem(i, 2)
        rest = value[:, P_COLS:].reshape(2, 128, D - P_COLS)

        @pl.when(stays)
        def _():
            q_keep[slot] = rest

        @pl.when(jnp.logical_not(stays))
        def _():
            q_send[slot] = rest
            q_copy(slot).start()

        value = dot(second_t[...], hidden_grad[...]).astype(BF16)

        over_z = (lax.rem(i, 3) == 1) & (i < 6)

        @pl.when(jnp.logical_not(over_z))
        def _():
            j = i - jnp.where(i > 1, 1, 0) - jnp.where(i > 4, 1, 0)
            for k in range(4):
                first, last = value[256 * k : 256 * k + 128], value[256 * k + 128 : 256 * (k + 1)]
                x_send[j, k] = jnp.where(x == 0, last, first)
                x_keep[j, k] = jnp.where(x == 0, first, last)
            x_copy(j).start()

        @pl.when(over_z)
        def _():
            j = i // 4
            for k in range(2):
                first, last = value[512 * k : 512 * k + 256], value[512 * k + 256 : 512 * (k + 1)]
                z_send[j, k] = jnp.where(links.low == 0, last, first)
                z_keep[j, k] = jnp.where(links.low == 0, first, last)
            z_copy(j).start()

        return 0

    lax.fori_loop(0, STEPS, feed_step, 0)

    swap_out[0] = grad_sum[other, :].astype(BF16)
    grad_core = links.send(swap_out.at[0], swap_in.at[0], links.core)
    swap_out[1] = out_sum[other, :].astype(BF16)
    out_core = links.send(swap_out.at[1], swap_in.at[1], links.core)
    grad_core.wait_recv()

    def norm_rows(i, totals):
        rows = pl.ds(pl.multiple_of(128 * i, 128), 128)
        upstream = grad_sum[rows, :] + swap_in[0, rows, :].astype(F32)
        normal = unit[rows, :]
        scaled = upstream * gains
        inner = (
            scaled
            - jnp.mean(scaled, axis=-1, keepdims=True)
            - normal * jnp.mean(scaled * normal, axis=-1, keepdims=True)
        )
        value = cot[rows, :].astype(F32)
        grad = value + inverse[rows, 0:1] * inner
        o_grad[rows, :] = grad
        low[rows, :] = grad.astype(BF16)
        return (
            totals[0] + jnp.sum(upstream * normal, axis=0, keepdims=True),
            totals[1] + jnp.sum(value, axis=0, keepdims=True),
        )

    zero = jnp.zeros((1, D), F32)
    totals = lax.fori_loop(0, 4, norm_rows, (zero, zero))
    for k, value in enumerate(totals):
        for j in range(8):
            o_small[pl.ds(32 + 8 * k + j, 1), :] = value[:, 128 * j : 128 * (j + 1)]
    swap_out[2, :, :WIDTH] = dot_nt(low[...], wout[theirs, :]).astype(BF16)
    heads_core = links.send(
        swap_out.at[2, :, pl.ds(0, WIDTH)], swap_in.at[2, :, pl.ds(0, WIDTH)], links.core
    )
    o_heads[own, :] = dot_nt(low[...], wout[mine, :]).astype(BF16)

    def out_grad(high, value):
        value = value.astype(BF16)
        for low_bit in range(2):
            for i in range(2):
                for j in range(2):
                    at = 256 * low_bit + 128 * i + 64 * j
                    first, last = value[at : at + 32], value[at + 32 : at + 64]
                    rows = pl.multiple_of(256 * high + at // 2, 32)
                    second_t[pl.ds(rows, 32), :] = jnp.where(c == 0, first, last)
                    second_t[pl.ds(FRAMES + rows, 32), :] = jnp.where(c == 0, last, first)

    out_grad(c, dot_tn(att[...], low[...]))
    out_grad(1 - c, dot_tn(att_came[...], low[...]))
    wo_core = links.send(second_t.at[other], second.at[other], links.core)
    out_core.wait_recv()

    def out_rows(i, _):
        rows = pl.ds(pl.multiple_of(128 * i, 128), 128)
        o_out[rows, :] = (
            stem[rows, :]
            + (out_sum[rows, :] + swap_in[1, rows, :].astype(F32))
            + bias_down[...].astype(F32).reshape(1, D)
        ).astype(BF16)
        return 0

    lax.fori_loop(0, 4, out_rows, 0)
    heads_core.wait_recv()
    o_heads[other, :] = swap_in[2, :, :WIDTH]

    def add_p(i, _):
        p_copy(i).wait()
        value = p_keep[i] + p_came[i]
        stays = lax.rem(i, 2) == x

        @pl.when(stays)
        def _():
            o_p[i // 2] = value

        @pl.when(jnp.logical_not(stays))
        def _():
            o_p_away[i // 2] = value

        return 0

    def add_q(i, _):
        q_copy(i).wait()
        o_q[i // 2, lax.rem(i, 2)] = q_keep[i, y] + q_came[i, y]
        o_q_away[i // 2, lax.rem(i, 2)] = q_keep[i, 1 - y] + q_came[i, 1 - y]
        return 0

    def columns(i):
        return pl.ds(pl.multiple_of(STEP * i, STEP), STEP)

    def add_x(i, _):
        x_copy(i).wait()
        for k in range(4):
            value = x_keep[i, k] + x_came[i, k]
            o_x[k, :, columns(i)] = jnp.where(y == 0, value[:64], value[64:])
            o_x_away[k, :, columns(i)] = jnp.where(y == 0, value[64:], value[:64])
        return 0

    def add_z(i, _):
        z_copy(i).wait()
        for k in range(2):
            value = z_keep[i, k] + z_came[i, k]
            o_z[k, :, columns(i)] = jnp.where(x == 0, value[:128], value[128:])
            o_z_away[k, :, columns(i)] = jnp.where(x == 0, value[128:], value[:128])
        return 0

    wo_core.wait_recv()
    for high in range(2):
        for i in range(2):
            for j in range(2):
                for out, low_bit in ((o_wo, links.low), (o_wo_away, 1 - links.low)):
                    at = 256 * high + 128 * low_bit + 64 * i + 32 * j
                    rows = pl.ds(pl.multiple_of(at, 32), 32)
                    came = pl.ds(pl.multiple_of(FRAMES + at, 32), 32)
                    out[high, i, j] = second_t[rows, :] + second[came, :]
    lax.fori_loop(0, STEPS, add_p, 0)
    lax.fori_loop(0, 4, add_q, 0)
    lax.fori_loop(0, X_STEPS, add_x, 0)
    lax.fori_loop(0, STEPS - X_STEPS, add_z, 0)
    links.drain()


def middle(att, stem, wout, gain, w_up, w_down, bias_up, bias_down, cot):
    hbm, vm = pl.BlockSpec(memory_space=HBM), pl.BlockSpec(memory_space=VMEM)
    low = lambda *shape: pltpu.VMEM(shape, BF16)
    full = lambda *shape: pltpu.VMEM(shape, F32)
    copies = 29
    return pl.pallas_call(
        middle_kernel,
        out_shape=[
            jax.ShapeDtypeStruct((FRAMES, D), BF16),
            jax.ShapeDtypeStruct((FRAMES, D), F32),
            jax.ShapeDtypeStruct((CHIP, WIDTH), BF16),
            jax.ShapeDtypeStruct((48, 128), F32),
            *[jax.ShapeDtypeStruct((4, 128, P_COLS), BF16)] * 2,
            *[jax.ShapeDtypeStruct((2, 2, 128, D - P_COLS), BF16)] * 2,
            *[jax.ShapeDtypeStruct((4, 64, X_COLS), BF16)] * 2,
            *[jax.ShapeDtypeStruct((2, 128, 2 * D - X_COLS), BF16)] * 2,
            *[jax.ShapeDtypeStruct((2, 2, 2, ROWS, D), BF16)] * 2,
        ],
        in_specs=[hbm] * 3 + [vm] + [hbm] * 2 + [vm] * 2 + [hbm],
        out_specs=[vm] * 14,
        scratch_shapes=[
            low(FRAMES, WIDTH),
            low(FRAMES, WIDTH),
            full(FRAMES, D),
            low(D, D),
            low(STEPS, D, STEP),
            low(STEPS, STEP, D),
            low(CHIP, D),
            low(CHIP, D),
            low(D, CHIP),
            full(FRAMES, D),
            full(FRAMES, 128),
            low(CHIP, STEP),
            low(CHIP, STEP),
            full(CHIP, D),
            full(CHIP, D),
            low(FRAMES, D),
            low(3, FRAMES, D),
            low(3, FRAMES, D),
            *[low(STEPS, 128, P_COLS)] * 3,
            *[low(4, 2, 128, D - P_COLS)] * 3,
            *[low(X_STEPS, 4, 128, STEP)] * 3,
            *[low(STEPS - X_STEPS, 2, 256, STEP)] * 3,
            full(32, 128),
            pltpu.SemaphoreType.DMA((4 + 4 * STEPS,)),
            pltpu.SemaphoreType.DMA((copies,)),
            pltpu.SemaphoreType.DMA((copies,)),
        ],
        name="middle",
        cost_estimate=pl.CostEstimate(
            flops=28_000_000_000, bytes_accessed=40_000_000, transcendentals=4_000_000
        ),
        compiler_params=pltpu.CompilerParams(
            collective_id=1, has_side_effects=True, vmem_limit_bytes=63 << 20
        ),
    )(att, stem, wout, gain, w_up, w_down, bias_up, bias_down, cot)


def tail_kernel(*refs):
    (
        p_in,
        p_came,
        q_in,
        q_came,
        x_in,
        x_came,
        z_in,
        z_came,
        wo_in,
        wo_came,
        small_in,
        dq_in,
        dkv_in,
        seen_in,
        wqkv_in,
        joint_in,
        stem_in,
        grad_in,
        gain,
        wskip_in,
    ) = refs[:20]
    o_in, o_skip, o_down, o_up, o_qkv, o_wo, o_wskip, o_small, o_gain = refs[20:29]
    (
        dq,
        dkv,
        wide_buf,
        wq,
        wkv,
        joint,
        stem,
        grad,
        chip_out,
        chip_in,
        chip_own,
        halo_out,
        halo_in,
        halo_sum,
        halo,
        low,
        low_own,
        low_r1,
        low_r2,
        low_r3,
        low_r4,
        join_low,
        p_own,
        p_r2,
        p_r3,
        q_own,
        q_r2,
        q_r3,
        q_r4,
        x_own,
        x_r2,
        x_r3,
        z_own,
        z_r2,
        z_r3,
        z_r4,
        up_out,
        up_in_last,
        unit_own,
        unit_r1,
        unit_r2,
        unit_r3,
        wo_own,
        wo_r1,
        wo_r2,
        wo_r3,
        wo_r4,
        join_out,
        skip_own,
        skip_out,
        skip_r0,
        skip_r1,
        skip_r2,
        skip_r3,
        sums,
        small_steps,
        small_into,
        gain_steps,
        gain_into,
        loads,
        sends,
        recvs,
    ) = refs[29:]
    links = Links(sends, recvs)
    y, c = links.y, links.c
    loading = []

    def load(src, dst):
        copy = pltpu.make_async_copy(src, dst, loads.at[len(loading)])
        copy.start()
        loading.append(copy)
        return copy

    seen = wide_buf.at[pl.ds(0, CHIP + HALO)]
    far, near = pl.ds(CHIP, HALO), pl.ds(0, CHIP)
    got_wkv = [load(head_columns(wqkv_in, 1 + i, c), wkv.at[:, pl.ds(WIDTH * i, WIDTH)]) for i in (0, 1)]
    got_far = load(dkv_in.at[far], dkv.at[far])
    links.greet()
    got_wo = [load(wo_in, wo_own), load(wo_came, wo_r1)]
    got_dq = load(dq_in, dq)
    got_near = load(dkv_in.at[near], dkv.at[near])
    got_seen = load(seen_in, seen)
    got_small = load(small_in, small_steps.at[0])
    got_p = [
        [
            load(p_in.at[:, pl.ds(64 * i, 64)], p_own.at[i]),
            load(p_came.at[:, pl.ds(64 * i, 64)], p_r2.at[i]),
        ]
        for i in range(2)
    ]
    got_x = []
    for i, core in enumerate((1 - c, c)):
        rows = pl.ds(pl.multiple_of(32 * core, 32), 32)
        got_x.append([load(x_in.at[:, rows], x_own.at[i]), load(x_came.at[:, rows], x_r2.at[i])])
    got_q = [load(q_in, q_own), load(q_came, q_r2)]
    got_z = [load(z_in, z_own), load(z_came, z_r2)]
    got_wq = load(head_columns(wqkv_in, 0, c), wq)
    got_stem = load(stem_in, stem)
    got_grad = load(grad_in, grad)
    got_joint = load(joint_in, joint)
    halo[pl.ds(0, EDGE), :] = jnp.zeros((EDGE, D), BF16)
    halo[pl.ds(EDGE + HALO, EDGE), :] = jnp.zeros((EDGE, D), BF16)

    def to_down(i):
        def done(value):
            o_down[pl.ds(64 * i, 64), pl.ds(0, P_COLS)] = value

        return done

    def to_down_rest(value):
        o_down[:, pl.ds(P_COLS, D - P_COLS)] = value

    def put_up(b, core, value):
        o_up[:, pl.ds(pl.multiple_of(256 * b + 128 * core, 128), 128)] = value

    def pass_up(at, value):
        part = pl.ds(at, value.shape[1])
        up_out[:, part] = value
        up_last.append(links.send(up_out.at[:, part], up_in_last.at[:, part], links.core))

    def to_up_other(value):
        pass_up(0, value)

    def to_up_mine(value):
        for t in range(X_COLS // 128):
            put_up(UP_BLOCKS[t], c, value[:, 128 * t : 128 * (t + 1)])

    def to_up_rest(value):
        pass_up(X_COLS, jnp.where(c == 0, value[32:], value[:32]))
        mine = jnp.where(c == 0, value[:32], value[32:])
        for t in range(X_COLS // 128, 16):
            at = 128 * t - X_COLS
            put_up(UP_BLOCKS[t], c, mine[:, at : at + 128])

    def take_up():
        for copy in up_last:
            copy.wait_recv()
        for t in range(16):
            put_up(UP_BLOCKS[t], 1 - c, up_in_last[:, 128 * t : 128 * (t + 1)])

    up_last = []

    def room(rows, cols):
        return sums.at[pl.ds(0, rows), pl.ds(0, cols)]

    p0, p1 = [
        LateUnit(
            links, p_own.at[i], (None, p_r2.at[i], p_r3.at[i]), room(64, P_COLS), True, to_down(i)
        )
        for i in range(2)
    ]
    x0, x1 = [
        LateUnit(
            links, x_own.at[i], (None, x_r2.at[i], x_r3.at[i]), room(32, X_COLS), False, done
        )
        for i, done in enumerate((to_up_other, to_up_mine))
    ]
    rest_q = PairUnit(links, q_own, (q_r2, q_r3, q_r4), True, to_down_rest)
    rest_z = PairUnit(links, z_own, (z_r2, z_r3, z_r4), False, to_up_rest)

    def to_wo(value):
        o_wo[...] = value

    def to_qkv(i):
        def done(value):
            o_qkv[:, pl.ds(D * i, D)] = value

        return done

    def to_wskip(q, half):
        def done(value):
            o_wskip[pl.ds(ROWS * half, ROWS), pl.ds(SKIP_COLS * q, SKIP_COLS)] = value

        return done

    def unit(k, y_first, done):
        came = (unit_r1.at[k], unit_r2.at[k], unit_r3.at[k])
        return Unit(links, unit_own.at[k], came, room(ROWS, D), y_first, done)

    wo = HighUnit(links, wo_own, (wo_r1, wo_r2, wo_r3, wo_r4), to_wo)
    unit_q, unit_v = unit(0, False, to_qkv(0)), unit(1, True, to_qkv(2))
    unit_k = LowUnit(links, low_own, (low_r1, low_r2, low_r3, low_r4), None, False, to_qkv(1))

    def skip_unit(k, y_first, done):
        came = (skip_r1.at[k], skip_r2.at[k], skip_r3.at[k])
        return Unit(links, skip_own.at[k], came, None, y_first, done, straight=True)

    skips = [
        [skip_unit(2 * q + half, half == 0, to_wskip(q, half)) for half in range(2)]
        for q in range(SKIPS)
    ]

    def to_small(value):
        o_small[...] = value

    def to_gain(value):
        o_gain[...] = value

    small = Small(links, small_steps, small_into, to_small)
    gain_sum = Small(links, gain_steps, gain_into, to_gain)

    for copy in (*got_wkv, got_far):
        copy.wait()

    def halo_part(core):
        at = pl.multiple_of(CHIP + HALF * core, 128)
        return dot_nt(dkv[pl.ds(at, HALF), :], wkv[...])

    halo_out[...] = halo_part(1 - c).astype(BF16)
    halo_core = links.send(halo_out, halo_in, links.core)
    mine = halo_part(c)
    halo_core.wait_recv()
    halo_sum[...] = (mine + halo_in[...].astype(F32)).astype(BF16)
    part_at = pl.ds(pl.multiple_of(EDGE + HALF * c, 128), HALF)
    part = halo.at[part_at]
    halo_y = links.send(halo_sum, part, links.over_y)
    got_near.wait()
    got_seen.wait()
    columns = pl.ds(pl.multiple_of(WIDTH * c, WIDTH), WIDTH)

    def place(k, i, value):
        value = value.astype(BF16)
        for j in range(2):
            for m in range(2):
                at = 128 * j + 64 * m
                first, second = value[at : at + 32], value[at + 32 : at + 64]
                mine, theirs = jnp.where(c == 0, first, second), jnp.where(c == 0, second, first)
                if k == 1:
                    low_own[i // 2, i % 2, j, m, :, columns] = mine
                else:
                    unit_own[k // 2, i, j, m, :, columns] = mine
                if k == 1:
                    join_low[i // 2, i % 2, j, m] = theirs
                else:
                    join_out[k // 2, i, j, m] = theirs

    def join(k):
        if k == 1:
            return links.send(join_low, low_own.at[:, :, :, :, :, columns], links.core)
        there = unit_own.at[k // 2, :, :, :, :, columns]
        return links.send(join_out.at[k // 2], there, links.core)

    def kv_rows(i, _):
        value = dot(seen[:, pl.ds(pl.multiple_of(256 * i, 256), 256)].T, dkv[...])
        place(1, i, value[:, :WIDTH])
        place(2, i, value[:, WIDTH:])
        return 0

    def q_rows(i, _):
        place(0, i, dot(seen[near, pl.ds(pl.multiple_of(256 * i, 256), 256)].T, dq[...]))
        return 0

    def chip_part(at):
        rows = pl.ds(at, 256)
        return dot_nt(dq[rows, :], wq[...]) + dot_nt(dkv[rows, :], wkv[...])

    def other_frames(i, _):
        at = pl.multiple_of(256 * i, 256)
        chip_out[pl.ds(at, 256), :] = chip_part(FRAMES + at).astype(BF16)
        return 0

    def own_frames(i, _):
        at = pl.multiple_of(256 * i, 256)
        chip_own[pl.ds(at, 256), :] = chip_part(at)
        return 0

    gains = gain[...].astype(F32).reshape(1, D)

    def norm_rows(i, total):
        at = pl.multiple_of(128 * i, 128)
        rows = pl.ds(at, 128)
        upstream = (
            chip_own[rows, :]
            + chip_in[rows, :].astype(F32)
            + halo[pl.ds(pl.multiple_of(at + 256 * (2 * c + y), 128), 128), :].astype(F32)
        )
        value = stem[rows, :]
        center = value - jnp.mean(value, axis=-1, keepdims=True)
        inverse = lax.rsqrt(jnp.mean(center * center, axis=-1, keepdims=True) + epsilon)
        unit_value = center * inverse
        scaled = upstream * gains
        inner = (
            scaled
            - jnp.mean(scaled, axis=-1, keepdims=True)
            - unit_value * jnp.mean(scaled * unit_value, axis=-1, keepdims=True)
        )
        low[rows, :] = (grad[rows, :] + inverse * inner).astype(BF16)
        return total + jnp.sum(upstream * unit_value, axis=0, keepdims=True)

    def skip_part(q):
        def skip_rows(i, _):
            value = dot(
                joint[pl.ds(pl.multiple_of(512 * i, 512), 512), :],
                low[:, SKIP_COLS * q : SKIP_COLS * (q + 1)],
            ).astype(BF16)
            for j in range(2):
                for m in range(2):
                    for half in range(2):
                        at = 256 * j + 128 * m + 32 * half
                        first, second = value[at : at + 32], value[at + 64 : at + 96]
                        skip_own[2 * q + half, i, j, m] = jnp.where(c == 0, first, second)
                        skip_out[2 * q + half, i, j, m] = jnp.where(c == 0, second, first)
            return 0

        lax.fori_loop(0, 4, skip_rows, 0)
        both = pl.ds(2 * q, 2)
        return links.send(skip_out.at[both], skip_r0.at[both], links.core)

    def skip_begin(q, copy):
        copy.wait_recv()
        for half in range(2):
            skips[q][half].add_core(skip_r0.at[2 * q + half])
            skips[q][half].send_first()

    def joined_part(i):
        value = dot_nt(low[...], wide_buf[pl.ds(256 * i, 256), :]).astype(BF16)
        out = o_in if i < 4 else o_skip
        out[:, pl.ds(256 * (i % 4), 256)] = value

    wo.begin(*got_wo)
    lax.fori_loop(0, 4, kv_rows, 0)
    join_v, join_k = join(2), join(1)
    for one, got in ((p0, got_p[0]), (p1, got_p[1]), (x0, got_x[0]), (x1, got_x[1])):
        one.begin(*got)
    rest_q.begin(*got_q)
    rest_z.begin(*got_z)
    got_small.wait()
    small.send()
    join_v.wait_recv()
    unit_v.send_first()
    join_k.wait_recv()
    unit_k.send_first()
    got_dq.wait()
    lax.fori_loop(0, 4, q_rows, 0)
    join_q = join(0)
    got_wskip = load(wskip_in, wide_buf)
    got_wq.wait()
    lax.fori_loop(0, 2, other_frames, 0)
    chip_core = links.send(chip_out, chip_in, links.core)
    join_q.wait_recv()
    unit_q.send_first()
    lax.fori_loop(0, 2, own_frames, 0)
    wo.turn_second()
    halo_y.wait_recv()
    halo_rest = links.send(part, part, links.core)
    small.turn()
    chip_core.wait_recv()
    got_stem.wait()
    got_grad.wait()
    halo_rest.wait_recv()
    total = lax.fori_loop(0, 4, norm_rows, jnp.zeros((1, D), F32))
    gain_steps[0] = jnp.concatenate(
        [total[:, 128 * i : 128 * (i + 1)] for i in range(8)], axis=0
    )
    gain_sum.send()
    got_joint.wait()
    p0.turn_third()
    rest_q.turn_third()
    skip_core0 = skip_part(0)
    skip_core1 = skip_part(1)
    skip_begin(0, skip_core0)
    skip_core2 = skip_part(2)
    p1.turn_third()
    skip_begin(1, skip_core1)
    skip_core3 = skip_part(3)
    rest_z.turn_third()
    skip_begin(2, skip_core2)
    skip_begin(3, skip_core3)
    got_wskip.wait()
    joined_part(0)
    joined_part(1)
    gain_sum.turn()
    joined_part(2)
    joined_part(3)
    x0.turn_third()
    joined_part(4)
    joined_part(5)
    joined_part(6)
    unit_q.turn_first()
    joined_part(7)
    p0.turn_fourth()
    skips[0][1].turn_first()
    unit_v.turn_first()
    x1.turn_third()
    p1.turn_fourth()
    skips[1][1].turn_first()
    wo.turn_third()
    small.turn()
    skips[2][1].turn_first()
    skips[0][0].turn_first()
    skips[3][1].turn_first()
    x0.turn_fourth()
    p0.finish()
    skips[1][0].turn_first()
    p1.finish()
    unit_k.turn_first()
    skips[2][0].turn_first()
    x0.finish()
    unit_v.turn_second()
    small.turn()
    skips[3][0].turn_first()
    gain_sum.turn()
    skips[0][0].turn_second()
    x1.turn_fourth()
    rest_q.finish()
    skips[1][0].turn_second()
    rest_z.finish()
    unit_q.turn_second()
    unit_v.turn_third()
    skips[0][1].turn_second()
    x1.finish()
    wo.finish()
    unit_k.turn_second()
    take_up()
    skips[1][1].turn_second()
    skips[2][0].turn_second()
    skips[2][1].turn_second()
    unit_v.turn_fourth()
    skips[3][0].turn_second()
    gain_sum.turn()
    skips[3][1].turn_second()
    small.turn()
    unit_k.turn_third()
    skips[0][0].finish()
    skips[1][0].finish()
    unit_q.turn_third()
    skips[0][1].finish()
    skips[1][1].finish()
    unit_v.finish()
    unit_q.turn_fourth()
    skips[2][0].finish()
    gain_sum.turn()
    skips[2][1].finish()
    unit_q.finish()
    skips[3][0].finish()
    skips[3][1].finish()
    small.turn()
    gain_sum.turn()
    unit_k.finish()
    links.drain()


def tail(late, small, dq, dkv, seen, wqkv, joint, stem, grad, gain, wskip):
    hbm, vm = pl.BlockSpec(memory_space=HBM), pl.BlockSpec(memory_space=VMEM)
    n_small = small.shape[0]
    out_shape = [
        jax.ShapeDtypeStruct((FRAMES, D), BF16),
        jax.ShapeDtypeStruct((FRAMES, D), BF16),
        jax.ShapeDtypeStruct((128, D), F32),
        jax.ShapeDtypeStruct((32, 4096), F32),
        jax.ShapeDtypeStruct((32, 3 * D), F32),
        jax.ShapeDtypeStruct((32, D), F32),
        jax.ShapeDtypeStruct((64, D), F32),
        jax.ShapeDtypeStruct((n_small, 128), F32),
        jax.ShapeDtypeStruct((8, 128), F32),
    ]
    low = lambda *shape: pltpu.VMEM(shape, BF16)
    full = lambda *shape: pltpu.VMEM(shape, F32)
    skip = (ROWS, SKIP_COLS)
    copies = 116
    scratch = [
        low(CHIP, WIDTH),
        low(CHIP + HALO, D),
        low(2 * D, D),
        low(D, WIDTH),
        low(D, D),
        low(2 * D, FRAMES),
        full(FRAMES, D),
        full(FRAMES, D),
        low(FRAMES, D),
        low(FRAMES, D),
        full(FRAMES, D),
        low(HALF, D),
        low(HALF, D),
        low(HALF, D),
        low(HALO + 2 * EDGE, D),
        low(FRAMES, D),
        low(2, 2, 2, 2, ROWS, D),
        low(2, 2, 2, ROWS, D),
        low(2, 2, ROWS, D),
        low(2, ROWS, D),
        low(ROWS, D),
        low(2, 2, 2, 2, ROWS, WIDTH),
        low(2, 4, 64, P_COLS),
        low(2, 4, 64, P_COLS),
        low(2, 6, 64, P_COLS),
        low(2, 2, 128, D - P_COLS),
        low(2, 2, 128, D - P_COLS),
        low(2, 128, D - P_COLS),
        low(128, D - P_COLS),
        low(2, 4, 32, X_COLS),
        low(2, 4, 32, X_COLS),
        low(2, 6, 32, X_COLS),
        low(2, 2, 64, 2 * D - X_COLS),
        low(2, 2, 64, 2 * D - X_COLS),
        low(2, 64, 2 * D - X_COLS),
        low(64, 2 * D - X_COLS),
        full(32, 2 * D),
        full(32, 2 * D),
        low(2, 4, 2, 2, ROWS, D),
        low(2, 4, 2, ROWS, D),
        low(2, 4, ROWS, D),
        low(2, 6, ROWS, D),
        low(2, 2, 2, ROWS, D),
        low(2, 2, 2, ROWS, D),
        low(2, 2, ROWS, D),
        low(2, ROWS, D),
        low(ROWS, D),
        low(2, 4, 2, 2, ROWS, WIDTH),
        low(2 * SKIPS, 4, 2, 2, *skip),
        low(2 * SKIPS, 4, 2, 2, *skip),
        low(2 * SKIPS, 4, 2, 2, *skip),
        low(2 * SKIPS, 4, 2, *skip),
        low(2 * SKIPS, 4, *skip),
        low(2 * SKIPS, 3, *skip),
        full(64, X_COLS),
        full(5, n_small, 128),
        full(5, n_small, 128),
        full(5, 8, 128),
        full(5, 8, 128),
        pltpu.SemaphoreType.DMA((28,)),
        pltpu.SemaphoreType.DMA((copies,)),
        pltpu.SemaphoreType.DMA((copies,)),
    ]
    return pl.pallas_call(
        tail_kernel,
        out_shape=out_shape,
        in_specs=[hbm] * 18 + [vm, hbm],
        out_specs=[vm] * 9,
        scratch_shapes=scratch,
        name="tail",
        cost_estimate=pl.CostEstimate(
            flops=17_000_000_000, bytes_accessed=60_000_000, transcendentals=0
        ),
        compiler_params=pltpu.CompilerParams(
            collective_id=0, has_side_effects=True, vmem_limit_bytes=63 << 20
        ),
    )(
        *late[:6],
        *[value.reshape(2, 2, 64, 2 * D - X_COLS) for value in late[6:8]],
        *late[8:],
        small,
        dq,
        dkv,
        seen,
        wqkv,
        joint,
        stem,
        grad,
        gain,
        wskip,
    )


def finish_kernel(count, *refs):
    ins, small, gain = refs[:count], refs[count], refs[count + 1]
    outs, smalls = refs[count + 2 : 2 * count + 2], refs[2 * count + 2 : 2 * count + 6]
    held, loads, stores = refs[2 * count + 6 : 3 * count + 6], refs[-2], refs[-1]
    got = [pltpu.make_async_copy(a, b, loads.at[i]) for i, (a, b) in enumerate(zip(ins, held))]
    for copy in got:
        copy.start()
    device = lax.axis_index("rows") * 4 + lax.axis_index("seq")
    smalls[0][...] = small[pl.ds(device, 1), :]
    row, lane = device // 4, lax.rem(device, 4) * 32
    values = [gain[pl.ds(row, 1), :], small[pl.ds(32 + row, 1), :], small[pl.ds(40 + row, 1), :]]
    for out, value in zip(smalls[1:], values):
        out[...] = pltpu.roll(value, lax.rem(128 - lane, 128), 1)[:, :32]
    put = [pltpu.make_async_copy(a, b, stores.at[i]) for i, (a, b) in enumerate(zip(held, outs))]
    for copy, after in zip(got, put):
        copy.wait()
        after.start()
    for copy in put:
        copy.wait()


def finish(results, small, gain):
    hbm, vm = pl.BlockSpec(memory_space=HBM), pl.BlockSpec(memory_space=VMEM)
    count = len(results)
    return pl.pallas_call(
        functools.partial(finish_kernel, count),
        out_shape=[
            *[jax.ShapeDtypeStruct(a.shape, a.dtype) for a in results],
            *[jax.ShapeDtypeStruct((1, size), F32) for size in (128, 32, 32, 32)],
        ],
        in_specs=[hbm] * count + [vm] * 2,
        out_specs=[hbm] * count + [vm] * 4,
        scratch_shapes=[
            *[pltpu.VMEM(a.shape, a.dtype) for a in results],
            pltpu.SemaphoreType.DMA((count,)),
            pltpu.SemaphoreType.DMA((count,)),
        ],
        name="finish",
        compiler_params=pltpu.CompilerParams(vmem_limit_bytes=63 << 20),
    )(*results, small, gain)


def swap_low(value):
    return lax.ppermute(value, "rows", [(r, r ^ 2) for r in range(8)])


def swap_x(value):
    return lax.ppermute(value, "rows", [(r, r ^ 1) for r in range(8)])


def swap_chip(value):
    return lax.ppermute(value, "seq", [(i, i ^ 2) for i in range(4)])


def body_chips(
    inputs,
    skip_feats,
    seg_ids,
    frame_valid,
    w_skip,
    gain_one,
    w_qkv,
    w_out,
    gain_two,
    w_up,
    b_up,
    w_down,
    b_down,
    cotangent,
):
    here = lax.axis_index("seq")
    c = here % 2
    heads = H // 2
    first, second_in, cot = inputs[0], skip_feats[0], cotangent[0]
    stem_out, normed_seen, q, kv, joint = front(first, second_in, w_skip, gain_one, w_qkv)
    attended, attended_t, lse = attend(q, kv, seg_ids, frame_valid, 128, 256, heads)
    output, middle_grad, grad_heads, small, *sums = middle(
        attended,
        stem_out,
        w_out,
        gain_two,
        w_up,
        w_down,
        b_up.reshape(32, 128),
        b_down,
        cot,
    )
    late = []
    swaps = (swap_x, swap_chip, swap_chip, swap_x, swap_low)
    for here, away, swap in zip(sums[::2], sums[1::2], swaps):
        late += [here, swap(away)]
    dq, dkv, output = attend_back(
        q, kv, grad_heads, attended_t, lse, seg_ids, frame_valid, output, 128, 256, heads
    )
    *results, small_sum, gain_sum = tail(
        late,
        small,
        dq,
        dkv,
        normed_seen,
        w_qkv,
        joint,
        stem_out,
        middle_grad,
        gain_one,
        w_skip,
    )
    *results, up_bias, gain_a, gain_b, down_bias = finish(results, small_sum, gain_sum)
    input_grad, skip_grad, down_share, up_share, qkv_share, out_share, skip_share = results
    return (
        output[None],
        input_grad[None],
        skip_grad[None],
        skip_share,
        gain_a.reshape(32),
        qkv_share,
        out_share,
        gain_b.reshape(32),
        up_share,
        up_bias.reshape(128),
        down_share,
        down_bias.reshape(32),
    )


def block_scores(q_blk, pos_blk, seg_blk, all_keys, seg_row, valid_row, slopes, score_scale):
    key_pos = jnp.arange(all_keys.shape[0])
    scores = (
        jnp.einsum("qhd,khd->hqk", q_blk, all_keys, preferred_element_type=jnp.float32)
        * score_scale
    )
    distance = jnp.abs(pos_blk[:, None] - key_pos[None, :]).astype(jnp.float32)
    scores = scores - slopes[:, None, None] * distance[None]
    allowed = (seg_blk[:, None] == seg_row[None, :]) & (
        (valid_row[None, :] == 1) | (pos_blk[:, None] == key_pos[None, :])
    )
    return jnp.where(allowed[None], scores, -jnp.inf)


def split_row(packed_row, heads_local):
    length = packed_row.shape[0]
    qkv_rows = packed_row.reshape(length, 3, heads_local, HD)
    return (qkv_rows[:, 0], qkv_rows[:, 1], qkv_rows[:, 2])


def attend_row(packed_row, seg_row, valid_row, slopes, heads_local, block_rows, score_scale):
    length = packed_row.shape[0]
    queries, all_keys, all_values = split_row(packed_row, heads_local)
    count = length // block_rows
    positions = jnp.arange(length)

    def one_block(block_in):
        q_blk, pos_blk, seg_blk = block_in
        scores = block_scores(
            q_blk, pos_blk, seg_blk, all_keys, seg_row, valid_row, slopes, score_scale
        )
        peak = jnp.max(scores, axis=-1, keepdims=True)
        log_total = peak + jnp.log(jnp.sum(jnp.exp(scores - peak), axis=-1, keepdims=True))
        attn_probs = jnp.exp(scores - log_total).astype(jnp.bfloat16)
        attended = jnp.einsum(
            "hqk,khd->qhd", attn_probs, all_values, preferred_element_type=jnp.float32
        )
        return (attended.astype(jnp.bfloat16), log_total[..., 0])

    attended, log_total = lax.map(
        one_block,
        (
            queries.reshape(count, block_rows, heads_local, HD),
            positions.reshape(count, block_rows),
            seg_row.reshape(count, block_rows),
        ),
    )
    return (attended.reshape(length, 1, heads_local * HD), log_total)


def attend_row_back(
    packed_row,
    log_total,
    grad_row,
    seg_row,
    valid_row,
    slopes,
    heads_local,
    block_rows,
    score_scale,
):
    length = packed_row.shape[0]
    queries, all_keys, all_values = split_row(packed_row, heads_local)
    count = length // block_rows
    positions = jnp.arange(length)
    grad_out = grad_row.reshape(count, block_rows, heads_local, HD)

    def one_block(carry, block_in):
        key_grad, value_grad = carry
        q_blk, pos_blk, seg_blk, total_blk, grad_blk = block_in
        scores = block_scores(
            q_blk, pos_blk, seg_blk, all_keys, seg_row, valid_row, slopes, score_scale
        )
        soft = jnp.exp(scores - total_blk[..., None])
        value_grad = value_grad + jnp.einsum(
            "hqk,qhd->khd", soft.astype(jnp.bfloat16), grad_blk, preferred_element_type=jnp.float32
        )
        prob_grad = jnp.einsum(
            "qhd,khd->hqk", grad_blk, all_values, preferred_element_type=jnp.float32
        )
        score_grad = (
            soft * (prob_grad - jnp.sum(soft * prob_grad, axis=-1, keepdims=True))
        ).astype(jnp.bfloat16)
        query_grad = (
            jnp.einsum("hqk,khd->qhd", score_grad, all_keys, preferred_element_type=jnp.float32)
            * score_scale
        )
        key_grad = (
            key_grad
            + jnp.einsum("hqk,qhd->khd", score_grad, q_blk, preferred_element_type=jnp.float32)
            * score_scale
        )
        return ((key_grad, value_grad), query_grad)

    zero_rows = jnp.zeros((length, heads_local, HD), jnp.float32)
    (key_grad, value_grad), query_grad = lax.scan(
        one_block,
        (zero_rows, zero_rows),
        (
            queries.reshape(count, block_rows, heads_local, HD),
            positions.reshape(count, block_rows),
            seg_row.reshape(count, block_rows),
            log_total,
            grad_out,
        ),
    )
    stacked = jnp.stack([query_grad.reshape(length, heads_local, HD), key_grad, value_grad], axis=1)
    return stacked.astype(jnp.bfloat16).reshape(length, 3, 1, heads_local * HD)


def body(
    inputs,
    skip_feats,
    seg_ids,
    frame_valid,
    w_skip,
    gain_one,
    w_qkv,
    w_out,
    gain_two,
    w_up,
    b_up,
    w_down,
    b_down,
    cotangent,
):
    parts = lax.axis_size("seq")
    heads_local = H // parts
    width_local = heads_local * HD
    rows_here = inputs.shape[0]
    frames = inputs.shape[1]
    length = frames * parts
    block_rows = min(512, length)
    score_scale = 1.0 / math.sqrt(HD)
    first_head = lax.axis_index("seq") * heads_local
    slopes = jnp.exp2(-8.0 * (first_head + jnp.arange(heads_local) + 1).astype(jnp.float32) / H)
    gain_first = gain_one.astype(jnp.float32)
    gain_second = gain_two.astype(jnp.float32)
    bias_up = b_up.astype(jnp.float32)
    joined = jnp.concatenate([inputs, skip_feats], axis=-1)
    stem_out = jnp.einsum("rfc,cd->rfd", joined, w_skip, preferred_element_type=jnp.float32)
    unit_one, inverse_one, normed = norm_forward(stem_out, gain_first)
    normed = normed.astype(jnp.bfloat16)
    packed = jnp.einsum("rfd,de->rfe", normed, w_qkv, preferred_element_type=jnp.float32).astype(
        jnp.bfloat16
    )
    packed = packed.reshape(rows_here, frames, 3, parts, width_local)
    by_heads = lax.all_to_all(packed, "seq", split_axis=3, concat_axis=1, tiled=True)

    def forward_row(row_data):
        return attend_row(
            row_data[0], row_data[1], row_data[2], slopes, heads_local, block_rows, score_scale
        )

    attended, log_total = lax.map(forward_row, (by_heads, seg_ids, frame_valid))
    by_frames = lax.all_to_all(attended, "seq", split_axis=1, concat_axis=2, tiled=True)
    mixed_out = by_frames.reshape(rows_here, frames, D)
    middle = stem_out + jnp.einsum(
        "rfd,de->rfe", mixed_out, w_out, preferred_element_type=jnp.float32
    )
    unit_two, inverse_two, second = norm_forward(middle, gain_second)
    second = second.astype(jnp.bfloat16)
    hidden = jnp.einsum("rfd,dk->rfk", second, w_up, preferred_element_type=jnp.float32) + bias_up
    active_full, gelu_back = jax.vjp(gelu_exact, hidden)
    active = active_full.astype(jnp.bfloat16)
    result = (
        middle
        + jnp.einsum("rfk,kd->rfd", active, w_down, preferred_element_type=jnp.float32)
        + b_down.astype(jnp.float32)
    )
    output = result.astype(jnp.bfloat16)
    cot_full = cotangent.astype(jnp.float32)
    down_grad = jnp.einsum("rfk,rfd->kd", active, cotangent, preferred_element_type=jnp.float32)
    bias_down_grad = jnp.sum(cot_full, axis=(0, 1))
    active_grad = jnp.einsum("rfd,kd->rfk", cotangent, w_down, preferred_element_type=jnp.float32)
    hidden_grad = gelu_back(active_grad)[0].astype(jnp.bfloat16)
    up_grad = jnp.einsum("rfd,rfk->dk", second, hidden_grad, preferred_element_type=jnp.float32)
    bias_up_grad = jnp.sum(hidden_grad.astype(jnp.float32), axis=(0, 1))
    second_grad = jnp.einsum("rfk,dk->rfd", hidden_grad, w_up, preferred_element_type=jnp.float32)
    middle_part, gain_two_grad = norm_backward(second_grad, unit_two, inverse_two, gain_second)
    middle_grad = cot_full + middle_part
    middle_low = middle_grad.astype(jnp.bfloat16)
    out_grad = jnp.einsum("rfd,rfe->de", mixed_out, middle_low, preferred_element_type=jnp.float32)
    mixed_grad = jnp.einsum(
        "rfe,de->rfd", middle_low, w_out, preferred_element_type=jnp.float32
    ).astype(jnp.bfloat16)
    grad_heads = lax.all_to_all(
        mixed_grad.reshape(rows_here, frames, parts, width_local),
        "seq",
        split_axis=2,
        concat_axis=1,
        tiled=True,
    )

    def backward_row(row_data):
        return attend_row_back(
            row_data[0],
            row_data[1],
            row_data[2],
            row_data[3],
            row_data[4],
            slopes,
            heads_local,
            block_rows,
            score_scale,
        )

    packed_grad = lax.map(backward_row, (by_heads, log_total, grad_heads, seg_ids, frame_valid))
    packed_back = lax.all_to_all(packed_grad, "seq", split_axis=1, concat_axis=3, tiled=True)
    packed_back = packed_back.reshape(rows_here, frames, 3 * D)
    qkv_grad = jnp.einsum("rfd,rfe->de", normed, packed_back, preferred_element_type=jnp.float32)
    normed_grad = jnp.einsum("rfe,de->rfd", packed_back, w_qkv, preferred_element_type=jnp.float32)
    stem_part, gain_one_grad = norm_backward(normed_grad, unit_one, inverse_one, gain_first)
    stem_low = (middle_grad + stem_part).astype(jnp.bfloat16)
    skip_w_grad = jnp.einsum("rfc,rfd->cd", joined, stem_low, preferred_element_type=jnp.float32)
    joined_grad = jnp.einsum("rfd,cd->rfc", stem_low, w_skip, preferred_element_type=jnp.float32)
    input_grad = joined_grad[..., :D].astype(jnp.bfloat16)
    skip_grad = joined_grad[..., D:].astype(jnp.bfloat16)
    (
        skip_share,
        gain_one_share,
        qkv_share,
        out_share,
        gain_two_share,
        up_share,
        bias_up_share,
        down_share,
        bias_down_share,
    ) = (
        lax.psum_scatter(skip_w_grad, ("rows", "seq"), scatter_dimension=0, tiled=True),
        lax.psum_scatter(gain_one_grad, ("rows", "seq"), scatter_dimension=0, tiled=True),
        lax.psum_scatter(qkv_grad, ("rows", "seq"), scatter_dimension=0, tiled=True),
        lax.psum_scatter(out_grad, ("rows", "seq"), scatter_dimension=0, tiled=True),
        lax.psum_scatter(gain_two_grad, ("rows", "seq"), scatter_dimension=0, tiled=True),
        lax.psum_scatter(up_grad, ("rows", "seq"), scatter_dimension=0, tiled=True),
        lax.psum_scatter(bias_up_grad, ("rows", "seq"), scatter_dimension=0, tiled=True),
        lax.psum_scatter(down_grad, ("rows", "seq"), scatter_dimension=0, tiled=True),
        lax.psum_scatter(bias_down_grad, ("rows", "seq"), scatter_dimension=0, tiled=True),
    )
    return (
        output,
        input_grad,
        skip_grad,
        skip_share,
        gain_one_share,
        qkv_share,
        out_share,
        gain_two_share,
        up_share,
        bias_up_share,
        down_share,
        bias_down_share,
    )


def solution(mesh):
    fits = (mesh.shape["rows"], mesh.shape["seq"]) == (8, 4)
    return jax.shard_map(
        body_chips if fits else body,
        mesh=mesh,
        in_specs=(
            P("rows", "seq", None),
            P("rows", "seq", None),
            P("rows", None),
            P("rows", None),
            P(),
            P(),
            P(),
            P(),
            P(),
            P(),
            P(),
            P(),
            P(),
            P("rows", "seq", None),
        ),
        out_specs=(
            P("rows", "seq", None),
            P("rows", "seq", None),
            P("rows", "seq", None),
            P(("rows", "seq"), None),
            P(("rows", "seq")),
            P(("rows", "seq"), None),
            P(("rows", "seq"), None),
            P(("rows", "seq")),
            P(("rows", "seq"), None),
            P(("rows", "seq")),
            P(("rows", "seq"), None),
            P(("rows", "seq")),
        ),
        check_vma=False,
    )
```

```python
import functools
import math

import jax
import jax.numpy as jnp
from jax import lax
from jax.experimental import pallas as pl
from jax.experimental.pallas import tpu as pltpu
from jax.sharding import PartitionSpec as P

D = 1024
H = 16
HD = 64
MOST = 682

epsilon = 1e-05

F32 = jnp.float32
BF16 = jnp.bfloat16
LOG2E = 1.4426950408889634
ROWS = 32
CHIP = 1024
HALO = 768
FRAMES = 512
HALF = HALO // 2
EDGE = CHIP - HALO
WIDTH = D // 2
SKIPS = 4
SKIP_COLS = D // SKIPS
FAR = 1e30
MESH = pl.DeviceIdType.MESH
VMEM = pltpu.MemorySpace.VMEM
SMEM = pltpu.MemorySpace.SMEM
HBM = pltpu.MemorySpace.HBM


def norm_forward(value, gain_vec):
    center = value - jnp.mean(value, axis=-1, keepdims=True)
    spread = jnp.mean(center * center, axis=-1, keepdims=True)
    inverse = lax.rsqrt(spread + epsilon)
    unit = center * inverse
    return (unit, inverse, unit * gain_vec)


def norm_backward(upstream, unit, inverse, gain_vec):
    scaled = upstream * gain_vec
    gain_grad = jnp.sum(upstream * unit, axis=tuple(range(upstream.ndim - 1)))
    inner = (
        scaled
        - jnp.mean(scaled, axis=-1, keepdims=True)
        - unit * jnp.mean(scaled * unit, axis=-1, keepdims=True)
    )
    return (inverse * inner, gain_grad)


def gelu_exact(value):
    return jax.nn.gelu(value, approximate=False)


def mm(equation, left, right):
    return jnp.einsum(equation, left, right, preferred_element_type=F32)


def dot(left, right):
    return jnp.dot(left, right, preferred_element_type=F32)


def dot_nt(left, right):
    return lax.dot_general(left, right, (((1,), (1,)), ((), ())), preferred_element_type=F32)


def dot_tn(left, right):
    return lax.dot_general(left, right, (((0,), (0,)), ((), ())), preferred_element_type=F32)


class Links:
    def __init__(self, sends, recvs):
        row, col = lax.axis_index("rows"), lax.axis_index("seq")
        self.z, self.x, self.y, self.c = row // 2, row % 2, col // 2, col % 2
        z, x, y, c = self.z, self.x, self.y, self.c
        self.high, self.low = z // 2, z % 2
        self.is_end = z == 3 * self.high
        self.is_inner = z == 1 + self.high
        self.core = (row, y * 2 + 1 - c)
        self.over_y = (row, (1 - y) * 2 + c)
        self.over_x = (z * 2 + 1 - x, col)
        self.over_low = ((self.high * 2 + 1 - self.low) * 2 + x, col)
        self.over_high = (((1 - self.high) * 2 + self.low) * 2 + x, col)
        self.over_mirror = ((3 - z) * 2 + x, col)
        self.sends, self.recvs, self.count, self.started = sends, recvs, 0, []

    def greet(self, near=False):
        barrier = pltpu.get_barrier_semaphore()
        peers = [self.core, self.over_y]
        if not near:
            peers += [self.over_x, self.over_low, self.over_high, self.over_mirror]
        for peer in peers:
            pl.semaphore_signal(barrier, inc=1, device_id=peer, device_id_type=MESH)
        pl.semaphore_wait(barrier, len(peers))

    def reserve(self, number):
        self.count += number
        return self.count - number

    def copy(self, src, dst, at, peer):
        return pltpu.make_async_remote_copy(
            src, dst, self.sends.at[at], self.recvs.at[at], device_id=peer, device_id_type=MESH
        )

    def send(self, src, dst, peer, here=None):
        copy = self.copy(src, dst, self.reserve(1), peer)
        if here is None:
            copy.start()
        else:
            pl.when(here)(copy.start)
        self.started.append((copy, here))
        return copy

    def drain(self):
        assert self.count <= self.sends.shape[0]
        for copy, here in self.started:
            if here is None:
                copy.wait_send()
            else:
                pl.when(here)(copy.wait_send)


def head_columns(wqkv, part, core):
    return wqkv.at[:, pl.ds(pl.multiple_of(D * part + WIDTH * core, WIDTH), WIDTH)]


def front_kernel(*refs):
    first_in, second_in, wskip_in, gain, wqkv_in = refs[:5]
    outs = refs[5:10]
    first, second, wskip, wq, wkv, o_stem, o_seen, o_q, o_kv, o_joint, loads, stores, sends, recvs = refs[10:]
    storing = []

    def store(k, *at):
        src, dst = (o_stem, o_seen, o_q, o_kv, o_joint)[k].at[*at], outs[k].at[*at]
        copy = pltpu.make_async_copy(src, dst, stores.at[len(storing)])
        copy.start()
        storing.append(copy)

    links = Links(sends, recvs)
    y, c = links.y, links.c
    loading = []

    def load(src, dst):
        copy = pltpu.make_async_copy(src, dst, loads.at[len(loading)])
        copy.start()
        loading.append(copy)
        return copy

    got = [load(first_in, first), load(second_in, second), load(wskip_in, wskip)]
    got_wkv = [
        load(head_columns(wqkv_in, 1 + i, c), wkv.at[:, pl.ds(WIDTH * i, WIDTH)]) for i in (0, 1)
    ]
    got_wq = load(head_columns(wqkv_in, 0, c), wq)
    links.greet(near=True)
    for copy in got:
        copy.wait()
    gains = gain[...].astype(F32).reshape(1, D)
    base = jnp.where(y == 0, EDGE, 0) + HALF * c

    def piece(i, chip):
        return 128 * jnp.where(chip == 0, i, 2 - i)

    def send_piece(i):
        at = lax.rem(base + piece(i, y) + FRAMES * c, CHIP)
        there = CHIP + HALF * c + piece(i, y)
        src = o_seen.at[pl.ds(pl.multiple_of(at, 128), 128)]
        dst = o_seen.at[pl.ds(pl.multiple_of(there, 128), 128)]
        return links.send(src, dst, links.over_y)

    pieces, across = [], []
    for turn in range(2):
        at = pl.multiple_of(256 * (1 - c if turn == 0 else c), 256)
        rows = pl.ds(at, 256)
        value = dot(first[rows, :], wskip[:D, :]) + dot(second[rows, :], wskip[D:, :])
        o_stem[rows, :] = value
        center = value - jnp.mean(value, axis=-1, keepdims=True)
        rate = lax.rsqrt(jnp.mean(center * center, axis=-1, keepdims=True) + epsilon)
        o_seen[rows, :] = (center * rate * gains).astype(BF16)
        pieces.append(send_piece(turn))
        there = o_seen.at[pl.ds(pl.multiple_of(FRAMES + at, 256), 256)]
        across.append(links.send(o_seen.at[rows], there, links.core))
    store(0, pl.ds(0, FRAMES))
    for copy in across:
        copy.wait_recv()
    pieces.append(send_piece(2))
    store(1, pl.ds(0, CHIP))
    for copy in (*got_wkv, got_wq):
        copy.wait()

    def own_part(i, _):
        rows = pl.ds(pl.multiple_of(256 * i, 256), 256)
        o_q[rows, :] = dot(o_seen[rows, :], wq[...]).astype(BF16)
        o_kv[rows, :] = dot(o_seen[rows, :], wkv[...]).astype(BF16)
        return 0

    lax.fori_loop(0, 4, own_part, 0)
    store(2, pl.ds(0, CHIP))
    store(3, pl.ds(0, CHIP))
    o_joint[:D, :] = first[...].T
    forward = []

    def far_part(i, core):
        at = pl.multiple_of(CHIP + HALF * core + piece(i, 1 - y), 128)
        rows = pl.ds(at, 128)
        o_kv[rows, :] = dot(o_seen[rows, :], wkv[...]).astype(BF16)

    for i in range(3):
        pieces[i].wait_recv()
        at = pl.multiple_of(CHIP + HALF * c + piece(i, 1 - y), 128)
        rows = o_seen.at[pl.ds(at, 128)]
        forward.append(links.send(rows, rows, links.core))
        if i == 0:
            o_joint[D:, :] = second[...].T
            store(4, pl.ds(0, 2 * D))
        far_part(i, c)
        if i > 0:
            forward[i - 1].wait_recv()
            far_part(i - 1, 1 - c)
    forward[2].wait_recv()
    store(1, pl.ds(CHIP, HALO))
    far_part(2, 1 - c)
    store(3, pl.ds(CHIP, HALO))
    links.drain()
    for copy in storing:
        copy.wait()


def front(first, second, wskip, gain, wqkv):
    hbm, vm = pl.BlockSpec(memory_space=HBM), pl.BlockSpec(memory_space=VMEM)
    low = lambda *shape: pltpu.VMEM(shape, BF16)
    return pl.pallas_call(
        front_kernel,
        out_shape=[
            jax.ShapeDtypeStruct((FRAMES, D), F32),
            jax.ShapeDtypeStruct((CHIP + HALO, D), BF16),
            jax.ShapeDtypeStruct((CHIP, WIDTH), BF16),
            jax.ShapeDtypeStruct((CHIP + HALO, 2 * WIDTH), BF16),
            jax.ShapeDtypeStruct((2 * D, FRAMES), BF16),
        ],
        in_specs=[hbm] * 3 + [vm, hbm],
        out_specs=[hbm] * 5,
        scratch_shapes=[
            low(FRAMES, D),
            low(FRAMES, D),
            low(2 * D, D),
            low(D, WIDTH),
            low(D, 2 * WIDTH),
            pltpu.VMEM((FRAMES, D), F32),
            low(CHIP + HALO, D),
            low(CHIP, WIDTH),
            low(CHIP + HALO, 2 * WIDTH),
            low(2 * D, FRAMES),
            pltpu.SemaphoreType.DMA((6,)),
            pltpu.SemaphoreType.DMA((7,)),
            pltpu.SemaphoreType.DMA((8,)),
            pltpu.SemaphoreType.DMA((8,)),
        ],
        name="front",
        cost_estimate=pl.CostEstimate(
            flops=8_000_000_000, bytes_accessed=24_000_000, transcendentals=0
        ),
        compiler_params=pltpu.CompilerParams(
            collective_id=2, has_side_effects=True, vmem_limit_bytes=63 << 20
        ),
    )(first, second, wskip, gain, wqkv)


class Frames:
    def __init__(self, seg_at, seg, valid, key_code, query_seg):
        here = lax.axis_index("seq")
        self.seg_at = seg_at
        self.own, self.other = FRAMES * here, FRAMES * (here + 1 - 2 * (here % 2))
        self.halo = jnp.where(here // 2 == 0, CHIP, CHIP - HALO)
        self.core = here % 2
        places = [(0, FRAMES, self.own), (FRAMES, FRAMES, self.other), (CHIP, HALO, self.halo)]
        for at, count, frame in places:
            span = pl.ds(pl.multiple_of(frame, 256), count)
            code = jnp.where(valid[0:1, span] == 1, seg[0:1, span], -1).astype(F32)
            key_code[pl.ds(at, count), :] = jnp.broadcast_to(code, (128, count)).T
            if at < CHIP:
                query_seg[:, pl.ds(at, count)] = jnp.broadcast_to(
                    seg[0:1, span].astype(F32), (8, count)
                )

    def frame(self, at):
        late = jnp.where(at < CHIP, self.other - FRAMES, self.halo - CHIP)
        return at + jnp.where(at < FRAMES, self.own, late)

    def meet(self, keys_at, keys, queries_at, queries):
        k, q = self.frame(keys_at), self.frame(queries_at)
        return (self.seg_at[0, k] <= self.seg_at[0, q + queries - 1]) & (
            self.seg_at[0, k + keys - 1] >= self.seg_at[0, q]
        )

    def slope(self, h):
        values = [LOG2E * 2.0 ** (-8.0 * (core * H // 2 + h + 1) / H) for core in (0, 1)]
        return jnp.where(self.core == 0, values[0], values[1])


def set_distances(dist, key_at, query_at, key_code, query_seg):
    keys, queries = dist.shape
    rows = lax.broadcasted_iota(jnp.int32, (keys, queries), 0) + key_at
    cols = lax.broadcasted_iota(jnp.int32, (keys, queries), 1) + query_at
    apart = jnp.abs(rows - cols)
    allowed = (key_code == query_seg) | (apart == 0)
    dist[...] = jnp.where(allowed, apart.astype(F32), FAR)


def wide(code, queries):
    return jnp.concatenate([code] * (queries // 128), axis=1) if queries > 128 else code


def both_heads(ref, pair, queries):
    first = ref[pl.ds(128 * pair, HD), queries]
    second = ref[pl.ds(128 * pair + HD, HD), queries]
    blank = jnp.zeros_like(first)
    return jnp.concatenate(
        [
            jnp.concatenate([first, blank], axis=0),
            jnp.concatenate([blank, second], axis=0),
        ],
        axis=1,
    )


def both_slopes(dist, frames, pair):
    value = dist[...]
    return jnp.concatenate(
        [value * frames.slope(2 * pair), value * frames.slope(2 * pair + 1)], axis=1
    )


def attend_kernel(
    bq,
    bk,
    heads,
    seg_at,
    q_in,
    kv_in,
    seg,
    valid,
    o_out,
    o_outt,
    lse,
    q,
    kv,
    out,
    outt,
    loads,
    stores,
    kcode,
    qseg,
    qt,
    vt,
    dist,
    acc,
    top,
    total,
    heads_q,
    scores,
    probs,
):
    width = heads * HD
    pairs = range(heads // 2)
    c1 = LOG2E / math.sqrt(HD)
    keys, values = pl.ds(0, width), pl.ds(width, width)
    got = [
        pltpu.make_async_copy(q_in, q, loads.at[0]),
        pltpu.make_async_copy(kv_in.at[:, values], kv.at[:, values], loads.at[1]),
        pltpu.make_async_copy(kv_in.at[:, keys], kv.at[:, keys], loads.at[2]),
    ]
    for copy in got:
        copy.start()
    frames = Frames(seg_at, seg, valid, kcode, qseg)
    got[0].wait()
    qt[...] = q[...].T
    got[1].wait()
    vt[...] = kv[:, width:].T
    got[2].wait()

    def results(i):
        rows = pl.ds(pl.multiple_of(i * bq, bq), bq)
        return [
            pltpu.make_async_copy(out.at[rows], o_out.at[rows], stores.at[0, i]),
            pltpu.make_async_copy(outt.at[:, rows], o_outt.at[:, rows], stores.at[1, i]),
        ]

    def q_block(i, _):
        queries = pl.ds(pl.multiple_of(i * bq, bq), bq)
        acc[...] = jnp.zeros_like(acc)
        total[...] = jnp.zeros_like(total)
        top[...] = jnp.full_like(top, -3e38)
        for pair in pairs:
            heads_q[pair] = both_heads(qt, pair, queries)

        def k_block(j, _):
            @pl.when(frames.meet(j * bk, bk, i * bq, bq))
            def _():
                ks = pl.ds(pl.multiple_of(j * bk, bk), bk)
                set_distances(
                    dist,
                    frames.frame(j * bk),
                    frames.frame(i * bq),
                    wide(kcode[ks, :], bq),
                    qseg[0:1, queries],
                )
                for pair in pairs:
                    scores[pair] = dot(kv[ks, pl.ds(128 * pair, 128)], heads_q[pair])
                fades = []
                for pair in pairs:
                    line = pl.ds(pair, 1)
                    score = scores[pair] * c1 - both_slopes(dist, frames, pair)
                    was = top[line, :]
                    now = jnp.maximum(was, jnp.max(score, axis=0, keepdims=True))
                    prob = jnp.exp2(score - now)
                    fade = jnp.exp2(was - now)
                    total[line, :] = total[line, :] * fade + jnp.sum(prob, axis=0, keepdims=True)
                    top[line, :] = now
                    probs[pair] = prob.astype(BF16)
                    fades.append(fade)
                for pair in pairs:
                    value = dot(vt[pl.ds(128 * pair, 128), ks], probs[pair])
                    for e in range(2):
                        at, lanes = pl.ds(128 * pair + HD * e, HD), slice(bq * e, bq * (e + 1))
                        acc[at, :] = (
                            acc[at, :] * fades[pair][:, lanes]
                            + value[HD * e : HD * (e + 1), lanes]
                        )

            return 0

        lax.fori_loop(0, kv.shape[0] // bk, k_block, 0)
        for pair in pairs:
            rate = 1.0 / total[pl.ds(pair, 1), :]
            for e in range(2):
                at = pl.ds(128 * pair + HD * e, HD)
                acc[at, :] = acc[at, :] * rate[:, bq * e : bq * (e + 1)]
        lse[:, pl.ds(pl.multiple_of(2 * i * bq, 2 * bq), 2 * bq)] = top[...] + jnp.log2(total[...])
        out[queries, :] = acc[...].T.astype(BF16)
        outt[:, queries] = acc[...].astype(BF16)
        for copy in results(i):
            copy.start()
        return 0

    count = q.shape[0] // bq
    lax.fori_loop(0, count, q_block, 0)

    def settle(i, _):
        for copy in results(i):
            copy.wait()
        return 0

    lax.fori_loop(0, count, settle, 0)


def attend(q, kv, seg, valid, bq, bk, heads):
    frames = q.shape[0]
    vm, sm, hbm = [pl.BlockSpec(memory_space=m) for m in (VMEM, SMEM, HBM)]
    return pl.pallas_call(
        functools.partial(attend_kernel, bq, bk, heads),
        out_shape=(
            jax.ShapeDtypeStruct((frames, heads * HD), BF16),
            jax.ShapeDtypeStruct((heads * HD, frames), BF16),
            jax.ShapeDtypeStruct((heads // 2, 2 * frames), F32),
        ),
        in_specs=[sm, hbm, hbm, vm, vm],
        out_specs=(hbm, hbm, vm),
        scratch_shapes=[
            pltpu.VMEM(q.shape, BF16),
            pltpu.VMEM(kv.shape, BF16),
            pltpu.VMEM((frames, heads * HD), BF16),
            pltpu.VMEM((heads * HD, frames), BF16),
            pltpu.SemaphoreType.DMA((3,)),
            pltpu.SemaphoreType.DMA((2, frames // bq)),
            pltpu.VMEM((kv.shape[0], 128), F32),
            pltpu.VMEM((8, frames), F32),
            pltpu.VMEM((heads * HD, frames), BF16),
            pltpu.VMEM((heads * HD, kv.shape[0]), BF16),
            pltpu.VMEM((bk, bq), F32),
            pltpu.VMEM((heads * HD, bq), F32),
            pltpu.VMEM((heads // 2, 2 * bq), F32),
            pltpu.VMEM((heads // 2, 2 * bq), F32),
            pltpu.VMEM((heads // 2, 2 * HD, 2 * bq), BF16),
            pltpu.VMEM((heads // 2, bk, 2 * bq), F32),
            pltpu.VMEM((heads // 2, bk, 2 * bq), BF16),
        ],
        name="attend",
        cost_estimate=pl.CostEstimate(
            flops=8_000_000_000, bytes_accessed=8_000_000, transcendentals=4_000_000
        ),
        compiler_params=pltpu.CompilerParams(vmem_limit_bytes=63 << 20),
    )(seg, q, kv, seg, valid)


def attend_back_kernel(
    bq,
    bk,
    heads,
    seg_at,
    q_in,
    kv_in,
    grad_in,
    outt_in,
    lse,
    seg,
    valid,
    passed_in,
    o_dq,
    o_dkv,
    o_passed,
    q,
    kv,
    grad,
    outt,
    passed,
    dq,
    dkv,
    loads,
    stores,
    kcode,
    qseg,
    qt,
    kt,
    gradt,
    delta,
    dist,
    dqt,
    sums,
    heads_q,
    heads_g,
    rows_q,
    rows_g,
    scores,
    prob_grads,
    probs,
    score_grads,
):
    width = heads * HD
    pairs = range(heads // 2)
    c1 = LOG2E / math.sqrt(HD)
    scale = 1.0 / math.sqrt(HD)
    lane = lax.broadcasted_iota(jnp.int32, (bq, 128), 1)
    places = [(q_in, q), (grad_in, grad), (outt_in, outt), (kv_in, kv), (passed_in, passed)]
    got = [pltpu.make_async_copy(a, b, loads.at[i]) for i, (a, b) in enumerate(places)]
    for copy in got:
        copy.start()
    sums[...] = jnp.zeros_like(sums)
    frames = Frames(seg_at, seg, valid, kcode, qseg)
    got[0].wait()
    qt[...] = q[...].T
    got[1].wait()
    gradt[...] = grad[...].T
    got[2].wait()
    got[3].wait()
    kt[...] = kv[:, :width].T
    got[4].wait()
    stored = [pltpu.make_async_copy(passed, o_passed, stores.at[0])]
    stored[0].start()

    def dq_copy(i):
        rows = pl.ds(pl.multiple_of(i * bq, bq), bq)
        return pltpu.make_async_copy(dq.at[rows], o_dq.at[rows], stores.at[1 + i])

    def q_block(i, _):
        qs = pl.multiple_of(i * bq, bq)
        queries = pl.ds(qs, bq)
        dqt[...] = jnp.zeros_like(dqt)
        for pair in pairs:
            at = pl.ds(128 * pair, 128)
            heads_q[pair] = both_heads(qt, pair, queries)
            heads_g[pair] = both_heads(gradt, pair, queries)
            product = outt[at, queries].astype(F32) * gradt[at, queries].astype(F32)
            for e in range(2):
                rows = pl.ds(bq * e, bq)
                keep = (lane < HD) if e == 0 else (lane >= HD)
                for to, ref in ((rows_q, q), (rows_g, grad)):
                    value = ref[queries, at]
                    to[pair, rows, :] = jnp.where(keep, value, jnp.zeros_like(value))
                delta[pl.ds(pair, 1), rows] = jnp.sum(
                    product[HD * e : HD * (e + 1)], axis=0, keepdims=True
                )

        def k_block(j, _):
            @pl.when(frames.meet(j * bk, bk, i * bq, bq))
            def _():
                ks = pl.ds(pl.multiple_of(j * bk, bk), bk)
                set_distances(
                    dist,
                    frames.frame(j * bk),
                    frames.frame(i * bq),
                    wide(kcode[ks, :], bq),
                    qseg[0:1, queries],
                )
                for pair in pairs:
                    scores[pair] = dot(kv[ks, pl.ds(128 * pair, 128)], heads_q[pair])
                    prob_grads[pair] = dot(
                        kv[ks, pl.ds(width + 128 * pair, 128)], heads_g[pair]
                    )
                lines = pl.ds(pl.multiple_of(2 * qs, 2 * bq), 2 * bq)
                for pair in pairs:
                    line = pl.ds(pair, 1)
                    prob = jnp.exp2(
                        scores[pair] * c1 - both_slopes(dist, frames, pair) - lse[line, lines]
                    )
                    probs[pair] = prob.astype(BF16)
                    score_grads[pair] = (prob * (prob_grads[pair] - delta[line, :])).astype(BF16)
                for pair in pairs:
                    at = pl.ds(128 * pair, 128)
                    sums[ks, pl.ds(width + 128 * pair, 128)] += dot(probs[pair], rows_g[pair])
                    sums[ks, at] += dot(score_grads[pair], rows_q[pair])
                    value = dot(kt[at, ks], score_grads[pair])
                    for e in range(2):
                        dqt[pl.ds(128 * pair + HD * e, HD), :] += value[
                            HD * e : HD * (e + 1), bq * e : bq * (e + 1)
                        ]

            return 0

        lax.fori_loop(0, kv.shape[0] // bk, k_block, 0)
        dq[pl.ds(qs, bq), :] = (dqt[...] * scale).T.astype(BF16)
        dq_copy(i).start()
        return 0

    count = q.shape[0] // bq
    lax.fori_loop(0, count, q_block, 0)
    parts = [(CHIP, HALO), (0, FRAMES), (FRAMES, FRAMES)]
    for i, (at, rows) in enumerate(parts):
        part = pl.ds(at, rows)
        dkv[part, :width] = (sums[part, :width] * scale).astype(BF16)
        dkv[part, width:] = sums[part, width:].astype(BF16)
        copy = pltpu.make_async_copy(dkv.at[part], o_dkv.at[part], stores.at[1 + count + i])
        copy.start()
        stored.append(copy)
    for copy in [*stored, *[dq_copy(i) for i in range(count)]]:
        copy.wait()


def attend_back(q, kv, grad, outt, lse, seg, valid, passed, bq, bk, heads):
    vm, sm, hbm = [pl.BlockSpec(memory_space=m) for m in (VMEM, SMEM, HBM)]
    return pl.pallas_call(
        functools.partial(attend_back_kernel, bq, bk, heads),
        out_shape=(
            jax.ShapeDtypeStruct(q.shape, BF16),
            jax.ShapeDtypeStruct(kv.shape, BF16),
            jax.ShapeDtypeStruct(passed.shape, passed.dtype),
        ),
        in_specs=[sm] + [hbm] * 4 + [vm] * 3 + [hbm],
        out_specs=(hbm, hbm, hbm),
        scratch_shapes=[
            pltpu.VMEM(q.shape, BF16),
            pltpu.VMEM(kv.shape, BF16),
            pltpu.VMEM(grad.shape, BF16),
            pltpu.VMEM(outt.shape, BF16),
            pltpu.VMEM(passed.shape, passed.dtype),
            pltpu.VMEM(q.shape, BF16),
            pltpu.VMEM(kv.shape, BF16),
            pltpu.SemaphoreType.DMA((5,)),
            pltpu.SemaphoreType.DMA((4 + q.shape[0] // bq,)),
            pltpu.VMEM((kv.shape[0], 128), F32),
            pltpu.VMEM((8, q.shape[0]), F32),
            pltpu.VMEM((heads * HD, q.shape[0]), BF16),
            pltpu.VMEM((heads * HD, kv.shape[0]), BF16),
            pltpu.VMEM((heads * HD, q.shape[0]), BF16),
            pltpu.VMEM((heads // 2, 2 * bq), F32),
            pltpu.VMEM((bk, bq), F32),
            pltpu.VMEM((heads * HD, bq), F32),
            pltpu.VMEM(kv.shape, F32),
            *[pltpu.VMEM((heads // 2, 2 * HD, 2 * bq), BF16)] * 2,
            *[pltpu.VMEM((heads // 2, 2 * bq, 2 * HD), BF16)] * 2,
            *[pltpu.VMEM((heads // 2, bk, 2 * bq), F32)] * 2,
            *[pltpu.VMEM((heads // 2, bk, 2 * bq), BF16)] * 2,
        ],
        name="attend_back",
        cost_estimate=pl.CostEstimate(
            flops=20_000_000_000, bytes_accessed=16_000_000, transcendentals=4_000_000
        ),
        compiler_params=pltpu.CompilerParams(vmem_limit_bytes=63 << 20),
    )(seg, q, kv, grad, outt, lse, seg, valid, passed)


def add_into(value, other):
    def step(i, _):
        value[i] = value[i] + other[i]
        return 0

    lax.fori_loop(0, value.shape[0], step, 0)


class Unit:
    def __init__(self, links, own, came, sums, y_first, done, straight=False):
        self.links, self.own, self.came, self.sums = links, own, came, sums
        self.y_first, self.done, self.straight = y_first, done, straight

    def add_core(self, r0):
        for k in range(4):
            for i in range(2):
                add_into(self.own.at[k, i], r0.at[k, i])

    def send_first(self):
        n, a = self.links, self.own
        if self.y_first:
            self.first = n.send(a.at[:, :, 1 - n.y], self.came[0], n.over_y)
        else:
            self.first = n.send(a.at[:, 1 - n.x], self.came[0], n.over_x)

    def turn_first(self):
        self.first.wait_recv()
        n, a, b = self.links, self.own, self.came[0]
        for k in range(4):
            add_into(a.at[k, :, n.y] if self.y_first else a.at[k, n.x], b.at[k])
        if self.y_first:
            self.second = n.send(a.at[:, 1 - n.x, n.y], self.came[1], n.over_x)
        else:
            self.second = n.send(a.at[:, n.x, 1 - n.y], self.came[1], n.over_y)

    def chip(self, at):
        return self.own.at[at, self.links.x, self.links.y]

    def turn_second(self):
        self.second.wait_recv()
        self.after_second()

    def after_second(self):
        n, to = self.links, self.came[2]
        add_into(self.chip(slice(None)), self.came[1])
        if self.straight:
            low, high = 1 - n.low, 1 - n.high
            places = [(2 * n.high + low, n.over_low), (2 * high + n.low, n.over_high), (3 - n.z, n.over_mirror)]
            self.third = [n.send(self.chip(p), to.at[j], peer) for j, (p, peer) in enumerate(places)]
        else:
            part = self.chip(pl.ds(1 - n.high, 3))
            self.third = n.send(part, to.at[pl.ds(0, 3)], n.over_low, n.is_end)

    def turn_third(self):
        n = self.links

        @pl.when(n.is_inner)
        def _():
            self.third.wait_recv()
            add_into(self.chip(pl.ds(1 - n.high, 3)), self.came[2].at[pl.ds(0, 3)])

        part = self.chip(pl.ds(2 - 2 * n.high, 2))
        self.fourth = n.send(part, self.came[2].at[pl.ds(3, 2)], n.over_mirror, n.is_inner)

    def turn_fourth(self):
        n = self.links

        @pl.when(n.is_inner)
        def _():
            self.fourth.wait_recv()
            add_into(self.chip(pl.ds(2 * n.high, 2)), self.came[2].at[pl.ds(3, 2)])

        self.fifth = n.send(self.chip(3 * n.high), self.came[2].at[5], n.over_low, n.is_inner)

    def finish(self):
        n = self.links
        if self.straight:
            for copy in self.third:
                copy.wait_recv()
            value = self.chip(n.z)[...].astype(F32)
            for j in range(3):
                value = value + self.came[2][j].astype(F32)
            self.done(value)
            return
        self.sums[...] = self.chip(n.z)[...].astype(F32)

        @pl.when(n.is_end)
        def _():
            self.fifth.wait_recv()
            self.sums[...] += self.came[2][5].astype(F32)

        self.done(self.sums[...])


class LowUnit(Unit):
    def send_first(self):
        n = self.links
        self.first = n.send(self.own.at[:, 1 - n.low], self.came[0], n.over_low)

    def turn_first(self):
        self.first.wait_recv()
        n = self.links
        for k in range(2):
            for i in range(2):
                add_into(self.own.at[k, n.low, i], self.came[0].at[k, i])
        self.second = n.send(self.own.at[:, n.low, 1 - n.x], self.came[1], n.over_x)

    def turn_second(self):
        self.second.wait_recv()
        n = self.links
        for k in range(2):
            add_into(self.own.at[k, n.low, n.x], self.came[1].at[k])
        self.third = n.send(self.own.at[:, n.low, n.x, 1 - n.y], self.came[2], n.over_y)

    def turn_third(self):
        self.third.wait_recv()
        n = self.links
        add_into(self.own.at[:, n.low, n.x, n.y], self.came[2])
        self.fourth = n.send(self.own.at[1 - n.high, n.low, n.x, n.y], self.came[3], n.over_high)

    def finish(self):
        self.fourth.wait_recv()
        n = self.links
        value = self.own[n.high, n.low, n.x, n.y].astype(F32)
        self.done(value + self.came[3][...].astype(F32))


class HighUnit:
    def __init__(self, links, own, came, done):
        self.links, self.own, self.came, self.done = links, own, came, done

    def begin(self, *loads):
        for copy in loads:
            copy.wait()
        n = self.links
        for k in range(2):
            for i in range(2):
                add_into(self.own.at[k, i], self.came[0].at[k, i])
        self.second = n.send(self.own.at[:, 1 - n.x], self.came[1], n.over_x)

    def turn_second(self):
        self.second.wait_recv()
        n = self.links
        for k in range(2):
            add_into(self.own.at[k, n.x], self.came[1].at[k])
        self.third = n.send(self.own.at[:, n.x, 1 - n.y], self.came[2], n.over_y)

    def turn_third(self):
        self.third.wait_recv()
        n = self.links
        add_into(self.own.at[:, n.x, n.y], self.came[2])
        self.fourth = n.send(self.own.at[1 - n.high, n.x, n.y], self.came[3], n.over_high)

    def finish(self):
        self.fourth.wait_recv()
        n = self.links
        self.done(self.own[n.high, n.x, n.y].astype(F32) + self.came[3][...].astype(F32))


class LateUnit(Unit):
    def chip(self, at):
        return self.own.at[at]

    def begin(self, *loads):
        for copy in loads:
            copy.wait()
        self.after_second()


class PairUnit:
    def __init__(self, links, own, came, over_x, done):
        self.links, self.own, self.came, self.done = links, own, came, done
        self.at, self.peer = (links.x, links.over_x) if over_x else (links.y, links.over_y)

    def begin(self, *loads):
        for copy in loads:
            copy.wait()
        for k in range(2):
            add_into(self.own.at[k], self.came[0].at[k])
        self.third = self.links.send(self.own.at[:, 1 - self.at], self.came[1], self.peer)

    def turn_third(self):
        n = self.links
        self.third.wait_recv()
        for k in range(2):
            value = self.own.at[k, self.at]
            value[...] = value[...] + self.came[1][k]
        self.fourth = n.send(self.own.at[1 - n.high, self.at], self.came[2], n.over_high)

    def finish(self):
        self.fourth.wait_recv()
        value = self.own[self.links.high, self.at].astype(F32)
        self.done(value + self.came[2][...].astype(F32))


class Small:
    def __init__(self, links, steps, into, done):
        self.links, self.steps, self.into, self.done, self.at = links, steps, into, done, 0
        self.stages = [links.core, links.over_y, links.over_x, links.over_low, links.over_high]

    def send(self):
        self.flying = self.links.send(
            self.steps.at[self.at], self.into.at[self.at], self.stages[self.at]
        )

    def turn(self):
        self.flying.wait_recv()
        value = self.steps[self.at] + self.into[self.at]
        self.at += 1
        if self.at == len(self.stages):
            self.done(value)
        else:
            self.steps[self.at] = value
            self.send()


STEPS = 8
STEP = 256
P_COLS = 640
X_STEPS = 6
X_COLS = STEP * X_STEPS
UP_BLOCKS = [2 * i + j for i in (0, 2, 3, 5, 6, 7, 1, 4) for j in (0, 1)]


def middle_kernel(*refs):
    (
        att_in_hbm,
        stem_in,
        wout_in,
        gain,
        up_hbm,
        down_hbm,
        bias_up,
        bias_down,
        cot_in,
    ) = refs[:9]
    o_out, o_grad, o_heads, o_small = refs[9:13]
    o_p, o_p_away, o_q, o_q_away, o_x, o_x_away, o_z, o_z_away, o_wo, o_wo_away = refs[13:23]
    (
        att,
        att_came,
        stem,
        wout,
        ups,
        downs,
        cot,
        second,
        second_t,
        unit,
        inverse,
        active,
        hidden_grad,
        out_sum,
        grad_sum,
        low,
        swap_out,
        swap_in,
        p_send,
        p_keep,
        p_came,
        q_send,
        q_keep,
        q_came,
        x_send,
        x_keep,
        x_came,
        z_send,
        z_keep,
        z_came,
        biases,
        loads,
        sends,
        recvs,
    ) = refs[23:]
    links = Links(sends, recvs)
    x, y, c = links.x, links.y, links.c
    loading = []

    def load(src, dst):
        copy = pltpu.make_async_copy(src, dst, loads.at[len(loading)])
        copy.start()
        loading.append(copy)
        return copy

    own, other = pl.ds(0, FRAMES), pl.ds(FRAMES, FRAMES)
    got_att = load(att_in_hbm.at[own], att)
    got_wout = load(wout_in, wout)
    got_stem = load(stem_in, stem)
    got_cot = load(cot_in, cot.at[own])
    got_ups, got_downs = [], []
    for i in range(STEPS):
        for j in range(2):
            at = pl.multiple_of(128 * (4 * i + 2 * j + c), 128)
            part = pl.ds(128 * j, 128)
            got_ups.append(load(up_hbm.at[:, pl.ds(at, 128)], ups.at[i, :, part]))
            got_downs.append(load(down_hbm.at[pl.ds(at, 128), :], downs.at[i, part, :]))
    links.greet()
    att_core = links.send(att_in_hbm.at[other], att_came, links.core)
    cot_core = links.send(cot_in, cot.at[other], links.core)
    mine = pl.ds(pl.multiple_of(WIDTH * c, WIDTH), WIDTH)
    theirs = pl.ds(pl.multiple_of(WIDTH * (1 - c), WIDTH), WIDTH)

    got_att.wait()
    got_wout.wait()
    got_stem.wait()
    att_core.wait_recv()
    gains = gain[...].astype(F32).reshape(1, D)
    second_core = []
    for part in range(2):
        rows = pl.ds(256 * part, 256)
        value = stem[rows, :] + dot(att[rows, :], wout[mine, :]) + dot(att_came[rows, :], wout[theirs, :])
        stem[rows, :] = value
        center = value - jnp.mean(value, axis=-1, keepdims=True)
        rate = lax.rsqrt(jnp.mean(center * center, axis=-1, keepdims=True) + epsilon)
        normal = center * rate
        unit[rows, :] = normal
        inverse[rows, :] = jnp.broadcast_to(rate, (256, 128))
        second[rows, :] = (normal * gains).astype(BF16)
        second_core.append(
            links.send(second.at[rows], second.at[pl.ds(FRAMES + 256 * part, 256)], links.core)
        )
    second_t[:, :FRAMES] = second[own, :].T
    biases[...] = bias_up[...].astype(F32)
    out_sum[...] = jnp.zeros_like(out_sum)
    grad_sum[...] = jnp.zeros_like(grad_sum)
    o_small[...] = jnp.zeros_like(o_small)
    for copy in [got_cot, *got_ups, *got_downs]:
        copy.wait()
    cot_core.wait_recv()
    for copy in second_core:
        copy.wait_recv()
    second_t[:, FRAMES:] = second[other, :].T

    p_at, q_at, x_at, z_at = [links.reserve(k) for k in (STEPS, 4, X_STEPS, STEPS - X_STEPS)]

    def p_copy(i):
        return links.copy(p_send.at[i], p_came.at[i], p_at + i, links.over_y)

    def q_copy(i):
        return links.copy(q_send.at[i], q_came.at[i], q_at + i, links.over_low)

    def x_copy(i):
        return links.copy(x_send.at[i], x_came.at[i], x_at + i, links.over_x)

    def z_copy(i):
        return links.copy(z_send.at[i], z_came.at[i], z_at + i, links.over_low)

    def feed_step(i, _):
        up, down = ups[i], downs[i]
        bias = jnp.concatenate([biases[pl.ds(4 * i + 2 * j + c, 1), :] for j in (0, 1)], axis=1)
        total = jnp.zeros((1, STEP), F32)
        for half in (own, other):
            hidden = dot(second[half, :], up) + bias
            active_grad = dot_nt(cot[half, :], down)
            share = 0.5 + 0.5 * lax.erf(hidden * math.sqrt(0.5))
            slope = share + hidden * (
                jnp.exp(-0.5 * hidden * hidden) * (1.0 / math.sqrt(2.0 * math.pi))
            )
            a = (hidden * share).astype(BF16)
            g = (active_grad * slope).astype(BF16)
            active[half, :] = a
            hidden_grad[half, :] = g
            total = total + jnp.sum(g.astype(F32), axis=0, keepdims=True)
            out_sum[half, :] += dot(a, down)
            grad_sum[half, :] += dot_nt(g, up)
        for j in range(2):
            o_small[pl.ds(4 * i + 2 * j + c, 1), :] = total[:, 128 * j : 128 * (j + 1)]
        value = dot_tn(active[...], cot[...]).astype(BF16)
        p_send[i] = jnp.where(y == 0, value[128:, :P_COLS], value[:128, :P_COLS])
        p_keep[i] = jnp.where(y == 0, value[:128, :P_COLS], value[128:, :P_COLS])
        p_copy(i).start()
        stays = lax.rem(i // 2, 2) == links.low
        slot = 2 * (i // 4) + lax.rem(i, 2)
        rest = value[:, P_COLS:].reshape(2, 128, D - P_COLS)

        @pl.when(stays)
        def _():
            q_keep[slot] = rest

        @pl.when(jnp.logical_not(stays))
        def _():
            q_send[slot] = rest
            q_copy(slot).start()

        value = dot(second_t[...], hidden_grad[...]).astype(BF16)

        over_z = (lax.rem(i, 3) == 1) & (i < 6)

        @pl.when(jnp.logical_not(over_z))
        def _():
            j = i - jnp.where(i > 1, 1, 0) - jnp.where(i > 4, 1, 0)
            for k in range(4):
                first, last = value[256 * k : 256 * k + 128], value[256 * k + 128 : 256 * (k + 1)]
                x_send[j, k] = jnp.where(x == 0, last, first)
                x_keep[j, k] = jnp.where(x == 0, first, last)
            x_copy(j).start()

        @pl.when(over_z)
        def _():
            j = i // 4
            for k in range(2):
                first, last = value[512 * k : 512 * k + 256], value[512 * k + 256 : 512 * (k + 1)]
                z_send[j, k] = jnp.where(links.low == 0, last, first)
                z_keep[j, k] = jnp.where(links.low == 0, first, last)
            z_copy(j).start()

        return 0

    lax.fori_loop(0, STEPS, feed_step, 0)

    swap_out[0] = grad_sum[other, :].astype(BF16)
    grad_core = links.send(swap_out.at[0], swap_in.at[0], links.core)
    swap_out[1] = out_sum[other, :].astype(BF16)
    out_core = links.send(swap_out.at[1], swap_in.at[1], links.core)
    grad_core.wait_recv()

    def norm_rows(i, totals):
        rows = pl.ds(pl.multiple_of(128 * i, 128), 128)
        upstream = grad_sum[rows, :] + swap_in[0, rows, :].astype(F32)
        normal = unit[rows, :]
        scaled = upstream * gains
        inner = (
            scaled
            - jnp.mean(scaled, axis=-1, keepdims=True)
            - normal * jnp.mean(scaled * normal, axis=-1, keepdims=True)
        )
        value = cot[rows, :].astype(F32)
        grad = value + inverse[rows, 0:1] * inner
        o_grad[rows, :] = grad
        low[rows, :] = grad.astype(BF16)
        return (
            totals[0] + jnp.sum(upstream * normal, axis=0, keepdims=True),
            totals[1] + jnp.sum(value, axis=0, keepdims=True),
        )

    zero = jnp.zeros((1, D), F32)
    totals = lax.fori_loop(0, 4, norm_rows, (zero, zero))
    for k, value in enumerate(totals):
        for j in range(8):
            o_small[pl.ds(32 + 8 * k + j, 1), :] = value[:, 128 * j : 128 * (j + 1)]
    swap_out[2, :, :WIDTH] = dot_nt(low[...], wout[theirs, :]).astype(BF16)
    heads_core = links.send(
        swap_out.at[2, :, pl.ds(0, WIDTH)], swap_in.at[2, :, pl.ds(0, WIDTH)], links.core
    )
    o_heads[own, :] = dot_nt(low[...], wout[mine, :]).astype(BF16)

    def out_grad(high, value):
        value = value.astype(BF16)
        for low_bit in range(2):
            for i in range(2):
                for j in range(2):
                    at = 256 * low_bit + 128 * i + 64 * j
                    first, last = value[at : at + 32], value[at + 32 : at + 64]
                    rows = pl.multiple_of(256 * high + at // 2, 32)
                    second_t[pl.ds(rows, 32), :] = jnp.where(c == 0, first, last)
                    second_t[pl.ds(FRAMES + rows, 32), :] = jnp.where(c == 0, last, first)

    out_grad(c, dot_tn(att[...], low[...]))
    out_grad(1 - c, dot_tn(att_came[...], low[...]))
    wo_core = links.send(second_t.at[other], second.at[other], links.core)
    out_core.wait_recv()

    def out_rows(i, _):
        rows = pl.ds(pl.multiple_of(128 * i, 128), 128)
        o_out[rows, :] = (
            stem[rows, :]
            + (out_sum[rows, :] + swap_in[1, rows, :].astype(F32))
            + bias_down[...].astype(F32).reshape(1, D)
        ).astype(BF16)
        return 0

    lax.fori_loop(0, 4, out_rows, 0)
    heads_core.wait_recv()
    o_heads[other, :] = swap_in[2, :, :WIDTH]

    def add_p(i, _):
        p_copy(i).wait()
        value = p_keep[i] + p_came[i]
        stays = lax.rem(i, 2) == x

        @pl.when(stays)
        def _():
            o_p[i // 2] = value

        @pl.when(jnp.logical_not(stays))
        def _():
            o_p_away[i // 2] = value

        return 0

    def add_q(i, _):
        q_copy(i).wait()
        o_q[i // 2, lax.rem(i, 2)] = q_keep[i, y] + q_came[i, y]
        o_q_away[i // 2, lax.rem(i, 2)] = q_keep[i, 1 - y] + q_came[i, 1 - y]
        return 0

    def columns(i):
        return pl.ds(pl.multiple_of(STEP * i, STEP), STEP)

    def add_x(i, _):
        x_copy(i).wait()
        for k in range(4):
            value = x_keep[i, k] + x_came[i, k]
            o_x[k, :, columns(i)] = jnp.where(y == 0, value[:64], value[64:])
            o_x_away[k, :, columns(i)] = jnp.where(y == 0, value[64:], value[:64])
        return 0

    def add_z(i, _):
        z_copy(i).wait()
        for k in range(2):
            value = z_keep[i, k] + z_came[i, k]
            o_z[k, :, columns(i)] = jnp.where(x == 0, value[:128], value[128:])
            o_z_away[k, :, columns(i)] = jnp.where(x == 0, value[128:], value[:128])
        return 0

    wo_core.wait_recv()
    for high in range(2):
        for i in range(2):
            for j in range(2):
                for out, low_bit in ((o_wo, links.low), (o_wo_away, 1 - links.low)):
                    at = 256 * high + 128 * low_bit + 64 * i + 32 * j
                    rows = pl.ds(pl.multiple_of(at, 32), 32)
                    came = pl.ds(pl.multiple_of(FRAMES + at, 32), 32)
                    out[high, i, j] = second_t[rows, :] + second[came, :]
    lax.fori_loop(0, STEPS, add_p, 0)
    lax.fori_loop(0, 4, add_q, 0)
    lax.fori_loop(0, X_STEPS, add_x, 0)
    lax.fori_loop(0, STEPS - X_STEPS, add_z, 0)
    links.drain()


def middle(att, stem, wout, gain, w_up, w_down, bias_up, bias_down, cot):
    hbm, vm = pl.BlockSpec(memory_space=HBM), pl.BlockSpec(memory_space=VMEM)
    low = lambda *shape: pltpu.VMEM(shape, BF16)
    full = lambda *shape: pltpu.VMEM(shape, F32)
    copies = 29
    return pl.pallas_call(
        middle_kernel,
        out_shape=[
            jax.ShapeDtypeStruct((FRAMES, D), BF16),
            jax.ShapeDtypeStruct((FRAMES, D), F32),
            jax.ShapeDtypeStruct((CHIP, WIDTH), BF16),
            jax.ShapeDtypeStruct((48, 128), F32),
            *[jax.ShapeDtypeStruct((4, 128, P_COLS), BF16)] * 2,
            *[jax.ShapeDtypeStruct((2, 2, 128, D - P_COLS), BF16)] * 2,
            *[jax.ShapeDtypeStruct((4, 64, X_COLS), BF16)] * 2,
            *[jax.ShapeDtypeStruct((2, 128, 2 * D - X_COLS), BF16)] * 2,
            *[jax.ShapeDtypeStruct((2, 2, 2, ROWS, D), BF16)] * 2,
        ],
        in_specs=[hbm] * 3 + [vm] + [hbm] * 2 + [vm] * 2 + [hbm],
        out_specs=[vm] * 14,
        scratch_shapes=[
            low(FRAMES, WIDTH),
            low(FRAMES, WIDTH),
            full(FRAMES, D),
            low(D, D),
            low(STEPS, D, STEP),
            low(STEPS, STEP, D),
            low(CHIP, D),
            low(CHIP, D),
            low(D, CHIP),
            full(FRAMES, D),
            full(FRAMES, 128),
            low(CHIP, STEP),
            low(CHIP, STEP),
            full(CHIP, D),
            full(CHIP, D),
            low(FRAMES, D),
            low(3, FRAMES, D),
            low(3, FRAMES, D),
            *[low(STEPS, 128, P_COLS)] * 3,
            *[low(4, 2, 128, D - P_COLS)] * 3,
            *[low(X_STEPS, 4, 128, STEP)] * 3,
            *[low(STEPS - X_STEPS, 2, 256, STEP)] * 3,
            full(32, 128),
            pltpu.SemaphoreType.DMA((4 + 4 * STEPS,)),
            pltpu.SemaphoreType.DMA((copies,)),
            pltpu.SemaphoreType.DMA((copies,)),
        ],
        name="middle",
        cost_estimate=pl.CostEstimate(
            flops=28_000_000_000, bytes_accessed=40_000_000, transcendentals=4_000_000
        ),
        compiler_params=pltpu.CompilerParams(
            collective_id=1, has_side_effects=True, vmem_limit_bytes=63 << 20
        ),
    )(att, stem, wout, gain, w_up, w_down, bias_up, bias_down, cot)


def tail_kernel(*refs):
    (
        p_in,
        p_came,
        q_in,
        q_came,
        x_in,
        x_came,
        z_in,
        z_came,
        wo_in,
        wo_came,
        small_in,
        dq_in,
        dkv_in,
        seen_in,
        wqkv_in,
        joint_in,
        stem_in,
        grad_in,
        gain,
        wskip_in,
    ) = refs[:20]
    o_in, o_skip, o_down, o_up, o_qkv, o_wo, o_wskip, o_small, o_gain = refs[20:29]
    (
        dq,
        dkv,
        wide_buf,
        wq,
        wkv,
        joint,
        stem,
        grad,
        chip_out,
        chip_in,
        chip_own,
        halo_out,
        halo_in,
        halo_sum,
        halo,
        low,
        low_own,
        low_r1,
        low_r2,
        low_r3,
        low_r4,
        join_low,
        p_own,
        p_r2,
        p_r3,
        q_own,
        q_r2,
        q_r3,
        q_r4,
        x_own,
        x_r2,
        x_r3,
        z_own,
        z_r2,
        z_r3,
        z_r4,
        up_out,
        up_in_last,
        unit_own,
        unit_r1,
        unit_r2,
        unit_r3,
        wo_own,
        wo_r1,
        wo_r2,
        wo_r3,
        wo_r4,
        join_out,
        skip_own,
        skip_out,
        skip_r0,
        skip_r1,
        skip_r2,
        skip_r3,
        sums,
        small_steps,
        small_into,
        gain_steps,
        gain_into,
        loads,
        sends,
        recvs,
    ) = refs[29:]
    links = Links(sends, recvs)
    y, c = links.y, links.c
    loading = []

    def load(src, dst):
        copy = pltpu.make_async_copy(src, dst, loads.at[len(loading)])
        copy.start()
        loading.append(copy)
        return copy

    seen = wide_buf.at[pl.ds(0, CHIP + HALO)]
    far, near = pl.ds(CHIP, HALO), pl.ds(0, CHIP)
    got_wkv = [load(head_columns(wqkv_in, 1 + i, c), wkv.at[:, pl.ds(WIDTH * i, WIDTH)]) for i in (0, 1)]
    got_far = load(dkv_in.at[far], dkv.at[far])
    links.greet()
    got_wo = [load(wo_in, wo_own), load(wo_came, wo_r1)]
    got_dq = load(dq_in, dq)
    got_near = load(dkv_in.at[near], dkv.at[near])
    got_seen = load(seen_in, seen)
    got_small = load(small_in, small_steps.at[0])
    got_p = [
        [
            load(p_in.at[:, pl.ds(64 * i, 64)], p_own.at[i]),
            load(p_came.at[:, pl.ds(64 * i, 64)], p_r2.at[i]),
        ]
        for i in range(2)
    ]
    got_x = []
    for i, core in enumerate((1 - c, c)):
        rows = pl.ds(pl.multiple_of(32 * core, 32), 32)
        got_x.append([load(x_in.at[:, rows], x_own.at[i]), load(x_came.at[:, rows], x_r2.at[i])])
    got_q = [load(q_in, q_own), load(q_came, q_r2)]
    got_z = [load(z_in, z_own), load(z_came, z_r2)]
    got_wq = load(head_columns(wqkv_in, 0, c), wq)
    got_stem = load(stem_in, stem)
    got_grad = load(grad_in, grad)
    got_joint = load(joint_in, joint)
    halo[pl.ds(0, EDGE), :] = jnp.zeros((EDGE, D), BF16)
    halo[pl.ds(EDGE + HALO, EDGE), :] = jnp.zeros((EDGE, D), BF16)

    def to_down(i):
        def done(value):
            o_down[pl.ds(64 * i, 64), pl.ds(0, P_COLS)] = value

        return done

    def to_down_rest(value):
        o_down[:, pl.ds(P_COLS, D - P_COLS)] = value

    def put_up(b, core, value):
        o_up[:, pl.ds(pl.multiple_of(256 * b + 128 * core, 128), 128)] = value

    def pass_up(at, value):
        part = pl.ds(at, value.shape[1])
        up_out[:, part] = value
        up_last.append(links.send(up_out.at[:, part], up_in_last.at[:, part], links.core))

    def to_up_other(value):
        pass_up(0, value)

    def to_up_mine(value):
        for t in range(X_COLS // 128):
            put_up(UP_BLOCKS[t], c, value[:, 128 * t : 128 * (t + 1)])

    def to_up_rest(value):
        pass_up(X_COLS, jnp.where(c == 0, value[32:], value[:32]))
        mine = jnp.where(c == 0, value[:32], value[32:])
        for t in range(X_COLS // 128, 16):
            at = 128 * t - X_COLS
            put_up(UP_BLOCKS[t], c, mine[:, at : at + 128])

    def take_up():
        for copy in up_last:
            copy.wait_recv()
        for t in range(16):
            put_up(UP_BLOCKS[t], 1 - c, up_in_last[:, 128 * t : 128 * (t + 1)])

    up_last = []

    def room(rows, cols):
        return sums.at[pl.ds(0, rows), pl.ds(0, cols)]

    p0, p1 = [
        LateUnit(
            links, p_own.at[i], (None, p_r2.at[i], p_r3.at[i]), room(64, P_COLS), True, to_down(i)
        )
        for i in range(2)
    ]
    x0, x1 = [
        LateUnit(
            links, x_own.at[i], (None, x_r2.at[i], x_r3.at[i]), room(32, X_COLS), False, done
        )
        for i, done in enumerate((to_up_other, to_up_mine))
    ]
    rest_q = PairUnit(links, q_own, (q_r2, q_r3, q_r4), True, to_down_rest)
    rest_z = PairUnit(links, z_own, (z_r2, z_r3, z_r4), False, to_up_rest)

    def to_wo(value):
        o_wo[...] = value

    def to_qkv(i):
        def done(value):
            o_qkv[:, pl.ds(D * i, D)] = value

        return done

    def to_wskip(q, half):
        def done(value):
            o_wskip[pl.ds(ROWS * half, ROWS), pl.ds(SKIP_COLS * q, SKIP_COLS)] = value

        return done

    def unit(k, y_first, done):
        came = (unit_r1.at[k], unit_r2.at[k], unit_r3.at[k])
        return Unit(links, unit_own.at[k], came, room(ROWS, D), y_first, done)

    wo = HighUnit(links, wo_own, (wo_r1, wo_r2, wo_r3, wo_r4), to_wo)
    unit_q, unit_v = unit(0, False, to_qkv(0)), unit(1, False, to_qkv(2))
    unit_k = LowUnit(links, low_own, (low_r1, low_r2, low_r3, low_r4), None, False, to_qkv(1))

    def skip_unit(k, y_first, done):
        came = (skip_r1.at[k], skip_r2.at[k], skip_r3.at[k])
        return Unit(links, skip_own.at[k], came, None, y_first, done, straight=True)

    skips = [
        [skip_unit(2 * q + half, half == 0, to_wskip(q, half)) for half in range(2)]
        for q in range(SKIPS)
    ]

    def to_small(value):
        o_small[...] = value

    def to_gain(value):
        o_gain[...] = value

    small = Small(links, small_steps, small_into, to_small)
    gain_sum = Small(links, gain_steps, gain_into, to_gain)

    for copy in (*got_wkv, got_far):
        copy.wait()

    def halo_part(core):
        at = pl.multiple_of(CHIP + HALF * core, 128)
        return dot_nt(dkv[pl.ds(at, HALF), :], wkv[...])

    halo_out[...] = halo_part(1 - c).astype(BF16)
    halo_core = links.send(halo_out, halo_in, links.core)
    mine = halo_part(c)
    halo_core.wait_recv()
    halo_sum[...] = (mine + halo_in[...].astype(F32)).astype(BF16)
    part_at = pl.ds(pl.multiple_of(EDGE + HALF * c, 128), HALF)
    part = halo.at[part_at]
    halo_y = links.send(halo_sum, part, links.over_y)
    got_near.wait()
    got_seen.wait()
    columns = pl.ds(pl.multiple_of(WIDTH * c, WIDTH), WIDTH)

    def place(k, i, value):
        value = value.astype(BF16)
        for j in range(2):
            for m in range(2):
                at = 128 * j + 64 * m
                first, second = value[at : at + 32], value[at + 32 : at + 64]
                mine, theirs = jnp.where(c == 0, first, second), jnp.where(c == 0, second, first)
                if k == 1:
                    low_own[i // 2, i % 2, j, m, :, columns] = mine
                else:
                    unit_own[k // 2, i, j, m, :, columns] = mine
                if k == 1:
                    join_low[i // 2, i % 2, j, m] = theirs
                else:
                    join_out[k // 2, i, j, m] = theirs

    def join(k):
        if k == 1:
            return links.send(join_low, low_own.at[:, :, :, :, :, columns], links.core)
        there = unit_own.at[k // 2, :, :, :, :, columns]
        return links.send(join_out.at[k // 2], there, links.core)

    def kv_rows(i, _):
        value = dot(seen[:, pl.ds(pl.multiple_of(256 * i, 256), 256)].T, dkv[...])
        place(1, i, value[:, :WIDTH])
        place(2, i, value[:, WIDTH:])
        return 0

    def q_rows(i, _):
        place(0, i, dot(seen[near, pl.ds(pl.multiple_of(256 * i, 256), 256)].T, dq[...]))
        return 0

    def chip_part(at):
        rows = pl.ds(at, 256)
        return dot_nt(dq[rows, :], wq[...]) + dot_nt(dkv[rows, :], wkv[...])

    def other_frames(i, _):
        at = pl.multiple_of(256 * i, 256)
        chip_out[pl.ds(at, 256), :] = chip_part(FRAMES + at).astype(BF16)
        return 0

    def own_frames(i, _):
        at = pl.multiple_of(256 * i, 256)
        chip_own[pl.ds(at, 256), :] = chip_part(at)
        return 0

    gains = gain[...].astype(F32).reshape(1, D)

    def norm_rows(i, total):
        at = pl.multiple_of(128 * i, 128)
        rows = pl.ds(at, 128)
        upstream = (
            chip_own[rows, :]
            + chip_in[rows, :].astype(F32)
            + halo[pl.ds(pl.multiple_of(at + 256 * (2 * c + y), 128), 128), :].astype(F32)
        )
        value = stem[rows, :]
        center = value - jnp.mean(value, axis=-1, keepdims=True)
        inverse = lax.rsqrt(jnp.mean(center * center, axis=-1, keepdims=True) + epsilon)
        unit_value = center * inverse
        scaled = upstream * gains
        inner = (
            scaled
            - jnp.mean(scaled, axis=-1, keepdims=True)
            - unit_value * jnp.mean(scaled * unit_value, axis=-1, keepdims=True)
        )
        low[rows, :] = (grad[rows, :] + inverse * inner).astype(BF16)
        return total + jnp.sum(upstream * unit_value, axis=0, keepdims=True)

    def skip_part(q):
        def skip_rows(i, _):
            value = dot(
                joint[pl.ds(pl.multiple_of(512 * i, 512), 512), :],
                low[:, SKIP_COLS * q : SKIP_COLS * (q + 1)],
            ).astype(BF16)
            for j in range(2):
                for m in range(2):
                    for half in range(2):
                        at = 256 * j + 128 * m + 32 * half
                        first, second = value[at : at + 32], value[at + 64 : at + 96]
                        skip_own[2 * q + half, i, j, m] = jnp.where(c == 0, first, second)
                        skip_out[2 * q + half, i, j, m] = jnp.where(c == 0, second, first)
            return 0

        lax.fori_loop(0, 4, skip_rows, 0)
        both = pl.ds(2 * q, 2)
        return links.send(skip_out.at[both], skip_r0.at[both], links.core)

    def skip_begin(q, copy):
        copy.wait_recv()
        for half in range(2):
            skips[q][half].add_core(skip_r0.at[2 * q + half])
            skips[q][half].send_first()

    def joined_part(i):
        value = dot_nt(low[...], wide_buf[pl.ds(256 * i, 256), :]).astype(BF16)
        out = o_in if i < 4 else o_skip
        out[:, pl.ds(256 * (i % 4), 256)] = value

    wo.begin(*got_wo)
    lax.fori_loop(0, 4, kv_rows, 0)
    join_v, join_k = join(2), join(1)
    for one, got in ((p0, got_p[0]), (p1, got_p[1]), (x0, got_x[0]), (x1, got_x[1])):
        one.begin(*got)
    rest_q.begin(*got_q)
    rest_z.begin(*got_z)
    got_small.wait()
    small.send()
    join_v.wait_recv()
    unit_v.send_first()
    join_k.wait_recv()
    unit_k.send_first()
    got_dq.wait()
    lax.fori_loop(0, 4, q_rows, 0)
    join_q = join(0)
    got_wskip = load(wskip_in, wide_buf)
    got_wq.wait()
    lax.fori_loop(0, 2, other_frames, 0)
    chip_core = links.send(chip_out, chip_in, links.core)
    join_q.wait_recv()
    unit_q.send_first()
    lax.fori_loop(0, 2, own_frames, 0)
    wo.turn_second()
    halo_y.wait_recv()
    halo_rest = links.send(part, part, links.core)
    small.turn()
    chip_core.wait_recv()
    got_stem.wait()
    got_grad.wait()
    halo_rest.wait_recv()
    total = lax.fori_loop(0, 4, norm_rows, jnp.zeros((1, D), F32))
    gain_steps[0] = jnp.concatenate(
        [total[:, 128 * i : 128 * (i + 1)] for i in range(8)], axis=0
    )
    gain_sum.send()
    got_joint.wait()
    p0.turn_third()
    rest_q.turn_third()
    skip_core0 = skip_part(0)
    skip_core1 = skip_part(1)
    skip_begin(0, skip_core0)
    skip_core2 = skip_part(2)
    p1.turn_third()
    skip_begin(1, skip_core1)
    skip_core3 = skip_part(3)
    rest_z.turn_third()
    skip_begin(2, skip_core2)
    wo.turn_third()
    skip_begin(3, skip_core3)
    got_wskip.wait()
    joined_part(0)
    small.turn()
    joined_part(1)
    gain_sum.turn()
    joined_part(2)
    joined_part(3)
    x0.turn_third()
    unit_v.turn_first()
    joined_part(4)
    joined_part(5)
    joined_part(6)
    joined_part(7)
    p0.turn_fourth()
    skips[0][0].turn_first()
    x1.turn_third()
    p1.turn_fourth()
    skips[1][0].turn_first()
    unit_q.turn_first()
    skips[2][0].turn_first()
    skips[0][1].turn_first()
    skips[3][0].turn_first()
    gain_sum.turn()
    p0.finish()
    p1.finish()
    skips[1][1].turn_first()
    unit_k.turn_first()
    x0.turn_fourth()
    skips[2][1].turn_first()
    unit_v.turn_second()
    skips[3][1].turn_first()
    rest_q.finish()
    small.turn()
    skips[0][0].turn_second()
    x1.turn_fourth()
    x0.finish()
    rest_z.finish()
    unit_q.turn_second()
    unit_v.turn_third()
    skips[1][0].turn_second()
    skips[0][1].turn_second()
    skips[2][0].turn_second()
    wo.finish()
    skips[1][1].turn_second()
    unit_q.turn_third()
    x1.finish()
    skips[3][0].turn_second()
    unit_v.turn_fourth()
    gain_sum.turn()
    skips[2][1].turn_second()
    take_up()
    skips[3][1].turn_second()
    small.turn()
    unit_k.turn_second()
    unit_q.turn_fourth()
    skips[0][0].finish()
    unit_k.turn_third()
    skips[1][0].finish()
    unit_v.finish()
    skips[0][1].finish()
    skips[2][0].finish()
    gain_sum.turn()
    skips[1][1].finish()
    skips[3][0].finish()
    unit_q.finish()
    skips[2][1].finish()
    gain_sum.turn()
    skips[3][1].finish()
    small.turn()
    unit_k.finish()
    links.drain()


def tail(late, small, dq, dkv, seen, wqkv, joint, stem, grad, gain, wskip):
    hbm, vm = pl.BlockSpec(memory_space=HBM), pl.BlockSpec(memory_space=VMEM)
    n_small = small.shape[0]
    out_shape = [
        jax.ShapeDtypeStruct((FRAMES, D), BF16),
        jax.ShapeDtypeStruct((FRAMES, D), BF16),
        jax.ShapeDtypeStruct((128, D), F32),
        jax.ShapeDtypeStruct((32, 4096), F32),
        jax.ShapeDtypeStruct((32, 3 * D), F32),
        jax.ShapeDtypeStruct((32, D), F32),
        jax.ShapeDtypeStruct((64, D), F32),
        jax.ShapeDtypeStruct((n_small, 128), F32),
        jax.ShapeDtypeStruct((8, 128), F32),
    ]
    low = lambda *shape: pltpu.VMEM(shape, BF16)
    full = lambda *shape: pltpu.VMEM(shape, F32)
    skip = (ROWS, SKIP_COLS)
    copies = 116
    scratch = [
        low(CHIP, WIDTH),
        low(CHIP + HALO, D),
        low(2 * D, D),
        low(D, WIDTH),
        low(D, D),
        low(2 * D, FRAMES),
        full(FRAMES, D),
        full(FRAMES, D),
        low(FRAMES, D),
        low(FRAMES, D),
        full(FRAMES, D),
        low(HALF, D),
        low(HALF, D),
        low(HALF, D),
        low(HALO + 2 * EDGE, D),
        low(FRAMES, D),
        low(2, 2, 2, 2, ROWS, D),
        low(2, 2, 2, ROWS, D),
        low(2, 2, ROWS, D),
        low(2, ROWS, D),
        low(ROWS, D),
        low(2, 2, 2, 2, ROWS, WIDTH),
        low(2, 4, 64, P_COLS),
        low(2, 4, 64, P_COLS),
        low(2, 6, 64, P_COLS),
        low(2, 2, 128, D - P_COLS),
        low(2, 2, 128, D - P_COLS),
        low(2, 128, D - P_COLS),
        low(128, D - P_COLS),
        low(2, 4, 32, X_COLS),
        low(2, 4, 32, X_COLS),
        low(2, 6, 32, X_COLS),
        low(2, 2, 64, 2 * D - X_COLS),
        low(2, 2, 64, 2 * D - X_COLS),
        low(2, 64, 2 * D - X_COLS),
        low(64, 2 * D - X_COLS),
        full(32, 2 * D),
        full(32, 2 * D),
        low(2, 4, 2, 2, ROWS, D),
        low(2, 4, 2, ROWS, D),
        low(2, 4, ROWS, D),
        low(2, 6, ROWS, D),
        low(2, 2, 2, ROWS, D),
        low(2, 2, 2, ROWS, D),
        low(2, 2, ROWS, D),
        low(2, ROWS, D),
        low(ROWS, D),
        low(2, 4, 2, 2, ROWS, WIDTH),
        low(2 * SKIPS, 4, 2, 2, *skip),
        low(2 * SKIPS, 4, 2, 2, *skip),
        low(2 * SKIPS, 4, 2, 2, *skip),
        low(2 * SKIPS, 4, 2, *skip),
        low(2 * SKIPS, 4, *skip),
        low(2 * SKIPS, 3, *skip),
        full(64, X_COLS),
        full(5, n_small, 128),
        full(5, n_small, 128),
        full(5, 8, 128),
        full(5, 8, 128),
        pltpu.SemaphoreType.DMA((28,)),
        pltpu.SemaphoreType.DMA((copies,)),
        pltpu.SemaphoreType.DMA((copies,)),
    ]
    return pl.pallas_call(
        tail_kernel,
        out_shape=out_shape,
        in_specs=[hbm] * 18 + [vm, hbm],
        out_specs=[vm] * 9,
        scratch_shapes=scratch,
        name="tail",
        cost_estimate=pl.CostEstimate(
            flops=17_000_000_000, bytes_accessed=60_000_000, transcendentals=0
        ),
        compiler_params=pltpu.CompilerParams(
            collective_id=0, has_side_effects=True, vmem_limit_bytes=63 << 20
        ),
    )(
        *late[:6],
        *[value.reshape(2, 2, 64, 2 * D - X_COLS) for value in late[6:8]],
        *late[8:],
        small,
        dq,
        dkv,
        seen,
        wqkv,
        joint,
        stem,
        grad,
        gain,
        wskip,
    )


def finish_kernel(count, *refs):
    ins, small, gain = refs[:count], refs[count], refs[count + 1]
    outs, smalls = refs[count + 2 : 2 * count + 2], refs[2 * count + 2 : 2 * count + 6]
    held, loads, stores = refs[2 * count + 6 : 3 * count + 6], refs[-2], refs[-1]
    got = [pltpu.make_async_copy(a, b, loads.at[i]) for i, (a, b) in enumerate(zip(ins, held))]
    for copy in got:
        copy.start()
    device = lax.axis_index("rows") * 4 + lax.axis_index("seq")
    smalls[0][...] = small[pl.ds(device, 1), :]
    row, lane = device // 4, lax.rem(device, 4) * 32
    values = [gain[pl.ds(row, 1), :], small[pl.ds(32 + row, 1), :], small[pl.ds(40 + row, 1), :]]
    for out, value in zip(smalls[1:], values):
        out[...] = pltpu.roll(value, lax.rem(128 - lane, 128), 1)[:, :32]
    put = [pltpu.make_async_copy(a, b, stores.at[i]) for i, (a, b) in enumerate(zip(held, outs))]
    for copy, after in zip(got, put):
        copy.wait()
        after.start()
    for copy in put:
        copy.wait()


def finish(results, small, gain):
    hbm, vm = pl.BlockSpec(memory_space=HBM), pl.BlockSpec(memory_space=VMEM)
    count = len(results)
    return pl.pallas_call(
        functools.partial(finish_kernel, count),
        out_shape=[
            *[jax.ShapeDtypeStruct(a.shape, a.dtype) for a in results],
            *[jax.ShapeDtypeStruct((1, size), F32) for size in (128, 32, 32, 32)],
        ],
        in_specs=[hbm] * count + [vm] * 2,
        out_specs=[hbm] * count + [vm] * 4,
        scratch_shapes=[
            *[pltpu.VMEM(a.shape, a.dtype) for a in results],
            pltpu.SemaphoreType.DMA((count,)),
            pltpu.SemaphoreType.DMA((count,)),
        ],
        name="finish",
        compiler_params=pltpu.CompilerParams(vmem_limit_bytes=63 << 20),
    )(*results, small, gain)


def swap_low(value):
    return lax.ppermute(value, "rows", [(r, r ^ 2) for r in range(8)])


def swap_x(value):
    return lax.ppermute(value, "rows", [(r, r ^ 1) for r in range(8)])


def swap_chip(value):
    return lax.ppermute(value, "seq", [(i, i ^ 2) for i in range(4)])


def body_chips(
    inputs,
    skip_feats,
    seg_ids,
    frame_valid,
    w_skip,
    gain_one,
    w_qkv,
    w_out,
    gain_two,
    w_up,
    b_up,
    w_down,
    b_down,
    cotangent,
):
    here = lax.axis_index("seq")
    c = here % 2
    heads = H // 2
    first, second_in, cot = inputs[0], skip_feats[0], cotangent[0]
    stem_out, normed_seen, q, kv, joint = front(first, second_in, w_skip, gain_one, w_qkv)
    attended, attended_t, lse = attend(q, kv, seg_ids, frame_valid, 128, 256, heads)
    output, middle_grad, grad_heads, small, *sums = middle(
        attended,
        stem_out,
        w_out,
        gain_two,
        w_up,
        w_down,
        b_up.reshape(32, 128),
        b_down,
        cot,
    )
    late = []
    swaps = (swap_x, swap_chip, swap_chip, swap_x, swap_low)
    for here, away, swap in zip(sums[::2], sums[1::2], swaps):
        late += [here, swap(away)]
    dq, dkv, output = attend_back(
        q, kv, grad_heads, attended_t, lse, seg_ids, frame_valid, output, 128, 256, heads
    )
    *results, small_sum, gain_sum = tail(
        late,
        small,
        dq,
        dkv,
        normed_seen,
        w_qkv,
        joint,
        stem_out,
        middle_grad,
        gain_one,
        w_skip,
    )
    *results, up_bias, gain_a, gain_b, down_bias = finish(results, small_sum, gain_sum)
    input_grad, skip_grad, down_share, up_share, qkv_share, out_share, skip_share = results
    return (
        output[None],
        input_grad[None],
        skip_grad[None],
        skip_share,
        gain_a.reshape(32),
        qkv_share,
        out_share,
        gain_b.reshape(32),
        up_share,
        up_bias.reshape(128),
        down_share,
        down_bias.reshape(32),
    )


def block_scores(q_blk, pos_blk, seg_blk, all_keys, seg_row, valid_row, slopes, score_scale):
    key_pos = jnp.arange(all_keys.shape[0])
    scores = (
        jnp.einsum("qhd,khd->hqk", q_blk, all_keys, preferred_element_type=jnp.float32)
        * score_scale
    )
    distance = jnp.abs(pos_blk[:, None] - key_pos[None, :]).astype(jnp.float32)
    scores = scores - slopes[:, None, None] * distance[None]
    allowed = (seg_blk[:, None] == seg_row[None, :]) & (
        (valid_row[None, :] == 1) | (pos_blk[:, None] == key_pos[None, :])
    )
    return jnp.where(allowed[None], scores, -jnp.inf)


def split_row(packed_row, heads_local):
    length = packed_row.shape[0]
    qkv_rows = packed_row.reshape(length, 3, heads_local, HD)
    return (qkv_rows[:, 0], qkv_rows[:, 1], qkv_rows[:, 2])


def attend_row(packed_row, seg_row, valid_row, slopes, heads_local, block_rows, score_scale):
    length = packed_row.shape[0]
    queries, all_keys, all_values = split_row(packed_row, heads_local)
    count = length // block_rows
    positions = jnp.arange(length)

    def one_block(block_in):
        q_blk, pos_blk, seg_blk = block_in
        scores = block_scores(
            q_blk, pos_blk, seg_blk, all_keys, seg_row, valid_row, slopes, score_scale
        )
        peak = jnp.max(scores, axis=-1, keepdims=True)
        log_total = peak + jnp.log(jnp.sum(jnp.exp(scores - peak), axis=-1, keepdims=True))
        attn_probs = jnp.exp(scores - log_total).astype(jnp.bfloat16)
        attended = jnp.einsum(
            "hqk,khd->qhd", attn_probs, all_values, preferred_element_type=jnp.float32
        )
        return (attended.astype(jnp.bfloat16), log_total[..., 0])

    attended, log_total = lax.map(
        one_block,
        (
            queries.reshape(count, block_rows, heads_local, HD),
            positions.reshape(count, block_rows),
            seg_row.reshape(count, block_rows),
        ),
    )
    return (attended.reshape(length, 1, heads_local * HD), log_total)


def attend_row_back(
    packed_row,
    log_total,
    grad_row,
    seg_row,
    valid_row,
    slopes,
    heads_local,
    block_rows,
    score_scale,
):
    length = packed_row.shape[0]
    queries, all_keys, all_values = split_row(packed_row, heads_local)
    count = length // block_rows
    positions = jnp.arange(length)
    grad_out = grad_row.reshape(count, block_rows, heads_local, HD)

    def one_block(carry, block_in):
        key_grad, value_grad = carry
        q_blk, pos_blk, seg_blk, total_blk, grad_blk = block_in
        scores = block_scores(
            q_blk, pos_blk, seg_blk, all_keys, seg_row, valid_row, slopes, score_scale
        )
        soft = jnp.exp(scores - total_blk[..., None])
        value_grad = value_grad + jnp.einsum(
            "hqk,qhd->khd", soft.astype(jnp.bfloat16), grad_blk, preferred_element_type=jnp.float32
        )
        prob_grad = jnp.einsum(
            "qhd,khd->hqk", grad_blk, all_values, preferred_element_type=jnp.float32
        )
        score_grad = (
            soft * (prob_grad - jnp.sum(soft * prob_grad, axis=-1, keepdims=True))
        ).astype(jnp.bfloat16)
        query_grad = (
            jnp.einsum("hqk,khd->qhd", score_grad, all_keys, preferred_element_type=jnp.float32)
            * score_scale
        )
        key_grad = (
            key_grad
            + jnp.einsum("hqk,qhd->khd", score_grad, q_blk, preferred_element_type=jnp.float32)
            * score_scale
        )
        return ((key_grad, value_grad), query_grad)

    zero_rows = jnp.zeros((length, heads_local, HD), jnp.float32)
    (key_grad, value_grad), query_grad = lax.scan(
        one_block,
        (zero_rows, zero_rows),
        (
            queries.reshape(count, block_rows, heads_local, HD),
            positions.reshape(count, block_rows),
            seg_row.reshape(count, block_rows),
            log_total,
            grad_out,
        ),
    )
    stacked = jnp.stack([query_grad.reshape(length, heads_local, HD), key_grad, value_grad], axis=1)
    return stacked.astype(jnp.bfloat16).reshape(length, 3, 1, heads_local * HD)


def body(
    inputs,
    skip_feats,
    seg_ids,
    frame_valid,
    w_skip,
    gain_one,
    w_qkv,
    w_out,
    gain_two,
    w_up,
    b_up,
    w_down,
    b_down,
    cotangent,
):
    parts = lax.axis_size("seq")
    heads_local = H // parts
    width_local = heads_local * HD
    rows_here = inputs.shape[0]
    frames = inputs.shape[1]
    length = frames * parts
    block_rows = min(512, length)
    score_scale = 1.0 / math.sqrt(HD)
    first_head = lax.axis_index("seq") * heads_local
    slopes = jnp.exp2(-8.0 * (first_head + jnp.arange(heads_local) + 1).astype(jnp.float32) / H)
    gain_first = gain_one.astype(jnp.float32)
    gain_second = gain_two.astype(jnp.float32)
    bias_up = b_up.astype(jnp.float32)
    joined = jnp.concatenate([inputs, skip_feats], axis=-1)
    stem_out = jnp.einsum("rfc,cd->rfd", joined, w_skip, preferred_element_type=jnp.float32)
    unit_one, inverse_one, normed = norm_forward(stem_out, gain_first)
    normed = normed.astype(jnp.bfloat16)
    packed = jnp.einsum("rfd,de->rfe", normed, w_qkv, preferred_element_type=jnp.float32).astype(
        jnp.bfloat16
    )
    packed = packed.reshape(rows_here, frames, 3, parts, width_local)
    by_heads = lax.all_to_all(packed, "seq", split_axis=3, concat_axis=1, tiled=True)

    def forward_row(row_data):
        return attend_row(
            row_data[0], row_data[1], row_data[2], slopes, heads_local, block_rows, score_scale
        )

    attended, log_total = lax.map(forward_row, (by_heads, seg_ids, frame_valid))
    by_frames = lax.all_to_all(attended, "seq", split_axis=1, concat_axis=2, tiled=True)
    mixed_out = by_frames.reshape(rows_here, frames, D)
    middle = stem_out + jnp.einsum(
        "rfd,de->rfe", mixed_out, w_out, preferred_element_type=jnp.float32
    )
    unit_two, inverse_two, second = norm_forward(middle, gain_second)
    second = second.astype(jnp.bfloat16)
    hidden = jnp.einsum("rfd,dk->rfk", second, w_up, preferred_element_type=jnp.float32) + bias_up
    active_full, gelu_back = jax.vjp(gelu_exact, hidden)
    active = active_full.astype(jnp.bfloat16)
    result = (
        middle
        + jnp.einsum("rfk,kd->rfd", active, w_down, preferred_element_type=jnp.float32)
        + b_down.astype(jnp.float32)
    )
    output = result.astype(jnp.bfloat16)
    cot_full = cotangent.astype(jnp.float32)
    down_grad = jnp.einsum("rfk,rfd->kd", active, cotangent, preferred_element_type=jnp.float32)
    bias_down_grad = jnp.sum(cot_full, axis=(0, 1))
    active_grad = jnp.einsum("rfd,kd->rfk", cotangent, w_down, preferred_element_type=jnp.float32)
    hidden_grad = gelu_back(active_grad)[0].astype(jnp.bfloat16)
    up_grad = jnp.einsum("rfd,rfk->dk", second, hidden_grad, preferred_element_type=jnp.float32)
    bias_up_grad = jnp.sum(hidden_grad.astype(jnp.float32), axis=(0, 1))
    second_grad = jnp.einsum("rfk,dk->rfd", hidden_grad, w_up, preferred_element_type=jnp.float32)
    middle_part, gain_two_grad = norm_backward(second_grad, unit_two, inverse_two, gain_second)
    middle_grad = cot_full + middle_part
    middle_low = middle_grad.astype(jnp.bfloat16)
    out_grad = jnp.einsum("rfd,rfe->de", mixed_out, middle_low, preferred_element_type=jnp.float32)
    mixed_grad = jnp.einsum(
        "rfe,de->rfd", middle_low, w_out, preferred_element_type=jnp.float32
    ).astype(jnp.bfloat16)
    grad_heads = lax.all_to_all(
        mixed_grad.reshape(rows_here, frames, parts, width_local),
        "seq",
        split_axis=2,
        concat_axis=1,
        tiled=True,
    )

    def backward_row(row_data):
        return attend_row_back(
            row_data[0],
            row_data[1],
            row_data[2],
            row_data[3],
            row_data[4],
            slopes,
            heads_local,
            block_rows,
            score_scale,
        )

    packed_grad = lax.map(backward_row, (by_heads, log_total, grad_heads, seg_ids, frame_valid))
    packed_back = lax.all_to_all(packed_grad, "seq", split_axis=1, concat_axis=3, tiled=True)
    packed_back = packed_back.reshape(rows_here, frames, 3 * D)
    qkv_grad = jnp.einsum("rfd,rfe->de", normed, packed_back, preferred_element_type=jnp.float32)
    normed_grad = jnp.einsum("rfe,de->rfd", packed_back, w_qkv, preferred_element_type=jnp.float32)
    stem_part, gain_one_grad = norm_backward(normed_grad, unit_one, inverse_one, gain_first)
    stem_low = (middle_grad + stem_part).astype(jnp.bfloat16)
    skip_w_grad = jnp.einsum("rfc,rfd->cd", joined, stem_low, preferred_element_type=jnp.float32)
    joined_grad = jnp.einsum("rfd,cd->rfc", stem_low, w_skip, preferred_element_type=jnp.float32)
    input_grad = joined_grad[..., :D].astype(jnp.bfloat16)
    skip_grad = joined_grad[..., D:].astype(jnp.bfloat16)
    (
        skip_share,
        gain_one_share,
        qkv_share,
        out_share,
        gain_two_share,
        up_share,
        bias_up_share,
        down_share,
        bias_down_share,
    ) = (
        lax.psum_scatter(skip_w_grad, ("rows", "seq"), scatter_dimension=0, tiled=True),
        lax.psum_scatter(gain_one_grad, ("rows", "seq"), scatter_dimension=0, tiled=True),
        lax.psum_scatter(qkv_grad, ("rows", "seq"), scatter_dimension=0, tiled=True),
        lax.psum_scatter(out_grad, ("rows", "seq"), scatter_dimension=0, tiled=True),
        lax.psum_scatter(gain_two_grad, ("rows", "seq"), scatter_dimension=0, tiled=True),
        lax.psum_scatter(up_grad, ("rows", "seq"), scatter_dimension=0, tiled=True),
        lax.psum_scatter(bias_up_grad, ("rows", "seq"), scatter_dimension=0, tiled=True),
        lax.psum_scatter(down_grad, ("rows", "seq"), scatter_dimension=0, tiled=True),
        lax.psum_scatter(bias_down_grad, ("rows", "seq"), scatter_dimension=0, tiled=True),
    )
    return (
        output,
        input_grad,
        skip_grad,
        skip_share,
        gain_one_share,
        qkv_share,
        out_share,
        gain_two_share,
        up_share,
        bias_up_share,
        down_share,
        bias_down_share,
    )


def solution(mesh):
    fits = (mesh.shape["rows"], mesh.shape["seq"]) == (8, 4)
    return jax.shard_map(
        body_chips if fits else body,
        mesh=mesh,
        in_specs=(
            P("rows", "seq", None),
            P("rows", "seq", None),
            P("rows", None),
            P("rows", None),
            P(),
            P(),
            P(),
            P(),
            P(),
            P(),
            P(),
            P(),
            P(),
            P("rows", "seq", None),
        ),
        out_specs=(
            P("rows", "seq", None),
            P("rows", "seq", None),
            P("rows", "seq", None),
            P(("rows", "seq"), None),
            P(("rows", "seq")),
            P(("rows", "seq"), None),
            P(("rows", "seq"), None),
            P(("rows", "seq")),
            P(("rows", "seq"), None),
            P(("rows", "seq")),
            P(("rows", "seq"), None),
            P(("rows", "seq")),
        ),
        check_vma=False,
    )
```

```python
import functools
import math

import jax
import jax.numpy as jnp
from jax import lax
from jax.experimental import pallas as pl
from jax.experimental.pallas import tpu as pltpu
from jax.sharding import PartitionSpec as P

D = 1024
H = 16
HD = 64
MOST = 682

epsilon = 1e-05

F32 = jnp.float32
BF16 = jnp.bfloat16
LOG2E = 1.4426950408889634
ROWS = 32
CHIP = 1024
HALO = 768
FRAMES = 512
HALF = HALO // 2
EDGE = CHIP - HALO
WIDTH = D // 2
SKIPS = 4
SKIP_COLS = D // SKIPS
FAR = 1e30
VMEM_ALL = 67_043_328
MESH = pl.DeviceIdType.MESH
VMEM = pltpu.MemorySpace.VMEM
SMEM = pltpu.MemorySpace.SMEM
HBM = pltpu.MemorySpace.HBM


def norm_forward(value, gain_vec):
    center = value - jnp.mean(value, axis=-1, keepdims=True)
    spread = jnp.mean(center * center, axis=-1, keepdims=True)
    inverse = lax.rsqrt(spread + epsilon)
    unit = center * inverse
    return (unit, inverse, unit * gain_vec)


def norm_backward(upstream, unit, inverse, gain_vec):
    scaled = upstream * gain_vec
    gain_grad = jnp.sum(upstream * unit, axis=tuple(range(upstream.ndim - 1)))
    inner = (
        scaled
        - jnp.mean(scaled, axis=-1, keepdims=True)
        - unit * jnp.mean(scaled * unit, axis=-1, keepdims=True)
    )
    return (inverse * inner, gain_grad)


def gelu_exact(value):
    return jax.nn.gelu(value, approximate=False)


def mm(equation, left, right):
    return jnp.einsum(equation, left, right, preferred_element_type=F32)


def dot(left, right):
    return jnp.dot(left, right, preferred_element_type=F32)


def dot_nt(left, right):
    return lax.dot_general(left, right, (((1,), (1,)), ((), ())), preferred_element_type=F32)


def dot_tn(left, right):
    return lax.dot_general(left, right, (((0,), (0,)), ((), ())), preferred_element_type=F32)


class Links:
    def __init__(self, sends, recvs):
        row, col = lax.axis_index("rows"), lax.axis_index("seq")
        self.z, self.x, self.y, self.c = row // 2, row % 2, col // 2, col % 2
        z, x, y, c = self.z, self.x, self.y, self.c
        self.high, self.low = z // 2, z % 2
        self.is_end = z == 3 * self.high
        self.is_inner = z == 1 + self.high
        self.core = (row, y * 2 + 1 - c)
        self.over_y = (row, (1 - y) * 2 + c)
        self.over_x = (z * 2 + 1 - x, col)
        self.over_low = ((self.high * 2 + 1 - self.low) * 2 + x, col)
        self.over_high = (((1 - self.high) * 2 + self.low) * 2 + x, col)
        self.over_mirror = ((3 - z) * 2 + x, col)
        self.sends, self.recvs, self.count, self.started = sends, recvs, 0, []

    def greet(self, near=False):
        barrier = pltpu.get_barrier_semaphore()
        peers = [self.core, self.over_y]
        if not near:
            peers += [self.over_x, self.over_low, self.over_high, self.over_mirror]
        for peer in peers:
            pl.semaphore_signal(barrier, inc=1, device_id=peer, device_id_type=MESH)
        pl.semaphore_wait(barrier, len(peers))

    def reserve(self, number):
        self.count += number
        return self.count - number

    def copy(self, src, dst, at, peer):
        return pltpu.make_async_remote_copy(
            src, dst, self.sends.at[at], self.recvs.at[at], device_id=peer, device_id_type=MESH
        )

    def send(self, src, dst, peer, here=None):
        copy = self.copy(src, dst, self.reserve(1), peer)
        if here is None:
            copy.start()
        else:
            pl.when(here)(copy.start)
        self.started.append((copy, here))
        return copy

    def drain(self):
        assert self.count <= self.sends.shape[0]
        for copy, here in self.started:
            if here is None:
                copy.wait_send()
            else:
                pl.when(here)(copy.wait_send)


def head_columns(wqkv, part, core):
    return wqkv.at[:, pl.ds(pl.multiple_of(D * part + WIDTH * core, WIDTH), WIDTH)]


def front_kernel(*refs):
    first_in, second_in, wskip_in, gain, wqkv_in = refs[:5]
    outs = refs[5:10]
    first, second, wskip, wq, wkv, o_stem, o_seen, o_q, o_kv, o_joint, loads, stores, sends, recvs = refs[10:]
    storing = []

    def store(k, *at):
        src, dst = (o_stem, o_seen, o_q, o_kv, o_joint)[k].at[*at], outs[k].at[*at]
        copy = pltpu.make_async_copy(src, dst, stores.at[len(storing)])
        copy.start()
        storing.append(copy)

    links = Links(sends, recvs)
    y, c = links.y, links.c
    loading = []

    def load(src, dst):
        copy = pltpu.make_async_copy(src, dst, loads.at[len(loading)])
        copy.start()
        loading.append(copy)
        return copy

    got = [load(first_in, first), load(second_in, second), load(wskip_in, wskip)]
    got_wkv = [
        load(head_columns(wqkv_in, 1 + i, c), wkv.at[:, pl.ds(WIDTH * i, WIDTH)]) for i in (0, 1)
    ]
    got_wq = load(head_columns(wqkv_in, 0, c), wq)
    links.greet(near=True)
    for copy in got:
        copy.wait()
    gains = gain[...].astype(F32).reshape(1, D)
    base = jnp.where(y == 0, EDGE, 0) + HALF * c

    def piece(i, chip):
        return 128 * jnp.where(chip == 0, i, 2 - i)

    def send_piece(i):
        at = lax.rem(base + piece(i, y) + FRAMES * c, CHIP)
        there = CHIP + HALF * c + piece(i, y)
        src = o_seen.at[pl.ds(pl.multiple_of(at, 128), 128)]
        dst = o_seen.at[pl.ds(pl.multiple_of(there, 128), 128)]
        return links.send(src, dst, links.over_y)

    pieces, across = [], []
    for turn in range(2):
        at = pl.multiple_of(256 * (1 - c if turn == 0 else c), 256)
        rows = pl.ds(at, 256)
        value = dot(first[rows, :], wskip[:D, :]) + dot(second[rows, :], wskip[D:, :])
        o_stem[rows, :] = value
        center = value - jnp.mean(value, axis=-1, keepdims=True)
        rate = lax.rsqrt(jnp.mean(center * center, axis=-1, keepdims=True) + epsilon)
        o_seen[rows, :] = (center * rate * gains).astype(BF16)
        pieces.append(send_piece(turn))
        there = o_seen.at[pl.ds(pl.multiple_of(FRAMES + at, 256), 256)]
        across.append(links.send(o_seen.at[rows], there, links.core))
    store(0, pl.ds(0, FRAMES))
    for copy in across:
        copy.wait_recv()
    pieces.append(send_piece(2))
    store(1, pl.ds(0, CHIP))
    for copy in (*got_wkv, got_wq):
        copy.wait()

    def own_part(i, _):
        rows = pl.ds(pl.multiple_of(256 * i, 256), 256)
        o_q[rows, :] = dot(o_seen[rows, :], wq[...]).astype(BF16)
        o_kv[rows, :] = dot(o_seen[rows, :], wkv[...]).astype(BF16)
        return 0

    lax.fori_loop(0, 4, own_part, 0)
    store(2, pl.ds(0, CHIP))
    store(3, pl.ds(0, CHIP))
    o_joint[:D, :] = first[...].T
    forward = []

    def far_part(i, core):
        at = pl.multiple_of(CHIP + HALF * core + piece(i, 1 - y), 128)
        rows = pl.ds(at, 128)
        o_kv[rows, :] = dot(o_seen[rows, :], wkv[...]).astype(BF16)

    for i in range(3):
        pieces[i].wait_recv()
        at = pl.multiple_of(CHIP + HALF * c + piece(i, 1 - y), 128)
        rows = o_seen.at[pl.ds(at, 128)]
        forward.append(links.send(rows, rows, links.core))
        if i == 0:
            o_joint[D:, :] = second[...].T
            store(4, pl.ds(0, 2 * D))
        far_part(i, c)
        if i > 0:
            forward[i - 1].wait_recv()
            far_part(i - 1, 1 - c)
    forward[2].wait_recv()
    store(1, pl.ds(CHIP, HALO))
    far_part(2, 1 - c)
    store(3, pl.ds(CHIP, HALO))
    links.drain()
    for copy in storing:
        copy.wait()


def front(first, second, wskip, gain, wqkv):
    hbm, vm = pl.BlockSpec(memory_space=HBM), pl.BlockSpec(memory_space=VMEM)
    low = lambda *shape: pltpu.VMEM(shape, BF16)
    return pl.pallas_call(
        front_kernel,
        out_shape=[
            jax.ShapeDtypeStruct((FRAMES, D), F32),
            jax.ShapeDtypeStruct((CHIP + HALO, D), BF16),
            jax.ShapeDtypeStruct((CHIP, WIDTH), BF16),
            jax.ShapeDtypeStruct((CHIP + HALO, 2 * WIDTH), BF16),
            jax.ShapeDtypeStruct((2 * D, FRAMES), BF16),
        ],
        in_specs=[hbm] * 3 + [vm, hbm],
        out_specs=[hbm] * 5,
        scratch_shapes=[
            low(FRAMES, D),
            low(FRAMES, D),
            low(2 * D, D),
            low(D, WIDTH),
            low(D, 2 * WIDTH),
            pltpu.VMEM((FRAMES, D), F32),
            low(CHIP + HALO, D),
            low(CHIP, WIDTH),
            low(CHIP + HALO, 2 * WIDTH),
            low(2 * D, FRAMES),
            pltpu.SemaphoreType.DMA((6,)),
            pltpu.SemaphoreType.DMA((7,)),
            pltpu.SemaphoreType.DMA((8,)),
            pltpu.SemaphoreType.DMA((8,)),
        ],
        name="front",
        cost_estimate=pl.CostEstimate(
            flops=8_000_000_000, bytes_accessed=24_000_000, transcendentals=0
        ),
        compiler_params=pltpu.CompilerParams(
            collective_id=2, has_side_effects=True, vmem_limit_bytes=VMEM_ALL
        ),
    )(first, second, wskip, gain, wqkv)


class Frames:
    def __init__(self, seg_at, seg, valid, key_code, query_seg):
        here = lax.axis_index("seq")
        self.seg_at = seg_at
        self.own, self.other = FRAMES * here, FRAMES * (here + 1 - 2 * (here % 2))
        self.halo = jnp.where(here // 2 == 0, CHIP, CHIP - HALO)
        self.core = here % 2
        places = [(0, FRAMES, self.own), (FRAMES, FRAMES, self.other), (CHIP, HALO, self.halo)]
        for at, count, frame in places:
            span = pl.ds(pl.multiple_of(frame, 256), count)
            code = jnp.where(valid[0:1, span] == 1, seg[0:1, span], -1).astype(F32)
            key_code[pl.ds(at, count), :] = jnp.broadcast_to(code, (128, count)).T
            if at < CHIP:
                query_seg[:, pl.ds(at, count)] = jnp.broadcast_to(
                    seg[0:1, span].astype(F32), (8, count)
                )

    def frame(self, at):
        late = jnp.where(at < CHIP, self.other - FRAMES, self.halo - CHIP)
        return at + jnp.where(at < FRAMES, self.own, late)

    def meet(self, keys_at, keys, queries_at, queries):
        k, q = self.frame(keys_at), self.frame(queries_at)
        return (self.seg_at[0, k] <= self.seg_at[0, q + queries - 1]) & (
            self.seg_at[0, k + keys - 1] >= self.seg_at[0, q]
        )

    def slope(self, h):
        values = [LOG2E * 2.0 ** (-8.0 * (core * H // 2 + h + 1) / H) for core in (0, 1)]
        return jnp.where(self.core == 0, values[0], values[1])


def set_distances(dist, key_at, query_at, key_code, query_seg):
    keys, queries = dist.shape
    rows = lax.broadcasted_iota(jnp.int32, (keys, queries), 0) + key_at
    cols = lax.broadcasted_iota(jnp.int32, (keys, queries), 1) + query_at
    apart = jnp.abs(rows - cols)
    allowed = (key_code == query_seg) | (apart == 0)
    dist[...] = jnp.where(allowed, apart.astype(F32), FAR)


def wide(code, queries):
    return jnp.concatenate([code] * (queries // 128), axis=1) if queries > 128 else code


def both_heads(ref, pair, queries):
    first = ref[pl.ds(128 * pair, HD), queries]
    second = ref[pl.ds(128 * pair + HD, HD), queries]
    blank = jnp.zeros_like(first)
    return jnp.concatenate(
        [
            jnp.concatenate([first, blank], axis=0),
            jnp.concatenate([blank, second], axis=0),
        ],
        axis=1,
    )


def both_slopes(dist, frames, pair):
    value = dist[...]
    return jnp.concatenate(
        [value * frames.slope(2 * pair), value * frames.slope(2 * pair + 1)], axis=1
    )


def attend_kernel(
    bq,
    bk,
    heads,
    seg_at,
    q_in,
    kv_in,
    seg,
    valid,
    o_out,
    o_outt,
    lse,
    q,
    kv,
    out,
    outt,
    loads,
    stores,
    kcode,
    qseg,
    qt,
    vt,
    dist,
    acc,
    top,
    total,
    heads_q,
    scores,
    probs,
):
    width = heads * HD
    pairs = range(heads // 2)
    c1 = LOG2E / math.sqrt(HD)
    keys, values = pl.ds(0, width), pl.ds(width, width)
    got = [
        pltpu.make_async_copy(q_in, q, loads.at[0]),
        pltpu.make_async_copy(kv_in.at[:, values], kv.at[:, values], loads.at[1]),
        pltpu.make_async_copy(kv_in.at[:, keys], kv.at[:, keys], loads.at[2]),
    ]
    for copy in got:
        copy.start()
    frames = Frames(seg_at, seg, valid, kcode, qseg)
    got[0].wait()
    qt[...] = q[...].T
    got[1].wait()
    vt[...] = kv[:, width:].T
    got[2].wait()

    def results(i):
        rows = pl.ds(pl.multiple_of(i * bq, bq), bq)
        return [
            pltpu.make_async_copy(out.at[rows], o_out.at[rows], stores.at[0, i]),
            pltpu.make_async_copy(outt.at[:, rows], o_outt.at[:, rows], stores.at[1, i]),
        ]

    def q_block(i, _):
        queries = pl.ds(pl.multiple_of(i * bq, bq), bq)
        acc[...] = jnp.zeros_like(acc)
        total[...] = jnp.zeros_like(total)
        top[...] = jnp.full_like(top, -3e38)
        for pair in pairs:
            heads_q[pair] = both_heads(qt, pair, queries)

        def k_block(j, _):
            @pl.when(frames.meet(j * bk, bk, i * bq, bq))
            def _():
                ks = pl.ds(pl.multiple_of(j * bk, bk), bk)
                set_distances(
                    dist,
                    frames.frame(j * bk),
                    frames.frame(i * bq),
                    wide(kcode[ks, :], bq),
                    qseg[0:1, queries],
                )
                for pair in pairs:
                    scores[pair] = dot(kv[ks, pl.ds(128 * pair, 128)], heads_q[pair])
                fades = []
                for pair in pairs:
                    line = pl.ds(pair, 1)
                    score = scores[pair] * c1 - both_slopes(dist, frames, pair)
                    was = top[line, :]
                    now = jnp.maximum(was, jnp.max(score, axis=0, keepdims=True))
                    prob = jnp.exp2(score - now)
                    fade = jnp.exp2(was - now)
                    total[line, :] = total[line, :] * fade + jnp.sum(prob, axis=0, keepdims=True)
                    top[line, :] = now
                    probs[pair] = prob.astype(BF16)
                    fades.append(fade)
                for pair in pairs:
                    value = dot(vt[pl.ds(128 * pair, 128), ks], probs[pair])
                    for e in range(2):
                        at, lanes = pl.ds(128 * pair + HD * e, HD), slice(bq * e, bq * (e + 1))
                        acc[at, :] = (
                            acc[at, :] * fades[pair][:, lanes]
                            + value[HD * e : HD * (e + 1), lanes]
                        )

            return 0

        lax.fori_loop(0, kv.shape[0] // bk, k_block, 0)
        for pair in pairs:
            rate = 1.0 / total[pl.ds(pair, 1), :]
            for e in range(2):
                at = pl.ds(128 * pair + HD * e, HD)
                acc[at, :] = acc[at, :] * rate[:, bq * e : bq * (e + 1)]
        lse[:, pl.ds(pl.multiple_of(2 * i * bq, 2 * bq), 2 * bq)] = top[...] + jnp.log2(total[...])
        out[queries, :] = acc[...].T.astype(BF16)
        outt[:, queries] = acc[...].astype(BF16)
        for copy in results(i):
            copy.start()
        return 0

    count = q.shape[0] // bq
    lax.fori_loop(0, count, q_block, 0)

    def settle(i, _):
        for copy in results(i):
            copy.wait()
        return 0

    lax.fori_loop(0, count, settle, 0)


def attend(q, kv, seg, valid, bq, bk, heads):
    frames = q.shape[0]
    vm, sm, hbm = [pl.BlockSpec(memory_space=m) for m in (VMEM, SMEM, HBM)]
    return pl.pallas_call(
        functools.partial(attend_kernel, bq, bk, heads),
        out_shape=(
            jax.ShapeDtypeStruct((frames, heads * HD), BF16),
            jax.ShapeDtypeStruct((heads * HD, frames), BF16),
            jax.ShapeDtypeStruct((heads // 2, 2 * frames), F32),
        ),
        in_specs=[sm, hbm, hbm, vm, vm],
        out_specs=(hbm, hbm, vm),
        scratch_shapes=[
            pltpu.VMEM(q.shape, BF16),
            pltpu.VMEM(kv.shape, BF16),
            pltpu.VMEM((frames, heads * HD), BF16),
            pltpu.VMEM((heads * HD, frames), BF16),
            pltpu.SemaphoreType.DMA((3,)),
            pltpu.SemaphoreType.DMA((2, frames // bq)),
            pltpu.VMEM((kv.shape[0], 128), F32),
            pltpu.VMEM((8, frames), F32),
            pltpu.VMEM((heads * HD, frames), BF16),
            pltpu.VMEM((heads * HD, kv.shape[0]), BF16),
            pltpu.VMEM((bk, bq), F32),
            pltpu.VMEM((heads * HD, bq), F32),
            pltpu.VMEM((heads // 2, 2 * bq), F32),
            pltpu.VMEM((heads // 2, 2 * bq), F32),
            pltpu.VMEM((heads // 2, 2 * HD, 2 * bq), BF16),
            pltpu.VMEM((heads // 2, bk, 2 * bq), F32),
            pltpu.VMEM((heads // 2, bk, 2 * bq), BF16),
        ],
        name="attend",
        cost_estimate=pl.CostEstimate(
            flops=8_000_000_000, bytes_accessed=8_000_000, transcendentals=4_000_000
        ),
        compiler_params=pltpu.CompilerParams(vmem_limit_bytes=VMEM_ALL),
    )(seg, q, kv, seg, valid)


def attend_back_kernel(
    bq,
    bk,
    heads,
    seg_at,
    q_in,
    kv_in,
    grad_in,
    outt_in,
    lse,
    seg,
    valid,
    passed_in,
    o_dq,
    o_dkv,
    o_passed,
    q,
    kv,
    grad,
    outt,
    passed,
    dq,
    dkv,
    loads,
    stores,
    kcode,
    qseg,
    qt,
    kt,
    gradt,
    delta,
    dist,
    dqt,
    sums,
    heads_q,
    heads_g,
    rows_q,
    rows_g,
    scores,
    prob_grads,
    probs,
    score_grads,
):
    width = heads * HD
    pairs = range(heads // 2)
    c1 = LOG2E / math.sqrt(HD)
    scale = 1.0 / math.sqrt(HD)
    lane = lax.broadcasted_iota(jnp.int32, (bq, 128), 1)
    places = [(q_in, q), (grad_in, grad), (outt_in, outt), (kv_in, kv), (passed_in, passed)]
    got = [pltpu.make_async_copy(a, b, loads.at[i]) for i, (a, b) in enumerate(places)]
    for copy in got:
        copy.start()
    sums[...] = jnp.zeros_like(sums)
    frames = Frames(seg_at, seg, valid, kcode, qseg)
    got[0].wait()
    qt[...] = q[...].T
    got[1].wait()
    gradt[...] = grad[...].T
    got[2].wait()
    got[3].wait()
    kt[...] = kv[:, :width].T
    got[4].wait()
    stored = [pltpu.make_async_copy(passed, o_passed, stores.at[0])]
    stored[0].start()

    def dq_copy(i):
        rows = pl.ds(pl.multiple_of(i * bq, bq), bq)
        return pltpu.make_async_copy(dq.at[rows], o_dq.at[rows], stores.at[1 + i])

    def q_block(i, _):
        qs = pl.multiple_of(i * bq, bq)
        queries = pl.ds(qs, bq)
        dqt[...] = jnp.zeros_like(dqt)
        for pair in pairs:
            at = pl.ds(128 * pair, 128)
            heads_q[pair] = both_heads(qt, pair, queries)
            heads_g[pair] = both_heads(gradt, pair, queries)
            product = outt[at, queries].astype(F32) * gradt[at, queries].astype(F32)
            for e in range(2):
                rows = pl.ds(bq * e, bq)
                keep = (lane < HD) if e == 0 else (lane >= HD)
                for to, ref in ((rows_q, q), (rows_g, grad)):
                    value = ref[queries, at]
                    to[pair, rows, :] = jnp.where(keep, value, jnp.zeros_like(value))
                delta[pl.ds(pair, 1), rows] = jnp.sum(
                    product[HD * e : HD * (e + 1)], axis=0, keepdims=True
                )

        def k_block(j, _):
            @pl.when(frames.meet(j * bk, bk, i * bq, bq))
            def _():
                ks = pl.ds(pl.multiple_of(j * bk, bk), bk)
                set_distances(
                    dist,
                    frames.frame(j * bk),
                    frames.frame(i * bq),
                    wide(kcode[ks, :], bq),
                    qseg[0:1, queries],
                )
                for pair in pairs:
                    scores[pair] = dot(kv[ks, pl.ds(128 * pair, 128)], heads_q[pair])
                    prob_grads[pair] = dot(
                        kv[ks, pl.ds(width + 128 * pair, 128)], heads_g[pair]
                    )
                lines = pl.ds(pl.multiple_of(2 * qs, 2 * bq), 2 * bq)
                for pair in pairs:
                    line = pl.ds(pair, 1)
                    prob = jnp.exp2(
                        scores[pair] * c1 - both_slopes(dist, frames, pair) - lse[line, lines]
                    )
                    probs[pair] = prob.astype(BF16)
                    score_grads[pair] = (prob * (prob_grads[pair] - delta[line, :])).astype(BF16)
                for pair in pairs:
                    at = pl.ds(128 * pair, 128)
                    sums[ks, pl.ds(width + 128 * pair, 128)] += dot(probs[pair], rows_g[pair])
                    sums[ks, at] += dot(score_grads[pair], rows_q[pair])
                    value = dot(kt[at, ks], score_grads[pair])
                    for e in range(2):
                        dqt[pl.ds(128 * pair + HD * e, HD), :] += value[
                            HD * e : HD * (e + 1), bq * e : bq * (e + 1)
                        ]

            return 0

        lax.fori_loop(0, kv.shape[0] // bk, k_block, 0)
        dq[pl.ds(qs, bq), :] = (dqt[...] * scale).T.astype(BF16)
        dq_copy(i).start()
        return 0

    count = q.shape[0] // bq
    lax.fori_loop(0, count, q_block, 0)
    parts = [(CHIP, HALO), (0, FRAMES), (FRAMES, FRAMES)]
    for i, (at, rows) in enumerate(parts):
        part = pl.ds(at, rows)
        dkv[part, :width] = (sums[part, :width] * scale).astype(BF16)
        dkv[part, width:] = sums[part, width:].astype(BF16)
        copy = pltpu.make_async_copy(dkv.at[part], o_dkv.at[part], stores.at[1 + count + i])
        copy.start()
        stored.append(copy)
    for copy in [*stored, *[dq_copy(i) for i in range(count)]]:
        copy.wait()


def attend_back(q, kv, grad, outt, lse, seg, valid, passed, bq, bk, heads):
    vm, sm, hbm = [pl.BlockSpec(memory_space=m) for m in (VMEM, SMEM, HBM)]
    return pl.pallas_call(
        functools.partial(attend_back_kernel, bq, bk, heads),
        out_shape=(
            jax.ShapeDtypeStruct(q.shape, BF16),
            jax.ShapeDtypeStruct(kv.shape, BF16),
            jax.ShapeDtypeStruct(passed.shape, passed.dtype),
        ),
        in_specs=[sm] + [hbm] * 4 + [vm] * 3 + [hbm],
        out_specs=(hbm, hbm, hbm),
        scratch_shapes=[
            pltpu.VMEM(q.shape, BF16),
            pltpu.VMEM(kv.shape, BF16),
            pltpu.VMEM(grad.shape, BF16),
            pltpu.VMEM(outt.shape, BF16),
            pltpu.VMEM(passed.shape, passed.dtype),
            pltpu.VMEM(q.shape, BF16),
            pltpu.VMEM(kv.shape, BF16),
            pltpu.SemaphoreType.DMA((5,)),
            pltpu.SemaphoreType.DMA((4 + q.shape[0] // bq,)),
            pltpu.VMEM((kv.shape[0], 128), F32),
            pltpu.VMEM((8, q.shape[0]), F32),
            pltpu.VMEM((heads * HD, q.shape[0]), BF16),
            pltpu.VMEM((heads * HD, kv.shape[0]), BF16),
            pltpu.VMEM((heads * HD, q.shape[0]), BF16),
            pltpu.VMEM((heads // 2, 2 * bq), F32),
            pltpu.VMEM((bk, bq), F32),
            pltpu.VMEM((heads * HD, bq), F32),
            pltpu.VMEM(kv.shape, F32),
            *[pltpu.VMEM((heads // 2, 2 * HD, 2 * bq), BF16)] * 2,
            *[pltpu.VMEM((heads // 2, 2 * bq, 2 * HD), BF16)] * 2,
            *[pltpu.VMEM((heads // 2, bk, 2 * bq), F32)] * 2,
            *[pltpu.VMEM((heads // 2, bk, 2 * bq), BF16)] * 2,
        ],
        name="attend_back",
        cost_estimate=pl.CostEstimate(
            flops=20_000_000_000, bytes_accessed=16_000_000, transcendentals=4_000_000
        ),
        compiler_params=pltpu.CompilerParams(vmem_limit_bytes=VMEM_ALL),
    )(seg, q, kv, grad, outt, lse, seg, valid, passed)


def add_into(value, other):
    def step(i, _):
        value[i] = value[i] + other[i]
        return 0

    lax.fori_loop(0, value.shape[0], step, 0)


class Unit:
    def __init__(self, links, own, came, sums, y_first, done, straight=False):
        self.links, self.own, self.came, self.sums = links, own, came, sums
        self.y_first, self.done, self.straight = y_first, done, straight

    def add_core(self, r0):
        for k in range(4):
            for i in range(2):
                add_into(self.own.at[k, i], r0.at[k, i])

    def send_first(self):
        n, a = self.links, self.own
        if self.y_first:
            self.first = n.send(a.at[:, :, 1 - n.y], self.came[0], n.over_y)
        else:
            self.first = n.send(a.at[:, 1 - n.x], self.came[0], n.over_x)

    def turn_first(self):
        self.first.wait_recv()
        n, a, b = self.links, self.own, self.came[0]
        for k in range(4):
            add_into(a.at[k, :, n.y] if self.y_first else a.at[k, n.x], b.at[k])
        if self.y_first:
            self.second = n.send(a.at[:, 1 - n.x, n.y], self.came[1], n.over_x)
        else:
            self.second = n.send(a.at[:, n.x, 1 - n.y], self.came[1], n.over_y)

    def chip(self, at):
        return self.own.at[at, self.links.x, self.links.y]

    def turn_second(self):
        self.second.wait_recv()
        self.after_second()

    def after_second(self):
        n, to = self.links, self.came[2]
        add_into(self.chip(slice(None)), self.came[1])
        if self.straight:
            low, high = 1 - n.low, 1 - n.high
            places = [(2 * n.high + low, n.over_low), (2 * high + n.low, n.over_high), (3 - n.z, n.over_mirror)]
            self.third = [n.send(self.chip(p), to.at[j], peer) for j, (p, peer) in enumerate(places)]
        else:
            part = self.chip(pl.ds(1 - n.high, 3))
            self.third = n.send(part, to.at[pl.ds(0, 3)], n.over_low, n.is_end)

    def turn_third(self):
        n = self.links

        @pl.when(n.is_inner)
        def _():
            self.third.wait_recv()
            add_into(self.chip(pl.ds(1 - n.high, 3)), self.came[2].at[pl.ds(0, 3)])

        part = self.chip(pl.ds(2 - 2 * n.high, 2))
        self.fourth = n.send(part, self.came[2].at[pl.ds(3, 2)], n.over_mirror, n.is_inner)

    def turn_fourth(self):
        n = self.links

        @pl.when(n.is_inner)
        def _():
            self.fourth.wait_recv()
            add_into(self.chip(pl.ds(2 * n.high, 2)), self.came[2].at[pl.ds(3, 2)])

        self.fifth = n.send(self.chip(3 * n.high), self.came[2].at[5], n.over_low, n.is_inner)

    def finish(self):
        n = self.links
        if self.straight:
            for copy in self.third:
                copy.wait_recv()
            value = self.chip(n.z)[...].astype(F32)
            for j in range(3):
                value = value + self.came[2][j].astype(F32)
            self.done(value)
            return
        self.sums[...] = self.chip(n.z)[...].astype(F32)

        @pl.when(n.is_end)
        def _():
            self.fifth.wait_recv()
            self.sums[...] += self.came[2][5].astype(F32)

        self.done(self.sums[...])


class LowUnit(Unit):
    def send_first(self):
        n = self.links
        self.first = n.send(self.own.at[:, 1 - n.low], self.came[0], n.over_low)

    def turn_first(self):
        self.first.wait_recv()
        n = self.links
        for k in range(2):
            for i in range(2):
                add_into(self.own.at[k, n.low, i], self.came[0].at[k, i])
        self.second = n.send(self.own.at[:, n.low, 1 - n.x], self.came[1], n.over_x)

    def turn_second(self):
        self.second.wait_recv()
        n = self.links
        for k in range(2):
            add_into(self.own.at[k, n.low, n.x], self.came[1].at[k])
        self.third = n.send(self.own.at[:, n.low, n.x, 1 - n.y], self.came[2], n.over_y)

    def turn_third(self):
        self.third.wait_recv()
        n = self.links
        add_into(self.own.at[:, n.low, n.x, n.y], self.came[2])
        self.fourth = n.send(self.own.at[1 - n.high, n.low, n.x, n.y], self.came[3], n.over_high)

    def finish(self):
        self.fourth.wait_recv()
        n = self.links
        value = self.own[n.high, n.low, n.x, n.y].astype(F32)
        self.done(value + self.came[3][...].astype(F32))


class HighUnit:
    def __init__(self, links, own, came, done):
        self.links, self.own, self.came, self.done = links, own, came, done

    def begin(self, *loads):
        for copy in loads:
            copy.wait()
        n = self.links
        for k in range(2):
            for i in range(2):
                add_into(self.own.at[k, i], self.came[0].at[k, i])
        self.second = n.send(self.own.at[:, 1 - n.x], self.came[1], n.over_x)

    def turn_second(self):
        self.second.wait_recv()
        n = self.links
        for k in range(2):
            add_into(self.own.at[k, n.x], self.came[1].at[k])
        self.third = n.send(self.own.at[:, n.x, 1 - n.y], self.came[2], n.over_y)

    def turn_third(self):
        self.third.wait_recv()
        n = self.links
        add_into(self.own.at[:, n.x, n.y], self.came[2])
        self.fourth = n.send(self.own.at[1 - n.high, n.x, n.y], self.came[3], n.over_high)

    def finish(self):
        self.fourth.wait_recv()
        n = self.links
        self.done(self.own[n.high, n.x, n.y].astype(F32) + self.came[3][...].astype(F32))


class LateUnit(Unit):
    def chip(self, at):
        return self.own.at[at]

    def begin(self, *loads):
        for copy in loads:
            copy.wait()
        self.after_second()


class PairUnit:
    def __init__(self, links, own, came, over_x, done):
        self.links, self.own, self.came, self.done = links, own, came, done
        self.at, self.peer = (links.x, links.over_x) if over_x else (links.y, links.over_y)

    def begin(self, *loads):
        for copy in loads:
            copy.wait()
        for k in range(2):
            add_into(self.own.at[k], self.came[0].at[k])
        self.third = self.links.send(self.own.at[:, 1 - self.at], self.came[1], self.peer)

    def turn_third(self):
        n = self.links
        self.third.wait_recv()
        for k in range(2):
            value = self.own.at[k, self.at]
            value[...] = value[...] + self.came[1][k]
        self.fourth = n.send(self.own.at[1 - n.high, self.at], self.came[2], n.over_high)

    def finish(self):
        self.fourth.wait_recv()
        value = self.own[self.links.high, self.at].astype(F32)
        self.done(value + self.came[2][...].astype(F32))


class Small:
    def __init__(self, links, steps, into, done):
        self.links, self.steps, self.into, self.done, self.at = links, steps, into, done, 0
        self.stages = [links.core, links.over_y, links.over_x, links.over_low, links.over_high]

    def send(self):
        self.flying = self.links.send(
            self.steps.at[self.at], self.into.at[self.at], self.stages[self.at]
        )

    def turn(self):
        self.flying.wait_recv()
        value = self.steps[self.at] + self.into[self.at]
        self.at += 1
        if self.at == len(self.stages):
            self.done(value)
        else:
            self.steps[self.at] = value
            self.send()


STEPS = 8
STEP = 256
P_COLS = 640
X_STEPS = 6
X_COLS = STEP * X_STEPS
UP_BLOCKS = [2 * i + j for i in (0, 2, 3, 5, 6, 7, 1, 4) for j in (0, 1)]


def middle_kernel(*refs):
    (
        att_in_hbm,
        stem_in,
        wout_in,
        gain,
        up_hbm,
        down_hbm,
        bias_up,
        bias_down,
        cot_in,
    ) = refs[:9]
    o_out, o_grad, o_heads, o_small = refs[9:13]
    o_p, o_p_away, o_q, o_q_away, o_x, o_x_away, o_z, o_z_away, o_wo, o_wo_away = refs[13:23]
    (
        att,
        att_came,
        stem,
        wout,
        ups,
        downs,
        cot,
        second,
        second_t,
        unit,
        inverse,
        active,
        hidden_grad,
        out_sum,
        grad_sum,
        low,
        swap_out,
        swap_in,
        p_send,
        p_keep,
        p_came,
        q_send,
        q_keep,
        q_came,
        x_send,
        x_keep,
        x_came,
        z_send,
        z_keep,
        z_came,
        biases,
        loads,
        sends,
        recvs,
    ) = refs[23:]
    links = Links(sends, recvs)
    x, y, c = links.x, links.y, links.c
    loading = []

    def load(src, dst):
        copy = pltpu.make_async_copy(src, dst, loads.at[len(loading)])
        copy.start()
        loading.append(copy)
        return copy

    own, other = pl.ds(0, FRAMES), pl.ds(FRAMES, FRAMES)
    got_att = load(att_in_hbm.at[own], att)
    got_wout = load(wout_in, wout)
    got_stem = load(stem_in, stem)
    got_cot = load(cot_in, cot.at[own])
    got_ups, got_downs = [], []
    for i in range(STEPS):
        for j in range(2):
            at = pl.multiple_of(128 * (4 * i + 2 * j + c), 128)
            part = pl.ds(128 * j, 128)
            got_ups.append(load(up_hbm.at[:, pl.ds(at, 128)], ups.at[i, :, part]))
            got_downs.append(load(down_hbm.at[pl.ds(at, 128), :], downs.at[i, part, :]))
    links.greet()
    att_core = links.send(att_in_hbm.at[other], att_came, links.core)
    cot_core = links.send(cot_in, cot.at[other], links.core)
    mine = pl.ds(pl.multiple_of(WIDTH * c, WIDTH), WIDTH)
    theirs = pl.ds(pl.multiple_of(WIDTH * (1 - c), WIDTH), WIDTH)

    got_att.wait()
    got_wout.wait()
    got_stem.wait()
    att_core.wait_recv()
    gains = gain[...].astype(F32).reshape(1, D)
    second_core = []
    for part in range(2):
        rows = pl.ds(256 * part, 256)
        value = stem[rows, :] + dot(att[rows, :], wout[mine, :]) + dot(att_came[rows, :], wout[theirs, :])
        stem[rows, :] = value
        center = value - jnp.mean(value, axis=-1, keepdims=True)
        rate = lax.rsqrt(jnp.mean(center * center, axis=-1, keepdims=True) + epsilon)
        normal = center * rate
        unit[rows, :] = normal
        inverse[rows, :] = jnp.broadcast_to(rate, (256, 128))
        second[rows, :] = (normal * gains).astype(BF16)
        second_core.append(
            links.send(second.at[rows], second.at[pl.ds(FRAMES + 256 * part, 256)], links.core)
        )
    second_t[:, :FRAMES] = second[own, :].T
    biases[...] = bias_up[...].astype(F32)
    out_sum[...] = jnp.zeros_like(out_sum)
    grad_sum[...] = jnp.zeros_like(grad_sum)
    o_small[...] = jnp.zeros_like(o_small)
    for copy in [got_cot, *got_ups, *got_downs]:
        copy.wait()
    cot_core.wait_recv()
    for copy in second_core:
        copy.wait_recv()
    second_t[:, FRAMES:] = second[other, :].T

    p_at, q_at, x_at, z_at = [links.reserve(k) for k in (STEPS, 4, X_STEPS, STEPS - X_STEPS)]

    def p_copy(i):
        return links.copy(p_send.at[i], p_came.at[i], p_at + i, links.over_y)

    def q_copy(i):
        return links.copy(q_send.at[i], q_came.at[i], q_at + i, links.over_low)

    def x_copy(i):
        return links.copy(x_send.at[i], x_came.at[i], x_at + i, links.over_x)

    def z_copy(i):
        return links.copy(z_send.at[i], z_came.at[i], z_at + i, links.over_low)

    def feed_step(i, _):
        up, down = ups[i], downs[i]
        bias = jnp.concatenate([biases[pl.ds(4 * i + 2 * j + c, 1), :] for j in (0, 1)], axis=1)
        total = jnp.zeros((1, STEP), F32)
        for half in (own, other):
            hidden = dot(second[half, :], up) + bias
            active_grad = dot_nt(cot[half, :], down)
            share = 0.5 + 0.5 * lax.erf(hidden * math.sqrt(0.5))
            slope = share + hidden * (
                jnp.exp(-0.5 * hidden * hidden) * (1.0 / math.sqrt(2.0 * math.pi))
            )
            a = (hidden * share).astype(BF16)
            g = (active_grad * slope).astype(BF16)
            active[half, :] = a
            hidden_grad[half, :] = g
            total = total + jnp.sum(g.astype(F32), axis=0, keepdims=True)
            out_sum[half, :] += dot(a, down)
            grad_sum[half, :] += dot_nt(g, up)
        for j in range(2):
            o_small[pl.ds(4 * i + 2 * j + c, 1), :] = total[:, 128 * j : 128 * (j + 1)]
        value = dot_tn(active[...], cot[...]).astype(BF16)
        p_send[i] = jnp.where(y == 0, value[128:, :P_COLS], value[:128, :P_COLS])
        p_keep[i] = jnp.where(y == 0, value[:128, :P_COLS], value[128:, :P_COLS])
        p_copy(i).start()
        stays = lax.rem(i // 2, 2) == links.low
        slot = 2 * (i // 4) + lax.rem(i, 2)
        rest = value[:, P_COLS:].reshape(2, 128, D - P_COLS)

        @pl.when(stays)
        def _():
            q_keep[slot] = rest

        @pl.when(jnp.logical_not(stays))
        def _():
            q_send[slot] = rest
            q_copy(slot).start()

        value = dot(second_t[...], hidden_grad[...]).astype(BF16)

        over_z = (lax.rem(i, 3) == 1) & (i < 6)

        @pl.when(jnp.logical_not(over_z))
        def _():
            j = i - jnp.where(i > 1, 1, 0) - jnp.where(i > 4, 1, 0)
            for k in range(4):
                first, last = value[256 * k : 256 * k + 128], value[256 * k + 128 : 256 * (k + 1)]
                x_send[j, k] = jnp.where(x == 0, last, first)
                x_keep[j, k] = jnp.where(x == 0, first, last)
            x_copy(j).start()

        @pl.when(over_z)
        def _():
            j = i // 4
            for k in range(2):
                first, last = value[512 * k : 512 * k + 256], value[512 * k + 256 : 512 * (k + 1)]
                z_send[j, k] = jnp.where(links.low == 0, last, first)
                z_keep[j, k] = jnp.where(links.low == 0, first, last)
            z_copy(j).start()

        return 0

    lax.fori_loop(0, STEPS, feed_step, 0)

    swap_out[0] = grad_sum[other, :].astype(BF16)
    grad_core = links.send(swap_out.at[0], swap_in.at[0], links.core)
    swap_out[1] = out_sum[other, :].astype(BF16)
    out_core = links.send(swap_out.at[1], swap_in.at[1], links.core)
    grad_core.wait_recv()

    def norm_rows(i, totals):
        rows = pl.ds(pl.multiple_of(128 * i, 128), 128)
        upstream = grad_sum[rows, :] + swap_in[0, rows, :].astype(F32)
        normal = unit[rows, :]
        scaled = upstream * gains
        inner = (
            scaled
            - jnp.mean(scaled, axis=-1, keepdims=True)
            - normal * jnp.mean(scaled * normal, axis=-1, keepdims=True)
        )
        value = cot[rows, :].astype(F32)
        grad = value + inverse[rows, 0:1] * inner
        o_grad[rows, :] = grad
        low[rows, :] = grad.astype(BF16)
        return (
            totals[0] + jnp.sum(upstream * normal, axis=0, keepdims=True),
            totals[1] + jnp.sum(value, axis=0, keepdims=True),
        )

    zero = jnp.zeros((1, D), F32)
    totals = lax.fori_loop(0, 4, norm_rows, (zero, zero))
    for k, value in enumerate(totals):
        for j in range(8):
            o_small[pl.ds(32 + 8 * k + j, 1), :] = value[:, 128 * j : 128 * (j + 1)]
    swap_out[2, :, :WIDTH] = dot_nt(low[...], wout[theirs, :]).astype(BF16)
    heads_core = links.send(
        swap_out.at[2, :, pl.ds(0, WIDTH)], swap_in.at[2, :, pl.ds(0, WIDTH)], links.core
    )
    o_heads[own, :] = dot_nt(low[...], wout[mine, :]).astype(BF16)

    def out_grad(high, value):
        value = value.astype(BF16)
        for low_bit in range(2):
            for i in range(2):
                for j in range(2):
                    at = 256 * low_bit + 128 * i + 64 * j
                    first, last = value[at : at + 32], value[at + 32 : at + 64]
                    rows = pl.multiple_of(256 * high + at // 2, 32)
                    second_t[pl.ds(rows, 32), :] = jnp.where(c == 0, first, last)
                    second_t[pl.ds(FRAMES + rows, 32), :] = jnp.where(c == 0, last, first)

    out_grad(c, dot_tn(att[...], low[...]))
    out_grad(1 - c, dot_tn(att_came[...], low[...]))
    wo_core = links.send(second_t.at[other], second.at[other], links.core)
    out_core.wait_recv()

    def out_rows(i, _):
        rows = pl.ds(pl.multiple_of(128 * i, 128), 128)
        o_out[rows, :] = (
            stem[rows, :]
            + (out_sum[rows, :] + swap_in[1, rows, :].astype(F32))
            + bias_down[...].astype(F32).reshape(1, D)
        ).astype(BF16)
        return 0

    lax.fori_loop(0, 4, out_rows, 0)
    heads_core.wait_recv()
    o_heads[other, :] = swap_in[2, :, :WIDTH]

    def add_p(i, _):
        p_copy(i).wait()
        value = p_keep[i] + p_came[i]
        stays = lax.rem(i, 2) == x

        @pl.when(stays)
        def _():
            o_p[i // 2] = value

        @pl.when(jnp.logical_not(stays))
        def _():
            o_p_away[i // 2] = value

        return 0

    def add_q(i, _):
        q_copy(i).wait()
        o_q[i // 2, lax.rem(i, 2)] = q_keep[i, y] + q_came[i, y]
        o_q_away[i // 2, lax.rem(i, 2)] = q_keep[i, 1 - y] + q_came[i, 1 - y]
        return 0

    def columns(i):
        return pl.ds(pl.multiple_of(STEP * i, STEP), STEP)

    def add_x(i, _):
        x_copy(i).wait()
        for k in range(4):
            value = x_keep[i, k] + x_came[i, k]
            o_x[k, :, columns(i)] = jnp.where(y == 0, value[:64], value[64:])
            o_x_away[k, :, columns(i)] = jnp.where(y == 0, value[64:], value[:64])
        return 0

    def add_z(i, _):
        z_copy(i).wait()
        for k in range(2):
            value = z_keep[i, k] + z_came[i, k]
            o_z[k, :, columns(i)] = jnp.where(x == 0, value[:128], value[128:])
            o_z_away[k, :, columns(i)] = jnp.where(x == 0, value[128:], value[:128])
        return 0

    wo_core.wait_recv()
    for high in range(2):
        for i in range(2):
            for j in range(2):
                for out, low_bit in ((o_wo, links.low), (o_wo_away, 1 - links.low)):
                    at = 256 * high + 128 * low_bit + 64 * i + 32 * j
                    rows = pl.ds(pl.multiple_of(at, 32), 32)
                    came = pl.ds(pl.multiple_of(FRAMES + at, 32), 32)
                    out[high, i, j] = second_t[rows, :] + second[came, :]
    lax.fori_loop(0, STEPS, add_p, 0)
    lax.fori_loop(0, 4, add_q, 0)
    lax.fori_loop(0, X_STEPS, add_x, 0)
    lax.fori_loop(0, STEPS - X_STEPS, add_z, 0)
    links.drain()


def middle(att, stem, wout, gain, w_up, w_down, bias_up, bias_down, cot):
    hbm, vm = pl.BlockSpec(memory_space=HBM), pl.BlockSpec(memory_space=VMEM)
    low = lambda *shape: pltpu.VMEM(shape, BF16)
    full = lambda *shape: pltpu.VMEM(shape, F32)
    copies = 29
    return pl.pallas_call(
        middle_kernel,
        out_shape=[
            jax.ShapeDtypeStruct((FRAMES, D), BF16),
            jax.ShapeDtypeStruct((FRAMES, D), F32),
            jax.ShapeDtypeStruct((CHIP, WIDTH), BF16),
            jax.ShapeDtypeStruct((48, 128), F32),
            *[jax.ShapeDtypeStruct((4, 128, P_COLS), BF16)] * 2,
            *[jax.ShapeDtypeStruct((2, 2, 128, D - P_COLS), BF16)] * 2,
            *[jax.ShapeDtypeStruct((4, 64, X_COLS), BF16)] * 2,
            *[jax.ShapeDtypeStruct((2, 128, 2 * D - X_COLS), BF16)] * 2,
            *[jax.ShapeDtypeStruct((2, 2, 2, ROWS, D), BF16)] * 2,
        ],
        in_specs=[hbm] * 3 + [vm] + [hbm] * 2 + [vm] * 2 + [hbm],
        out_specs=[vm] * 14,
        scratch_shapes=[
            low(FRAMES, WIDTH),
            low(FRAMES, WIDTH),
            full(FRAMES, D),
            low(D, D),
            low(STEPS, D, STEP),
            low(STEPS, STEP, D),
            low(CHIP, D),
            low(CHIP, D),
            low(D, CHIP),
            full(FRAMES, D),
            full(FRAMES, 128),
            low(CHIP, STEP),
            low(CHIP, STEP),
            full(CHIP, D),
            full(CHIP, D),
            low(FRAMES, D),
            low(3, FRAMES, D),
            low(3, FRAMES, D),
            *[low(STEPS, 128, P_COLS)] * 3,
            *[low(4, 2, 128, D - P_COLS)] * 3,
            *[low(X_STEPS, 4, 128, STEP)] * 3,
            *[low(STEPS - X_STEPS, 2, 256, STEP)] * 3,
            full(32, 128),
            pltpu.SemaphoreType.DMA((4 + 4 * STEPS,)),
            pltpu.SemaphoreType.DMA((copies,)),
            pltpu.SemaphoreType.DMA((copies,)),
        ],
        name="middle",
        cost_estimate=pl.CostEstimate(
            flops=28_000_000_000, bytes_accessed=40_000_000, transcendentals=4_000_000
        ),
        compiler_params=pltpu.CompilerParams(
            collective_id=1, has_side_effects=True, vmem_limit_bytes=VMEM_ALL
        ),
    )(att, stem, wout, gain, w_up, w_down, bias_up, bias_down, cot)


def tail_kernel(*refs):
    (
        p_in,
        p_came,
        q_in,
        q_came,
        x_in,
        x_came,
        z_in,
        z_came,
        wo_in,
        wo_came,
        small_in,
        dq_in,
        dkv_in,
        seen_in,
        wqkv_in,
        joint_in,
        stem_in,
        grad_in,
        gain,
        wskip_in,
    ) = refs[:20]
    o_in, o_skip, o_down, o_up, o_qkv, o_wo, o_wskip, o_small, o_gain = refs[20:29]
    (
        dq,
        dkv,
        wide_buf,
        wq,
        wkv,
        joint,
        stem,
        grad,
        chip_out,
        chip_in,
        chip_own,
        halo_out,
        halo_in,
        halo_sum,
        halo,
        low,
        low_own,
        low_r1,
        low_r2,
        low_r3,
        low_r4,
        join_low,
        p_own,
        p_r2,
        p_r3,
        q_own,
        q_r2,
        q_r3,
        q_r4,
        x_own,
        x_r2,
        x_r3,
        z_own,
        z_r2,
        z_r3,
        z_r4,
        up_out,
        up_in_last,
        unit_own,
        unit_r1,
        unit_r2,
        unit_r3,
        wo_own,
        wo_r1,
        wo_r2,
        wo_r3,
        wo_r4,
        join_out,
        skip_own,
        skip_out,
        skip_r0,
        skip_r1,
        skip_r2,
        skip_r3,
        sums,
        small_steps,
        small_into,
        gain_steps,
        gain_into,
        loads,
        sends,
        recvs,
    ) = refs[29:]
    links = Links(sends, recvs)
    y, c = links.y, links.c
    loading = []

    def load(src, dst):
        copy = pltpu.make_async_copy(src, dst, loads.at[len(loading)])
        copy.start()
        loading.append(copy)
        return copy

    seen = wide_buf.at[pl.ds(0, CHIP + HALO)]
    far, near = pl.ds(CHIP, HALO), pl.ds(0, CHIP)
    got_wkv = [load(head_columns(wqkv_in, 1 + i, c), wkv.at[:, pl.ds(WIDTH * i, WIDTH)]) for i in (0, 1)]
    got_far = load(dkv_in.at[far], dkv.at[far])
    links.greet()
    got_wo = [load(wo_in, wo_own), load(wo_came, wo_r1)]
    got_dq = load(dq_in, dq)
    got_near = load(dkv_in.at[near], dkv.at[near])
    got_seen = load(seen_in, seen)
    got_small = load(small_in, small_steps.at[0])
    got_p = [
        [
            load(p_in.at[:, pl.ds(64 * i, 64)], p_own.at[i]),
            load(p_came.at[:, pl.ds(64 * i, 64)], p_r2.at[i]),
        ]
        for i in range(2)
    ]
    got_x = []
    for i, core in enumerate((1 - c, c)):
        rows = pl.ds(pl.multiple_of(32 * core, 32), 32)
        got_x.append([load(x_in.at[:, rows], x_own.at[i]), load(x_came.at[:, rows], x_r2.at[i])])
    got_q = [load(q_in, q_own), load(q_came, q_r2)]
    got_z = [load(z_in, z_own), load(z_came, z_r2)]
    got_wq = load(head_columns(wqkv_in, 0, c), wq)
    got_stem = load(stem_in, stem)
    got_grad = load(grad_in, grad)
    got_joint = load(joint_in, joint)
    halo[pl.ds(0, EDGE), :] = jnp.zeros((EDGE, D), BF16)
    halo[pl.ds(EDGE + HALO, EDGE), :] = jnp.zeros((EDGE, D), BF16)

    def to_down(i):
        def done(value):
            o_down[pl.ds(64 * i, 64), pl.ds(0, P_COLS)] = value

        return done

    def to_down_rest(value):
        o_down[:, pl.ds(P_COLS, D - P_COLS)] = value

    def put_up(b, core, value):
        o_up[:, pl.ds(pl.multiple_of(256 * b + 128 * core, 128), 128)] = value

    def pass_up(at, value):
        part = pl.ds(at, value.shape[1])
        up_out[:, part] = value
        up_last.append(links.send(up_out.at[:, part], up_in_last.at[:, part], links.core))

    def to_up_other(value):
        pass_up(0, value)

    def to_up_mine(value):
        for t in range(X_COLS // 128):
            put_up(UP_BLOCKS[t], c, value[:, 128 * t : 128 * (t + 1)])

    def to_up_rest(value):
        pass_up(X_COLS, jnp.where(c == 0, value[32:], value[:32]))
        mine = jnp.where(c == 0, value[:32], value[32:])
        for t in range(X_COLS // 128, 16):
            at = 128 * t - X_COLS
            put_up(UP_BLOCKS[t], c, mine[:, at : at + 128])

    def take_up():
        for copy in up_last:
            copy.wait_recv()
        for t in range(16):
            put_up(UP_BLOCKS[t], 1 - c, up_in_last[:, 128 * t : 128 * (t + 1)])

    up_last = []

    def room(rows, cols):
        return sums.at[pl.ds(0, rows), pl.ds(0, cols)]

    p0, p1 = [
        LateUnit(
            links, p_own.at[i], (None, p_r2.at[i], p_r3.at[i]), room(64, P_COLS), True, to_down(i)
        )
        for i in range(2)
    ]
    x0, x1 = [
        LateUnit(
            links, x_own.at[i], (None, x_r2.at[i], x_r3.at[i]), room(32, X_COLS), False, done
        )
        for i, done in enumerate((to_up_other, to_up_mine))
    ]
    rest_q = PairUnit(links, q_own, (q_r2, q_r3, q_r4), True, to_down_rest)
    rest_z = PairUnit(links, z_own, (z_r2, z_r3, z_r4), False, to_up_rest)

    def to_wo(value):
        o_wo[...] = value

    def to_qkv(i):
        def done(value):
            o_qkv[:, pl.ds(D * i, D)] = value

        return done

    def to_wskip(q, half):
        def done(value):
            o_wskip[pl.ds(ROWS * half, ROWS), pl.ds(SKIP_COLS * q, SKIP_COLS)] = value

        return done

    def unit(k, y_first, done):
        came = (unit_r1.at[k], unit_r2.at[k], unit_r3.at[k])
        return Unit(links, unit_own.at[k], came, room(ROWS, D), y_first, done)

    wo = HighUnit(links, wo_own, (wo_r1, wo_r2, wo_r3, wo_r4), to_wo)
    unit_q, unit_v = unit(0, False, to_qkv(0)), unit(1, False, to_qkv(2))
    unit_k = LowUnit(links, low_own, (low_r1, low_r2, low_r3, low_r4), None, False, to_qkv(1))

    def skip_unit(k, y_first, done):
        came = (skip_r1.at[k], skip_r2.at[k], skip_r3.at[k])
        return Unit(links, skip_own.at[k], came, None, y_first, done, straight=True)

    skips = [
        [skip_unit(2 * q + half, half == 0, to_wskip(q, half)) for half in range(2)]
        for q in range(SKIPS)
    ]

    def to_small(value):
        o_small[...] = value

    def to_gain(value):
        o_gain[...] = value

    small = Small(links, small_steps, small_into, to_small)
    gain_sum = Small(links, gain_steps, gain_into, to_gain)

    for copy in (*got_wkv, got_far):
        copy.wait()

    def halo_part(core):
        at = pl.multiple_of(CHIP + HALF * core, 128)
        return dot_nt(dkv[pl.ds(at, HALF), :], wkv[...])

    halo_out[...] = halo_part(1 - c).astype(BF16)
    halo_core = links.send(halo_out, halo_in, links.core)
    mine = halo_part(c)
    halo_core.wait_recv()
    halo_sum[...] = (mine + halo_in[...].astype(F32)).astype(BF16)
    part_at = pl.ds(pl.multiple_of(EDGE + HALF * c, 128), HALF)
    part = halo.at[part_at]
    halo_y = links.send(halo_sum, part, links.over_y)
    got_near.wait()
    got_seen.wait()
    columns = pl.ds(pl.multiple_of(WIDTH * c, WIDTH), WIDTH)

    def place(k, i, value):
        value = value.astype(BF16)
        for j in range(2):
            for m in range(2):
                at = 128 * j + 64 * m
                first, second = value[at : at + 32], value[at + 32 : at + 64]
                mine, theirs = jnp.where(c == 0, first, second), jnp.where(c == 0, second, first)
                if k == 1:
                    low_own[i // 2, i % 2, j, m, :, columns] = mine
                else:
                    unit_own[k // 2, i, j, m, :, columns] = mine
                if k == 1:
                    join_low[i // 2, i % 2, j, m] = theirs
                else:
                    join_out[k // 2, i, j, m] = theirs

    def join(k):
        if k == 1:
            return links.send(join_low, low_own.at[:, :, :, :, :, columns], links.core)
        there = unit_own.at[k // 2, :, :, :, :, columns]
        return links.send(join_out.at[k // 2], there, links.core)

    def kv_rows(i, _):
        value = dot(seen[:, pl.ds(pl.multiple_of(256 * i, 256), 256)].T, dkv[...])
        place(1, i, value[:, :WIDTH])
        place(2, i, value[:, WIDTH:])
        return 0

    def q_rows(i, _):
        place(0, i, dot(seen[near, pl.ds(pl.multiple_of(256 * i, 256), 256)].T, dq[...]))
        return 0

    def chip_part(at):
        rows = pl.ds(at, 256)
        return dot_nt(dq[rows, :], wq[...]) + dot_nt(dkv[rows, :], wkv[...])

    def other_frames(i, _):
        at = pl.multiple_of(256 * i, 256)
        chip_out[pl.ds(at, 256), :] = chip_part(FRAMES + at).astype(BF16)
        return 0

    def own_frames(i, _):
        at = pl.multiple_of(256 * i, 256)
        chip_own[pl.ds(at, 256), :] = chip_part(at)
        return 0

    gains = gain[...].astype(F32).reshape(1, D)

    def norm_rows(i, total):
        at = pl.multiple_of(128 * i, 128)
        rows = pl.ds(at, 128)
        upstream = (
            chip_own[rows, :]
            + chip_in[rows, :].astype(F32)
            + halo[pl.ds(pl.multiple_of(at + 256 * (2 * c + y), 128), 128), :].astype(F32)
        )
        value = stem[rows, :]
        center = value - jnp.mean(value, axis=-1, keepdims=True)
        inverse = lax.rsqrt(jnp.mean(center * center, axis=-1, keepdims=True) + epsilon)
        unit_value = center * inverse
        scaled = upstream * gains
        inner = (
            scaled
            - jnp.mean(scaled, axis=-1, keepdims=True)
            - unit_value * jnp.mean(scaled * unit_value, axis=-1, keepdims=True)
        )
        low[rows, :] = (grad[rows, :] + inverse * inner).astype(BF16)
        return total + jnp.sum(upstream * unit_value, axis=0, keepdims=True)

    def skip_part(q):
        def skip_rows(i, _):
            value = dot(
                joint[pl.ds(pl.multiple_of(512 * i, 512), 512), :],
                low[:, SKIP_COLS * q : SKIP_COLS * (q + 1)],
            ).astype(BF16)
            for j in range(2):
                for m in range(2):
                    for half in range(2):
                        at = 256 * j + 128 * m + 32 * half
                        first, second = value[at : at + 32], value[at + 64 : at + 96]
                        skip_own[2 * q + half, i, j, m] = jnp.where(c == 0, first, second)
                        skip_out[2 * q + half, i, j, m] = jnp.where(c == 0, second, first)
            return 0

        lax.fori_loop(0, 4, skip_rows, 0)
        both = pl.ds(2 * q, 2)
        return links.send(skip_out.at[both], skip_r0.at[both], links.core)

    def skip_begin(q, copy):
        copy.wait_recv()
        for half in range(2):
            skips[q][half].add_core(skip_r0.at[2 * q + half])
            skips[q][half].send_first()

    def joined_part(i):
        value = dot_nt(low[...], wide_buf[pl.ds(256 * i, 256), :]).astype(BF16)
        out = o_in if i < 4 else o_skip
        out[:, pl.ds(256 * (i % 4), 256)] = value

    wo.begin(*got_wo)
    lax.fori_loop(0, 4, kv_rows, 0)
    join_v, join_k = join(2), join(1)
    for one, got in ((p0, got_p[0]), (p1, got_p[1]), (x0, got_x[0]), (x1, got_x[1])):
        one.begin(*got)
    rest_q.begin(*got_q)
    rest_z.begin(*got_z)
    got_small.wait()
    small.send()
    join_v.wait_recv()
    unit_v.send_first()
    join_k.wait_recv()
    unit_k.send_first()
    got_dq.wait()
    lax.fori_loop(0, 4, q_rows, 0)
    join_q = join(0)
    got_wskip = load(wskip_in, wide_buf)
    got_wq.wait()
    lax.fori_loop(0, 2, other_frames, 0)
    chip_core = links.send(chip_out, chip_in, links.core)
    join_q.wait_recv()
    unit_q.send_first()
    lax.fori_loop(0, 2, own_frames, 0)
    wo.turn_second()
    halo_y.wait_recv()
    halo_rest = links.send(part, part, links.core)
    small.turn()
    chip_core.wait_recv()
    got_stem.wait()
    got_grad.wait()
    halo_rest.wait_recv()
    total = lax.fori_loop(0, 4, norm_rows, jnp.zeros((1, D), F32))
    gain_steps[0] = jnp.concatenate(
        [total[:, 128 * i : 128 * (i + 1)] for i in range(8)], axis=0
    )
    gain_sum.send()
    got_joint.wait()
    p0.turn_third()
    rest_q.turn_third()
    skip_core0 = skip_part(0)
    skip_core1 = skip_part(1)
    skip_begin(0, skip_core0)
    skip_core2 = skip_part(2)
    p1.turn_third()
    skip_begin(1, skip_core1)
    skip_core3 = skip_part(3)
    rest_z.turn_third()
    skip_begin(2, skip_core2)
    wo.turn_third()
    skip_begin(3, skip_core3)
    got_wskip.wait()
    joined_part(0)
    small.turn()
    joined_part(1)
    gain_sum.turn()
    joined_part(2)
    joined_part(3)
    x0.turn_third()
    unit_v.turn_first()
    joined_part(4)
    joined_part(5)
    joined_part(6)
    joined_part(7)
    p0.turn_fourth()
    skips[0][0].turn_first()
    x1.turn_third()
    p1.turn_fourth()
    skips[1][0].turn_first()
    unit_q.turn_first()
    skips[2][0].turn_first()
    skips[0][1].turn_first()
    skips[3][0].turn_first()
    gain_sum.turn()
    p0.finish()
    p1.finish()
    skips[1][1].turn_first()
    unit_k.turn_first()
    x0.turn_fourth()
    skips[2][1].turn_first()
    unit_v.turn_second()
    skips[3][1].turn_first()
    rest_q.finish()
    small.turn()
    skips[0][0].turn_second()
    x1.turn_fourth()
    x0.finish()
    rest_z.finish()
    unit_q.turn_second()
    unit_v.turn_third()
    skips[1][0].turn_second()
    skips[0][1].turn_second()
    skips[2][0].turn_second()
    wo.finish()
    skips[1][1].turn_second()
    unit_q.turn_third()
    x1.finish()
    skips[3][0].turn_second()
    unit_v.turn_fourth()
    gain_sum.turn()
    skips[2][1].turn_second()
    take_up()
    skips[3][1].turn_second()
    small.turn()
    unit_k.turn_second()
    unit_q.turn_fourth()
    skips[0][0].finish()
    unit_k.turn_third()
    skips[1][0].finish()
    unit_v.finish()
    skips[0][1].finish()
    skips[2][0].finish()
    gain_sum.turn()
    skips[1][1].finish()
    skips[3][0].finish()
    unit_q.finish()
    skips[2][1].finish()
    gain_sum.turn()
    skips[3][1].finish()
    small.turn()
    unit_k.finish()
    links.drain()


def tail(late, small, dq, dkv, seen, wqkv, joint, stem, grad, gain, wskip):
    hbm, vm = pl.BlockSpec(memory_space=HBM), pl.BlockSpec(memory_space=VMEM)
    n_small = small.shape[0]
    out_shape = [
        jax.ShapeDtypeStruct((FRAMES, D), BF16),
        jax.ShapeDtypeStruct((FRAMES, D), BF16),
        jax.ShapeDtypeStruct((128, D), F32),
        jax.ShapeDtypeStruct((32, 4096), F32),
        jax.ShapeDtypeStruct((32, 3 * D), F32),
        jax.ShapeDtypeStruct((32, D), F32),
        jax.ShapeDtypeStruct((64, D), F32),
        jax.ShapeDtypeStruct((n_small, 128), F32),
        jax.ShapeDtypeStruct((8, 128), F32),
    ]
    low = lambda *shape: pltpu.VMEM(shape, BF16)
    full = lambda *shape: pltpu.VMEM(shape, F32)
    skip = (ROWS, SKIP_COLS)
    copies = 116
    scratch = [
        low(CHIP, WIDTH),
        low(CHIP + HALO, D),
        low(2 * D, D),
        low(D, WIDTH),
        low(D, D),
        low(2 * D, FRAMES),
        full(FRAMES, D),
        full(FRAMES, D),
        low(FRAMES, D),
        low(FRAMES, D),
        full(FRAMES, D),
        low(HALF, D),
        low(HALF, D),
        low(HALF, D),
        low(HALO + 2 * EDGE, D),
        low(FRAMES, D),
        low(2, 2, 2, 2, ROWS, D),
        low(2, 2, 2, ROWS, D),
        low(2, 2, ROWS, D),
        low(2, ROWS, D),
        low(ROWS, D),
        low(2, 2, 2, 2, ROWS, WIDTH),
        low(2, 4, 64, P_COLS),
        low(2, 4, 64, P_COLS),
        low(2, 6, 64, P_COLS),
        low(2, 2, 128, D - P_COLS),
        low(2, 2, 128, D - P_COLS),
        low(2, 128, D - P_COLS),
        low(128, D - P_COLS),
        low(2, 4, 32, X_COLS),
        low(2, 4, 32, X_COLS),
        low(2, 6, 32, X_COLS),
        low(2, 2, 64, 2 * D - X_COLS),
        low(2, 2, 64, 2 * D - X_COLS),
        low(2, 64, 2 * D - X_COLS),
        low(64, 2 * D - X_COLS),
        full(32, 2 * D),
        full(32, 2 * D),
        low(2, 4, 2, 2, ROWS, D),
        low(2, 4, 2, ROWS, D),
        low(2, 4, ROWS, D),
        low(2, 6, ROWS, D),
        low(2, 2, 2, ROWS, D),
        low(2, 2, 2, ROWS, D),
        low(2, 2, ROWS, D),
        low(2, ROWS, D),
        low(ROWS, D),
        low(2, 4, 2, 2, ROWS, WIDTH),
        low(2 * SKIPS, 4, 2, 2, *skip),
        low(2 * SKIPS, 4, 2, 2, *skip),
        low(2 * SKIPS, 4, 2, 2, *skip),
        low(2 * SKIPS, 4, 2, *skip),
        low(2 * SKIPS, 4, *skip),
        low(2 * SKIPS, 3, *skip),
        full(64, X_COLS),
        full(5, n_small, 128),
        full(5, n_small, 128),
        full(5, 8, 128),
        full(5, 8, 128),
        pltpu.SemaphoreType.DMA((28,)),
        pltpu.SemaphoreType.DMA((copies,)),
        pltpu.SemaphoreType.DMA((copies,)),
    ]
    return pl.pallas_call(
        tail_kernel,
        out_shape=out_shape,
        in_specs=[hbm] * 18 + [vm, hbm],
        out_specs=[vm] * 9,
        scratch_shapes=scratch,
        name="tail",
        cost_estimate=pl.CostEstimate(
            flops=17_000_000_000, bytes_accessed=60_000_000, transcendentals=0
        ),
        compiler_params=pltpu.CompilerParams(
            collective_id=0, has_side_effects=True, vmem_limit_bytes=VMEM_ALL
        ),
    )(
        *late[:6],
        *[value.reshape(2, 2, 64, 2 * D - X_COLS) for value in late[6:8]],
        *late[8:],
        small,
        dq,
        dkv,
        seen,
        wqkv,
        joint,
        stem,
        grad,
        gain,
        wskip,
    )


def finish_kernel(count, *refs):
    ins, small, gain = refs[:count], refs[count], refs[count + 1]
    outs, smalls = refs[count + 2 : 2 * count + 2], refs[2 * count + 2 : 2 * count + 6]
    held, loads, stores = refs[2 * count + 6 : 3 * count + 6], refs[-2], refs[-1]
    got = [pltpu.make_async_copy(a, b, loads.at[i]) for i, (a, b) in enumerate(zip(ins, held))]
    for copy in got:
        copy.start()
    device = lax.axis_index("rows") * 4 + lax.axis_index("seq")
    smalls[0][...] = small[pl.ds(device, 1), :]
    row, lane = device // 4, lax.rem(device, 4) * 32
    values = [gain[pl.ds(row, 1), :], small[pl.ds(32 + row, 1), :], small[pl.ds(40 + row, 1), :]]
    for out, value in zip(smalls[1:], values):
        out[...] = pltpu.roll(value, lax.rem(128 - lane, 128), 1)[:, :32]
    put = [pltpu.make_async_copy(a, b, stores.at[i]) for i, (a, b) in enumerate(zip(held, outs))]
    for copy, after in zip(got, put):
        copy.wait()
        after.start()
    for copy in put:
        copy.wait()


def finish(results, small, gain):
    hbm, vm = pl.BlockSpec(memory_space=HBM), pl.BlockSpec(memory_space=VMEM)
    count = len(results)
    return pl.pallas_call(
        functools.partial(finish_kernel, count),
        out_shape=[
            *[jax.ShapeDtypeStruct(a.shape, a.dtype) for a in results],
            *[jax.ShapeDtypeStruct((1, size), F32) for size in (128, 32, 32, 32)],
        ],
        in_specs=[hbm] * count + [vm] * 2,
        out_specs=[hbm] * count + [vm] * 4,
        scratch_shapes=[
            *[pltpu.VMEM(a.shape, a.dtype) for a in results],
            pltpu.SemaphoreType.DMA((count,)),
            pltpu.SemaphoreType.DMA((count,)),
        ],
        name="finish",
        compiler_params=pltpu.CompilerParams(vmem_limit_bytes=VMEM_ALL),
    )(*results, small, gain)


def swap_low(value):
    return lax.ppermute(value, "rows", [(r, r ^ 2) for r in range(8)])


def swap_x(value):
    return lax.ppermute(value, "rows", [(r, r ^ 1) for r in range(8)])


def swap_chip(value):
    return lax.ppermute(value, "seq", [(i, i ^ 2) for i in range(4)])


def body_chips(
    inputs,
    skip_feats,
    seg_ids,
    frame_valid,
    w_skip,
    gain_one,
    w_qkv,
    w_out,
    gain_two,
    w_up,
    b_up,
    w_down,
    b_down,
    cotangent,
):
    here = lax.axis_index("seq")
    c = here % 2
    heads = H // 2
    first, second_in, cot = inputs[0], skip_feats[0], cotangent[0]
    stem_out, normed_seen, q, kv, joint = front(first, second_in, w_skip, gain_one, w_qkv)
    attended, attended_t, lse = attend(q, kv, seg_ids, frame_valid, 128, 256, heads)
    output, middle_grad, grad_heads, small, *sums = middle(
        attended,
        stem_out,
        w_out,
        gain_two,
        w_up,
        w_down,
        b_up.reshape(32, 128),
        b_down,
        cot,
    )
    late = []
    swaps = (swap_x, swap_chip, swap_chip, swap_x, swap_low)
    for here, away, swap in zip(sums[::2], sums[1::2], swaps):
        late += [here, swap(away)]
    dq, dkv, output = attend_back(
        q, kv, grad_heads, attended_t, lse, seg_ids, frame_valid, output, 128, 256, heads
    )
    *results, small_sum, gain_sum = tail(
        late,
        small,
        dq,
        dkv,
        normed_seen,
        w_qkv,
        joint,
        stem_out,
        middle_grad,
        gain_one,
        w_skip,
    )
    *results, up_bias, gain_a, gain_b, down_bias = finish(results, small_sum, gain_sum)
    input_grad, skip_grad, down_share, up_share, qkv_share, out_share, skip_share = results
    return (
        output[None],
        input_grad[None],
        skip_grad[None],
        skip_share,
        gain_a.reshape(32),
        qkv_share,
        out_share,
        gain_b.reshape(32),
        up_share,
        up_bias.reshape(128),
        down_share,
        down_bias.reshape(32),
    )


def block_scores(q_blk, pos_blk, seg_blk, all_keys, seg_row, valid_row, slopes, score_scale):
    key_pos = jnp.arange(all_keys.shape[0])
    scores = (
        jnp.einsum("qhd,khd->hqk", q_blk, all_keys, preferred_element_type=jnp.float32)
        * score_scale
    )
    distance = jnp.abs(pos_blk[:, None] - key_pos[None, :]).astype(jnp.float32)
    scores = scores - slopes[:, None, None] * distance[None]
    allowed = (seg_blk[:, None] == seg_row[None, :]) & (
        (valid_row[None, :] == 1) | (pos_blk[:, None] == key_pos[None, :])
    )
    return jnp.where(allowed[None], scores, -jnp.inf)


def split_row(packed_row, heads_local):
    length = packed_row.shape[0]
    qkv_rows = packed_row.reshape(length, 3, heads_local, HD)
    return (qkv_rows[:, 0], qkv_rows[:, 1], qkv_rows[:, 2])


def attend_row(packed_row, seg_row, valid_row, slopes, heads_local, block_rows, score_scale):
    length = packed_row.shape[0]
    queries, all_keys, all_values = split_row(packed_row, heads_local)
    count = length // block_rows
    positions = jnp.arange(length)

    def one_block(block_in):
        q_blk, pos_blk, seg_blk = block_in
        scores = block_scores(
            q_blk, pos_blk, seg_blk, all_keys, seg_row, valid_row, slopes, score_scale
        )
        peak = jnp.max(scores, axis=-1, keepdims=True)
        log_total = peak + jnp.log(jnp.sum(jnp.exp(scores - peak), axis=-1, keepdims=True))
        attn_probs = jnp.exp(scores - log_total).astype(jnp.bfloat16)
        attended = jnp.einsum(
            "hqk,khd->qhd", attn_probs, all_values, preferred_element_type=jnp.float32
        )
        return (attended.astype(jnp.bfloat16), log_total[..., 0])

    attended, log_total = lax.map(
        one_block,
        (
            queries.reshape(count, block_rows, heads_local, HD),
            positions.reshape(count, block_rows),
            seg_row.reshape(count, block_rows),
        ),
    )
    return (attended.reshape(length, 1, heads_local * HD), log_total)


def attend_row_back(
    packed_row,
    log_total,
    grad_row,
    seg_row,
    valid_row,
    slopes,
    heads_local,
    block_rows,
    score_scale,
):
    length = packed_row.shape[0]
    queries, all_keys, all_values = split_row(packed_row, heads_local)
    count = length // block_rows
    positions = jnp.arange(length)
    grad_out = grad_row.reshape(count, block_rows, heads_local, HD)

    def one_block(carry, block_in):
        key_grad, value_grad = carry
        q_blk, pos_blk, seg_blk, total_blk, grad_blk = block_in
        scores = block_scores(
            q_blk, pos_blk, seg_blk, all_keys, seg_row, valid_row, slopes, score_scale
        )
        soft = jnp.exp(scores - total_blk[..., None])
        value_grad = value_grad + jnp.einsum(
            "hqk,qhd->khd", soft.astype(jnp.bfloat16), grad_blk, preferred_element_type=jnp.float32
        )
        prob_grad = jnp.einsum(
            "qhd,khd->hqk", grad_blk, all_values, preferred_element_type=jnp.float32
        )
        score_grad = (
            soft * (prob_grad - jnp.sum(soft * prob_grad, axis=-1, keepdims=True))
        ).astype(jnp.bfloat16)
        query_grad = (
            jnp.einsum("hqk,khd->qhd", score_grad, all_keys, preferred_element_type=jnp.float32)
            * score_scale
        )
        key_grad = (
            key_grad
            + jnp.einsum("hqk,qhd->khd", score_grad, q_blk, preferred_element_type=jnp.float32)
            * score_scale
        )
        return ((key_grad, value_grad), query_grad)

    zero_rows = jnp.zeros((length, heads_local, HD), jnp.float32)
    (key_grad, value_grad), query_grad = lax.scan(
        one_block,
        (zero_rows, zero_rows),
        (
            queries.reshape(count, block_rows, heads_local, HD),
            positions.reshape(count, block_rows),
            seg_row.reshape(count, block_rows),
            log_total,
            grad_out,
        ),
    )
    stacked = jnp.stack([query_grad.reshape(length, heads_local, HD), key_grad, value_grad], axis=1)
    return stacked.astype(jnp.bfloat16).reshape(length, 3, 1, heads_local * HD)


def body(
    inputs,
    skip_feats,
    seg_ids,
    frame_valid,
    w_skip,
    gain_one,
    w_qkv,
    w_out,
    gain_two,
    w_up,
    b_up,
    w_down,
    b_down,
    cotangent,
):
    parts = lax.axis_size("seq")
    heads_local = H // parts
    width_local = heads_local * HD
    rows_here = inputs.shape[0]
    frames = inputs.shape[1]
    length = frames * parts
    block_rows = min(512, length)
    score_scale = 1.0 / math.sqrt(HD)
    first_head = lax.axis_index("seq") * heads_local
    slopes = jnp.exp2(-8.0 * (first_head + jnp.arange(heads_local) + 1).astype(jnp.float32) / H)
    gain_first = gain_one.astype(jnp.float32)
    gain_second = gain_two.astype(jnp.float32)
    bias_up = b_up.astype(jnp.float32)
    joined = jnp.concatenate([inputs, skip_feats], axis=-1)
    stem_out = jnp.einsum("rfc,cd->rfd", joined, w_skip, preferred_element_type=jnp.float32)
    unit_one, inverse_one, normed = norm_forward(stem_out, gain_first)
    normed = normed.astype(jnp.bfloat16)
    packed = jnp.einsum("rfd,de->rfe", normed, w_qkv, preferred_element_type=jnp.float32).astype(
        jnp.bfloat16
    )
    packed = packed.reshape(rows_here, frames, 3, parts, width_local)
    by_heads = lax.all_to_all(packed, "seq", split_axis=3, concat_axis=1, tiled=True)

    def forward_row(row_data):
        return attend_row(
            row_data[0], row_data[1], row_data[2], slopes, heads_local, block_rows, score_scale
        )

    attended, log_total = lax.map(forward_row, (by_heads, seg_ids, frame_valid))
    by_frames = lax.all_to_all(attended, "seq", split_axis=1, concat_axis=2, tiled=True)
    mixed_out = by_frames.reshape(rows_here, frames, D)
    middle = stem_out + jnp.einsum(
        "rfd,de->rfe", mixed_out, w_out, preferred_element_type=jnp.float32
    )
    unit_two, inverse_two, second = norm_forward(middle, gain_second)
    second = second.astype(jnp.bfloat16)
    hidden = jnp.einsum("rfd,dk->rfk", second, w_up, preferred_element_type=jnp.float32) + bias_up
    active_full, gelu_back = jax.vjp(gelu_exact, hidden)
    active = active_full.astype(jnp.bfloat16)
    result = (
        middle
        + jnp.einsum("rfk,kd->rfd", active, w_down, preferred_element_type=jnp.float32)
        + b_down.astype(jnp.float32)
    )
    output = result.astype(jnp.bfloat16)
    cot_full = cotangent.astype(jnp.float32)
    down_grad = jnp.einsum("rfk,rfd->kd", active, cotangent, preferred_element_type=jnp.float32)
    bias_down_grad = jnp.sum(cot_full, axis=(0, 1))
    active_grad = jnp.einsum("rfd,kd->rfk", cotangent, w_down, preferred_element_type=jnp.float32)
    hidden_grad = gelu_back(active_grad)[0].astype(jnp.bfloat16)
    up_grad = jnp.einsum("rfd,rfk->dk", second, hidden_grad, preferred_element_type=jnp.float32)
    bias_up_grad = jnp.sum(hidden_grad.astype(jnp.float32), axis=(0, 1))
    second_grad = jnp.einsum("rfk,dk->rfd", hidden_grad, w_up, preferred_element_type=jnp.float32)
    middle_part, gain_two_grad = norm_backward(second_grad, unit_two, inverse_two, gain_second)
    middle_grad = cot_full + middle_part
    middle_low = middle_grad.astype(jnp.bfloat16)
    out_grad = jnp.einsum("rfd,rfe->de", mixed_out, middle_low, preferred_element_type=jnp.float32)
    mixed_grad = jnp.einsum(
        "rfe,de->rfd", middle_low, w_out, preferred_element_type=jnp.float32
    ).astype(jnp.bfloat16)
    grad_heads = lax.all_to_all(
        mixed_grad.reshape(rows_here, frames, parts, width_local),
        "seq",
        split_axis=2,
        concat_axis=1,
        tiled=True,
    )

    def backward_row(row_data):
        return attend_row_back(
            row_data[0],
            row_data[1],
            row_data[2],
            row_data[3],
            row_data[4],
            slopes,
            heads_local,
            block_rows,
            score_scale,
        )

    packed_grad = lax.map(backward_row, (by_heads, log_total, grad_heads, seg_ids, frame_valid))
    packed_back = lax.all_to_all(packed_grad, "seq", split_axis=1, concat_axis=3, tiled=True)
    packed_back = packed_back.reshape(rows_here, frames, 3 * D)
    qkv_grad = jnp.einsum("rfd,rfe->de", normed, packed_back, preferred_element_type=jnp.float32)
    normed_grad = jnp.einsum("rfe,de->rfd", packed_back, w_qkv, preferred_element_type=jnp.float32)
    stem_part, gain_one_grad = norm_backward(normed_grad, unit_one, inverse_one, gain_first)
    stem_low = (middle_grad + stem_part).astype(jnp.bfloat16)
    skip_w_grad = jnp.einsum("rfc,rfd->cd", joined, stem_low, preferred_element_type=jnp.float32)
    joined_grad = jnp.einsum("rfd,cd->rfc", stem_low, w_skip, preferred_element_type=jnp.float32)
    input_grad = joined_grad[..., :D].astype(jnp.bfloat16)
    skip_grad = joined_grad[..., D:].astype(jnp.bfloat16)
    (
        skip_share,
        gain_one_share,
        qkv_share,
        out_share,
        gain_two_share,
        up_share,
        bias_up_share,
        down_share,
        bias_down_share,
    ) = (
        lax.psum_scatter(skip_w_grad, ("rows", "seq"), scatter_dimension=0, tiled=True),
        lax.psum_scatter(gain_one_grad, ("rows", "seq"), scatter_dimension=0, tiled=True),
        lax.psum_scatter(qkv_grad, ("rows", "seq"), scatter_dimension=0, tiled=True),
        lax.psum_scatter(out_grad, ("rows", "seq"), scatter_dimension=0, tiled=True),
        lax.psum_scatter(gain_two_grad, ("rows", "seq"), scatter_dimension=0, tiled=True),
        lax.psum_scatter(up_grad, ("rows", "seq"), scatter_dimension=0, tiled=True),
        lax.psum_scatter(bias_up_grad, ("rows", "seq"), scatter_dimension=0, tiled=True),
        lax.psum_scatter(down_grad, ("rows", "seq"), scatter_dimension=0, tiled=True),
        lax.psum_scatter(bias_down_grad, ("rows", "seq"), scatter_dimension=0, tiled=True),
    )
    return (
        output,
        input_grad,
        skip_grad,
        skip_share,
        gain_one_share,
        qkv_share,
        out_share,
        gain_two_share,
        up_share,
        bias_up_share,
        down_share,
        bias_down_share,
    )


def solution(mesh):
    fits = (mesh.shape["rows"], mesh.shape["seq"]) == (8, 4)
    return jax.shard_map(
        body_chips if fits else body,
        mesh=mesh,
        in_specs=(
            P("rows", "seq", None),
            P("rows", "seq", None),
            P("rows", None),
            P("rows", None),
            P(),
            P(),
            P(),
            P(),
            P(),
            P(),
            P(),
            P(),
            P(),
            P("rows", "seq", None),
        ),
        out_specs=(
            P("rows", "seq", None),
            P("rows", "seq", None),
            P("rows", "seq", None),
            P(("rows", "seq"), None),
            P(("rows", "seq")),
            P(("rows", "seq"), None),
            P(("rows", "seq"), None),
            P(("rows", "seq")),
            P(("rows", "seq"), None),
            P(("rows", "seq")),
            P(("rows", "seq"), None),
            P(("rows", "seq")),
        ),
        check_vma=False,
    )
```
